128 devices in a mesh: dp: 8 (over z, x_hi), wide: 8 (over y, core), narrow: 2 (over x_lo).
Axes of the slice: x: 4 (x_hi: 2, x_lo: 2; x = x_hi * 2 + x_lo), y: 4, z: 4, core: 2. Of those that a mesh axis runs over, the one named last changes fastest.
Arguments:
- layer_input: bfloat16 [24576, 1536], P(('dp', 'wide'), 'narrow'), may hold values from -90 to 90
- text_states: bfloat16 [16, 64, 1536], P('dp', None, 'narrow'), may hold values from -6 to 6
- cotangent: bfloat16 [24576, 1536], P(('dp', 'wide'), 'narrow'), may hold values from -6 to 6
- first_gain: bfloat16 [1536], P('narrow'), may hold values from 0.5 to 1.5
- first_shift: bfloat16 [1536], P('narrow'), may hold values from -3 to 3
- query_weight: bfloat16 [1536, 1536], P('narrow', 'wide'), may hold values from -0.15625 to 0.15625
- key_weight: bfloat16 [1536, 1536], P('narrow', 'wide'), may hold values from -0.15625 to 0.15625
- value_weight: bfloat16 [1536, 1536], P('narrow', 'wide'), may hold values from -0.15625 to 0.15625
- output_weight: bfloat16 [1536, 1536], P('wide', 'narrow'), may hold values from -1 to 1
- second_gain: bfloat16 [1536], P('narrow'), may hold values from 0.5 to 1.5
- second_shift: bfloat16 [1536], P('narrow'), may hold values from -3 to 3
- cross_query: bfloat16 [1536, 1536], P('narrow', 'wide'), may hold values from -0.15625 to 0.15625
- cross_key: bfloat16 [1536, 1536], P('narrow', 'wide'), may hold values from -0.15625 to 0.15625
- cross_value: bfloat16 [1536, 1536], P('narrow', 'wide'), may hold values from -0.15625 to 0.15625
- cross_output: bfloat16 [1536, 1536], P('wide', 'narrow'), may hold values from -0.625 to 0.625
- third_gain: bfloat16 [1536], P('narrow'), may hold values from 0.5 to 1.5
- third_shift: bfloat16 [1536], P('narrow'), may hold values from -3 to 3
- expand_weight: bfloat16 [1536, 6144], P('narrow', 'wide'), may hold values from -0.15625 to 0.15625
- contract_weight: bfloat16 [6144, 1536], P('wide', 'narrow'), may hold values from -0.078125 to 0.078125
Outputs:
- layer_output: bfloat16 [24576, 1536], P(('dp', 'wide'), 'narrow')
- input_grad: float32 [24576, 1536], P(('dp', 'wide'), 'narrow')
- text_grad: float32 [16, 64, 1536], P('dp', None, 'narrow')
- first_gain_grad: float32 [1536], P('narrow')
- first_shift_grad: float32 [1536], P('narrow')
- query_weight_grad: float32 [1536, 1536], P('narrow', 'wide')
- key_weight_grad: float32 [1536, 1536], P('narrow', 'wide')
- value_weight_grad: float32 [1536, 1536], P('narrow', 'wide')
- output_weight_grad: float32 [1536, 1536], P('wide', 'narrow')
- second_gain_grad: float32 [1536], P('narrow')
- second_shift_grad: float32 [1536], P('narrow')
- cross_query_grad: float32 [1536, 1536], P('narrow', 'wide')
- cross_key_grad: float32 [1536, 1536], P('narrow', 'wide')
- cross_value_grad: float32 [1536, 1536], P('narrow', 'wide')
- cross_output_grad: float32 [1536, 1536], P('wide', 'narrow')
- third_gain_grad: float32 [1536], P('narrow')
- third_shift_grad: float32 [1536], P('narrow')
- expand_weight_grad: float32 [1536, 6144], P('narrow', 'wide')
- contract_weight_grad: float32 [6144, 1536], P('wide', 'narrow')
The draws below stay inside these ranges and needn't reach their ends.
All inputs are finite; a program needn't handle non-finite values.
Results may differ from the reference program's by a relative error of at most 0.035.
Values may be sent and summed in bfloat16 or wider, within the bound.
A program may use at most 256 MiB of HBM per device.

```python
import math
import jax
import jax.numpy as jnp
from jax import lax

D = 1536
HEADS = 24
HDIM = 64
FF = 6144
TEXT = 64
QBLOCK = 512
LEN = 1536
HD = 1536
CLIPS = 16
TOKENS = 24576


def draw_layer_input(key, part):
    base_key, row_key, col_key = jax.random.split(key, 3)
    position = jnp.arange(D).astype(jnp.float32) / D
    col_scale = jnp.exp(jax.random.uniform(col_key, (1, D), minval=-1.15, maxval=1.15) + 1.1 * (position[None, :] - 0.5))
    row_scale = jnp.exp(jax.random.uniform(row_key, (TOKENS, 1), minval=-0.92, maxval=1.38))
    base = jnp.clip(jax.random.normal(base_key, (TOKENS, D)), -4.0, 4.0)
    return (base * row_scale * col_scale).astype(jnp.bfloat16)


def block_levels(rng, shape, cuts, least, largest):
    level = 1.0
    for axis_at, blocks in cuts:
        steps = jax.random.uniform(jax.random.fold_in(jax.random.fold_in(rng, 6), axis_at), (blocks,), jnp.float32, least / len(cuts), largest / len(cuts))
        level = level * jnp.repeat(jnp.exp(steps), shape[axis_at] // blocks).reshape((-1,) + (1,) * (len(shape) - 1 - axis_at))
    return level


def noise(own_key, dims, width, bound, pieces=(), held_as=jnp.bfloat16):
    level = block_levels(own_key, dims, pieces, -0.22, 0.18) if pieces else 1.0
    result = jax.random.normal(own_key, dims, jnp.float32) * width * level
    return jnp.minimum(jnp.maximum(result, -bound), bound).astype(held_as)


def setup_inputs(seed: int = 0) -> dict:
    splits = jax.random.split(jax.random.key(seed), 20)
    return {
        "layer_input": draw_layer_input(jax.random.fold_in(splits[19], 71), 0),
        "text_states": noise(splits[1], (CLIPS, TEXT, D), 1.0, 6.0, ((0, 8), (2, 2))),
        "cotangent": noise(splits[2], (TOKENS, D), 1.0, 6.0, ((0, 64), (1, 2))),
        "first_gain": jnp.clip(1.0 + 0.1 * jax.random.normal(splits[3], (D,), jnp.float32), 0.5, 1.5).astype(jnp.bfloat16),
        "first_shift": noise(splits[4], (D,), 0.5, 3.0, ((0, 2),)),
        "query_weight": noise(splits[5], (D, HD), D ** -0.5, 0.15625, ((0, 2), (1, 8))),
        "key_weight": noise(splits[6], (D, HD), D ** -0.5, 0.15625, ((0, 2), (1, 8))),
        "value_weight": noise(splits[7], (D, HD), D ** -0.5, 0.15625, ((0, 2), (1, 8))),
        "output_weight": noise(splits[8], (HD, D), (HD * 32 // LEN) ** -0.5, 1.0, ((0, 8), (1, 2))),
        "second_gain": jnp.clip(1.0 + 0.1 * jax.random.normal(splits[9], (D,), jnp.float32), 0.5, 1.5).astype(jnp.bfloat16),
        "second_shift": noise(splits[10], (D,), 0.5, 3.0, ((0, 2),)),
        "cross_query": noise(splits[11], (D, HD), D ** -0.5, 0.15625, ((0, 2), (1, 8))),
        "cross_key": noise(splits[12], (D, HD), D ** -0.5, 0.15625, ((0, 2), (1, 8))),
        "cross_value": noise(splits[13], (D, HD), D ** -0.5, 0.15625, ((0, 2), (1, 8))),
        "cross_output": noise(splits[14], (HD, D), (HD * 4 // TEXT) ** -0.5, 0.625, ((0, 8), (1, 2))),
        "third_gain": jnp.clip(1.0 + 0.1 * jax.random.normal(splits[15], (D,), jnp.float32), 0.5, 1.5).astype(jnp.bfloat16),
        "third_shift": noise(splits[16], (D,), 0.5, 3.0, ((0, 2),)),
        "expand_weight": noise(splits[17], (D, FF), D ** -0.5, 0.15625, ((0, 2), (1, 8))),
        "contract_weight": noise(splits[18], (FF, D), FF ** -0.5, 0.078125, ((0, 8), (1, 2))),
    }


@jax.custom_vjp
def low(v):
    return lax.optimization_barrier(v.astype(jnp.bfloat16)).astype(jnp.float32)

@jax.custom_vjp
def low_back(v):
    return v

def low_keep(v):
    return (low(v), None)

def low_pass(kept, grad):
    return (grad,)

def back_keep(v):
    return (v, None)

def back_low(kept, grad):
    return (low(grad),)
low.defvjp(low_keep, low_pass)
low_back.defvjp(back_keep, back_low)
EPSILON = 1e-05
NEGATIVE = -1e+30
HIGHEST = lax.Precision.HIGHEST
ROOT_HALF = 0.7071067811865476

def product(left, right):
    return jnp.dot(left, right, precision=HIGHEST)

def layer_norm(values, gain, shift):
    average = lax.optimization_barrier(jnp.mean(values, axis=-1, keepdims=True))
    variance = lax.optimization_barrier(jnp.mean(values * values, axis=-1, keepdims=True)) - average * average
    return (values - average) * lax.rsqrt(variance + EPSILON) * gain + shift

def gelu_exact(values):
    return 0.5 * values * (1.0 + lax.erf(values * ROOT_HALF))

def attention(queries, keys, values, causal):
    length = queries.shape[0]
    block_count = length // QBLOCK
    split_q = queries.reshape(block_count, QBLOCK, HEADS, HDIM)
    split_k = keys.reshape(keys.shape[0], HEADS, HDIM)
    split_v = values.reshape(values.shape[0], HEADS, HDIM)
    factor = 1.0 / math.sqrt(HDIM)
    offsets = jnp.arange(block_count).astype(jnp.int32) * QBLOCK

    def per_block(portion, offset):
        scores = low_back(jnp.einsum('qhd,khd->hqk', portion, split_k, precision=HIGHEST) * factor)
        if causal:
            row_ids = offset + jnp.arange(QBLOCK).astype(jnp.int32)
            col_ids = jnp.arange(split_k.shape[0]).astype(jnp.int32)
            scores = jnp.where((row_ids[:, None] >= col_ids[None, :])[None], scores, NEGATIVE)
        weights = low(jax.nn.softmax(scores, axis=-1))
        return jnp.einsum('hqk,khd->qhd', weights, split_v, precision=HIGHEST)
    checked = jax.checkpoint(per_block)

    def mapped(inputs):
        return checked(inputs[0], inputs[1])
    blended = lax.map(mapped, (split_q, offsets))
    return blended.reshape(length, HEADS * HDIM)

def clip_layer(params, clip_in, clip_text):
    first_gain, first_shift, query_weight, key_weight, value_weight, output_weight, second_gain, second_shift, cross_query, cross_key, cross_value, cross_output, third_gain, third_shift, expand_weight, contract_weight = params
    normed = low(layer_norm(clip_in, first_gain, first_shift))
    queries = low(low_back(product(normed, query_weight)))
    keys = low(low_back(product(normed, key_weight)))
    values = low(low_back(product(normed, value_weight)))
    attended = low(low_back(attention(queries, keys, values, True)))
    middle_one = clip_in + low_back(product(attended, output_weight))
    normed_two = low(layer_norm(middle_one, second_gain, second_shift))
    cross_q = low(low_back(product(normed_two, cross_query)))
    text_keys = low(low_back(product(clip_text, cross_key)))
    text_values = low(low_back(product(clip_text, cross_value)))
    crossed = low(low_back(attention(cross_q, text_keys, text_values, False)))
    middle_two = middle_one + low_back(product(crossed, cross_output))
    normed_three = low(layer_norm(middle_two, third_gain, third_shift))
    expanded = low_back(product(normed_three, expand_weight))
    activated = low(gelu_exact(expanded))
    return middle_two + low_back(product(activated, contract_weight))

def whole_layer(params, inputs, texts):
    clips_in = inputs.reshape(CLIPS, LEN, D)
    checked = jax.checkpoint(clip_layer)

    def advance(carry, pair_in):
        return (carry, checked(params, pair_in[0], pair_in[1]))
    _, outputs = lax.scan(advance, jnp.zeros((), jnp.float32), (clips_in, texts))
    return outputs.reshape(CLIPS * LEN, D)

def reference(layer_input, text_states, cotangent, first_gain, first_shift, query_weight, key_weight, value_weight, output_weight, second_gain, second_shift, cross_query, cross_key, cross_value, cross_output, third_gain, third_shift, expand_weight, contract_weight):
    params = tuple((weight.astype(jnp.float32) for weight in (first_gain, first_shift, query_weight, key_weight, value_weight, output_weight, second_gain, second_shift, cross_query, cross_key, cross_value, cross_output, third_gain, third_shift, expand_weight, contract_weight)))
    inputs = layer_input.astype(jnp.float32)
    texts = text_states.astype(jnp.float32)
    outputs, pullback = jax.vjp(whole_layer, params, inputs, texts)
    grads, input_grad, text_grad = pullback(cotangent.astype(jnp.float32))
    return (outputs.astype(jnp.bfloat16), input_grad, text_grad, grads[0], grads[1], grads[2], grads[3], grads[4], grads[5], grads[6], grads[7], grads[8], grads[9], grads[10], grads[11], grads[12], grads[13], grads[14], grads[15])
```

```python
import functools
import math

import jax
import jax.numpy as jnp
from jax import lax
from jax.experimental import pallas as pl
from jax.experimental.pallas import tpu as pltpu
from jax.sharding import PartitionSpec as P

D = 1536
HALF = 768
HDIM = 64
HEADS = 3
COLS = HEADS * HDIM
BLOCK = 192
EPSILON = 1e-05
NEGATIVE = -1e30
ROOT_HALF = 0.7071067811865476
GAUSS_NORM = 0.3989422804014327
MESH = pl.DeviceIdType.MESH
VMEM = pltpu.VMEM
ANY = pl.ANY
bf16, f32 = jnp.bfloat16, jnp.float32


def dot(a, b):
    return lax.dot_general(a, b, (((1,), (0,)), ((), ())), preferred_element_type=f32)


def dot_flip(a, b):
    return lax.dot_general(a, b, (((1,), (1,)), ((), ())), preferred_element_type=f32)


def outer(a, b):
    return lax.dot_general(a, b, (((0,), (0,)), ((), ())), preferred_element_type=f32)


class Place:
    def __init__(self):
        self.dp, self.w, self.n = (lax.axis_index(a) for a in ("dp", "wide", "narrow"))
        self.y, self.c = lax.div(self.w, 2), lax.rem(self.w, 2)
        self.z, self.s = lax.div(self.dp, 2), lax.rem(self.dp, 2)
        self.up, self.down = lax.rem(self.y + 1, 4), lax.rem(self.y + 3, 4)
        self.across = 3 - self.y
        self.moved = lax.rem(lax.div(self.y, 2) + self.n, 2)
        self.clip = lax.div(self.y, 2)

    def spot(self, y, c):
        moved = lax.rem(lax.div(y, 2) + self.n, 2)
        return (lax.rem(y + moved, 2) * 2 + c) * 2 + moved

    def rows(self, y, c, start=0, size=BLOCK):
        return pl.ds(pl.multiple_of(self.spot(y, c) * BLOCK + start, 32), size)

    def half(self, n):
        return pl.ds(pl.multiple_of(n * HALF, HALF), HALF)

    def at_y(self, y):
        return {"wide": y * 2 + self.c}

    def core(self):
        return {"wide": self.y * 2 + 1 - self.c}

    def x(self):
        return {"narrow": 1 - self.n}

    def at_z(self, k):
        return {"dp": lax.rem(self.z + k, 4) * 2 + self.s}

    def at_dp(self, k):
        return {"dp": lax.rem(self.dp + k, 8)}

    def at_x(self, ds, dn):
        return {"dp": self.z * 2 + lax.rem(self.s + ds, 2), "narrow": lax.rem(self.n + dn, 2)}


def remote(src, dst, send, recv, peer):
    return pltpu.make_async_remote_copy(
        src_ref=src, dst_ref=dst, send_sem=send, recv_sem=recv, device_id=peer, device_id_type=MESH
    )


def greet(peers):
    barrier = pltpu.get_barrier_semaphore()
    for peer in peers:
        pl.semaphore_signal(barrier, inc=1, device_id=peer, device_id_type=MESH)
    pl.semaphore_wait(barrier, len(peers))


class Swap:
    def __init__(self, array, axis):
        self.ins = [array]
        shape = list(array.shape)
        shape[axis] *= 2
        self.outs = [jax.ShapeDtypeStruct(tuple(shape), array.dtype)]
        self.axis, self.copies, self.locals = axis, 1, 1

    def peers(self, at):
        return [("x", at.x())]

    def moves(self, at, ins, outs):
        where = (slice(None),) * self.axis + (pl.ds(pl.multiple_of(at.n * ins[0].shape[self.axis], ins[0].shape[self.axis]), ins[0].shape[self.axis]),)
        dst = outs[0].at[where]
        return [(ins[0], dst, at.x())], [(ins[0], dst)]


class Text:
    def __init__(self, array, back=False):
        self.ins, self.back, self.copies, self.locals = [array], back, 1, 1
        shape = (2, 64, HALF) if back else (64, D)
        self.outs = [jax.ShapeDtypeStruct(shape, array.dtype)]

    def peers(self, at):
        return [("x", at.x())]

    def moves(self, at, ins, outs):
        src, dst = ins[0], outs[0]
        if self.back:
            there = dst.at[at.n]
            return [(src.at[:, at.half(1 - at.n)], there, at.x())], [(src.at[:, at.half(at.n)], there)]
        there = dst.at[:, at.half(at.n)]
        return [(src.at[1 - at.n], there, at.x())], [(src.at[at.n], there)]


class SumZ:
    def __init__(self, array, by_rows):
        self.by_rows, self.copies, self.locals = by_rows, 3, 0
        rows, cols = array.shape
        shape = (2, 4, rows // 8, cols) if by_rows else (4, rows // 4, cols)
        self.ins = [array.reshape(shape)]
        kept = (2, rows // 8, cols) if by_rows else (rows // 4, cols)
        self.outs = [jax.ShapeDtypeStruct((3, *kept), array.dtype)]

    def peers(self, at):
        return [(f"z{k}", at.at_z(k)) for k in (1, 2, 3)]

    def moves(self, at, ins, outs):
        out = []
        for k in (1, 2, 3):
            q = lax.rem(at.z + k, 4)
            src = ins[0].at[:, q] if self.by_rows else ins[0].at[q]
            out.append((src, outs[0].at[k - 1], at.at_z(k)))
        return out, []

    def finish(self, outs):
        z = lax.div(lax.axis_index("dp"), 2)
        own = lax.dynamic_index_in_dim(self.ins[0], z, 1 if self.by_rows else 0, False)
        return (own.astype(f32) + outs[0].astype(f32).sum(axis=0)).astype(bf16)


class SumX:
    def __init__(self, array, by_rows):
        self.by_rows, self.copies, self.locals = by_rows, 3, 0
        if by_rows:
            two, rows, cols = array.shape
            self.ins, kept = [array.reshape(2, 2, rows // 2, cols)], (rows // 2, cols)
        else:
            rows, cols = array.shape
            self.ins, kept = [array.reshape(2, rows // 2, cols)], (rows // 2, HALF)
        self.outs = [jax.ShapeDtypeStruct((3, *kept), array.dtype)]

    order = ((0, 1), (1, 0), (1, 1))

    def peers(self, at):
        return [(f"x{a}{b}", at.at_x(a, b)) for a, b in self.order]

    def moves(self, at, ins, outs):
        out = []
        for i, (a, b) in enumerate(self.order):
            s, n = lax.rem(at.s + a, 2), lax.rem(at.n + b, 2)
            src = ins[0].at[n, s] if self.by_rows else ins[0].at[s, :, at.half(n)]
            out.append((src, outs[0].at[i], at.at_x(a, b)))
        return out, []

    def finish(self, outs):
        s, n = lax.rem(lax.axis_index("dp"), 2), lax.axis_index("narrow")
        if self.by_rows:
            own = lax.dynamic_index_in_dim(lax.dynamic_index_in_dim(self.ins[0], n, 0, False), s, 0, False)
        else:
            own = lax.dynamic_slice_in_dim(lax.dynamic_index_in_dim(self.ins[0], s, 0, False), n * HALF, HALF, 1)
        return (own.astype(f32) + outs[0].astype(f32).sum(axis=0)).astype(bf16)


class Spread:
    def __init__(self, array):
        self.ins, self.copies, self.locals = [array], 7, 1
        self.outs = [jax.ShapeDtypeStruct((8, *array.shape), array.dtype)]

    def peers(self, at):
        return [(f"d{k}", at.at_dp(k)) for k in range(1, 8)]

    def moves(self, at, ins, outs):
        dst = outs[0].at[at.dp]
        return [(ins[0], dst, at.at_dp(k)) for k in range(1, 8)], [(ins[0], dst)]

    def finish(self, outs):
        eight, rows, cols = outs[0].shape
        return outs[0].reshape(eight * rows, cols).astype(f32)


class ToRing:
    def __init__(self, array):
        self.ins, self.copies, self.locals = [array], 7, 1
        self.outs = [jax.ShapeDtypeStruct((8, *array.shape), array.dtype)]

    def peers(self, at):
        return [(f"w{k}", {"wide": lax.rem(at.w + k, 8)}) for k in range(1, 8)]

    def moves(self, at, ins, outs):
        dst = outs[0].at[at.w]
        return [(ins[0], dst, peer) for _, peer in self.peers(at)], [(ins[0], dst)]


class ToClips:
    def __init__(self, array):
        self.ins, self.copies, self.locals = [array], 15, 1
        self.outs = [jax.ShapeDtypeStruct((8, 2, array.shape[0], HALF), array.dtype)]

    order = tuple((k, b) for k in range(8) for b in range(2))[1:]

    def peers(self, at):
        return [(f"c{k}{b}", {**at.at_dp(k), "narrow": lax.rem(at.n + b, 2)}) for k, b in self.order]

    def moves(self, at, ins, outs):
        dst = outs[0].at[at.dp, at.n]
        far = []
        for (k, b), (_, peer) in zip(self.order, self.peers(at)):
            far.append((ins[0].at[:, at.half(lax.rem(at.n + b, 2))], dst, peer))
        return far, [(ins[0].at[:, at.half(at.n)], dst)]


class Relay:
    def __init__(self, array, back=False):
        self.ins, self.back, self.copies, self.locals = [array], back, 2, 1
        shape = (384, HALF) if back else (BLOCK, D)
        self.outs = [jax.ShapeDtypeStruct(shape, array.dtype)]

    def peers(self, at):
        return [
            ("x", at.x()),
            ("a0", {"wide": at.across * 2 + at.c}),
            ("a1", {"wide": at.across * 2 + at.c, "narrow": 1 - at.n}),
        ]


def relay_run(relay, at, src, dst, send, recv, local, base, finish):
    mine, other = at.half(at.n), at.half(1 - at.n)
    over = at.across * 2 + at.c
    if relay.back:
        row = pl.ds(pl.multiple_of(at.moved * BLOCK, BLOCK), BLOCK)
        to = recv.at[base + at.moved]
        own = src.at[:, mine], src.at[:, other]
        land = dst.at[0:BLOCK], dst.at[BLOCK : 2 * BLOCK]
    else:
        row = mine
        to = recv.at[base + at.n]
        own = src.at[0:BLOCK], src.at[BLOCK : 2 * BLOCK]
        land = dst.at[:, at.half(0)], dst.at[:, at.half(1)]
    target = dst.at[row] if relay.back else dst.at[:, row]

    def arrive(slot, part):
        return remote(own[0], part, send.at[base], recv.at[base + slot], at.x())

    @pl.when(at.moved == 0)
    def _():
        stay = pltpu.make_async_copy(own[0], target, local)
        if relay.back:
            go = remote(own[1], target, send.at[base], to, at.x())
        else:
            go = remote(own[1], target, send.at[base], to, {"wide": over})
        if not finish:
            go.start()
            stay.start()
        else:
            stay.wait()
            go.wait_send()
            if relay.back:
                arrive(1, land[1]).wait_recv()
            else:
                arrive(1 - at.n, dst.at[:, other]).wait_recv()

    @pl.when(at.moved == 1)
    def _():
        if relay.back:
            first = remote(own[1], target, send.at[base], to, {"wide": over, "narrow": 1 - at.n})
            second = remote(own[0], target, send.at[base + 1], to, {"wide": over})
        else:
            first = remote(own[1], target, send.at[base], to, {"wide": over, "narrow": 1 - at.n})
            second = remote(own[0], target, send.at[base + 1], to, at.x())
        if not finish:
            first.start()
            second.start()
        else:
            first.wait_send()
            second.wait_send()
            arrive(0, land[0]).wait_recv()
            arrive(1, land[1]).wait_recv()


def call(body, number, ins, outs, scratch=(), beside=(), peers=None, spaces=None):
    spaces = spaces or [VMEM] * len(ins)
    copies = sum(b.copies for b in beside)
    locals_ = sum(b.locals for b in beside)
    side_ins = [a for b in beside for a in b.ins]
    side_outs = [a for b in beside for a in b.outs]
    n_in, n_out, n_scratch = len(ins), len(outs), len(scratch)

    def kernel(*refs):
        at = Place()
        refs = list(refs)

        def take(count):
            out = refs[:count]
            del refs[:count]
            return out

        main_in, side_in = take(n_in), take(len(side_ins))
        main_out, side_out, kept = take(n_out), take(len(side_outs)), take(n_scratch)
        send, recv, local = take(3)
        known = dict(peers(at)) if peers else {}
        for b in beside:
            known.update(dict(b.peers(at)))
        if known:
            greet(list(known.values()))
        slot, place, todo = 0, 0, []
        for b in beside:
            i, o = [side_in.pop(0) for _ in b.ins], [side_out.pop(0) for _ in b.outs]
            if isinstance(b, Relay):
                run = functools.partial(relay_run, b, at, i[0], o[0], send, recv, local.at[place], slot)
                run(False)
                todo.append(functools.partial(run, True))
                slot, place = slot + 2, place + 1
                continue
            far, near = b.moves(at, i, o)
            for src, dst, peer in far:
                copy = remote(src, dst, send.at[slot], recv.at[slot], peer)
                copy.start()
                todo.append(copy.wait)
                slot += 1
            for src, dst in near:
                copy = pltpu.make_async_copy(src, dst, local.at[place])
                copy.start()
                todo.append(copy.wait)
                place += 1
        if body:
            body(at, main_in, main_out, kept)
        for wait in todo:
            wait()

    results = pl.pallas_call(
        kernel,
        out_shape=tuple(outs) + tuple(side_outs),
        in_specs=[pl.BlockSpec(memory_space=s) for s in spaces] + [pl.BlockSpec(memory_space=ANY)] * len(side_ins),
        out_specs=tuple([pl.BlockSpec(memory_space=VMEM)] * len(outs) + [pl.BlockSpec(memory_space=ANY)] * len(side_outs)),
        scratch_shapes=[
            *scratch,
            pltpu.SemaphoreType.DMA((max(copies, 1),)),
            pltpu.SemaphoreType.DMA((max(copies, 1),)),
            pltpu.SemaphoreType.DMA((max(locals_, 1),)),
        ],
        compiler_params=pltpu.CompilerParams(
            collective_id=number, has_side_effects=True, vmem_limit_bytes=58 << 20
        ),
    )(*ins, *side_ins)
    results = list(results)
    main, rest = results[: len(outs)], results[len(outs) :]
    sides = []
    for b in beside:
        sides.append(rest[: len(b.outs)])
        del rest[: len(b.outs)]
    return main, sides


def ring_peers(at):
    return [("up", at.at_y(at.up)), ("down", at.at_y(at.down)), ("core", at.core())]


def gather_times(number, block, weight, flip=False, out_type=bf16, beside=(), swap=False):
    width = weight.shape[0] if flip else weight.shape[1]
    depth = weight.shape[1] if flip else weight.shape[0]

    def body(at, ins, outs, kept):
        x, w = ins
        whole, product = outs[:2]
        send, recv, local = kept[:3]
        y, c, up, down = at.y, at.c, at.up, at.down
        far = lax.rem(y + 2, 4)

        def move(slot, y_from, c_from, peer, start=0, size=BLOCK, first=False):
            rows = at.rows(y_from, c_from, start, size)
            src = x if first else whole.at[rows]
            return remote(src, whole.at[rows], send.at[slot], recv.at[slot], peer)

        to_up, to_down = at.at_y(up), at.at_y(down)
        sends = [
            move(0, y, c, to_up, first=True),
            move(1, y, c, to_down, first=True),
            move(2, y, c, at.core(), first=True),
            move(3, down, c, to_up, 0, BLOCK // 2),
            move(4, up, c, to_down, BLOCK // 2, BLOCK // 2),
            move(5, down, c, at.core()),
            move(6, up, c, at.core()),
            move(7, far, c, at.core(), 0, BLOCK // 2),
            move(8, far, c, at.core(), BLOCK // 2, BLOCK // 2),
        ]
        for i in range(3):
            sends[i].start()
        own = pltpu.make_async_copy(x, whole.at[at.rows(y, c)], local.at[0])
        own.start()
        if swap:
            full = outs[2]
            mine = pl.ds(pl.multiple_of(at.n * HALF, HALF), HALF)
            pair = remote(w, full.at[mine], send.at[9], recv.at[9], at.x())
            pair.start()
            keep = pltpu.make_async_copy(w, full.at[mine], local.at[1])
            keep.start()
        else:
            full = w
        own.wait()

        def step(s, carry):
            @pl.when(s == 1)
            def _():
                sends[2].wait_recv()
                sends[1].wait_recv()
                sends[4].start()
                sends[6].start()
                sends[0].wait_recv()
                sends[3].start()
                sends[5].start()
                if swap:
                    pair.wait_recv()
                    keep.wait()

            @pl.when(s == 3)
            def _():
                sends[6].wait_recv()

            @pl.when(s == 5)
            def _():
                sends[5].wait_recv()

            @pl.when(s == 6)
            def _():
                sends[3].wait_recv()
                sends[7].start()
                sends[4].wait_recv()
                sends[8].start()

            @pl.when(s == 7)
            def _():
                sends[7].wait_recv()
                sends[8].wait_recv()

            g = lax.div(s, 2)
            off = g + lax.div(g, 2) - 2 * lax.div(g, 3)
            rows = at.rows(lax.rem(y + off, 4), lax.rem(c + s, 2))
            product[rows, :] = (dot_flip if flip else dot)(whole[rows, :], full[...]).astype(out_type)
            return carry

        if swap:
            def early(s, carry):
                return step(s + 1, carry)

            lax.fori_loop(0, 7, early, 0)
            step(0, 0)
        else:
            lax.fori_loop(0, 8, step, 0)
        for i in range(9):
            sends[i].wait_send()
        if swap:
            pair.wait_send()

    outs = [jax.ShapeDtypeStruct((D, D), bf16), jax.ShapeDtypeStruct((D, width), out_type)]
    if swap:
        outs.append(jax.ShapeDtypeStruct((D, width), bf16))
    sems = [pltpu.SemaphoreType.DMA((10,)), pltpu.SemaphoreType.DMA((10,)), pltpu.SemaphoreType.DMA((2,))]

    def peers(at):
        return ring_peers(at) + ([("x", at.x())] if swap else [])

    return call(body, number, [block, weight], outs, sems, beside, peers)


def times_scatter(number, values, weight, flip=False, beside=()):
    def body(at, ins, outs, kept):
        v, w = ins
        result = outs[0]
        send, recv, local, out_c, in_c, own, out_y, in_y, half_out, half_in = kept
        y, c, up, down = at.y, at.c, at.up, at.down
        top, low = slice(0, BLOCK // 2), slice(BLOCK // 2, BLOCK)
        to_up, to_down = at.at_y(up), at.at_y(down)
        cores = [remote(out_c.at[g], in_c.at[g], send.at[g], recv.at[g], at.core()) for g in range(4)]
        halves = [
            remote(half_out.at[0], half_in.at[0], send.at[4], recv.at[4], to_up),
            remote(half_out.at[1], half_in.at[1], send.at[5], recv.at[5], to_down),
        ]
        blocks = [
            remote(out_y.at[0], in_y.at[0], send.at[6], recv.at[6], to_up),
            remote(out_y.at[1], in_y.at[1], send.at[7], recv.at[7], to_down),
        ]

        def step(s, carry):
            g = lax.div(s, 2)
            off = lax.rem(6 - g + 3 * lax.div(g, 2) + 2 * lax.div(g, 3), 4)
            core = lax.rem(c + 1 + s, 2)
            rows = at.rows(lax.rem(y + off, 4), core)
            part = (dot_flip if flip else dot)(v[rows, :], w[...])

            @pl.when(lax.rem(s, 2) == 0)
            def _():
                out_c[g] = part.astype(bf16)
                remote(out_c.at[g], in_c.at[g], send.at[g], recv.at[g], at.core()).start()

            @pl.when(lax.rem(s, 2) == 1)
            def _():
                own[g] = part

            @pl.when(s == 2)
            def _():
                cores[0].wait_recv()
                half_out[0] = (own[0, top] + in_c[0, top].astype(f32)).astype(bf16)
                half_out[1] = (own[0, low] + in_c[0, low].astype(f32)).astype(bf16)
                halves[0].start()
                halves[1].start()

            return carry

        lax.fori_loop(0, 8, step, 0)
        for i, kind in enumerate((top, low)):
            rest = low if i == 0 else top
            cores[1 + i].wait_recv()
            halves[i].wait_recv()
            out_y[i, rest] = (own[1 + i, rest] + in_c[1 + i, rest].astype(f32)).astype(bf16)
            out_y[i, kind] = (own[1 + i, kind] + in_c[1 + i, kind].astype(f32) + half_in[i].astype(f32)).astype(bf16)
            blocks[i].start()
        cores[3].wait_recv()
        total = own[3] + in_c[3].astype(f32)
        blocks[0].wait_recv()
        blocks[1].wait_recv()
        result[...] = total + in_y[0].astype(f32) + in_y[1].astype(f32)
        for copy in cores + halves + blocks:
            copy.wait_send()

    scratch = [
        pltpu.SemaphoreType.DMA((8,)),
        pltpu.SemaphoreType.DMA((8,)),
        pltpu.SemaphoreType.DMA((1,)),
        VMEM((4, BLOCK, D), bf16),
        VMEM((4, BLOCK, D), bf16),
        VMEM((4, BLOCK, D), f32),
        VMEM((2, BLOCK, D), bf16),
        VMEM((2, BLOCK, D), bf16),
        VMEM((2, BLOCK // 2, D), bf16),
        VMEM((2, BLOCK // 2, D), bf16),
    ]
    (total,), sides = call(body, number, [values, weight], [jax.ShapeDtypeStruct((BLOCK, D), f32)], scratch, beside, ring_peers)
    return total, sides


def causal_forward(number, joined, beside=()):
    rows_at_once = 512

    def body(at, ins, outs, kept):
        (qkv,), (out, logs) = ins, outs
        lane = lax.broadcasted_iota(jnp.int32, (rows_at_once, 128), 1)
        square = (rows_at_once, rows_at_once)
        seen = lax.broadcasted_iota(jnp.int32, square, 0) >= lax.broadcasted_iota(jnp.int32, square, 1)
        for i in range(D // rows_at_once):
            before, upto = i * rows_at_once, (i + 1) * rows_at_once
            rows = slice(before, upto)
            log_total, blended = jnp.zeros((rows_at_once, 128), f32), []
            for h in range(HEADS):
                a = h * HDIM
                q = qkv[rows, a : a + HDIM] * jnp.asarray(0.125, bf16)
                k = qkv[0:upto, COLS + a : COLS + a + HDIM]
                v = qkv[0:upto, 2 * COLS + a : 2 * COLS + a + HDIM]
                scores = dot_flip(q, k)
                last = jnp.where(seen, scores[:, before:], NEGATIVE)
                scores = jnp.concatenate((scores[:, :before], last), axis=1) if i else last
                peak = jnp.max(scores, axis=1, keepdims=True)
                raised = jnp.exp(scores - peak)
                total = jnp.sum(raised, axis=1, keepdims=True)
                blended.append(dot(raised.astype(bf16), v) / total)
                log_total = jnp.where(lane == h, peak + jnp.log(total), log_total)
            out[rows, :] = jnp.concatenate(blended, axis=1).astype(bf16)
            logs[:, rows] = log_total.T[0:8, :]

    outs = [jax.ShapeDtypeStruct((D, COLS), bf16), jax.ShapeDtypeStruct((8, D), f32)]
    return call(body, number, [joined], outs, (), beside)


def causal_backward(number, joined, grad, logs, beside=()):
    at_once = 512

    def body(at, ins, outs, kept):
        (qkv, go, log_rows), (out,), (key_sum, value_sum) = ins, outs, kept
        square = (at_once, at_once)
        seen = lax.broadcasted_iota(jnp.int32, square, 1) >= lax.broadcasted_iota(jnp.int32, square, 0)
        blocks = D // at_once
        for h in range(HEADS):
            a = h * HDIM
            turned = qkv[:, COLS + a : COLS + a + HDIM].T
            query_parts = []
            for i in reversed(range(blocks)):
                before, upto = i * at_once, (i + 1) * at_once
                rows = slice(before, upto)
                q = qkv[rows, a : a + HDIM] * jnp.asarray(0.125, bf16)
                g = go[rows, a : a + HDIM]
                k = qkv[0:upto, COLS + a : COLS + a + HDIM]
                v = qkv[0:upto, 2 * COLS + a : 2 * COLS + a + HDIM]
                p = jnp.exp(dot_flip(k, q) - log_rows[h : h + 1, rows])
                last = jnp.where(seen, p[before:], 0.0)
                p = jnp.concatenate((p[:before], last), axis=0) if i else last
                dp = dot_flip(v, g)
                ds = (p * (dp - jnp.sum(p * dp, axis=0, keepdims=True))).astype(bf16)
                value_part, key_part = dot(p.astype(bf16), g), dot(ds, q)
                if i == blocks - 1:
                    key_sum[h, 0:upto, :] = key_part
                    value_sum[h, 0:upto, :] = value_part
                else:
                    key_sum[h, 0:upto, :] += key_part
                    value_sum[h, 0:upto, :] += value_part
                query_parts.append((dot(turned[:, 0:upto], ds) * 0.125).T)
            out[:, a : a + HDIM] = jnp.concatenate(query_parts[::-1], axis=0).astype(bf16)
        for h in range(HEADS):
            a = h * HDIM
            out[:, COLS + a : COLS + a + HDIM] = key_sum[h].astype(bf16)
            out[:, 2 * COLS + a : 2 * COLS + a + HDIM] = value_sum[h].astype(bf16)

    outs = [jax.ShapeDtypeStruct((D, 3 * COLS), bf16)]
    scratch = [VMEM((HEADS, D, HDIM), f32), VMEM((HEADS, D, HDIM), f32)]
    return call(body, number, [joined, grad, logs], outs, scratch, beside)


def cross_weights(q, k):
    scores = dot_flip(k, q)
    raised = jnp.exp(scores - jnp.max(scores, axis=0, keepdims=True))
    return raised / jnp.sum(raised, axis=0, keepdims=True)


def cross_forward(queries, text_pair):
    def kernel(q_ref, kv_ref, out):
        for h in range(HEADS):
            a = h * HDIM
            q = q_ref[:, a : a + HDIM] * jnp.asarray(0.125, bf16)
            p = cross_weights(q, kv_ref[:, a : a + HDIM])
            v = kv_ref[:, COLS + a : COLS + a + HDIM].T
            out[:, a : a + HDIM] = dot(v, p.astype(bf16)).T.astype(bf16)

    return pl.pallas_call(
        kernel,
        out_shape=jax.ShapeDtypeStruct(queries.shape, bf16),
        in_specs=[pl.BlockSpec(memory_space=VMEM)] * 2,
        out_specs=pl.BlockSpec(memory_space=VMEM),
    )(queries, text_pair)


def cross_backward(queries, text_pair, grad):
    def kernel(q_ref, kv_ref, g_ref, dq_ref, dkv_ref):
        for h in range(HEADS):
            a = h * HDIM
            q = q_ref[:, a : a + HDIM] * jnp.asarray(0.125, bf16)
            k, v = kv_ref[:, a : a + HDIM], kv_ref[:, COLS + a : COLS + a + HDIM]
            g = g_ref[:, a : a + HDIM]
            p = cross_weights(q, k)
            dp = dot_flip(v, g)
            ds = (p * (dp - jnp.sum(p * dp, axis=0, keepdims=True))).astype(bf16)
            dq_ref[:, a : a + HDIM] = (dot(k.T, ds) * 0.125).T.astype(bf16)
            dkv_ref[:, a : a + HDIM] = dot(ds, q).astype(bf16)
            dkv_ref[:, COLS + a : COLS + a + HDIM] = dot(p.astype(bf16), g).astype(bf16)

    return pl.pallas_call(
        kernel,
        out_shape=(jax.ShapeDtypeStruct(queries.shape, bf16), jax.ShapeDtypeStruct(text_pair.shape, bf16)),
        in_specs=[pl.BlockSpec(memory_space=VMEM)] * 3,
        out_specs=(pl.BlockSpec(memory_space=VMEM),) * 2,
    )(queries, text_pair, grad)


def gelu_exact(v):
    return 0.5 * v * (1.0 + lax.erf(v * ROOT_HALF))


def gelu_slope(v):
    return 0.5 * (1.0 + lax.erf(v * ROOT_HALF)) + v * jnp.exp(-0.5 * v * v) * GAUSS_NORM


def norm_forward(values, gain, shift):
    average = jnp.mean(values, axis=1, keepdims=True)
    variance = jnp.mean(values * values, axis=1, keepdims=True) - average * average
    factor = lax.rsqrt(variance + EPSILON)
    centred = (values - average) * factor
    return centred, factor, (centred * gain + shift).astype(bf16)


def norm_backward(incoming, centred, factor, gain):
    scaled = incoming * gain
    first = jnp.mean(scaled, axis=1, keepdims=True)
    second = jnp.mean(scaled * centred, axis=1, keepdims=True)
    result = factor * (scaled - first - centred * second)
    return result, jnp.sum(incoming * centred, axis=0), jnp.sum(incoming, axis=0)


def on_device(
    layer_input,
    text_states,
    cotangent,
    first_gain,
    first_shift,
    query_weight,
    key_weight,
    value_weight,
    output_weight,
    second_gain,
    second_shift,
    cross_query,
    cross_key,
    cross_value,
    cross_output,
    third_gain,
    third_shift,
    expand_weight,
    contract_weight,
):
    vectors = (first_gain, first_shift, second_gain, second_shift, third_gain, third_shift)
    vectors = jnp.concatenate([jnp.stack(vectors).astype(f32), jnp.zeros((2, HALF), f32)], axis=0)
    joined = jnp.concatenate((query_weight, key_weight, value_weight), axis=1)
    pair = jnp.concatenate((cross_key, cross_value), axis=1)

    _, ((x,), (text,), (vectors,)) = call(None, 0, [], [], (), [Relay(layer_input), Text(text_states), Swap(vectors, 1)])
    gain_one, shift_one, gain_two, shift_two, gain_three, shift_three = (vectors[i : i + 1] for i in range(6))
    source = x.astype(f32)
    centred_one, factor_one, normed_one = norm_forward(source, gain_one, shift_one)
    (all_one, qkv, joined), ((out_w,),) = gather_times(1, normed_one, joined, swap=True, beside=[Swap(output_weight, 1)])
    (attended, logs), ((cq_w,), (pair,), (co_w,)) = causal_forward(
        2, qkv, [Swap(cross_query, 0), Swap(pair, 0), Swap(cross_output, 1)]
    )
    branch, ((expand,),) = times_scatter(3, attended, out_w, beside=[Swap(expand_weight, 0)])
    middle_one = source + branch
    centred_two, factor_two, normed_two = norm_forward(middle_one, gain_two, shift_two)
    (all_two, cross_q), ((contract,),) = gather_times(4, normed_two, cq_w, beside=[Swap(contract_weight, 1)])
    text_pair = dot(text, pair).astype(bf16)
    crossed = cross_forward(cross_q, text_pair)
    branch, ((down,),) = times_scatter(6, crossed, co_w, beside=[Relay(cotangent)])
    middle_two = middle_one + branch
    centred_three, factor_three, normed_three = norm_forward(middle_two, gain_three, shift_three)
    (all_three, expanded), _ = gather_times(7, normed_three, expand, out_type=f32)
    activated = gelu_exact(expanded).astype(bf16)
    (all_down, grad_act), _ = gather_times(8, down, contract, flip=True)
    branch, _ = times_scatter(9, activated, contract)
    layer_output = (middle_two + branch).astype(bf16)

    grad_expand = (grad_act.astype(f32) * gelu_slope(expanded)).astype(bf16)
    contract_leg = SumZ(outer(activated, all_down).astype(bf16), False)
    expand_leg = SumZ(outer(all_three, grad_expand).astype(bf16), True)
    grad_three, (contract_got, (layer_output,)) = times_scatter(
        10, grad_expand, expand, flip=True, beside=[contract_leg, Relay(layer_output, True)]
    )
    back, third_gain_part, third_shift_part = norm_backward(grad_three, centred_three, factor_three, gain_three)
    grad_two = down.astype(f32) + back
    contract_leg = SumX(contract_leg.finish(contract_got), False)
    (all_mid_two, grad_crossed), (expand_got, contract_got) = gather_times(
        11, grad_two.astype(bf16), co_w, flip=True, beside=[expand_leg, contract_leg]
    )
    grad_cross_q, grad_pair = cross_backward(cross_q, text_pair, grad_crossed)
    text_part = lax.psum(dot_flip(grad_pair, pair).astype(bf16), "wide")
    query_pair_leg = SumZ(
        jnp.concatenate((outer(all_two, grad_cross_q), outer(text, grad_pair)), axis=1).astype(bf16), True
    )
    cross_out_leg = SumZ(outer(crossed, all_mid_two).astype(bf16), False)
    expand_leg = SumX(expand_leg.finish(expand_got), True)
    contract_leg = Spread(contract_leg.finish(contract_got))
    grad_normed, (expand_got, contract_got, query_pair_got, cross_out_got) = times_scatter(
        13, grad_cross_q, cq_w, flip=True, beside=[expand_leg, contract_leg, query_pair_leg, cross_out_leg]
    )
    contract_grad = contract_leg.finish(contract_got)
    back, second_gain_part, second_shift_part = norm_backward(grad_normed, centred_two, factor_two, gain_two)
    grad_one = grad_two + back
    expand_leg = Spread(expand_leg.finish(expand_got))
    query_pair_leg = SumX(query_pair_leg.finish(query_pair_got), True)
    cross_out_leg = SumX(cross_out_leg.finish(cross_out_got), False)
    (all_mid_one, grad_attended), (expand_got, query_pair_got, cross_out_got) = gather_times(
        14, grad_one.astype(bf16), out_w, flip=True, beside=[expand_leg, query_pair_leg, cross_out_leg]
    )
    expand_grad = expand_leg.finish(expand_got)
    output_leg = SumZ(outer(attended, all_mid_one).astype(bf16), False)
    query_pair_leg = Spread(query_pair_leg.finish(query_pair_got))
    cross_out_leg = Spread(cross_out_leg.finish(cross_out_got))
    (grad_qkv,), (output_got, query_pair_got, cross_out_got) = causal_backward(
        15, qkv, grad_attended, logs, [output_leg, query_pair_leg, cross_out_leg]
    )
    query_pair_grad = query_pair_leg.finish(query_pair_got)
    cross_output_grad = cross_out_leg.finish(cross_out_got)
    joined_leg = SumZ(outer(all_one, grad_qkv).astype(bf16), True)
    output_leg = SumX(output_leg.finish(output_got), False)
    grad_normed, (joined_got, output_got) = times_scatter(
        16, grad_qkv, joined, flip=True, beside=[joined_leg, output_leg]
    )
    back, first_gain_part, first_shift_part = norm_backward(grad_normed, centred_one, factor_one, gain_one)
    input_grad = (grad_one + back).astype(bf16)
    parts = jnp.stack(
        (first_gain_part, first_shift_part, second_gain_part, second_shift_part, third_gain_part, third_shift_part)
    )
    parts = jnp.concatenate([parts, jnp.zeros((2, D), f32)], axis=0)
    joined_leg = SumX(joined_leg.finish(joined_got), True)
    output_leg = Spread(output_leg.finish(output_got))
    _, ((input_grad,), joined_got, output_got, (text_grad,), (parts,)) = call(
        None, 17, [], [], (), [Relay(input_grad, True), joined_leg, output_leg, Text(text_part, True), ToRing(parts)]
    )
    output_grad = output_leg.finish(output_got)
    joined_leg = Spread(joined_leg.finish(joined_got))
    _, (joined_got, (parts,)) = call(None, 18, [], [], (), [joined_leg, ToClips(jnp.sum(parts, axis=0))])
    joined_grad = joined_leg.finish(joined_got)
    parts = jnp.sum(parts, axis=(0, 1))
    return (
        layer_output,
        input_grad.astype(f32),
        text_grad.astype(f32),
        parts[0],
        parts[1],
        joined_grad[:, :COLS],
        joined_grad[:, COLS : 2 * COLS],
        joined_grad[:, 2 * COLS :],
        output_grad,
        parts[2],
        parts[3],
        query_pair_grad[:, :COLS],
        query_pair_grad[:, COLS : 2 * COLS],
        query_pair_grad[:, 2 * COLS :],
        cross_output_grad,
        parts[4],
        parts[5],
        expand_grad,
        contract_grad,
    )


def solution(mesh):
    return jax.shard_map(
        on_device,
        mesh=mesh,
        in_specs=(
            P(("dp", "wide"), "narrow"),
            P("dp", None, "narrow"),
            P(("dp", "wide"), "narrow"),
            P("narrow"),
            P("narrow"),
            P("narrow", "wide"),
            P("narrow", "wide"),
            P("narrow", "wide"),
            P("wide", "narrow"),
            P("narrow"),
            P("narrow"),
            P("narrow", "wide"),
            P("narrow", "wide"),
            P("narrow", "wide"),
            P("wide", "narrow"),
            P("narrow"),
            P("narrow"),
            P("narrow", "wide"),
            P("wide", "narrow"),
        ),
        out_specs=(
            P(("dp", "wide"), "narrow"),
            P(("dp", "wide"), "narrow"),
            P("dp", None, "narrow"),
            P("narrow"),
            P("narrow"),
            P("narrow", "wide"),
            P("narrow", "wide"),
            P("narrow", "wide"),
            P("wide", "narrow"),
            P("narrow"),
            P("narrow"),
            P("narrow", "wide"),
            P("narrow", "wide"),
            P("narrow", "wide"),
            P("wide", "narrow"),
            P("narrow"),
            P("narrow"),
            P("narrow", "wide"),
            P("wide", "narrow"),
        ),
        check_vma=False,
    )
```

```python
import functools
import math

import jax
import jax.numpy as jnp
from jax import lax
from jax.experimental import pallas as pl
from jax.experimental.pallas import tpu as pltpu
from jax.sharding import PartitionSpec as P

D = 1536
HALF = 768
HDIM = 64
HEADS = 3
COLS = HEADS * HDIM
BLOCK = 192
EPSILON = 1e-05
NEGATIVE = -1e30
ROOT_HALF = 0.7071067811865476
GAUSS_NORM = 0.3989422804014327
MESH = pl.DeviceIdType.MESH
VMEM = pltpu.VMEM
ANY = pl.ANY
bf16, f32 = jnp.bfloat16, jnp.float32


def dot(a, b):
    return lax.dot_general(a, b, (((1,), (0,)), ((), ())), preferred_element_type=f32)


def dot_flip(a, b):
    return lax.dot_general(a, b, (((1,), (1,)), ((), ())), preferred_element_type=f32)


def outer(a, b):
    return lax.dot_general(a, b, (((0,), (0,)), ((), ())), preferred_element_type=f32)


class Place:
    def __init__(self):
        self.dp, self.w, self.n = (lax.axis_index(a) for a in ("dp", "wide", "narrow"))
        self.y, self.c = lax.div(self.w, 2), lax.rem(self.w, 2)
        self.z, self.s = lax.div(self.dp, 2), lax.rem(self.dp, 2)
        self.up, self.down = lax.rem(self.y + 1, 4), lax.rem(self.y + 3, 4)
        self.across = 3 - self.y
        self.moved = lax.rem(lax.div(self.y, 2) + self.n, 2)
        self.clip = lax.div(self.y, 2)

    def spot(self, y, c):
        moved = lax.rem(lax.div(y, 2) + self.n, 2)
        return (lax.rem(y + moved, 2) * 2 + c) * 2 + moved

    def rows(self, y, c, start=0, size=BLOCK):
        return pl.ds(pl.multiple_of(self.spot(y, c) * BLOCK + start, 32), size)

    def half(self, n):
        return pl.ds(pl.multiple_of(n * HALF, HALF), HALF)

    def at_y(self, y):
        return {"wide": y * 2 + self.c}

    def core(self):
        return {"wide": self.y * 2 + 1 - self.c}

    def x(self):
        return {"narrow": 1 - self.n}

    def at_z(self, k):
        return {"dp": lax.rem(self.z + k, 4) * 2 + self.s}

    def at_dp(self, k):
        return {"dp": lax.rem(self.dp + k, 8)}

    def at_x(self, ds, dn):
        return {"dp": self.z * 2 + lax.rem(self.s + ds, 2), "narrow": lax.rem(self.n + dn, 2)}


def remote(src, dst, send, recv, peer):
    return pltpu.make_async_remote_copy(
        src_ref=src, dst_ref=dst, send_sem=send, recv_sem=recv, device_id=peer, device_id_type=MESH
    )


def greet(peers):
    barrier = pltpu.get_barrier_semaphore()
    for peer in peers:
        pl.semaphore_signal(barrier, inc=1, device_id=peer, device_id_type=MESH)
    pl.semaphore_wait(barrier, len(peers))


class Give:
    def __init__(self, array):
        self.ins, self.copies, self.locals = [array], 1, 0
        self.outs = [jax.ShapeDtypeStruct(array.shape, array.dtype)]

    def peers(self, at):
        return [("x", at.x())]

    def moves(self, at, ins, outs):
        return [(ins[0], outs[0], at.x())], []


class GiveClip(Give):
    def __init__(self, array):
        super().__init__(array)
        self.outs = [jax.ShapeDtypeStruct(array.shape[1:], array.dtype)]

    def moves(self, at, ins, outs):
        return [(ins[0].at[1 - at.n], outs[0], at.x())], []


class SumZ:
    def __init__(self, array, by_rows):
        self.by_rows, self.copies, self.locals = by_rows, 3, 0
        rows, cols = array.shape
        shape = (2, 4, rows // 8, cols) if by_rows else (4, rows // 4, cols)
        self.ins = [array.reshape(shape)]
        kept = (2, rows // 8, cols) if by_rows else (rows // 4, cols)
        self.outs = [jax.ShapeDtypeStruct((3, *kept), array.dtype)]

    def peers(self, at):
        return [(f"z{k}", at.at_z(k)) for k in (1, 2, 3)]

    def moves(self, at, ins, outs):
        out = []
        for k in (1, 2, 3):
            q = lax.rem(at.z + k, 4)
            src = ins[0].at[:, q] if self.by_rows else ins[0].at[q]
            out.append((src, outs[0].at[k - 1], at.at_z(k)))
        return out, []

    def finish(self, outs):
        z = lax.div(lax.axis_index("dp"), 2)
        own = lax.dynamic_index_in_dim(self.ins[0], z, 1 if self.by_rows else 0, False)
        return (own.astype(f32) + outs[0].astype(f32).sum(axis=0)).astype(bf16)


class SumX:
    def __init__(self, array, by_rows):
        self.by_rows, self.copies, self.locals = by_rows, 3, 0
        if by_rows:
            two, rows, cols = array.shape
            self.ins, kept = [array.reshape(2, 2, rows // 2, cols)], (rows // 2, cols)
        else:
            rows, cols = array.shape
            self.ins, kept = [array.reshape(2, rows // 2, cols)], (rows // 2, HALF)
        self.outs = [jax.ShapeDtypeStruct((3, *kept), array.dtype)]

    order = ((0, 1), (1, 0), (1, 1))

    def peers(self, at):
        return [(f"x{a}{b}", at.at_x(a, b)) for a, b in self.order]

    def moves(self, at, ins, outs):
        out = []
        for i, (a, b) in enumerate(self.order):
            s, n = lax.rem(at.s + a, 2), lax.rem(at.n + b, 2)
            src = ins[0].at[n, s] if self.by_rows else ins[0].at[s, :, at.half(n)]
            out.append((src, outs[0].at[i], at.at_x(a, b)))
        return out, []

    def finish(self, outs):
        s, n = lax.rem(lax.axis_index("dp"), 2), lax.axis_index("narrow")
        if self.by_rows:
            own = lax.dynamic_index_in_dim(lax.dynamic_index_in_dim(self.ins[0], n, 0, False), s, 0, False)
        else:
            own = lax.dynamic_slice_in_dim(lax.dynamic_index_in_dim(self.ins[0], s, 0, False), n * HALF, HALF, 1)
        return (own.astype(f32) + outs[0].astype(f32).sum(axis=0)).astype(bf16)


class Spread:
    def __init__(self, array):
        self.ins, self.copies, self.locals = [array], 7, 1
        self.outs = [jax.ShapeDtypeStruct((8, *array.shape), array.dtype)]

    def peers(self, at):
        return [(f"d{k}", at.at_dp(k)) for k in range(1, 8)]

    def moves(self, at, ins, outs):
        dst = outs[0].at[at.dp]
        return [(ins[0], dst, at.at_dp(k)) for k in range(1, 8)], [(ins[0], dst)]

    def finish(self, outs):
        eight, rows, cols = outs[0].shape
        return outs[0].reshape(eight * rows, cols).astype(f32)


class ToRing:
    def __init__(self, array):
        self.ins, self.copies, self.locals = [array], 7, 1
        self.outs = [jax.ShapeDtypeStruct((8, *array.shape), array.dtype)]

    def peers(self, at):
        return [(f"w{k}", {"wide": lax.rem(at.w + k, 8)}) for k in range(1, 8)]

    def moves(self, at, ins, outs):
        dst = outs[0].at[at.w]
        return [(ins[0], dst, peer) for _, peer in self.peers(at)], [(ins[0], dst)]


class ToClips:
    def __init__(self, array):
        self.ins, self.copies, self.locals = [array], 15, 1
        self.outs = [jax.ShapeDtypeStruct((8, 2, array.shape[0], HALF), array.dtype)]

    order = tuple((k, b) for k in range(8) for b in range(2))[1:]

    def peers(self, at):
        return [(f"c{k}{b}", {**at.at_dp(k), "narrow": lax.rem(at.n + b, 2)}) for k, b in self.order]

    def moves(self, at, ins, outs):
        dst = outs[0].at[at.dp, at.n]
        far = []
        for (k, b), (_, peer) in zip(self.order, self.peers(at)):
            far.append((ins[0].at[:, at.half(lax.rem(at.n + b, 2))], dst, peer))
        return far, [(ins[0].at[:, at.half(at.n)], dst)]


class Relay:
    def __init__(self, array, back=False):
        self.ins, self.back, self.copies, self.locals = [array], back, 2, 1
        shape = (384, HALF) if back else (BLOCK, D)
        self.outs = [jax.ShapeDtypeStruct(shape, array.dtype)]

    def peers(self, at):
        return [
            ("x", at.x()),
            ("a0", {"wide": at.across * 2 + at.c}),
            ("a1", {"wide": at.across * 2 + at.c, "narrow": 1 - at.n}),
        ]


def relay_run(relay, at, src, dst, send, recv, local, base, finish):
    mine, other = at.half(at.n), at.half(1 - at.n)
    over = at.across * 2 + at.c
    if relay.back:
        row = pl.ds(pl.multiple_of(at.moved * BLOCK, BLOCK), BLOCK)
        to = recv.at[base + at.moved]
        own = src.at[:, mine], src.at[:, other]
        land = dst.at[0:BLOCK], dst.at[BLOCK : 2 * BLOCK]
    else:
        row = mine
        to = recv.at[base + at.n]
        own = src.at[0:BLOCK], src.at[BLOCK : 2 * BLOCK]
        land = dst.at[:, at.half(0)], dst.at[:, at.half(1)]
    target = dst.at[row] if relay.back else dst.at[:, row]

    def arrive(slot, part):
        return remote(own[0], part, send.at[base], recv.at[base + slot], at.x())

    @pl.when(at.moved == 0)
    def _():
        stay = pltpu.make_async_copy(own[0], target, local)
        if relay.back:
            go = remote(own[1], target, send.at[base], to, at.x())
        else:
            go = remote(own[1], target, send.at[base], to, {"wide": over})
        if not finish:
            go.start()
            stay.start()
        else:
            stay.wait()
            go.wait_send()
            if relay.back:
                arrive(1, land[1]).wait_recv()
            else:
                arrive(1 - at.n, dst.at[:, other]).wait_recv()

    @pl.when(at.moved == 1)
    def _():
        if relay.back:
            first = remote(own[1], target, send.at[base], to, {"wide": over, "narrow": 1 - at.n})
            second = remote(own[0], target, send.at[base + 1], to, {"wide": over})
        else:
            first = remote(own[1], target, send.at[base], to, {"wide": over, "narrow": 1 - at.n})
            second = remote(own[0], target, send.at[base + 1], to, at.x())
        if not finish:
            first.start()
            second.start()
        else:
            first.wait_send()
            second.wait_send()
            arrive(0, land[0]).wait_recv()
            arrive(1, land[1]).wait_recv()


def call(body, number, ins, outs, scratch=(), beside=(), peers=None, spaces=None, out_spaces=None):
    spaces = spaces or [VMEM] * len(ins)
    out_spaces = out_spaces or [VMEM] * len(outs)
    copies = sum(b.copies for b in beside)
    locals_ = sum(b.locals for b in beside)
    side_ins = [a for b in beside for a in b.ins]
    side_outs = [a for b in beside for a in b.outs]
    n_in, n_out, n_scratch = len(ins), len(outs), len(scratch)

    def kernel(*refs):
        at = Place()
        refs = list(refs)

        def take(count):
            out = refs[:count]
            del refs[:count]
            return out

        main_in, side_in = take(n_in), take(len(side_ins))
        main_out, side_out, kept = take(n_out), take(len(side_outs)), take(n_scratch)
        send, recv, local = take(3)
        known = dict(peers(at)) if peers else {}
        for b in beside:
            known.update(dict(b.peers(at)))
        if known:
            greet(list(known.values()))
        slot, place, todo = 0, 0, []
        for b in beside:
            i, o = [side_in.pop(0) for _ in b.ins], [side_out.pop(0) for _ in b.outs]
            if isinstance(b, Relay):
                run = functools.partial(relay_run, b, at, i[0], o[0], send, recv, local.at[place], slot)
                run(False)
                todo.append(functools.partial(run, True))
                slot, place = slot + 2, place + 1
                continue
            far, near = b.moves(at, i, o)
            for src, dst, peer in far:
                copy = remote(src, dst, send.at[slot], recv.at[slot], peer)
                copy.start()
                todo.append(copy.wait)
                slot += 1
            for src, dst in near:
                copy = pltpu.make_async_copy(src, dst, local.at[place])
                copy.start()
                todo.append(copy.wait)
                place += 1
        if body:
            body(at, main_in, main_out, kept)
        for wait in todo:
            wait()

    results = pl.pallas_call(
        kernel,
        out_shape=tuple(outs) + tuple(side_outs),
        in_specs=[pl.BlockSpec(memory_space=s) for s in spaces] + [pl.BlockSpec(memory_space=ANY)] * len(side_ins),
        out_specs=tuple(pl.BlockSpec(memory_space=m) for m in out_spaces + [ANY] * len(side_outs)),
        scratch_shapes=[
            *scratch,
            pltpu.SemaphoreType.DMA((max(copies, 1),)),
            pltpu.SemaphoreType.DMA((max(copies, 1),)),
            pltpu.SemaphoreType.DMA((max(locals_, 1),)),
        ],
        compiler_params=pltpu.CompilerParams(
            collective_id=number, has_side_effects=True, vmem_limit_bytes=58 << 20
        ),
    )(*ins, *side_ins)
    results = list(results)
    main, rest = results[: len(outs)], results[len(outs) :]
    sides = []
    for b in beside:
        sides.append(rest[: len(b.outs)])
        del rest[: len(b.outs)]
    return main, sides


def ring_peers(at):
    return [("up", at.at_y(at.up)), ("down", at.at_y(at.down)), ("core", at.core())]


def sems(count):
    return [pltpu.SemaphoreType.DMA((count,)), pltpu.SemaphoreType.DMA((count,)), pltpu.SemaphoreType.DMA((count,))]


def by_rows(count, size, work, carry=None):
    def step(i, carry):
        return work(pl.ds(pl.multiple_of(i * size, size), size), carry)

    return lax.fori_loop(0, count // size, step, carry)


class Whole:
    def __init__(self, at, own, got, full, sem, axis):
        size = own.shape[axis]
        self.copies = []
        for i, (part, n) in enumerate(((own, at.n), (got, 1 - at.n))):
            where = pl.ds(pl.multiple_of(n * size, size), size)
            target = full.at[where] if axis == 0 else full.at[:, where]
            self.copies.append(pltpu.make_async_copy(part, target, sem.at[i]))
            self.copies[-1].start()

    def wait(self):
        for copy in self.copies:
            copy.wait()


class Gather:
    slots = 9

    def __init__(self, at, x, whole, send, recv, local):
        self.at, self.x, self.whole = at, x, whole
        y, c, up, down = at.y, at.c, at.up, at.down
        far = lax.rem(y + 2, 4)
        half = BLOCK // 2

        def move(slot, y_from, peer, start=0, size=BLOCK, first=False):
            rows = at.rows(y_from, c, start, size)
            return remote(x if first else whole.at[rows], whole.at[rows], send.at[slot], recv.at[slot], peer)

        to_up, to_down, core = at.at_y(up), at.at_y(down), at.core()
        self.sends = [
            move(0, y, to_up, first=True),
            move(1, y, to_down, first=True),
            move(2, y, core, first=True),
            move(3, down, to_up, 0, half),
            move(4, up, to_down, half, half),
            move(5, down, core),
            move(6, up, core),
            move(7, far, core, 0, half),
            move(8, far, core, half, half),
        ]
        self.own = pltpu.make_async_copy(x, whole.at[at.rows(y, c)], local)

    def begin(self):
        for i in range(3):
            self.sends[i].start()
        self.own.start()
        self.own.wait()

    def pass_on(self):
        s = self.sends
        s[1].wait_recv()
        s[4].start()
        s[6].start()
        s[0].wait_recv()
        s[3].start()
        s[5].start()

    def pass_far(self):
        s = self.sends
        s[3].wait_recv()
        s[7].start()
        s[4].wait_recv()
        s[8].start()

    def got(self, *slots):
        for i in slots:
            self.sends[i].wait_recv()

    def end(self):
        for copy in self.sends:
            copy.wait_send()

    def each(self, work, before_last=None):
        at = self.at

        def step(s, carry):
            @pl.when(s == 1)
            def _():
                self.got(2)

            @pl.when(s == 2)
            def _():
                self.pass_on()

            @pl.when(s == 3)
            def _():
                self.got(6)

            @pl.when(s == 5)
            def _():
                self.got(5)

            @pl.when(s == 6)
            def _():
                self.pass_far()

            @pl.when(s == 7)
            def _():
                self.got(7, 8)

            g = lax.div(s, 2)
            off = g + lax.div(g, 2) - 2 * lax.div(g, 3)
            work(s, at.rows(lax.rem(at.y + off, 4), lax.rem(at.c + s, 2)))
            return carry

        lax.fori_loop(0, 8, step, 0)
        self.end()


class Scatter:
    slots = 8
    scratch = [
        VMEM((4, BLOCK, D), bf16),
        VMEM((4, BLOCK, D), bf16),
        VMEM((4, BLOCK, D), f32),
        VMEM((2, BLOCK, D), bf16),
        VMEM((2, BLOCK, D), bf16),
        VMEM((2, BLOCK // 2, D), bf16),
        VMEM((2, BLOCK // 2, D), bf16),
    ]

    def __init__(self, at, send, recv, refs):
        self.at, self.send, self.recv = at, send, recv
        self.out_c, self.in_c, self.own, self.out_y, self.in_y, self.half_out, self.half_in = refs
        to_up, to_down = at.at_y(at.up), at.at_y(at.down)
        self.cores = [self.core(g) for g in range(4)]
        self.halves = [
            remote(self.half_out.at[0], self.half_in.at[0], send.at[4], recv.at[4], to_up),
            remote(self.half_out.at[1], self.half_in.at[1], send.at[5], recv.at[5], to_down),
        ]
        self.blocks = [
            remote(self.out_y.at[0], self.in_y.at[0], send.at[6], recv.at[6], to_up),
            remote(self.out_y.at[1], self.in_y.at[1], send.at[7], recv.at[7], to_down),
        ]

    def core(self, g):
        return remote(self.out_c.at[g], self.in_c.at[g], self.send.at[g], self.recv.at[g], self.at.core())

    def both(self, g, rows):
        return self.own[g, rows] + self.in_c[g, rows].astype(f32)

    def products(self, product):
        at = self.at
        half = BLOCK // 2

        def step(s, carry):
            g = lax.div(s, 2)
            off = lax.rem(6 - g + 3 * lax.div(g, 2) + 2 * lax.div(g, 3), 4)
            part = product(at.rows(lax.rem(at.y + off, 4), lax.rem(at.c + 1 + s, 2)))

            @pl.when(lax.rem(s, 2) == 0)
            def _():
                self.out_c[g] = part.astype(bf16)
                self.core(g).start()

            @pl.when(lax.rem(s, 2) == 1)
            def _():
                self.own[g] = part

            @pl.when(s == 2)
            def _():
                self.cores[0].wait_recv()
                for i in range(2):

                    def add(rows, carry, i=i):
                        low = pl.ds(pl.multiple_of(rows.start + i * half, 32), 32)
                        self.half_out[i, rows] = self.both(0, low).astype(bf16)

                    by_rows(half, 32, add)
                    self.halves[i].start()

            return carry

        lax.fori_loop(0, 8, step, 0)

    def middle(self):
        half = BLOCK // 2
        for i in range(2):
            self.cores[1 + i].wait_recv()
            self.halves[i].wait_recv()

            def add(rows, carry, i=i):
                here = pl.ds(pl.multiple_of(rows.start + i * half, 32), 32)
                there = pl.ds(pl.multiple_of(rows.start + (1 - i) * half, 32), 32)
                self.out_y[i, here] = (self.both(1 + i, here) + self.half_in[i, rows].astype(f32)).astype(bf16)
                self.out_y[i, there] = self.both(1 + i, there).astype(bf16)

            by_rows(half, 32, add)
            self.blocks[i].start()

    def arrive(self):
        self.cores[3].wait_recv()
        self.blocks[0].wait_recv()
        self.blocks[1].wait_recv()

    def total(self, rows):
        return self.both(3, rows) + self.in_y[0, rows].astype(f32) + self.in_y[1, rows].astype(f32)

    def end(self):
        for copy in self.cores + self.halves + self.blocks:
            copy.wait_send()


def standard(values):
    average = jnp.mean(values, axis=1, keepdims=True)
    variance = jnp.mean(values * values, axis=1, keepdims=True) - average * average
    factor = lax.rsqrt(variance + EPSILON)
    return (values - average) * factor, factor


def norm_back(incoming, centred, factor, gain):
    scaled = incoming * gain
    first = jnp.mean(scaled, axis=1, keepdims=True)
    second = jnp.mean(scaled * centred, axis=1, keepdims=True)
    return factor * (scaled - first - centred * second)


def two_sums(incoming, centred, carry):
    gains, shifts = carry
    return gains + jnp.sum(incoming * centred, axis=0, keepdims=True), shifts + jnp.sum(incoming, axis=0, keepdims=True)


def no_sums():
    return jnp.zeros((1, D), f32), jnp.zeros((1, D), f32)


def head(ref, rows, start):
    return ref[rows, start : start + HDIM]


def cross_weights(q, k):
    scores = dot_flip(k, q)
    raised = jnp.exp(scores - jnp.max(scores, axis=0, keepdims=True))
    return raised / jnp.sum(raised, axis=0, keepdims=True)


EIGHTH = 0.125


def shape(*dims, dtype=bf16):
    return jax.ShapeDtypeStruct(dims, dtype)


def enter(number, layer_input, vectors, joined, beside):
    relay = Relay(layer_input)

    def body(at, ins, outs, kept):
        (source, own_vectors, own_weight), (x, vectors, weight, all_rows, qkv) = ins, outs
        normed, whole, send, recv, local = kept
        half = at.half(at.n)
        moving = functools.partial(relay_run, relay, at, source, x, send, recv, local.at[0], 9)
        moving(False)
        stay = [
            pltpu.make_async_copy(own_vectors, vectors.at[:, half], local.at[1]),
            pltpu.make_async_copy(own_weight, weight.at[half], local.at[2]),
        ]
        go = [
            remote(own_vectors, vectors.at[:, half], send.at[11], recv.at[11], at.x()),
            remote(own_weight, weight.at[half], send.at[12], recv.at[12], at.x()),
        ]
        for copy in stay + go:
            copy.start()
        stay[0].wait()
        go[0].wait_recv()
        moving(True)

        def norm(rows, carry):
            centred, _ = standard(x[rows].astype(f32))
            normed[rows] = (centred * vectors[0:1] + vectors[1:2]).astype(bf16)

        by_rows(BLOCK, 32, norm)
        gather = Gather(at, normed, whole, send, recv, local.at[3])
        gather.begin()

        def work(s, rows):
            @pl.when(s == 7)
            def _():
                stay[1].wait()
                go[1].wait_recv()

            pltpu.make_async_copy(whole.at[rows], all_rows.at[rows], local.at[4 + s]).start()

        gather.each(work)

        def times(rows, carry):
            qkv[rows] = dot(whole[rows], weight[...]).astype(bf16)

        by_rows(D, BLOCK, times)
        for s in range(8):
            pltpu.make_async_copy(whole.at[0:BLOCK], all_rows.at[0:BLOCK], local.at[4 + s]).wait()
        for copy in go:
            copy.wait_send()

    return call(
        body,
        number,
        [layer_input, vectors, joined],
        [shape(BLOCK, D), shape(8, D, dtype=f32), shape(D, 3 * COLS), shape(D, D), shape(D, 3 * COLS)],
        [VMEM((BLOCK, D), bf16), VMEM((D, D), bf16), *sems(16)],
        beside,
        lambda at: ring_peers(at) + relay.peers(at) + [("x", at.x())],
        out_spaces=[VMEM, VMEM, VMEM, ANY, VMEM],
    )


def self_to_cross(number, attended, out_w, x, vectors, query_w, text_pair, beside):
    def body(at, ins, outs, kept):
        values, out_own, out_got, x, vectors, query_own, query_got, pair = ins
        middle, all_rows, queries, crossed = outs
        *refs, normed, whole, out_full, query_full, send, recv, local = kept
        weight = Whole(at, out_own, out_got, out_full, local.at[pl.ds(0, 2)], 1)
        later = Whole(at, query_own, query_got, query_full, local.at[pl.ds(2, 2)], 0)
        weight.wait()
        scatter = Scatter(at, send, recv, refs)
        scatter.products(lambda rows: dot(values[rows], out_full[...]))
        scatter.middle()
        later.wait()
        scatter.arrive()

        def norm(rows, carry):
            total = x[rows].astype(f32) + scatter.total(rows)
            middle[rows] = total
            centred, _ = standard(total)
            normed[rows] = (centred * vectors[2:3] + vectors[3:4]).astype(bf16)

        by_rows(BLOCK, 32, norm)
        gather = Gather(at, normed, whole, send.at[pl.ds(8, 9)], recv.at[pl.ds(8, 9)], local.at[4])
        gather.begin()

        def work(s, rows):
            pltpu.make_async_copy(whole.at[rows], all_rows.at[rows], local.at[5 + s]).start()
            q_all = dot(whole[rows], query_full[...]).astype(bf16)
            queries[rows] = q_all
            parts = []
            for h in range(HEADS):
                a = h * HDIM
                p = cross_weights(q_all[:, a : a + HDIM] * EIGHTH, pair[:, a : a + HDIM])
                v = pair[:, COLS + a : COLS + a + HDIM].T
                parts.append(dot(v, p.astype(bf16)).T)
            crossed[rows] = jnp.concatenate(parts, axis=1).astype(bf16)

        gather.each(work)
        for s in range(8):
            pltpu.make_async_copy(whole.at[0:BLOCK], all_rows.at[0:BLOCK], local.at[5 + s]).wait()
        scatter.end()

    return call(
        body,
        number,
        [attended, *out_w, x, vectors, *query_w, text_pair],
        [shape(BLOCK, D, dtype=f32), shape(D, D), shape(D, COLS), shape(D, COLS)],
        [*Scatter.scratch, VMEM((BLOCK, D), bf16), VMEM((D, D), bf16), VMEM((COLS, D), bf16), VMEM((D, COLS), bf16), *sems(17)],
        beside,
        ring_peers,
        spaces=[VMEM, ANY, ANY, VMEM, VMEM, ANY, ANY, VMEM],
        out_spaces=[VMEM, ANY, VMEM, VMEM],
    )


def feed_forward(number, crossed, cross_w, middle, vectors, expand_w, contract_w, all_down, beside):
    def body(at, ins, outs, kept):
        values, cross_own, cross_got, middle, vectors, expand_own, expand_got, contract_own, contract_got, all_down = ins
        after, all_rows, activated, grad = outs
        *refs, normed, whole, down, cross_full, expand_full, contract_full, send, recv, local = kept
        weight = Whole(at, cross_own, cross_got, cross_full, local.at[pl.ds(0, 2)], 1)
        later = [
            Whole(at, expand_own, expand_got, expand_full, local.at[pl.ds(2, 2)], 0),
            Whole(at, contract_own, contract_got, contract_full, local.at[pl.ds(4, 2)], 1),
            pltpu.make_async_copy(all_down, down, local.at[6]),
        ]
        later[2].start()
        weight.wait()
        scatter = Scatter(at, send, recv, refs)
        scatter.products(lambda rows: dot(values[rows], cross_full[...]))
        scatter.middle()
        for copy in later:
            copy.wait()
        scatter.arrive()

        def norm(rows, carry):
            total = middle[rows] + scatter.total(rows)
            after[rows] = total
            centred, _ = standard(total)
            normed[rows] = (centred * vectors[4:5] + vectors[5:6]).astype(bf16)

        by_rows(BLOCK, 32, norm)
        gather = Gather(at, normed, whole, send.at[pl.ds(8, 9)], recv.at[pl.ds(8, 9)], local.at[7])
        gather.begin()

        def work(s, rows):
            pltpu.make_async_copy(whole.at[rows], all_rows.at[rows], local.at[8 + s]).start()
            hidden = dot(whole[rows], expand_full[...])
            back = dot_flip(down[rows], contract_full[...])
            bell = 0.5 * (1.0 + lax.erf(hidden * ROOT_HALF))
            activated[rows] = (hidden * bell).astype(bf16)
            grad[rows] = (back * (bell + hidden * jnp.exp(-0.5 * hidden * hidden) * GAUSS_NORM)).astype(bf16)

        gather.each(work)
        for s in range(8):
            pltpu.make_async_copy(whole.at[0:BLOCK], all_rows.at[0:BLOCK], local.at[8 + s]).wait()
        scatter.end()

    return call(
        body,
        number,
        [crossed, *cross_w, middle, vectors, *expand_w, *contract_w, all_down],
        [shape(BLOCK, D, dtype=f32), shape(D, D), shape(D, HALF), shape(D, HALF)],
        [
            *Scatter.scratch,
            VMEM((BLOCK, D), bf16),
            VMEM((D, D), bf16),
            VMEM((D, D), bf16),
            VMEM((COLS, D), bf16),
            VMEM((D, HALF), bf16),
            VMEM((HALF, D), bf16),
            *sems(17),
        ],
        beside,
        ring_peers,
        spaces=[VMEM, ANY, ANY, VMEM, VMEM, ANY, ANY, ANY, ANY, ANY],
        out_spaces=[VMEM, ANY, VMEM, VMEM],
    )


def feed_forward_back(number, grad, expand_w, after, vectors, down, cross_w, queries, text_pair, beside):
    def body(at, ins, outs, kept):
        grad, expand_own, expand_got, after, vectors, down, cross_own, cross_got, queries, pair = ins
        grad_rows, all_rows, grad_queries, grad_pair, grad_vectors = outs
        *refs, rounded, whole, expand_full, cross_full, pair_sum, send, recv, local = kept
        weight = Whole(at, expand_own, expand_got, expand_full, local.at[pl.ds(0, 2)], 0)
        later = Whole(at, cross_own, cross_got, cross_full, local.at[pl.ds(2, 2)], 1)
        weight.wait()
        scatter = Scatter(at, send, recv, refs)
        scatter.products(lambda rows: dot_flip(grad[rows], expand_full[...]))
        scatter.middle()
        later.wait()
        scatter.arrive()

        def norm(rows, carry):
            incoming = scatter.total(rows)
            centred, factor = standard(after[rows])
            total = down[rows].astype(f32) + norm_back(incoming, centred, factor, vectors[4:5])
            grad_rows[rows] = total
            rounded[rows] = total.astype(bf16)
            return two_sums(incoming, centred, carry)

        gains, shifts = by_rows(BLOCK, 32, norm, no_sums())
        grad_vectors[0:1] = gains
        grad_vectors[1:2] = shifts
        gather = Gather(at, rounded, whole, send.at[pl.ds(8, 9)], recv.at[pl.ds(8, 9)], local.at[4])
        gather.begin()
        pair_sum[...] = jnp.zeros_like(pair_sum)

        def work(s, rows):
            pltpu.make_async_copy(whole.at[rows], all_rows.at[rows], local.at[5 + s]).start()
            back = dot_flip(whole[rows], cross_full[...]).astype(bf16)
            parts = []
            for h in range(HEADS):
                a = h * HDIM
                q = head(queries, rows, a) * EIGHTH
                k, v = pair[:, a : a + HDIM], pair[:, COLS + a : COLS + a + HDIM]
                g = back[:, a : a + HDIM]
                p = cross_weights(q, k)
                dp = dot_flip(v, g)
                ds = (p * (dp - jnp.sum(p * dp, axis=0, keepdims=True))).astype(bf16)
                parts.append((dot(k.T, ds) * 0.125).T)
                pair_sum[h] += dot(ds, q)
                pair_sum[HEADS + h] += dot(p.astype(bf16), g)
            grad_queries[rows] = jnp.concatenate(parts, axis=1).astype(bf16)

        gather.each(work)
        grad_pair[...] = jnp.concatenate([pair_sum[i] for i in range(2 * HEADS)], axis=1).astype(bf16)
        for s in range(8):
            pltpu.make_async_copy(whole.at[0:BLOCK], all_rows.at[0:BLOCK], local.at[5 + s]).wait()
        scatter.end()

    return call(
        body,
        number,
        [grad, *expand_w, after, vectors, down, *cross_w, queries, text_pair],
        [shape(BLOCK, D, dtype=f32), shape(D, D), shape(D, COLS), shape(64, 2 * COLS), shape(8, D, dtype=f32)],
        [
            *Scatter.scratch,
            VMEM((BLOCK, D), bf16),
            VMEM((D, D), bf16),
            VMEM((D, HALF), bf16),
            VMEM((COLS, D), bf16),
            VMEM((2 * HEADS, 64, HDIM), f32),
            *sems(17),
        ],
        beside,
        ring_peers,
        spaces=[VMEM, ANY, ANY, VMEM, VMEM, VMEM, ANY, ANY, VMEM, VMEM],
        out_spaces=[VMEM, ANY, VMEM, VMEM, VMEM],
    )


def cross_to_self_back(number, grad, query_w, middle, vectors, grad_rows, out_w, beside):
    def body(at, ins, outs, kept):
        grad, query_own, query_got, middle, vectors, before, out_own, out_got = ins
        grad_rows, all_rows, grad_values, grad_vectors = outs
        *refs, rounded, whole, query_full, out_full, send, recv, local = kept
        weight = Whole(at, query_own, query_got, query_full, local.at[pl.ds(0, 2)], 0)
        later = Whole(at, out_own, out_got, out_full, local.at[pl.ds(2, 2)], 1)
        weight.wait()
        scatter = Scatter(at, send, recv, refs)
        scatter.products(lambda rows: dot_flip(grad[rows], query_full[...]))
        scatter.middle()
        later.wait()
        scatter.arrive()

        def norm(rows, carry):
            incoming = scatter.total(rows)
            centred, factor = standard(middle[rows])
            total = before[rows] + norm_back(incoming, centred, factor, vectors[2:3])
            grad_rows[rows] = total
            rounded[rows] = total.astype(bf16)
            return two_sums(incoming, centred, carry)

        gains, shifts = by_rows(BLOCK, 32, norm, no_sums())
        grad_vectors[0:1] = gains
        grad_vectors[1:2] = shifts
        gather = Gather(at, rounded, whole, send.at[pl.ds(8, 9)], recv.at[pl.ds(8, 9)], local.at[4])
        gather.begin()

        def work(s, rows):
            pltpu.make_async_copy(whole.at[rows], all_rows.at[rows], local.at[5 + s]).start()
            grad_values[rows] = dot_flip(whole[rows], out_full[...]).astype(bf16)

        gather.each(work)
        for s in range(8):
            pltpu.make_async_copy(whole.at[0:BLOCK], all_rows.at[0:BLOCK], local.at[5 + s]).wait()
        scatter.end()

    return call(
        body,
        number,
        [grad, *query_w, middle, vectors, grad_rows, *out_w],
        [shape(BLOCK, D, dtype=f32), shape(D, D), shape(D, COLS), shape(8, D, dtype=f32)],
        [*Scatter.scratch, VMEM((BLOCK, D), bf16), VMEM((D, D), bf16), VMEM((D, COLS), bf16), VMEM((COLS, D), bf16), *sems(17)],
        beside,
        ring_peers,
        spaces=[VMEM, ANY, ANY, VMEM, VMEM, VMEM, ANY, ANY],
        out_spaces=[VMEM, ANY, VMEM, VMEM],
    )


def leave(number, grad, joined, x, vectors, grad_rows, beside):
    relay = Relay(jax.ShapeDtypeStruct((BLOCK, D), bf16), True)

    def body(at, ins, outs, kept):
        grad, weight, x, vectors, before = ins
        result, grad_vectors = outs
        *refs, rounded, send, recv, local = kept
        scatter = Scatter(at, send, recv, refs)
        scatter.products(lambda rows: dot_flip(grad[rows], weight[...]))
        scatter.middle()
        scatter.arrive()

        def norm(rows, carry):
            incoming = scatter.total(rows)
            centred, factor = standard(x[rows].astype(f32))
            total = before[rows] + norm_back(incoming, centred, factor, vectors[0:1])
            rounded[rows] = total.astype(bf16)
            return two_sums(incoming, centred, carry)

        gains, shifts = by_rows(BLOCK, 32, norm, no_sums())
        moving = functools.partial(relay_run, relay, at, rounded, result, send, recv, local.at[0], 8)
        moving(False)
        grad_vectors[0:1] = gains
        grad_vectors[1:2] = shifts
        moving(True)
        scatter.end()

    return call(
        body,
        number,
        [grad, joined, x, vectors, grad_rows],
        [shape(384, HALF), shape(8, D, dtype=f32)],
        [*Scatter.scratch, VMEM((BLOCK, D), bf16), *sems(10)],
        beside,
        lambda at: ring_peers(at) + relay.peers(at),
        out_spaces=[ANY, VMEM],
    )


def causal_forward(number, joined, down, beside):
    at_once = 512

    def body(at, ins, outs, kept):
        (qkv, block), (out, logs, all_rows), (send, recv, local) = ins, outs, kept
        gather = Gather(at, block, all_rows, send, recv, local.at[0])
        gather.begin()
        lane = lax.broadcasted_iota(jnp.int32, (at_once, 128), 1)
        square = (at_once, at_once)
        seen = lax.broadcasted_iota(jnp.int32, square, 0) >= lax.broadcasted_iota(jnp.int32, square, 1)
        for i in reversed(range(D // at_once)):
            before, upto = i * at_once, (i + 1) * at_once
            rows = slice(before, upto)
            log_total, blended = jnp.zeros((at_once, 128), f32), []
            for h in range(HEADS):
                a = h * HDIM
                q = head(qkv, rows, a) * EIGHTH
                k = head(qkv, slice(0, upto), COLS + a)
                v = head(qkv, slice(0, upto), 2 * COLS + a)
                scores = dot_flip(q, k)
                last = jnp.where(seen, scores[:, before:], NEGATIVE)
                scores = jnp.concatenate((scores[:, :before], last), axis=1) if i else last
                peak = jnp.max(scores, axis=1, keepdims=True)
                raised = jnp.exp(scores - peak)
                total = jnp.sum(raised, axis=1, keepdims=True)
                blended.append(dot(raised.astype(bf16), v) / total)
                log_total = jnp.where(lane == h, peak + jnp.log(total), log_total)
            out[rows, :] = jnp.concatenate(blended, axis=1).astype(bf16)
            logs[:, rows] = log_total.T[0:8, :]
            if i == 1:
                gather.pass_on()
        gather.pass_far()
        gather.got(2, 5, 6, 7, 8)
        gather.end()

    return call(
        body,
        number,
        [joined, down],
        [shape(D, COLS), shape(8, D, dtype=f32), shape(D, D)],
        sems(9),
        beside,
        ring_peers,
        out_spaces=[VMEM, VMEM, ANY],
    )


def causal_backward(number, joined, grad, logs, activated, contract_w, after, beside):
    at_once = 512

    def body(at, ins, outs, kept):
        (qkv, go, log_rows, activated, contract_own, contract_got, after), (out, result) = ins, outs
        *refs, contract_full, key_sum, value_sum, send, recv, local = kept
        weight = Whole(at, contract_own, contract_got, contract_full, local, 1)
        weight.wait()
        scatter = Scatter(at, send, recv, refs)
        scatter.products(lambda rows: dot(activated[rows], contract_full[...]))
        square = (at_once, at_once)
        seen = lax.broadcasted_iota(jnp.int32, square, 1) >= lax.broadcasted_iota(jnp.int32, square, 0)
        blocks = D // at_once
        for h in range(HEADS):
            a = h * HDIM
            turned = head(qkv, slice(0, D), COLS + a).T
            query_parts = []
            for i in reversed(range(blocks)):
                before, upto = i * at_once, (i + 1) * at_once
                rows = slice(before, upto)
                q = head(qkv, rows, a) * EIGHTH
                g = head(go, rows, a)
                k = head(qkv, slice(0, upto), COLS + a)
                v = head(qkv, slice(0, upto), 2 * COLS + a)
                p = jnp.exp(dot_flip(k, q) - log_rows[h : h + 1, rows])
                last = jnp.where(seen, p[before:], 0.0)
                p = jnp.concatenate((p[:before], last), axis=0) if i else last
                dp = dot_flip(v, g)
                ds = (p * (dp - jnp.sum(p * dp, axis=0, keepdims=True))).astype(bf16)
                value_part, key_part = dot(p.astype(bf16), g), dot(ds, q)
                if i == blocks - 1:
                    key_sum[h, 0:upto, :] = key_part
                    value_sum[h, 0:upto, :] = value_part
                else:
                    key_sum[h, 0:upto, :] += key_part
                    value_sum[h, 0:upto, :] += value_part
                query_parts.append((dot(turned[:, 0:upto], ds) * 0.125).T)
            out[:, a : a + HDIM] = jnp.concatenate(query_parts[::-1], axis=0).astype(bf16)
            if h == 0:
                scatter.middle()
        for h in range(HEADS):
            a = h * HDIM
            out[:, COLS + a : COLS + a + HDIM] = key_sum[h].astype(bf16)
            out[:, 2 * COLS + a : 2 * COLS + a + HDIM] = value_sum[h].astype(bf16)
        scatter.arrive()

        def finish(rows, carry):
            result[rows] = (after[rows] + scatter.total(rows)).astype(bf16)

        by_rows(BLOCK, 32, finish)
        scatter.end()

    return call(
        body,
        number,
        [joined, grad, logs, activated, *contract_w, after],
        [shape(D, 3 * COLS), shape(BLOCK, D)],
        [*Scatter.scratch, VMEM((HALF, D), bf16), VMEM((HEADS, D, HDIM), f32), VMEM((HEADS, D, HDIM), f32), *sems(8)],
        beside,
        ring_peers,
        spaces=[VMEM, VMEM, VMEM, VMEM, ANY, ANY, VMEM],
    )


def on_device(
    layer_input,
    text_states,
    cotangent,
    first_gain,
    first_shift,
    query_weight,
    key_weight,
    value_weight,
    output_weight,
    second_gain,
    second_shift,
    cross_query,
    cross_key,
    cross_value,
    cross_output,
    third_gain,
    third_shift,
    expand_weight,
    contract_weight,
):
    vectors = (first_gain, first_shift, second_gain, second_shift, third_gain, third_shift)
    vectors = jnp.concatenate([jnp.stack(vectors).astype(f32), jnp.zeros((2, HALF), f32)], axis=0)
    joined = jnp.concatenate((query_weight, key_weight, value_weight), axis=1)
    pair = jnp.concatenate((cross_key, cross_value), axis=1)
    n = lax.axis_index("narrow")

    (x, vectors, joined, all_one, qkv), ((down,), (text_got,)) = enter(
        1, layer_input, vectors, joined, [Relay(cotangent), GiveClip(text_states)]
    )
    text_parts = jnp.einsum("csd,dk->csk", text_states, pair, preferred_element_type=f32)
    (attended, logs, all_down), ((text_pair_got,), (out_got,), (query_got,), (cross_got,)) = causal_forward(
        2, qkv, down, [GiveClip(text_parts), Give(output_weight), Give(cross_query), Give(cross_output)]
    )
    out_w, query_w, cross_w = (output_weight, out_got), (cross_query, query_got), (cross_output, cross_got)
    text_pair = (lax.dynamic_index_in_dim(text_parts, n, 0, False) + text_pair_got).astype(bf16)
    (middle, all_two, cross_q, crossed), ((expand_got,), (contract_got,)) = self_to_cross(
        3, attended, out_w, x, vectors, query_w, text_pair, [Give(expand_weight), Give(contract_weight)]
    )
    expand_w, contract_w = (expand_weight, expand_got), (contract_weight, contract_got)
    (after, all_three, activated, grad_expand), _ = feed_forward(
        4, crossed, cross_w, middle, vectors, expand_w, contract_w, all_down, []
    )

    contract_leg = SumZ(outer(activated, all_down).astype(bf16), False)
    expand_leg = SumZ(outer(all_three, grad_expand).astype(bf16), True)
    (grad_two, all_mid_two, grad_cross_q, grad_pair, third), (contract_sum, expand_sum) = feed_forward_back(
        5, grad_expand, expand_w, after, vectors, down, cross_w, cross_q, text_pair, [contract_leg, expand_leg]
    )
    own_text = lax.dynamic_index_in_dim(text_states, n, 0, False)
    first_half, second_half = jnp.where(n == 0, own_text, text_got), jnp.where(n == 0, text_got, own_text)
    text = jnp.concatenate((first_half, second_half), axis=1)
    query_pair_leg = SumZ(
        jnp.concatenate((outer(all_two, grad_cross_q), outer(text, grad_pair)), axis=1).astype(bf16), True
    )
    cross_leg = SumZ(outer(crossed, all_mid_two).astype(bf16), False)
    contract_leg, expand_leg = SumX(contract_leg.finish(contract_sum), False), SumX(expand_leg.finish(expand_sum), True)
    (grad_one, all_mid_one, grad_attended, second), sums = cross_to_self_back(
        6,
        grad_cross_q,
        query_w,
        middle,
        vectors,
        grad_two,
        out_w,
        [contract_leg, expand_leg, query_pair_leg, cross_leg, Give(grad_pair)],
    )
    contract_sum, expand_sum, query_pair_sum, cross_sum, (grad_pair_got,) = sums
    pairs = jnp.where(n == 0, jnp.stack((grad_pair, grad_pair_got)), jnp.stack((grad_pair_got, grad_pair)))
    text_grad = lax.psum(
        jnp.einsum("csk,dk->csd", pairs, pair, preferred_element_type=f32).astype(bf16), "wide"
    ).astype(f32)
    contract_leg, expand_leg = Spread(contract_leg.finish(contract_sum)), Spread(expand_leg.finish(expand_sum))
    query_pair_leg, cross_leg = SumX(query_pair_leg.finish(query_pair_sum), True), SumX(cross_leg.finish(cross_sum), False)
    output_leg = SumZ(outer(attended, all_mid_one).astype(bf16), False)
    (grad_qkv, layer_output), sums = causal_backward(
        7,
        qkv,
        grad_attended,
        logs,
        activated,
        contract_w,
        after,
        [contract_leg, expand_leg, query_pair_leg, cross_leg, output_leg],
    )
    contract_sum, expand_sum, query_pair_sum, cross_sum, output_sum = sums
    contract_grad, expand_grad = contract_leg.finish(contract_sum), expand_leg.finish(expand_sum)
    joined_leg = SumZ(outer(all_one, grad_qkv).astype(bf16), True)
    query_pair_leg, cross_leg = Spread(query_pair_leg.finish(query_pair_sum)), Spread(cross_leg.finish(cross_sum))
    output_leg = SumX(output_leg.finish(output_sum), False)
    (input_grad, first), sums = leave(
        8,
        grad_qkv,
        joined,
        x,
        vectors,
        grad_one,
        [joined_leg, output_leg, query_pair_leg, cross_leg, Relay(layer_output, True)],
    )
    joined_sum, output_sum, query_pair_sum, cross_sum, (layer_output,) = sums
    query_pair_grad, cross_output_grad = query_pair_leg.finish(query_pair_sum), cross_leg.finish(cross_sum)
    parts = jnp.concatenate((first[0:2], second[0:2], third[0:2], jnp.zeros((2, D), f32)), axis=0)
    joined_leg, output_leg = SumX(joined_leg.finish(joined_sum), True), Spread(output_leg.finish(output_sum))
    _, (joined_sum, output_sum, (parts,)) = call(None, 9, [], [], (), [joined_leg, output_leg, ToRing(parts)])
    output_grad = output_leg.finish(output_sum)
    joined_leg = Spread(joined_leg.finish(joined_sum))
    _, (joined_sum, (parts,)) = call(None, 10, [], [], (), [joined_leg, ToClips(jnp.sum(parts, axis=0))])
    joined_grad = joined_leg.finish(joined_sum)
    parts = jnp.sum(parts, axis=(0, 1))
    return (
        layer_output,
        input_grad.astype(f32),
        text_grad,
        parts[0],
        parts[1],
        joined_grad[:, :COLS],
        joined_grad[:, COLS : 2 * COLS],
        joined_grad[:, 2 * COLS :],
        output_grad,
        parts[2],
        parts[3],
        query_pair_grad[:, :COLS],
        query_pair_grad[:, COLS : 2 * COLS],
        query_pair_grad[:, 2 * COLS :],
        cross_output_grad,
        parts[4],
        parts[5],
        expand_grad,
        contract_grad,
    )


def solution(mesh):
    return jax.shard_map(
        on_device,
        mesh=mesh,
        in_specs=(
            P(("dp", "wide"), "narrow"),
            P("dp", None, "narrow"),
            P(("dp", "wide"), "narrow"),
            P("narrow"),
            P("narrow"),
            P("narrow", "wide"),
            P("narrow", "wide"),
            P("narrow", "wide"),
            P("wide", "narrow"),
            P("narrow"),
            P("narrow"),
            P("narrow", "wide"),
            P("narrow", "wide"),
            P("narrow", "wide"),
            P("wide", "narrow"),
            P("narrow"),
            P("narrow"),
            P("narrow", "wide"),
            P("wide", "narrow"),
        ),
        out_specs=(
            P(("dp", "wide"), "narrow"),
            P(("dp", "wide"), "narrow"),
            P("dp", None, "narrow"),
            P("narrow"),
            P("narrow"),
            P("narrow", "wide"),
            P("narrow", "wide"),
            P("narrow", "wide"),
            P("wide", "narrow"),
            P("narrow"),
            P("narrow"),
            P("narrow", "wide"),
            P("narrow", "wide"),
            P("narrow", "wide"),
            P("wide", "narrow"),
            P("narrow"),
            P("narrow"),
            P("narrow", "wide"),
            P("wide", "narrow"),
        ),
        check_vma=False,
    )
```

```python
import functools
import math

import jax
import jax.numpy as jnp
from jax import lax
from jax.experimental import pallas as pl
from jax.experimental.pallas import tpu as pltpu
from jax.sharding import PartitionSpec as P

D = 1536
HALF = 768
HDIM = 64
HEADS = 3
COLS = HEADS * HDIM
BLOCK = 192
EPSILON = 1e-05
NEGATIVE = -1e30
ROOT_HALF = 0.7071067811865476
GAUSS_NORM = 0.3989422804014327
MESH = pl.DeviceIdType.MESH
VMEM = pltpu.VMEM
ANY = pl.ANY
bf16, f32 = jnp.bfloat16, jnp.float32


def dot(a, b):
    return lax.dot_general(a, b, (((1,), (0,)), ((), ())), preferred_element_type=f32)


def dot_flip(a, b):
    return lax.dot_general(a, b, (((1,), (1,)), ((), ())), preferred_element_type=f32)


def outer(a, b):
    return lax.dot_general(a, b, (((0,), (0,)), ((), ())), preferred_element_type=f32)


class Place:
    def __init__(self):
        self.dp, self.w, self.n = (lax.axis_index(a) for a in ("dp", "wide", "narrow"))
        self.y, self.c = lax.div(self.w, 2), lax.rem(self.w, 2)
        self.z, self.s = lax.div(self.dp, 2), lax.rem(self.dp, 2)
        self.up, self.down = lax.rem(self.y + 1, 4), lax.rem(self.y + 3, 4)
        self.across = 3 - self.y
        self.moved = lax.rem(lax.div(self.y, 2) + self.n, 2)
        self.clip = lax.div(self.y, 2)

    def spot(self, y, c):
        moved = lax.rem(lax.div(y, 2) + self.n, 2)
        return (lax.rem(y + moved, 2) * 2 + c) * 2 + moved

    def rows(self, y, c, start=0, size=BLOCK):
        return pl.ds(pl.multiple_of(self.spot(y, c) * BLOCK + start, 32), size)

    def half(self, n):
        return pl.ds(pl.multiple_of(n * HALF, HALF), HALF)

    def at_y(self, y):
        return {"wide": y * 2 + self.c}

    def core(self):
        return {"wide": self.y * 2 + 1 - self.c}

    def x(self):
        return {"narrow": 1 - self.n}

    def at_z(self, k):
        return {"dp": lax.rem(self.z + k, 4) * 2 + self.s}

    def at_dp(self, k):
        return {"dp": lax.rem(self.dp + k, 8)}

    def at_x(self, ds, dn):
        return {"dp": self.z * 2 + lax.rem(self.s + ds, 2), "narrow": lax.rem(self.n + dn, 2)}


def remote(src, dst, send, recv, peer):
    return pltpu.make_async_remote_copy(
        src_ref=src, dst_ref=dst, send_sem=send, recv_sem=recv, device_id=peer, device_id_type=MESH
    )


def greet(peers):
    barrier = pltpu.get_barrier_semaphore()
    for peer in peers:
        pl.semaphore_signal(barrier, inc=1, device_id=peer, device_id_type=MESH)
    pl.semaphore_wait(barrier, len(peers))


class Give:
    def __init__(self, array):
        self.ins, self.copies, self.locals = [array], 1, 0
        self.outs = [jax.ShapeDtypeStruct(array.shape, array.dtype)]

    def peers(self, at):
        return [("x", at.x())]

    def moves(self, at, ins, outs):
        return [(ins[0], outs[0], at.x())], []


class GiveClip(Give):
    def __init__(self, array):
        super().__init__(array)
        self.outs = [jax.ShapeDtypeStruct(array.shape[1:], array.dtype)]

    def moves(self, at, ins, outs):
        return [(ins[0].at[1 - at.n], outs[0], at.x())], []


class SumZ:
    def __init__(self, array, by_rows):
        self.by_rows, self.copies, self.locals = by_rows, 3, 0
        rows, cols = array.shape
        shape = (2, 4, rows // 8, cols) if by_rows else (4, rows // 4, cols)
        self.ins = [array.reshape(shape)]
        kept = (2, rows // 8, cols) if by_rows else (rows // 4, cols)
        self.outs = [jax.ShapeDtypeStruct((3, *kept), array.dtype)]

    def peers(self, at):
        return [(f"z{k}", at.at_z(k)) for k in (1, 2, 3)]

    def moves(self, at, ins, outs):
        out = []
        for k in (1, 2, 3):
            q = lax.rem(at.z + k, 4)
            src = ins[0].at[:, q] if self.by_rows else ins[0].at[q]
            out.append((src, outs[0].at[k - 1], at.at_z(k)))
        return out, []

    def finish(self, outs):
        z = lax.div(lax.axis_index("dp"), 2)
        own = lax.dynamic_index_in_dim(self.ins[0], z, 1 if self.by_rows else 0, False)
        return (own.astype(f32) + outs[0].astype(f32).sum(axis=0)).astype(bf16)


class SumX:
    def __init__(self, array, by_rows):
        self.by_rows, self.copies, self.locals = by_rows, 3, 0
        if by_rows:
            two, rows, cols = array.shape
            self.ins, kept = [array.reshape(2, 2, rows // 2, cols)], (rows // 2, cols)
        else:
            rows, cols = array.shape
            self.ins, kept = [array.reshape(2, rows // 2, cols)], (rows // 2, HALF)
        self.outs = [jax.ShapeDtypeStruct((3, *kept), array.dtype)]

    order = ((0, 1), (1, 0), (1, 1))

    def peers(self, at):
        return [(f"x{a}{b}", at.at_x(a, b)) for a, b in self.order]

    def moves(self, at, ins, outs):
        out = []
        for i, (a, b) in enumerate(self.order):
            s, n = lax.rem(at.s + a, 2), lax.rem(at.n + b, 2)
            src = ins[0].at[n, s] if self.by_rows else ins[0].at[s, :, at.half(n)]
            out.append((src, outs[0].at[i], at.at_x(a, b)))
        return out, []

    def finish(self, outs):
        s, n = lax.rem(lax.axis_index("dp"), 2), lax.axis_index("narrow")
        if self.by_rows:
            own = lax.dynamic_index_in_dim(lax.dynamic_index_in_dim(self.ins[0], n, 0, False), s, 0, False)
        else:
            own = lax.dynamic_slice_in_dim(lax.dynamic_index_in_dim(self.ins[0], s, 0, False), n * HALF, HALF, 1)
        return (own.astype(f32) + outs[0].astype(f32).sum(axis=0)).astype(bf16)


class Spread:
    def __init__(self, array):
        self.ins, self.copies, self.locals = [array], 7, 1
        self.outs = [jax.ShapeDtypeStruct((8, *array.shape), array.dtype)]

    def peers(self, at):
        return [(f"d{k}", at.at_dp(k)) for k in range(1, 8)]

    def moves(self, at, ins, outs):
        dst = outs[0].at[at.dp]
        return [(ins[0], dst, at.at_dp(k)) for k in range(1, 8)], [(ins[0], dst)]

    def finish(self, outs):
        eight, rows, cols = outs[0].shape
        return outs[0].reshape(eight * rows, cols).astype(f32)


class ToRing:
    def __init__(self, array):
        self.ins, self.copies, self.locals = [array], 7, 1
        self.outs = [jax.ShapeDtypeStruct((8, *array.shape), array.dtype)]

    def peers(self, at):
        return [(f"w{k}", {"wide": lax.rem(at.w + k, 8)}) for k in range(1, 8)]

    def moves(self, at, ins, outs):
        dst = outs[0].at[at.w]
        return [(ins[0], dst, peer) for _, peer in self.peers(at)], [(ins[0], dst)]


class Trade:
    def __init__(self, array):
        self.ins, self.copies, self.locals = [array], 7, 1
        self.outs = [jax.ShapeDtypeStruct(array.shape, array.dtype)]

    def others(self, at):
        return [lax.rem(at.w + k, 8) for k in range(1, 8)]

    def peers(self, at):
        return [(f"w{k + 1}", {"wide": w}) for k, w in enumerate(self.others(at))]

    def moves(self, at, ins, outs):
        mine = at.spot(at.y, at.c)
        dst = outs[0].at[mine]
        far = [(ins[0].at[at.spot(lax.div(w, 2), lax.rem(w, 2))], dst, {"wide": w}) for w in self.others(at)]
        return far, [(ins[0].at[mine], dst)]


class ToSpots(ToRing):
    def moves(self, at, ins, outs):
        dst = outs[0].at[at.spot(at.y, at.c)]
        return [(ins[0], dst, peer) for _, peer in self.peers(at)], [(ins[0], dst)]


class ToClips:
    def __init__(self, array):
        self.ins, self.copies, self.locals = [array], 15, 1
        self.outs = [jax.ShapeDtypeStruct((8, 2, array.shape[0], HALF), array.dtype)]

    order = tuple((k, b) for k in range(8) for b in range(2))[1:]

    def peers(self, at):
        return [(f"c{k}{b}", {**at.at_dp(k), "narrow": lax.rem(at.n + b, 2)}) for k, b in self.order]

    def moves(self, at, ins, outs):
        dst = outs[0].at[at.dp, at.n]
        far = []
        for (k, b), (_, peer) in zip(self.order, self.peers(at)):
            far.append((ins[0].at[:, at.half(lax.rem(at.n + b, 2))], dst, peer))
        return far, [(ins[0].at[:, at.half(at.n)], dst)]


class Relay:
    def __init__(self, array, back=False):
        self.ins, self.back, self.copies, self.locals = [array], back, 2, 1
        shape = (384, HALF) if back else (BLOCK, D)
        self.outs = [jax.ShapeDtypeStruct(shape, array.dtype)]

    def peers(self, at):
        return [
            ("x", at.x()),
            ("a0", {"wide": at.across * 2 + at.c}),
            ("a1", {"wide": at.across * 2 + at.c, "narrow": 1 - at.n}),
        ]


def relay_run(relay, at, src, dst, send, recv, local, base, finish):
    mine, other = at.half(at.n), at.half(1 - at.n)
    over = at.across * 2 + at.c
    if relay.back:
        row = pl.ds(pl.multiple_of(at.moved * BLOCK, BLOCK), BLOCK)
        to = recv.at[base + at.moved]
        own = src.at[:, mine], src.at[:, other]
        land = dst.at[0:BLOCK], dst.at[BLOCK : 2 * BLOCK]
    else:
        row = mine
        to = recv.at[base + at.n]
        own = src.at[0:BLOCK], src.at[BLOCK : 2 * BLOCK]
        land = dst.at[:, at.half(0)], dst.at[:, at.half(1)]
    target = dst.at[row] if relay.back else dst.at[:, row]

    def arrive(slot, part):
        return remote(own[0], part, send.at[base], recv.at[base + slot], at.x())

    @pl.when(at.moved == 0)
    def _():
        stay = pltpu.make_async_copy(own[0], target, local)
        if relay.back:
            go = remote(own[1], target, send.at[base], to, at.x())
        else:
            go = remote(own[1], target, send.at[base], to, {"wide": over})
        if not finish:
            go.start()
            stay.start()
        else:
            stay.wait()
            go.wait_send()
            if relay.back:
                arrive(1, land[1]).wait_recv()
            else:
                arrive(1 - at.n, dst.at[:, other]).wait_recv()

    @pl.when(at.moved == 1)
    def _():
        if relay.back:
            first = remote(own[1], target, send.at[base], to, {"wide": over, "narrow": 1 - at.n})
            second = remote(own[0], target, send.at[base + 1], to, {"wide": over})
        else:
            first = remote(own[1], target, send.at[base], to, {"wide": over, "narrow": 1 - at.n})
            second = remote(own[0], target, send.at[base + 1], to, at.x())
        if not finish:
            first.start()
            second.start()
        else:
            first.wait_send()
            second.wait_send()
            arrive(0, land[0]).wait_recv()
            arrive(1, land[1]).wait_recv()


def call(body, number, ins, outs, scratch=(), beside=(), peers=None, spaces=None, out_spaces=None, late=False):
    spaces = spaces or [VMEM] * len(ins)
    out_spaces = out_spaces or [VMEM] * len(outs)
    copies = sum(b.copies for b in beside)
    locals_ = sum(b.locals for b in beside)
    side_ins = [a for b in beside for a in b.ins]
    side_outs = [a for b in beside for a in b.outs]
    n_in, n_out, n_scratch = len(ins), len(outs), len(scratch)

    def kernel(*refs):
        at = Place()
        refs = list(refs)

        def take(count):
            out = refs[:count]
            del refs[:count]
            return out

        main_in, side_in = take(n_in), take(len(side_ins))
        main_out, side_out, kept = take(n_out), take(len(side_outs)), take(n_scratch)
        send, recv, local = take(3)
        known = dict(peers(at)) if peers else {}
        for b in beside:
            known.update(dict(b.peers(at)))
        if known:
            greet(list(known.values()))
        side_refs = [([side_in.pop(0) for _ in b.ins], [side_out.pop(0) for _ in b.outs]) for b in beside]
        todo = []

        def start():
            slot, place = 0, 0
            for b, (i, o) in zip(beside, side_refs):
                if isinstance(b, Relay):
                    run = functools.partial(relay_run, b, at, i[0], o[0], send, recv, local.at[place], slot)
                    run(False)
                    todo.append(functools.partial(run, True))
                    slot, place = slot + 2, place + 1
                    continue
                far, near = b.moves(at, i, o)
                for src, dst, peer in far:
                    copy = remote(src, dst, send.at[slot], recv.at[slot], peer)
                    copy.start()
                    todo.append(copy.wait)
                    slot += 1
                for src, dst in near:
                    copy = pltpu.make_async_copy(src, dst, local.at[place])
                    copy.start()
                    todo.append(copy.wait)
                    place += 1

        at.start_beside = start
        if not late:
            start()
        if body:
            body(at, main_in, main_out, kept)
        for wait in todo:
            wait()

    results = pl.pallas_call(
        kernel,
        out_shape=tuple(outs) + tuple(side_outs),
        in_specs=[pl.BlockSpec(memory_space=s) for s in spaces] + [pl.BlockSpec(memory_space=ANY)] * len(side_ins),
        out_specs=tuple(pl.BlockSpec(memory_space=m) for m in out_spaces + [ANY] * len(side_outs)),
        scratch_shapes=[
            *scratch,
            pltpu.SemaphoreType.DMA((max(copies, 1),)),
            pltpu.SemaphoreType.DMA((max(copies, 1),)),
            pltpu.SemaphoreType.DMA((max(locals_, 1),)),
        ],
        compiler_params=pltpu.CompilerParams(
            collective_id=number, has_side_effects=True, vmem_limit_bytes=58 << 20
        ),
    )(*ins, *side_ins)
    results = list(results)
    main, rest = results[: len(outs)], results[len(outs) :]
    sides = []
    for b in beside:
        sides.append(rest[: len(b.outs)])
        del rest[: len(b.outs)]
    return main, sides


def ring_peers(at):
    return [("up", at.at_y(at.up)), ("down", at.at_y(at.down)), ("core", at.core())]


def sems(count):
    return [pltpu.SemaphoreType.DMA((count,)), pltpu.SemaphoreType.DMA((count,)), pltpu.SemaphoreType.DMA((count,))]


def by_rows(count, size, work, carry=None):
    def step(i, carry):
        return work(pl.ds(pl.multiple_of(i * size, size), size), carry)

    return lax.fori_loop(0, count // size, step, carry)


class Whole:
    def __init__(self, at, own, got, full, sem, axis):
        size = own.shape[axis]
        self.copies = []
        for i, (part, n) in enumerate(((own, at.n), (got, 1 - at.n))):
            where = pl.ds(pl.multiple_of(n * size, size), size)
            target = full.at[where] if axis == 0 else full.at[:, where]
            self.copies.append(pltpu.make_async_copy(part, target, sem.at[i]))
            self.copies[-1].start()

    def wait(self):
        for copy in self.copies:
            copy.wait()


class Gather:
    slots = 11

    def __init__(self, at, x, whole, send, recv, local, base=0):
        self.at, self.x, self.whole = at, x, whole
        y, c, up, down = at.y, at.c, at.up, at.down
        far = lax.rem(y + 2, 4)
        half = BLOCK // 2

        def move(slot, y_from, peer, start=0, size=BLOCK, first=False):
            rows = at.rows(y_from, c, start, size)
            src = whole.at[rows]
            if first:
                src = x if size == BLOCK else x.at[start : start + size]
            return remote(src, whole.at[rows], send.at[base + slot], recv.at[base + slot], peer)

        to_up, to_down, core = at.at_y(up), at.at_y(down), at.core()
        self.sends = [
            move(0, y, to_up, 0, half, first=True),
            move(1, y, to_up, half, half, first=True),
            move(2, y, to_down, half, half, first=True),
            move(3, y, to_down, 0, half, first=True),
            move(4, y, core, first=True),
            move(5, down, to_up, 0, half),
            move(6, up, to_down, half, half),
            move(7, down, core),
            move(8, up, core),
            move(9, far, core, 0, half),
            move(10, far, core, half, half),
        ]
        self.own = pltpu.make_async_copy(x, whole.at[at.rows(y, c)], local)

    def begin(self):
        for i in (0, 2, 1, 3, 4):
            self.sends[i].start()
        self.own.start()
        self.own.wait()

    def chain(self, *pairs):
        for arrived, leaving in pairs:
            self.sends[arrived].wait_recv()
            self.sends[leaving].start()

    def pass_on(self):
        self.chain((0, 5), (2, 6))

    def pass_near(self):
        self.chain((1, 7), (3, 8))

    def pass_far(self):
        self.chain((5, 9), (6, 10))

    def got(self, *slots):
        for i in slots:
            self.sends[i].wait_recv()

    def end(self):
        for copy in self.sends:
            copy.wait_send()

    def finish(self):
        self.pass_on()
        self.pass_near()
        self.pass_far()
        self.got(4, 7, 8, 9, 10)
        self.end()

    def each(self, work):
        at = self.at

        def step(s, carry):
            @pl.when(s == 1)
            def _():
                self.got(4)
                self.pass_on()

            @pl.when(s == 2)
            def _():
                self.pass_near()

            @pl.when(s == 3)
            def _():
                self.got(8)

            @pl.when(s == 5)
            def _():
                self.got(7)

            @pl.when(s == 6)
            def _():
                self.pass_far()

            @pl.when(s == 7)
            def _():
                self.got(9, 10)

            g = lax.div(s, 2)
            off = g + lax.div(g, 2) - 2 * lax.div(g, 3)
            work(s, at.rows(lax.rem(at.y + off, 4), lax.rem(at.c + s, 2)))
            return carry

        lax.fori_loop(0, 8, step, 0)
        self.end()


class Scatter:
    slots = 10
    scratch = [
        VMEM((4, BLOCK, D), bf16),
        VMEM((4, BLOCK, D), bf16),
        VMEM((4, BLOCK, D), f32),
        VMEM((2, BLOCK, D), bf16),
        VMEM((2, BLOCK, D), bf16),
        VMEM((2, BLOCK // 2, D), bf16),
        VMEM((2, BLOCK // 2, D), bf16),
    ]

    def __init__(self, at, send, recv, refs, base=0):
        self.at, self.send, self.recv, self.base = at, send, recv, base
        self.out_c, self.in_c, self.own, self.out_y, self.in_y, self.half_out, self.half_in = refs
        half = BLOCK // 2
        peers = at.at_y(at.up), at.at_y(at.down)

        def move(slot, src, dst, peer):
            return remote(src, dst, send.at[base + slot], recv.at[base + slot], peer)

        self.cores = [self.core(g) for g in range(4)]
        self.halves = [move(4 + i, self.half_out.at[i], self.half_in.at[i], peers[i]) for i in range(2)]
        free = [pl.ds((1 - i) * half, half) for i in range(2)]
        bound = [pl.ds(i * half, half) for i in range(2)]
        self.free = [move(6 + i, self.out_y.at[i, free[i]], self.in_y.at[i, free[i]], peers[i]) for i in range(2)]
        self.bound = [move(8 + i, self.out_y.at[i, bound[i]], self.in_y.at[i, bound[i]], peers[i]) for i in range(2)]

    def core(self, g):
        slot = self.base + g
        return remote(self.out_c.at[g], self.in_c.at[g], self.send.at[slot], self.recv.at[slot], self.at.core())

    def both(self, g, rows):
        return self.own[g, rows] + self.in_c[g, rows].astype(f32)

    def products(self, product):
        at = self.at
        half = BLOCK // 2

        def part_rows(rows, i):
            return pl.ds(pl.multiple_of(rows.start + i * half, 32), 32)

        def send_free(i):
            self.cores[1 + i].wait_recv()

            def add(rows, carry):
                there = part_rows(rows, 1 - i)
                self.out_y[i, there] = self.both(1 + i, there).astype(bf16)

            by_rows(half, 32, add)
            self.free[i].start()

        def step(s, carry):
            g = lax.div(s, 2)
            off = lax.rem(6 - g + 3 * lax.div(g, 2) + 2 * lax.div(g, 3), 4)
            part = product(at.rows(lax.rem(at.y + off, 4), lax.rem(at.c + 1 + s, 2)))

            @pl.when(lax.rem(s, 2) == 0)
            def _():
                self.out_c[g] = part.astype(bf16)
                self.core(g).start()

            @pl.when(lax.rem(s, 2) == 1)
            def _():
                self.own[g] = part

            @pl.when(s == 2)
            def _():
                self.cores[0].wait_recv()
                for i in range(2):

                    def add(rows, carry, i=i):
                        self.half_out[i, rows] = self.both(0, part_rows(rows, i)).astype(bf16)

                    by_rows(half, 32, add)
                    self.halves[i].start()

            @pl.when(s == 4)
            def _():
                send_free(0)

            @pl.when(s == 6)
            def _():
                send_free(1)

            return carry

        lax.fori_loop(0, 8, step, 0)

    def middle(self):
        half = BLOCK // 2
        for i in range(2):
            self.halves[i].wait_recv()

            def add(rows, carry, i=i):
                here = pl.ds(pl.multiple_of(rows.start + i * half, 32), 32)
                self.out_y[i, here] = (self.both(1 + i, here) + self.half_in[i, rows].astype(f32)).astype(bf16)

            by_rows(half, 32, add)
            self.bound[i].start()

    def arrive(self):
        self.cores[3].wait_recv()
        for copy in self.free + self.bound:
            copy.wait_recv()

    def total(self, rows):
        return self.both(3, rows) + self.in_y[0, rows].astype(f32) + self.in_y[1, rows].astype(f32)

    def end(self):
        for copy in self.cores + self.halves + self.free + self.bound:
            copy.wait_send()


def standard(values):
    average = jnp.mean(values, axis=1, keepdims=True)
    variance = jnp.mean(values * values, axis=1, keepdims=True) - average * average
    factor = lax.rsqrt(variance + EPSILON)
    return (values - average) * factor, factor


def norm_back(incoming, centred, factor, gain):
    scaled = incoming * gain
    first = jnp.mean(scaled, axis=1, keepdims=True)
    second = jnp.mean(scaled * centred, axis=1, keepdims=True)
    return factor * (scaled - first - centred * second)


def two_sums(incoming, centred, carry):
    gains, shifts = carry
    return gains + jnp.sum(incoming * centred, axis=0, keepdims=True), shifts + jnp.sum(incoming, axis=0, keepdims=True)


def no_sums():
    return jnp.zeros((1, D), f32), jnp.zeros((1, D), f32)


EIGHTH = 0.125


def shape(*dims, dtype=bf16):
    return jax.ShapeDtypeStruct(dims, dtype)


class Keep:
    def __init__(self, whole, out, sem, base):
        self.whole, self.out, self.sem, self.base = whole, out, sem, base

    def block(self, s, rows):
        pltpu.make_async_copy(self.whole.at[rows], self.out.at[rows], self.sem.at[self.base + s]).start()

    def wait(self):
        for s in range(8):
            some = pl.ds(0, BLOCK)
            pltpu.make_async_copy(self.whole.at[some], self.out.at[some], self.sem.at[self.base + s]).wait()


def enter(number, layer_input, vectors, weights, beside):
    relay = Relay(layer_input)

    def body(at, ins, outs, kept):
        (source, own_vectors, *own_weights), (x, vectors, weight, all_rows, qkv) = ins, outs
        normed, whole, send, recv, local = kept
        half = at.half(at.n)
        moving = functools.partial(relay_run, relay, at, source, x, send, recv, local.at[0], 11)
        moving(False)
        stay, go = [], []
        for i, (own, target) in enumerate(
            [(own_vectors, vectors.at[:, half])]
            + [(own, weight.at[j * COLS : (j + 1) * COLS, half]) for j, own in enumerate(own_weights)]
        ):
            stay.append(pltpu.make_async_copy(own, target, local.at[1 + i]))
            go.append(remote(own, target, send.at[13 + i], recv.at[13 + i], at.x()))
        stay[0].start()
        go[0].start()
        stay[0].wait()
        go[0].wait_recv()
        moving(True)
        for copy in stay[1:] + go[1:]:
            copy.start()

        def norm(rows, carry):
            centred, _ = standard(x[rows].astype(f32))
            normed[rows] = (centred * vectors[0:1] + vectors[1:2]).astype(bf16)

        by_rows(BLOCK, 32, norm)
        gather = Gather(at, normed, whole, send, recv, local.at[5])
        gather.begin()
        at.start_beside()
        keep = Keep(whole, all_rows, local, 6)
        gather.each(keep.block)
        for copy in stay[1:]:
            copy.wait()
        for copy in go[1:]:
            copy.wait_recv()

        def times(rows, carry):
            qkv[rows] = dot_flip(whole[rows], weight[...]).astype(bf16)

        by_rows(D, BLOCK, times)
        keep.wait()
        for copy in go:
            copy.wait_send()

    return call(
        body,
        number,
        [layer_input, vectors, *weights],
        [shape(BLOCK, D), shape(8, D, dtype=f32), shape(3 * COLS, D), shape(D, D), shape(D, 3 * COLS)],
        [VMEM((BLOCK, D), bf16), VMEM((D, D), bf16), *sems(17)],
        beside,
        lambda at: ring_peers(at) + relay.peers(at) + [("x", at.x())],
        out_spaces=[VMEM, VMEM, VMEM, ANY, VMEM],
        late=True,
    )


def causal_forward(number, joined, query_w, out_w, text_pair, beside):
    at_once = 512

    def body(at, ins, outs, kept):
        (qkv, query_own, query_got, out_own, out_got, pair), (out, logs, all_keys, all_values) = ins, outs
        parts, mixed, keys, values, send, recv, local = kept
        half, other = at.half(at.n), at.half(1 - at.n)
        for own, got, target, axis in ((query_own, query_got, keys, 0), (out_own, out_got, values, 1)):
            for cols, ref in ((half, own), (other, got)):
                for h in range(HEADS):
                    rows = slice(h * HDIM, (h + 1) * HDIM)
                    text = pair[:, axis * COLS + h * HDIM : axis * COLS + (h + 1) * HDIM]
                    product = dot(text, ref[rows, :])
                    target[rows, cols] = (product * EIGHTH if axis == 0 else product).astype(bf16)
        first = Gather(at, keys, all_keys, send, recv, local.at[0])
        second = Gather(at, values, all_values, send, recv, local.at[1], 11)
        first.begin()
        for i in range(3):
            for h in range(HEADS):
                a = i * COLS + h * HDIM
                piece = qkv[:, a : a + HDIM]
                parts[i, h] = piece * EIGHTH if i == 0 else piece
        square = (at_once, at_once)
        seen = lax.broadcasted_iota(jnp.int32, square, 0) >= lax.broadcasted_iota(jnp.int32, square, 1)

        def one(h, carry):
            for i in reversed(range(D // at_once)):
                before, upto = i * at_once, (i + 1) * at_once
                rows = slice(before, upto)
                scores = dot_flip(parts[0, h, rows], parts[1, h, 0:upto])
                last = jnp.where(seen, scores[:, before:], NEGATIVE)
                scores = jnp.concatenate((scores[:, :before], last), axis=1) if i else last
                peak = jnp.max(scores, axis=1, keepdims=True)
                raised = jnp.exp(scores - peak)
                total = jnp.sum(raised, axis=1, keepdims=True)
                mixed[h, rows] = (dot(raised.astype(bf16), parts[2, h, 0:upto]) / total).astype(bf16)
                column = jnp.broadcast_to(peak + jnp.log(total), (at_once, 128))
                logs[pl.ds(h, 1), rows] = column.T[0:1, :]

            @pl.when(h == 0)
            def _():
                first.pass_on()
                second.begin()
                first.pass_near()

            @pl.when(h == 1)
            def _():
                first.pass_far()
                second.pass_on()

            return carry

        lax.fori_loop(0, HEADS, one, 0)
        second.pass_near()
        out[...] = jnp.concatenate([mixed[h] for h in range(HEADS)], axis=1)
        second.pass_far()
        for gather in (first, second):
            gather.got(4, 7, 8, 9, 10)
            gather.end()

    return call(
        body,
        number,
        [joined, *query_w, *out_w, text_pair],
        [shape(D, COLS), shape(8, D, dtype=f32), shape(D, D), shape(D, D)],
        [VMEM((3, HEADS, D, HDIM), bf16), VMEM((HEADS, D, HDIM), bf16), VMEM((BLOCK, D), bf16), VMEM((BLOCK, D), bf16), *sems(22)],
        beside,
        ring_peers,
        out_spaces=[VMEM, VMEM, ANY, ANY],
    )


def forward_rest(number, attended, out_w, x, vectors, keys, values, down, expand_w, contract):
    def body(at, ins, outs, kept):
        mixed, out_own, out_got, x, vectors, keys, values, down, expand_own, expand_got, contract_own = ins
        middle, after, normed_two, weights, all_rows, all_down, activated, grad, contract_out = outs
        *refs, normed, whole, downs, out_full, expand_full, contract_full, key_full, value_full, branch, send, recv, local = kept
        half = at.half(at.n)
        weight = Whole(at, out_own, out_got, out_full, local.at[pl.ds(0, 2)], 1)
        swap = remote(contract_own, contract_full.at[:, half], send.at[32], recv.at[32], at.x())
        swap.start()
        later = [
            pltpu.make_async_copy(keys, key_full, local.at[2]),
            pltpu.make_async_copy(values, value_full, local.at[3]),
            pltpu.make_async_copy(contract_own, contract_full.at[:, half], local.at[4]),
        ]
        for copy in later:
            copy.start()
        later.append(Whole(at, expand_own, expand_got, expand_full, local.at[pl.ds(5, 2)], 0))
        weight.wait()
        scatter = Scatter(at, send, recv, refs)
        scatter.products(lambda rows: dot(mixed[rows], out_full[...]))
        scatter.middle()
        for copy in later:
            copy.wait()
        scatter.arrive()
        cotangents = Gather(at, down, downs, send, recv, local.at[7], 10)
        cotangents.begin()

        def norm_two(rows, carry):
            total = x[rows].astype(f32) + scatter.total(rows)
            middle[rows] = total
            centred, _ = standard(total)
            normed_two[rows] = (centred * vectors[2:3] + vectors[3:4]).astype(bf16)

        by_rows(BLOCK, 32, norm_two)

        def cross(b, carry):
            rows = pl.ds(pl.multiple_of(b * BLOCK, BLOCK), BLOCK)
            scores = dot_flip(key_full[rows], normed_two[...]).reshape(HEADS, 64, BLOCK)
            raised = jnp.exp(scores - jnp.max(scores, axis=1, keepdims=True))
            p = raised / jnp.sum(raised, axis=1, keepdims=True)
            p = p.reshape(BLOCK, BLOCK).T.astype(bf16)
            weights[b] = p
            part = dot(p, value_full[rows])

            @pl.when(b == 0)
            def _():
                branch[...] = part

            @pl.when(b > 0)
            def _():
                branch[...] += part

            @pl.when(b == 3)
            def _():
                cotangents.pass_on()
                cotangents.pass_near()

            return carry

        lax.fori_loop(0, 8, cross, 0)

        def norm_three(rows, carry):
            total = middle[rows] + branch[rows]
            after[rows] = total
            centred, _ = standard(total)
            normed[rows] = (centred * vectors[4:5] + vectors[5:6]).astype(bf16)

        by_rows(BLOCK, 32, norm_three)
        gather = Gather(at, normed, whole, send, recv, local.at[8], 21)
        gather.begin()
        cotangents.pass_far()
        cotangents.got(4, 7, 8, 9, 10)
        keep_down = pltpu.make_async_copy(downs, all_down, local.at[9])
        keep_down.start()
        swap.wait_recv()
        keep_contract = pltpu.make_async_copy(contract_full, contract_out, local.at[10])
        keep_contract.start()
        keep = Keep(whole, all_rows, local, 11)

        def work(s, rows):
            keep.block(s, rows)
            hidden = dot(whole[rows], expand_full[...])
            back = dot_flip(downs[rows], contract_full[...])
            bell = 0.5 * (1.0 + lax.erf(hidden * ROOT_HALF))
            activated[rows] = (hidden * bell).astype(bf16)
            grad[rows] = (back * (bell + hidden * jnp.exp(-0.5 * hidden * hidden) * GAUSS_NORM)).astype(bf16)

        gather.each(work)
        keep.wait()
        keep_down.wait()
        keep_contract.wait()
        cotangents.end()
        scatter.end()
        swap.wait_send()

    results, _ = call(
        body,
        number,
        [attended, *out_w, x, vectors, keys, values, down, *expand_w, contract],
        [
            shape(BLOCK, D, dtype=f32),
            shape(BLOCK, D, dtype=f32),
            shape(BLOCK, D),
            shape(8, BLOCK, BLOCK),
            shape(D, D),
            shape(D, D),
            shape(D, HALF),
            shape(D, HALF),
            shape(HALF, D),
        ],
        [
            *Scatter.scratch,
            VMEM((BLOCK, D), bf16),
            VMEM((D, D), bf16),
            VMEM((D, D), bf16),
            VMEM((COLS, D), bf16),
            VMEM((D, HALF), bf16),
            VMEM((HALF, D), bf16),
            VMEM((D, D), bf16),
            VMEM((D, D), bf16),
            VMEM((BLOCK, D), f32),
            *sems(33),
        ],
        (),
        lambda at: ring_peers(at) + [("x", at.x())],
        spaces=[VMEM, ANY, ANY, VMEM, VMEM, ANY, ANY, VMEM, ANY, ANY, ANY],
        out_spaces=[VMEM, VMEM, VMEM, VMEM, ANY, ANY, VMEM, VMEM, ANY],
    )
    return results


def backward_rest(number, grad, expand_w, after, middle, vectors, down, keys, values, weights, normed_two, out_w, beside):
    def body(at, ins, outs, kept):
        grad, expand_own, expand_got, after, middle, vectors, down, keys, values, weights, normed_two, out_own, out_got = ins
        grad_rows, rounded_two, grad_scores, all_two, all_rows, grad_mixed, grad_vectors = outs
        *refs, rounded, whole, second, out_full, expand_full, key_full, value_full, send, recv, local = kept
        weight = Whole(at, expand_own, expand_got, expand_full, local.at[pl.ds(0, 2)], 0)
        later = [
            pltpu.make_async_copy(keys, key_full, local.at[2]),
            pltpu.make_async_copy(values, value_full, local.at[3]),
        ]
        for copy in later:
            copy.start()
        later.append(Whole(at, out_own, out_got, out_full, local.at[pl.ds(4, 2)], 1))
        weight.wait()
        scatter = Scatter(at, send, recv, refs)
        scatter.products(lambda rows: dot_flip(grad[rows], expand_full[...]))
        scatter.middle()
        for copy in later:
            copy.wait()
        scatter.arrive()
        before = Gather(at, normed_two, all_two, send, recv, local.at[6], 10)
        before.begin()

        def norm_three(rows, carry):
            incoming = scatter.total(rows)
            centred, factor = standard(after[rows])
            total = down[rows].astype(f32) + norm_back(incoming, centred, factor, vectors[4:5])
            grad_rows[rows] = total
            rounded_two[rows] = total.astype(bf16)
            return two_sums(incoming, centred, carry)

        gains, shifts = by_rows(BLOCK, 32, norm_three, no_sums())
        grad_vectors[4:5] = gains
        grad_vectors[5:6] = shifts

        def cross(b, carry):
            rows = pl.ds(pl.multiple_of(b * BLOCK, BLOCK), BLOCK)
            p = weights[b].astype(f32).T.reshape(HEADS, 64, BLOCK)
            dp = dot_flip(value_full[rows], rounded_two[...]).reshape(HEADS, 64, BLOCK)
            ds = p * (dp - jnp.sum(p * dp, axis=1, keepdims=True))
            ds = ds.reshape(BLOCK, BLOCK).T.astype(bf16)
            grad_scores[b] = ds
            part = dot(ds, key_full[rows])

            @pl.when(b == 0)
            def _():
                second[...] = part

            @pl.when(b > 0)
            def _():
                second[...] += part

            @pl.when(b == 3)
            def _():
                before.pass_on()
                before.pass_near()

            return carry

        lax.fori_loop(0, 8, cross, 0)

        def norm_two(rows, carry):
            incoming = second[rows]
            centred, factor = standard(middle[rows])
            total = grad_rows[rows] + norm_back(incoming, centred, factor, vectors[2:3])
            grad_rows[rows] = total
            rounded[rows] = total.astype(bf16)
            return two_sums(incoming, centred, carry)

        gains, shifts = by_rows(BLOCK, 32, norm_two, no_sums())
        grad_vectors[2:3] = gains
        grad_vectors[3:4] = shifts
        gather = Gather(at, rounded, whole, send, recv, local.at[7], 21)
        gather.begin()
        before.pass_far()
        keep = Keep(whole, all_rows, local, 8)

        def work(s, rows):
            keep.block(s, rows)
            grad_mixed[rows] = dot_flip(whole[rows], out_full[...]).astype(bf16)

        gather.each(work)
        before.got(4, 7, 8, 9, 10)
        before.end()
        keep.wait()
        scatter.end()

    return call(
        body,
        number,
        [grad, *expand_w, after, middle, vectors, down, keys, values, weights, normed_two, *out_w],
        [
            shape(BLOCK, D, dtype=f32),
            shape(BLOCK, D),
            shape(8, BLOCK, BLOCK),
            shape(D, D),
            shape(D, D),
            shape(D, COLS),
            shape(8, D, dtype=f32),
        ],
        [
            *Scatter.scratch,
            VMEM((BLOCK, D), bf16),
            VMEM((D, D), bf16),
            VMEM((BLOCK, D), f32),
            VMEM((COLS, D), bf16),
            VMEM((D, HALF), bf16),
            VMEM((D, D), bf16),
            VMEM((D, D), bf16),
            *sems(32),
        ],
        beside,
        ring_peers,
        spaces=[VMEM, ANY, ANY, VMEM, VMEM, VMEM, VMEM, ANY, ANY, VMEM, VMEM, ANY, ANY],
        out_spaces=[VMEM, VMEM, VMEM, ANY, ANY, VMEM, VMEM],
    )


def causal_backward(number, joined, grad, logs, activated, contract, after, rounded_two, beside):
    at_once = 512

    def body(at, ins, outs, kept):
        (qkv, go, log_rows, activated, contract, after, block), (out, result, all_rows) = ins, outs
        *refs, parts, key_sum, value_sum, send, recv, local = kept
        scatter = Scatter(at, send, recv, refs)
        scatter.products(lambda rows: dot(activated[rows], contract[...]))
        gather = Gather(at, block, all_rows, send, recv, local.at[0], 10)
        for i in range(4):
            for h in range(HEADS):
                a = i * COLS + h * HDIM
                piece = qkv[:, a : a + HDIM] if i < 3 else go[:, h * HDIM : (h + 1) * HDIM]
                parts[i, h] = piece * EIGHTH if i == 0 else piece
        square = (at_once, at_once)
        seen = lax.broadcasted_iota(jnp.int32, square, 1) >= lax.broadcasted_iota(jnp.int32, square, 0)
        blocks = D // at_once

        def one(h, carry):
            turned = parts[1, h].T
            query_parts = []
            for i in reversed(range(blocks)):
                before, upto = i * at_once, (i + 1) * at_once
                rows = slice(before, upto)
                q, g = parts[0, h, rows], parts[3, h, rows]
                k, v = parts[1, h, 0:upto], parts[2, h, 0:upto]
                p = jnp.exp(dot_flip(k, q) - log_rows[pl.ds(h, 1), rows])
                last = jnp.where(seen, p[before:], 0.0)
                p = jnp.concatenate((p[:before], last), axis=0) if i else last
                dp = dot_flip(v, g)
                ds = (p * (dp - jnp.sum(p * dp, axis=0, keepdims=True))).astype(bf16)
                value_part, key_part = dot(p.astype(bf16), g), dot(ds, q)
                if i == blocks - 1:
                    key_sum[0:upto, :] = key_part
                    value_sum[0:upto, :] = value_part
                else:
                    key_sum[0:upto, :] += key_part
                    value_sum[0:upto, :] += value_part
                query_parts.append((dot(turned[:, 0:upto], ds) * EIGHTH).T)
            parts[0, h] = jnp.concatenate(query_parts[::-1], axis=0).astype(bf16)
            parts[1, h] = key_sum[...].astype(bf16)
            parts[2, h] = value_sum[...].astype(bf16)

            @pl.when(h == 0)
            def _():
                scatter.middle()
                gather.begin()

            @pl.when(h == 1)
            def _():
                gather.pass_on()
                gather.pass_near()

            return carry

        lax.fori_loop(0, HEADS, one, 0)
        gather.pass_far()
        for i in range(3):
            out[:, i * COLS : (i + 1) * COLS] = jnp.concatenate([parts[i, h] for h in range(HEADS)], axis=1)
        scatter.arrive()

        def finish(rows, carry):
            result[rows] = (after[rows] + scatter.total(rows)).astype(bf16)

        by_rows(BLOCK, 32, finish)
        gather.got(4, 7, 8, 9, 10)
        gather.end()
        scatter.end()

    return call(
        body,
        number,
        [joined, grad, logs, activated, contract, after, rounded_two],
        [shape(D, 3 * COLS), shape(BLOCK, D), shape(D, D)],
        [*Scatter.scratch, VMEM((4, HEADS, D, HDIM), bf16), VMEM((D, HDIM), f32), VMEM((D, HDIM), f32), *sems(21)],
        beside,
        ring_peers,
        out_spaces=[VMEM, VMEM, ANY],
    )


def leave(number, grad, joined, x, vectors, grad_rows, beside):
    relay = Relay(jax.ShapeDtypeStruct((BLOCK, D), bf16), True)

    def body(at, ins, outs, kept):
        grad, weight, x, vectors, before = ins
        result, grad_vectors = outs
        *refs, rounded, send, recv, local = kept
        scatter = Scatter(at, send, recv, refs)
        scatter.products(lambda rows: dot(grad[rows], weight[...]))
        scatter.middle()
        scatter.arrive()

        def norm(rows, carry):
            incoming = scatter.total(rows)
            centred, factor = standard(x[rows].astype(f32))
            total = before[rows] + norm_back(incoming, centred, factor, vectors[0:1])
            rounded[rows] = total.astype(bf16)
            return two_sums(incoming, centred, carry)

        gains, shifts = by_rows(BLOCK, 32, norm, no_sums())
        moving = functools.partial(relay_run, relay, at, rounded, result, send, recv, local.at[0], 10)
        moving(False)
        grad_vectors[0:1] = gains
        grad_vectors[1:2] = shifts
        moving(True)
        scatter.end()

    return call(
        body,
        number,
        [grad, joined, x, vectors, grad_rows],
        [shape(384, HALF), shape(8, D, dtype=f32)],
        [*Scatter.scratch, VMEM((BLOCK, D), bf16), *sems(12)],
        beside,
        lambda at: ring_peers(at) + relay.peers(at),
        out_spaces=[ANY, VMEM],
    )


def on_device(
    layer_input,
    text_states,
    cotangent,
    first_gain,
    first_shift,
    query_weight,
    key_weight,
    value_weight,
    output_weight,
    second_gain,
    second_shift,
    cross_query,
    cross_key,
    cross_value,
    cross_output,
    third_gain,
    third_shift,
    expand_weight,
    contract_weight,
):
    vectors = (first_gain, first_shift, second_gain, second_shift, third_gain, third_shift)
    vectors = jnp.concatenate([jnp.stack(vectors).astype(f32), jnp.zeros((2, HALF), f32)], axis=0)
    weights = [query_weight.T, key_weight.T, value_weight.T]
    query_t = cross_query.T
    pair_t = jnp.concatenate((cross_key.T, cross_value.T), axis=0)
    n = lax.axis_index("narrow")

    text_parts = dot_flip(text_states.reshape(128, HALF), pair_t).reshape(2, 64, 2 * COLS)
    (x, vectors, joined, all_one, qkv), ((text_pair_got,), (query_got,), (cross_got,), (text_got,)) = enter(
        1, layer_input, vectors, weights, [GiveClip(text_parts), Give(query_t), Give(cross_output), GiveClip(text_states)]
    )
    text_pair = (lax.dynamic_index_in_dim(text_parts, n, 0, False) + text_pair_got).astype(bf16)
    (attended, logs, all_keys, all_values), ((down,), (out_got,), (expand_got,)) = causal_forward(
        2,
        qkv,
        (query_t, query_got),
        (cross_output, cross_got),
        text_pair,
        [Relay(cotangent), Give(output_weight), Give(expand_weight)],
    )
    out_w, expand_w = (output_weight, out_got), (expand_weight, expand_got)
    middle, after, normed_two, cross_p, all_three, all_down, activated, grad_expand, contract = forward_rest(
        3, attended, out_w, x, vectors, all_keys, all_values, down, expand_w, contract_weight
    )

    contract_leg = SumZ(outer(activated, all_down).astype(bf16), False)
    expand_leg = SumZ(outer(all_three, grad_expand).astype(bf16), True)
    (grad_one, rounded_two, grad_scores, all_two, all_mid_one, grad_attended, late), sums = backward_rest(
        4,
        grad_expand,
        expand_w,
        after,
        middle,
        vectors,
        down,
        all_keys,
        all_values,
        cross_p,
        normed_two,
        out_w,
        [contract_leg, expand_leg, Trade(cross_p)],
    )
    contract_sum, expand_sum, (cross_p,) = sums
    contract_leg, expand_leg = SumX(contract_leg.finish(contract_sum), False), SumX(expand_leg.finish(expand_sum), True)
    output_leg = SumZ(outer(attended, all_mid_one).astype(bf16), False)
    (grad_qkv, layer_output, all_mid_two), sums = causal_backward(
        5,
        qkv,
        grad_attended,
        logs,
        activated,
        contract,
        after,
        rounded_two,
        [contract_leg, expand_leg, output_leg, Trade(grad_scores)],
    )
    contract_sum, expand_sum, output_sum, (grad_scores,) = sums

    joined_leg = SumZ(outer(grad_qkv, all_one).astype(bf16), False)
    grad_keys = outer(grad_scores.reshape(D, COLS), all_two).astype(bf16).reshape(HEADS, 64, D)
    grad_values = outer(cross_p.reshape(D, COLS), all_mid_two).astype(bf16).reshape(HEADS, 64, D)
    own_first = n == 0

    def whole(own, got):
        return jnp.concatenate((jnp.where(own_first, own, got), jnp.where(own_first, got, own)), axis=1)

    text = whole(lax.dynamic_index_in_dim(text_states, n, 0, False), text_got)
    heads_query = whole(query_t, query_got).reshape(HEADS, HDIM, D)
    heads_out = whole(cross_output, cross_got).reshape(HEADS, HDIM, D)
    text_heads = text_pair.reshape(64, 2, HEADS, HDIM)

    def heads(what, a, b):
        return jnp.einsum(what, a, b, preferred_element_type=f32)

    grad_text_keys = heads("hkf,hdf->khd", grad_keys, heads_query) * EIGHTH
    grad_text_values = heads("hkf,hdf->khd", grad_values, heads_out)
    grad_pair = jnp.stack((grad_text_keys, grad_text_values), axis=1).reshape(64, 2 * COLS).astype(bf16)
    grad_query = heads("khd,hkf->hdf", text_heads[:, 0], grad_keys).reshape(COLS, D) * EIGHTH
    grad_cross = heads("khd,hkf->hdf", text_heads[:, 1], grad_values).reshape(COLS, D)
    cross_leg = SumZ(jnp.concatenate((grad_query, outer(grad_pair, text), grad_cross), axis=0).astype(bf16), False)

    contract_leg, expand_leg = Spread(contract_leg.finish(contract_sum)), Spread(expand_leg.finish(expand_sum))
    output_leg = SumX(output_leg.finish(output_sum), False)
    (input_grad, first), sums = leave(
        6,
        grad_qkv,
        joined,
        x,
        vectors,
        grad_one,
        [joined_leg, cross_leg, contract_leg, expand_leg, output_leg, Relay(layer_output, True), Give(grad_pair)],
    )
    joined_sum, cross_sum, contract_sum, expand_sum, output_sum, (layer_output,), (grad_pair_got,) = sums
    contract_grad, expand_grad = contract_leg.finish(contract_sum), expand_leg.finish(expand_sum)
    parts = jnp.concatenate((first[0:2], late[2:6], jnp.zeros((2, D), f32)), axis=0)
    pairs = jnp.concatenate((jnp.where(own_first, grad_pair, grad_pair_got), jnp.where(own_first, grad_pair_got, grad_pair)), axis=0)
    text_part = dot(pairs, pair_t).astype(bf16).reshape(8, 16, HALF)
    joined_leg, cross_leg = SumX(joined_leg.finish(joined_sum), False), SumX(cross_leg.finish(cross_sum), False)
    output_leg = Spread(output_leg.finish(output_sum))
    _, (joined_sum, cross_sum, output_sum, (parts,), (text_part,)) = call(
        None, 7, [], [], (), [joined_leg, cross_leg, output_leg, ToRing(parts), Trade(text_part)]
    )
    output_grad = output_leg.finish(output_sum)
    joined_leg, cross_leg = Spread(joined_leg.finish(joined_sum)), Spread(cross_leg.finish(cross_sum))
    text_part = jnp.sum(text_part.astype(f32), axis=0).astype(bf16)
    _, (joined_sum, cross_sum, (parts,), (text_grad,)) = call(
        None, 8, [], [], (), [joined_leg, cross_leg, ToClips(jnp.sum(parts, axis=0)), ToSpots(text_part)]
    )
    joined_grad, cross_grad = joined_leg.finish(joined_sum), cross_leg.finish(cross_sum)
    parts = jnp.sum(parts, axis=(0, 1))
    return (
        layer_output,
        input_grad.astype(f32),
        text_grad.reshape(2, 64, HALF).astype(f32),
        parts[0],
        parts[1],
        joined_grad[:COLS].T,
        joined_grad[COLS : 2 * COLS].T,
        joined_grad[2 * COLS :].T,
        output_grad,
        parts[2],
        parts[3],
        cross_grad[:COLS].T,
        cross_grad[COLS : 2 * COLS].T,
        cross_grad[2 * COLS : 3 * COLS].T,
        cross_grad[3 * COLS :],
        parts[4],
        parts[5],
        expand_grad,
        contract_grad,
    )


def solution(mesh):
    return jax.shard_map(
        on_device,
        mesh=mesh,
        in_specs=(
            P(("dp", "wide"), "narrow"),
            P("dp", None, "narrow"),
            P(("dp", "wide"), "narrow"),
            P("narrow"),
            P("narrow"),
            P("narrow", "wide"),
            P("narrow", "wide"),
            P("narrow", "wide"),
            P("wide", "narrow"),
            P("narrow"),
            P("narrow"),
            P("narrow", "wide"),
            P("narrow", "wide"),
            P("narrow", "wide"),
            P("wide", "narrow"),
            P("narrow"),
            P("narrow"),
            P("narrow", "wide"),
            P("wide", "narrow"),
        ),
        out_specs=(
            P(("dp", "wide"), "narrow"),
            P(("dp", "wide"), "narrow"),
            P("dp", None, "narrow"),
            P("narrow"),
            P("narrow"),
            P("narrow", "wide"),
            P("narrow", "wide"),
            P("narrow", "wide"),
            P("wide", "narrow"),
            P("narrow"),
            P("narrow"),
            P("narrow", "wide"),
            P("narrow", "wide"),
            P("narrow", "wide"),
            P("wide", "narrow"),
            P("narrow"),
            P("narrow"),
            P("narrow", "wide"),
            P("wide", "narrow"),
        ),
        check_vma=False,
    )
```

```python
import functools
import math

import jax
import jax.numpy as jnp
from jax import lax
from jax.experimental import pallas as pl
from jax.experimental.pallas import tpu as pltpu
from jax.sharding import PartitionSpec as P

D = 1536
HALF = 768
HDIM = 64
HEADS = 3
COLS = HEADS * HDIM
BLOCK = 192
EPSILON = 1e-05
NEGATIVE = -1e30
ROOT_HALF = 0.7071067811865476
GAUSS_NORM = 0.3989422804014327
MESH = pl.DeviceIdType.MESH
VMEM = pltpu.VMEM
ANY = pl.ANY
bf16, f32 = jnp.bfloat16, jnp.float32


def dot(a, b):
    return lax.dot_general(a, b, (((1,), (0,)), ((), ())), preferred_element_type=f32)


def dot_flip(a, b):
    return lax.dot_general(a, b, (((1,), (1,)), ((), ())), preferred_element_type=f32)


def outer(a, b):
    return lax.dot_general(a, b, (((0,), (0,)), ((), ())), preferred_element_type=f32)


class Place:
    def __init__(self):
        self.dp, self.w, self.n = (lax.axis_index(a) for a in ("dp", "wide", "narrow"))
        self.y, self.c = lax.div(self.w, 2), lax.rem(self.w, 2)
        self.z, self.s = lax.div(self.dp, 2), lax.rem(self.dp, 2)
        self.up, self.down = lax.rem(self.y + 1, 4), lax.rem(self.y + 3, 4)
        self.across = 3 - self.y
        self.moved = lax.rem(lax.div(self.y, 2) + self.n, 2)
        self.clip = lax.div(self.y, 2)

    def spot(self, y, c):
        moved = lax.rem(lax.div(y, 2) + self.n, 2)
        return (lax.rem(y + moved, 2) * 2 + c) * 2 + moved

    def rows(self, y, c, start=0, size=BLOCK):
        return pl.ds(pl.multiple_of(self.spot(y, c) * BLOCK + start, 32), size)

    def half(self, n):
        return pl.ds(pl.multiple_of(n * HALF, HALF), HALF)

    def at_y(self, y):
        return {"wide": y * 2 + self.c}

    def core(self):
        return {"wide": self.y * 2 + 1 - self.c}

    def x(self):
        return {"narrow": 1 - self.n}

    def at_z(self, k):
        return {"dp": lax.rem(self.z + k, 4) * 2 + self.s}

    def at_dp(self, k):
        return {"dp": lax.rem(self.dp + k, 8)}

    def at_x(self, ds, dn):
        return {"dp": self.z * 2 + lax.rem(self.s + ds, 2), "narrow": lax.rem(self.n + dn, 2)}


def remote(src, dst, send, recv, peer):
    return pltpu.make_async_remote_copy(
        src_ref=src, dst_ref=dst, send_sem=send, recv_sem=recv, device_id=peer, device_id_type=MESH
    )


def greet(peers):
    barrier = pltpu.get_barrier_semaphore()
    for peer in peers:
        pl.semaphore_signal(barrier, inc=1, device_id=peer, device_id_type=MESH)
    pl.semaphore_wait(barrier, len(peers))


class Give:
    def __init__(self, array):
        self.ins, self.copies, self.locals = [array], 1, 0
        self.outs = [jax.ShapeDtypeStruct(array.shape, array.dtype)]

    def peers(self, at):
        return [("x", at.x())]

    def moves(self, at, ins, outs):
        return [(ins[0], outs[0], at.x())], []


class GiveClip(Give):
    def __init__(self, array):
        super().__init__(array)
        self.outs = [jax.ShapeDtypeStruct(array.shape[1:], array.dtype)]

    def moves(self, at, ins, outs):
        return [(ins[0].at[1 - at.n], outs[0], at.x())], []


class Trade:
    def __init__(self, array):
        self.ins, self.copies, self.locals = [array], 7, 1
        self.outs = [jax.ShapeDtypeStruct(array.shape, array.dtype)]

    def others(self, at):
        return [lax.rem(at.w + k, 8) for k in range(1, 8)]

    def peers(self, at):
        return [(f"w{k + 1}", {"wide": w}) for k, w in enumerate(self.others(at))]

    def moves(self, at, ins, outs):
        mine = at.spot(at.y, at.c)
        dst = outs[0].at[mine]
        far = [(ins[0].at[at.spot(lax.div(w, 2), lax.rem(w, 2))], dst, {"wide": w}) for w in self.others(at)]
        return far, [(ins[0].at[mine], dst)]


class Relay:
    def __init__(self, array, back=False):
        self.ins, self.back, self.copies, self.locals = [array], back, 2, 1
        shape = (384, HALF) if back else (BLOCK, D)
        self.outs = [jax.ShapeDtypeStruct(shape, array.dtype)]

    def peers(self, at):
        return [
            ("x", at.x()),
            ("a0", {"wide": at.across * 2 + at.c}),
            ("a1", {"wide": at.across * 2 + at.c, "narrow": 1 - at.n}),
        ]


def relay_run(relay, at, src, dst, send, recv, local, base, finish):
    mine, other = at.half(at.n), at.half(1 - at.n)
    over = at.across * 2 + at.c
    if relay.back:
        row = pl.ds(pl.multiple_of(at.moved * BLOCK, BLOCK), BLOCK)
        to = recv.at[base + at.moved]
        own = src.at[:, mine], src.at[:, other]
        land = dst.at[0:BLOCK], dst.at[BLOCK : 2 * BLOCK]
    else:
        row = mine
        to = recv.at[base + at.n]
        own = src.at[0:BLOCK], src.at[BLOCK : 2 * BLOCK]
        land = dst.at[:, at.half(0)], dst.at[:, at.half(1)]
    target = dst.at[row] if relay.back else dst.at[:, row]

    def arrive(slot, part):
        return remote(own[0], part, send.at[base], recv.at[base + slot], at.x())

    @pl.when(at.moved == 0)
    def _():
        stay = pltpu.make_async_copy(own[0], target, local)
        if relay.back:
            go = remote(own[1], target, send.at[base], to, at.x())
        else:
            go = remote(own[1], target, send.at[base], to, {"wide": over})
        if not finish:
            go.start()
            stay.start()
        else:
            stay.wait()
            go.wait_send()
            if relay.back:
                arrive(1, land[1]).wait_recv()
            else:
                arrive(1 - at.n, dst.at[:, other]).wait_recv()

    @pl.when(at.moved == 1)
    def _():
        if relay.back:
            first = remote(own[1], target, send.at[base], to, {"wide": over, "narrow": 1 - at.n})
            second = remote(own[0], target, send.at[base + 1], to, {"wide": over})
        else:
            first = remote(own[1], target, send.at[base], to, {"wide": over, "narrow": 1 - at.n})
            second = remote(own[0], target, send.at[base + 1], to, at.x())
        if not finish:
            first.start()
            second.start()
        else:
            first.wait_send()
            second.wait_send()
            arrive(0, land[0]).wait_recv()
            arrive(1, land[1]).wait_recv()


def call(body, number, ins, outs, scratch=(), beside=(), peers=None, spaces=None, out_spaces=None, late=False):
    spaces = spaces or [VMEM] * len(ins)
    out_spaces = out_spaces or [VMEM] * len(outs)
    copies = sum(b.copies for b in beside)
    locals_ = sum(b.locals for b in beside)
    side_ins = [a for b in beside for a in b.ins]
    side_outs = [a for b in beside for a in b.outs]
    n_in, n_out, n_scratch = len(ins), len(outs), len(scratch)

    def kernel(*refs):
        at = Place()
        refs = list(refs)

        def take(count):
            out = refs[:count]
            del refs[:count]
            return out

        main_in, side_in = take(n_in), take(len(side_ins))
        main_out, side_out, kept = take(n_out), take(len(side_outs)), take(n_scratch)
        send, recv, local = take(3)
        known = dict(peers(at)) if peers else {}
        for b in beside:
            known.update(dict(b.peers(at)))
        if known:
            greet(list(known.values()))
        side_refs = [([side_in.pop(0) for _ in b.ins], [side_out.pop(0) for _ in b.outs]) for b in beside]
        todo = []

        def start():
            slot, place = 0, 0
            for b, (i, o) in zip(beside, side_refs):
                if isinstance(b, Relay):
                    run = functools.partial(relay_run, b, at, i[0], o[0], send, recv, local.at[place], slot)
                    run(False)
                    todo.append(functools.partial(run, True))
                    slot, place = slot + 2, place + 1
                    continue
                far, near = b.moves(at, i, o)
                for src, dst, peer in far:
                    copy = remote(src, dst, send.at[slot], recv.at[slot], peer)
                    copy.start()
                    todo.append(copy.wait)
                    slot += 1
                for src, dst in near:
                    copy = pltpu.make_async_copy(src, dst, local.at[place])
                    copy.start()
                    todo.append(copy.wait)
                    place += 1

        at.start_beside = start
        if not late:
            start()
        if body:
            body(at, main_in, main_out, kept)
        for wait in todo:
            wait()

    results = pl.pallas_call(
        kernel,
        out_shape=tuple(outs) + tuple(side_outs),
        in_specs=[pl.BlockSpec(memory_space=s) for s in spaces] + [pl.BlockSpec(memory_space=ANY)] * len(side_ins),
        out_specs=tuple(pl.BlockSpec(memory_space=m) for m in out_spaces + [ANY] * len(side_outs)),
        scratch_shapes=[
            *scratch,
            pltpu.SemaphoreType.DMA((max(copies, 1),)),
            pltpu.SemaphoreType.DMA((max(copies, 1),)),
            pltpu.SemaphoreType.DMA((max(locals_, 1),)),
        ],
        compiler_params=pltpu.CompilerParams(
            collective_id=number, has_side_effects=True, vmem_limit_bytes=58 << 20
        ),
    )(*ins, *side_ins)
    results = list(results)
    main, rest = results[: len(outs)], results[len(outs) :]
    sides = []
    for b in beside:
        sides.append(rest[: len(b.outs)])
        del rest[: len(b.outs)]
    return main, sides


def ring_peers(at):
    return [("up", at.at_y(at.up)), ("down", at.at_y(at.down)), ("core", at.core())]


def sems(count):
    return [pltpu.SemaphoreType.DMA((count,)), pltpu.SemaphoreType.DMA((count,)), pltpu.SemaphoreType.DMA((count,))]


def by_rows(count, size, work, carry=None):
    def step(i, carry):
        return work(pl.ds(pl.multiple_of(i * size, size), size), carry)

    return lax.fori_loop(0, count // size, step, carry)


class Whole:
    def __init__(self, at, own, got, full, sem, axis):
        size = own.shape[axis]
        self.copies = []
        for i, (part, n) in enumerate(((own, at.n), (got, 1 - at.n))):
            where = pl.ds(pl.multiple_of(n * size, size), size)
            target = full.at[where] if axis == 0 else full.at[:, where]
            self.copies.append(pltpu.make_async_copy(part, target, sem.at[i]))
            self.copies[-1].start()

    def wait(self):
        for copy in self.copies:
            copy.wait()


class Reduce:
    slots, locals_, deep = 10, 2, 96

    @staticmethod
    def scratch(x_first, by_rows=False):
        deep = Reduce.deep
        first = (4, deep, HALF) if x_first else (2, 2, deep, HALF) if by_rows else (2, deep, D)
        return [VMEM((3, *first), bf16), VMEM(first, bf16), VMEM((3, deep, HALF), bf16), VMEM((2, deep, HALF), bf16)]

    @staticmethod
    def peers(at):
        return [(f"z{k}", at.at_z(k)) for k in (1, 2, 3)] + [(f"x{a}{b}", at.at_x(a, b)) for a, b in ((0, 1), (1, 0), (1, 1))]

    def __init__(self, at, src, out, refs, send, recv, local, base, place, x_first, by_rows=False):
        self.at, self.src, self.out = at, src, out
        self.land, self.total, self.land_two, self.last = refs
        self.x_first, self.by_rows = x_first, by_rows
        z_steps = [(at.at_z(k), lax.rem(at.z + k, 4)) for k in (1, 2, 3)]
        x_steps = [
            (at.at_x(a, b), (lax.rem(at.s + a, 2), lax.rem(at.n + b, 2))) for a, b in ((0, 1), (1, 0), (1, 1))
        ]
        first, second = (x_steps, z_steps) if x_first else (z_steps, x_steps)

        def move(slot, source, target, peer):
            return remote(source, target, send.at[base + slot], recv.at[base + slot], peer)

        self.one = [move(i, self.piece(where), self.land.at[i], peer) for i, (peer, where) in enumerate(first)]
        self.own = pltpu.make_async_copy(
            self.piece((at.s, at.n) if x_first else at.z), self.total, local.at[place]
        )
        self.two = [move(3 + i, self.part(where), self.land_two.at[i], peer) for i, (peer, where) in enumerate(second)]
        self.mine = at.z if x_first else (at.s, at.n)
        self.three = move(6, self.last.at[at.s], self.last.at[at.s], at.at_x(1, 0))
        target = out.at[at.z]
        self.four = [move(7 + i, self.last, target, peer) for i, (peer, _) in enumerate(z_steps)]
        self.stay = pltpu.make_async_copy(self.last, target, local.at[place + 1])

    def piece(self, where):
        if self.x_first:
            s, n = where
            return self.src.at[n, :, s] if self.by_rows else self.src.at[:, s, :, self.at.half(n)]
        return self.src.at[:, where] if self.by_rows else self.src.at[where]

    def part(self, where):
        if self.x_first:
            return self.total.at[where]
        s, n = where
        return self.total.at[n, s] if self.by_rows else self.total.at[s, :, self.at.half(n)]

    def first(self):
        for copy in self.one + [self.own]:
            copy.start()

    def second(self):
        self.own.wait()
        for copy in self.one:
            copy.wait_recv()
        lead = self.total.shape[:-2]
        count = math.prod(lead)

        def add(i, carry):
            at_lead = (i,) if len(lead) == 1 else (lax.div(i, lead[1]), lax.rem(i, lead[1]))
            for start in range(0, self.deep, 32):
                where = (*at_lead, slice(start, start + 32))
                got = self.total[where].astype(f32)
                for k in range(3):
                    got += self.land[(k, *where)].astype(f32)
                self.total[where] = got.astype(bf16)
            return carry

        lax.fori_loop(0, count, add, 0)
        for copy in self.two:
            copy.start()

    def third(self):
        for copy in self.two:
            copy.wait_recv()
        own = self.part(self.mine)
        s = self.at.s
        for start in range(0, self.deep, 32):
            rows = slice(start, start + 32)
            got = own[rows].astype(f32)
            for k in range(3):
                got += self.land_two[k, rows].astype(f32)
            self.last[s, rows] = got.astype(bf16)
        self.three.start()

    def fourth(self):
        self.three.wait_recv()
        for copy in self.four + [self.stay]:
            copy.start()

    def end(self):
        for copy in self.four:
            copy.wait()
        for copy in self.one + self.two + [self.three]:
            copy.wait_send()
        self.stay.wait()


class Gather:
    slots = 11

    def __init__(self, at, x, whole, send, recv, local, base=0):
        self.at, self.x, self.whole = at, x, whole
        y, c, up, down = at.y, at.c, at.up, at.down
        far = lax.rem(y + 2, 4)
        half = BLOCK // 2

        def move(slot, y_from, peer, start=0, size=BLOCK, first=False):
            rows = at.rows(y_from, c, start, size)
            src = whole.at[rows]
            if first:
                src = x if size == BLOCK else x.at[start : start + size]
            return remote(src, whole.at[rows], send.at[base + slot], recv.at[base + slot], peer)

        to_up, to_down, core = at.at_y(up), at.at_y(down), at.core()
        self.sends = [
            move(0, y, to_up, 0, half, first=True),
            move(1, y, to_up, half, half, first=True),
            move(2, y, to_down, half, half, first=True),
            move(3, y, to_down, 0, half, first=True),
            move(4, y, core, first=True),
            move(5, down, to_up, 0, half),
            move(6, up, to_down, half, half),
            move(7, down, core),
            move(8, up, core),
            move(9, far, core, 0, half),
            move(10, far, core, half, half),
        ]
        self.own = pltpu.make_async_copy(x, whole.at[at.rows(y, c)], local)

    def begin(self):
        for i in (0, 2, 1, 3, 4):
            self.sends[i].start()
        self.own.start()
        self.own.wait()

    def chain(self, *pairs):
        for arrived, leaving in pairs:
            self.sends[arrived].wait_recv()
            self.sends[leaving].start()

    def pass_on(self):
        self.chain((0, 5), (2, 6))

    def pass_near(self):
        self.chain((1, 7), (3, 8))

    def pass_far(self):
        self.chain((5, 9), (6, 10))

    def got(self, *slots):
        for i in slots:
            self.sends[i].wait_recv()

    def end(self):
        for copy in self.sends:
            copy.wait_send()

    def finish(self):
        self.pass_on()
        self.pass_near()
        self.pass_far()
        self.got(4, 7, 8, 9, 10)
        self.end()

    def each(self, work):
        at = self.at

        def step(s, carry):
            @pl.when(s == 1)
            def _():
                self.got(4)
                self.pass_on()

            @pl.when(s == 2)
            def _():
                self.pass_near()

            @pl.when(s == 3)
            def _():
                self.got(8)

            @pl.when(s == 5)
            def _():
                self.got(7)

            @pl.when(s == 6)
            def _():
                self.pass_far()

            @pl.when(s == 7)
            def _():
                self.got(9, 10)

            work(s, self.place(s))
            return carry

        lax.fori_loop(0, 8, step, 0)
        self.end()

    def place(self, s):
        g = lax.div(s, 2)
        off = g + lax.div(g, 2) - 2 * lax.div(g, 3)
        return self.at.rows(lax.rem(self.at.y + off, 4), lax.rem(self.at.c + s, 2))


class Scatter:
    slots = 10
    scratch = [
        VMEM((4, BLOCK, D), bf16),
        VMEM((4, BLOCK, D), bf16),
        VMEM((4, BLOCK, D), f32),
        VMEM((2, BLOCK, D), bf16),
        VMEM((2, BLOCK, D), bf16),
        VMEM((2, BLOCK // 2, D), bf16),
        VMEM((2, BLOCK // 2, D), bf16),
    ]

    def __init__(self, at, send, recv, refs, base=0):
        self.at, self.send, self.recv, self.base = at, send, recv, base
        self.out_c, self.in_c, self.own, self.out_y, self.in_y, self.half_out, self.half_in = refs
        half = BLOCK // 2
        peers = at.at_y(at.up), at.at_y(at.down)

        def move(slot, src, dst, peer):
            return remote(src, dst, send.at[base + slot], recv.at[base + slot], peer)

        self.cores = [self.core(g) for g in range(4)]
        self.halves = [move(4 + i, self.half_out.at[i], self.half_in.at[i], peers[i]) for i in range(2)]
        free = [pl.ds((1 - i) * half, half) for i in range(2)]
        bound = [pl.ds(i * half, half) for i in range(2)]
        self.free = [move(6 + i, self.out_y.at[i, free[i]], self.in_y.at[i, free[i]], peers[i]) for i in range(2)]
        self.bound = [move(8 + i, self.out_y.at[i, bound[i]], self.in_y.at[i, bound[i]], peers[i]) for i in range(2)]

    def core(self, g):
        slot = self.base + g
        return remote(self.out_c.at[g], self.in_c.at[g], self.send.at[slot], self.recv.at[slot], self.at.core())

    def both(self, g, rows):
        return self.own[g, rows] + self.in_c[g, rows].astype(f32)

    def products(self, product):
        at = self.at
        half = BLOCK // 2

        def part_rows(rows, i):
            return pl.ds(pl.multiple_of(rows.start + i * half, 32), 32)

        def send_free(i):
            self.cores[1 + i].wait_recv()

            def add(rows, carry):
                there = part_rows(rows, 1 - i)
                self.out_y[i, there] = self.both(1 + i, there).astype(bf16)

            by_rows(half, 32, add)
            self.free[i].start()

        def step(s, carry):
            g = lax.div(s, 2)
            off = lax.rem(6 - g + 3 * lax.div(g, 2) + 2 * lax.div(g, 3), 4)
            part = product(at.rows(lax.rem(at.y + off, 4), lax.rem(at.c + 1 + s, 2)))

            @pl.when(lax.rem(s, 2) == 0)
            def _():
                self.out_c[g] = part.astype(bf16)
                self.core(g).start()

            @pl.when(lax.rem(s, 2) == 1)
            def _():
                self.own[g] = part

            @pl.when(s == 2)
            def _():
                self.cores[0].wait_recv()
                for i in range(2):

                    def add(rows, carry, i=i):
                        self.half_out[i, rows] = self.both(0, part_rows(rows, i)).astype(bf16)

                    by_rows(half, 32, add)
                    self.halves[i].start()

            @pl.when(s == 4)
            def _():
                send_free(0)

            @pl.when(s == 6)
            def _():
                send_free(1)

            return carry

        lax.fori_loop(0, 8, step, 0)

    def middle(self):
        half = BLOCK // 2
        for i in range(2):
            self.halves[i].wait_recv()

            def add(rows, carry, i=i):
                here = pl.ds(pl.multiple_of(rows.start + i * half, 32), 32)
                self.out_y[i, here] = (self.both(1 + i, here) + self.half_in[i, rows].astype(f32)).astype(bf16)

            by_rows(half, 32, add)
            self.bound[i].start()

    def arrive(self):
        self.cores[3].wait_recv()
        for copy in self.free + self.bound:
            copy.wait_recv()

    def total(self, rows):
        return self.both(3, rows) + self.in_y[0, rows].astype(f32) + self.in_y[1, rows].astype(f32)

    def end(self):
        for copy in self.cores + self.halves + self.free + self.bound:
            copy.wait_send()


def standard(values):
    average = jnp.mean(values, axis=1, keepdims=True)
    variance = jnp.mean(values * values, axis=1, keepdims=True) - average * average
    factor = lax.rsqrt(variance + EPSILON)
    return (values - average) * factor, factor


def norm_back(incoming, centred, factor, gain):
    scaled = incoming * gain
    first = jnp.mean(scaled, axis=1, keepdims=True)
    second = jnp.mean(scaled * centred, axis=1, keepdims=True)
    return factor * (scaled - first - centred * second)


def two_sums(incoming, centred, carry):
    gains, shifts = carry
    return gains + jnp.sum(incoming * centred, axis=0, keepdims=True), shifts + jnp.sum(incoming, axis=0, keepdims=True)


def no_sums():
    return jnp.zeros((1, D), f32), jnp.zeros((1, D), f32)


EIGHTH = 0.125


def shape(*dims, dtype=bf16):
    return jax.ShapeDtypeStruct(dims, dtype)


class Keep:
    def __init__(self, whole, out, sem, base):
        self.whole, self.out, self.sem, self.base = whole, out, sem, base

    def block(self, s, rows):
        pltpu.make_async_copy(self.whole.at[rows], self.out.at[rows], self.sem.at[self.base + s]).start()

    def wait(self):
        for s in range(8):
            some = pl.ds(0, BLOCK)
            pltpu.make_async_copy(self.whole.at[some], self.out.at[some], self.sem.at[self.base + s]).wait()


def enter(number, layer_input, vectors, weights, beside):
    relay = Relay(layer_input)

    def body(at, ins, outs, kept):
        (source, own_vectors, *own_weights), (x, vectors, weight, all_rows, qkv) = ins, outs
        normed, whole, send, recv, local = kept
        half = at.half(at.n)
        moving = functools.partial(relay_run, relay, at, source, x, send, recv, local.at[0], 11)
        moving(False)
        stay, go = [], []
        for i, (own, target) in enumerate(
            [(own_vectors, vectors.at[:, half])]
            + [(own, weight.at[j * COLS : (j + 1) * COLS, half]) for j, own in enumerate(own_weights)]
        ):
            stay.append(pltpu.make_async_copy(own, target, local.at[1 + i]))
            go.append(remote(own, target, send.at[13 + i], recv.at[13 + i], at.x()))
        stay[0].start()
        go[0].start()
        stay[0].wait()
        go[0].wait_recv()
        moving(True)
        for copy in stay[1:] + go[1:]:
            copy.start()

        def norm(rows, carry):
            centred, _ = standard(x[rows].astype(f32))
            normed[rows] = (centred * vectors[0:1] + vectors[1:2]).astype(bf16)

        by_rows(BLOCK, 32, norm)
        gather = Gather(at, normed, whole, send, recv, local.at[5])
        gather.begin()
        at.start_beside()
        keep = Keep(whole, all_rows, local, 6)

        def times(rows):
            qkv[rows] = dot_flip(whole[rows], weight[...]).astype(bf16)

        def work(s, rows):
            keep.block(s, rows)

            @pl.when(s == 4)
            def _():
                for copy in stay[1:]:
                    copy.wait()
                for copy in go[1:]:
                    copy.wait_recv()

            @pl.when(s >= 4)
            def _():
                times(rows)

        gather.each(work)

        def rest(s, carry):
            times(gather.place(s))
            return carry

        lax.fori_loop(0, 4, rest, 0)
        keep.wait()
        for copy in go:
            copy.wait_send()

    return call(
        body,
        number,
        [layer_input, vectors, *weights],
        [shape(BLOCK, D), shape(8, D, dtype=f32), shape(3 * COLS, D), shape(D, D), shape(D, 3 * COLS)],
        [VMEM((BLOCK, D), bf16), VMEM((D, D), bf16), *sems(17)],
        beside,
        lambda at: ring_peers(at) + relay.peers(at) + [("x", at.x())],
        out_spaces=[VMEM, VMEM, VMEM, ANY, VMEM],
        late=True,
    )


def causal_forward(number, joined, query_w, out_w, text_pair, beside):
    at_once = 512

    def body(at, ins, outs, kept):
        (qkv, query_own, query_got, out_own, out_got, pair), (out, logs, all_keys, all_values) = ins, outs
        parts, mixed, keys, values, send, recv, local = kept
        half, other = at.half(at.n), at.half(1 - at.n)
        for own, got, target, axis in ((query_own, query_got, keys, 0), (out_own, out_got, values, 1)):
            for cols, ref in ((half, own), (other, got)):
                for h in range(HEADS):
                    rows = slice(h * HDIM, (h + 1) * HDIM)
                    text = pair[:, axis * COLS + h * HDIM : axis * COLS + (h + 1) * HDIM]
                    product = dot(text, ref[rows, :])
                    target[rows, cols] = (product * EIGHTH if axis == 0 else product).astype(bf16)
        first = Gather(at, keys, all_keys, send, recv, local.at[0])
        second = Gather(at, values, all_values, send, recv, local.at[1], 11)
        first.begin()
        for i in range(3):
            for h in range(HEADS):
                a = i * COLS + h * HDIM
                piece = qkv[:, a : a + HDIM]
                parts[i, h] = piece * EIGHTH if i == 0 else piece
        square = (at_once, at_once)
        seen = lax.broadcasted_iota(jnp.int32, square, 0) >= lax.broadcasted_iota(jnp.int32, square, 1)

        def one(h, carry):
            for i in reversed(range(D // at_once)):
                before, upto = i * at_once, (i + 1) * at_once
                rows = slice(before, upto)
                scores = dot_flip(parts[0, h, rows], parts[1, h, 0:upto])
                last = jnp.where(seen, scores[:, before:], NEGATIVE)
                scores = jnp.concatenate((scores[:, :before], last), axis=1) if i else last
                peak = jnp.max(scores, axis=1, keepdims=True)
                raised = jnp.exp(scores - peak)
                total = jnp.sum(raised, axis=1, keepdims=True)
                mixed[h, rows] = (dot(raised.astype(bf16), parts[2, h, 0:upto]) / total).astype(bf16)
                column = jnp.broadcast_to(peak + jnp.log(total), (at_once, 128))
                logs[pl.ds(h, 1), rows] = column.T[0:1, :]

            @pl.when(h == 0)
            def _():
                first.pass_on()
                second.begin()
                first.pass_near()

            @pl.when(h == 1)
            def _():
                first.pass_far()
                second.pass_on()

            return carry

        lax.fori_loop(0, HEADS, one, 0)
        second.pass_near()
        out[...] = jnp.concatenate([mixed[h] for h in range(HEADS)], axis=1)
        second.pass_far()
        for gather in (first, second):
            gather.got(4, 7, 8, 9, 10)
            gather.end()

    return call(
        body,
        number,
        [joined, *query_w, *out_w, text_pair],
        [shape(D, COLS), shape(8, D, dtype=f32), shape(D, D), shape(D, D)],
        [VMEM((3, HEADS, D, HDIM), bf16), VMEM((HEADS, D, HDIM), bf16), VMEM((BLOCK, D), bf16), VMEM((BLOCK, D), bf16), *sems(22)],
        beside,
        ring_peers,
        out_spaces=[VMEM, VMEM, ANY, ANY],
    )


def forward_rest(number, attended, out_w, x, vectors, keys, values, down, expand_w, contract):
    def body(at, ins, outs, kept):
        mixed, out_own, out_got, x, vectors, keys, values, down, expand_own, expand_got, contract_own = ins
        middle, after, normed_two, weights, all_rows, all_down, activated, grad, contract_out = outs
        *refs, normed, whole, downs, out_full, expand_full, contract_full, key_full, value_full, branch, send, recv, local = kept
        half = at.half(at.n)
        weight = Whole(at, out_own, out_got, out_full, local.at[pl.ds(0, 2)], 1)
        swap = remote(contract_own, contract_full.at[:, half], send.at[32], recv.at[32], at.x())
        swap.start()
        later = [
            pltpu.make_async_copy(keys, key_full, local.at[2]),
            pltpu.make_async_copy(values, value_full, local.at[3]),
            pltpu.make_async_copy(contract_own, contract_full.at[:, half], local.at[4]),
        ]
        for copy in later:
            copy.start()
        later.append(Whole(at, expand_own, expand_got, expand_full, local.at[pl.ds(5, 2)], 0))
        weight.wait()
        scatter = Scatter(at, send, recv, refs)
        scatter.products(lambda rows: dot(mixed[rows], out_full[...]))
        scatter.middle()
        for copy in later:
            copy.wait()
        scatter.arrive()
        cotangents = Gather(at, down, downs, send, recv, local.at[7], 10)
        cotangents.begin()

        def norm_two(rows, carry):
            total = x[rows].astype(f32) + scatter.total(rows)
            middle[rows] = total
            centred, _ = standard(total)
            normed_two[rows] = (centred * vectors[2:3] + vectors[3:4]).astype(bf16)

        by_rows(BLOCK, 32, norm_two)

        def cross(b, carry):
            rows = pl.ds(pl.multiple_of(b * BLOCK, BLOCK), BLOCK)
            scores = dot_flip(key_full[rows], normed_two[...]).reshape(HEADS, 64, BLOCK)
            raised = jnp.exp(scores - jnp.max(scores, axis=1, keepdims=True))
            p = raised / jnp.sum(raised, axis=1, keepdims=True)
            p = p.reshape(BLOCK, BLOCK).T.astype(bf16)
            weights[b] = p
            part = dot(p, value_full[rows])

            @pl.when(b == 0)
            def _():
                branch[...] = part

            @pl.when(b > 0)
            def _():
                branch[...] += part

            @pl.when(b == 3)
            def _():
                cotangents.pass_on()
                cotangents.pass_near()

            return carry

        lax.fori_loop(0, 8, cross, 0)

        def norm_three(rows, carry):
            total = middle[rows] + branch[rows]
            after[rows] = total
            centred, _ = standard(total)
            normed[rows] = (centred * vectors[4:5] + vectors[5:6]).astype(bf16)

        by_rows(BLOCK, 32, norm_three)
        gather = Gather(at, normed, whole, send, recv, local.at[8], 21)
        gather.begin()
        cotangents.pass_far()
        cotangents.got(4, 7, 8, 9, 10)
        keep_down = pltpu.make_async_copy(downs, all_down, local.at[9])
        keep_down.start()
        swap.wait_recv()
        keep_contract = pltpu.make_async_copy(contract_full, contract_out, local.at[10])
        keep_contract.start()
        keep = Keep(whole, all_rows, local, 11)

        def work(s, rows):
            keep.block(s, rows)
            hidden = dot(whole[rows], expand_full[...])
            back = dot_flip(downs[rows], contract_full[...])
            bell = 0.5 * (1.0 + lax.erf(hidden * ROOT_HALF))
            activated[rows] = (hidden * bell).astype(bf16)
            grad[rows] = (back * (bell + hidden * jnp.exp(-0.5 * hidden * hidden) * GAUSS_NORM)).astype(bf16)

        gather.each(work)
        keep.wait()
        keep_down.wait()
        keep_contract.wait()
        cotangents.end()
        scatter.end()
        swap.wait_send()

    results, _ = call(
        body,
        number,
        [attended, *out_w, x, vectors, keys, values, down, *expand_w, contract],
        [
            shape(BLOCK, D, dtype=f32),
            shape(BLOCK, D, dtype=f32),
            shape(BLOCK, D),
            shape(8, BLOCK, BLOCK),
            shape(D, D),
            shape(D, D),
            shape(D, HALF),
            shape(D, HALF),
            shape(HALF, D),
        ],
        [
            *Scatter.scratch,
            VMEM((BLOCK, D), bf16),
            VMEM((D, D), bf16),
            VMEM((D, D), bf16),
            VMEM((COLS, D), bf16),
            VMEM((D, HALF), bf16),
            VMEM((HALF, D), bf16),
            VMEM((D, D), bf16),
            VMEM((D, D), bf16),
            VMEM((BLOCK, D), f32),
            *sems(33),
        ],
        (),
        lambda at: ring_peers(at) + [("x", at.x())],
        spaces=[VMEM, ANY, ANY, VMEM, VMEM, ANY, ANY, VMEM, ANY, ANY, ANY],
        out_spaces=[VMEM, VMEM, VMEM, VMEM, ANY, ANY, VMEM, VMEM, ANY],
    )
    return results


def backward_rest(
    number, grad, expand_w, after, middle, vectors, down, keys, values, weights, normed_two, out_w, contract_sum, expand_sum, beside
):
    def body(at, ins, outs, kept):
        grad, expand_own, expand_got, after, middle, vectors, down, keys, values, weights, normed_two, out_own, out_got = ins[:13]
        grad_rows, rounded_two, grad_scores, all_two, all_rows, grad_mixed, grad_vectors = outs[:7]
        *refs, rounded, whole, second, out_full, expand_full, key_full, value_full, send, recv, local = kept
        reduces = [
            Reduce(at, ins[13], outs[7], refs[7:11], send, recv, local, 32, 16, False),
            Reduce(at, ins[14], outs[8], refs[11:15], send, recv, local, 42, 18, True, True),
        ]
        refs = refs[:7]
        for reduce in reduces:
            reduce.first()
        weight = Whole(at, expand_own, expand_got, expand_full, local.at[pl.ds(0, 2)], 0)
        later = [
            pltpu.make_async_copy(keys, key_full, local.at[2]),
            pltpu.make_async_copy(values, value_full, local.at[3]),
        ]
        for copy in later:
            copy.start()
        later.append(Whole(at, out_own, out_got, out_full, local.at[pl.ds(4, 2)], 1))
        weight.wait()
        scatter = Scatter(at, send, recv, refs)
        scatter.products(lambda rows: dot_flip(grad[rows], expand_full[...]))
        scatter.middle()
        for copy in later:
            copy.wait()
        scatter.arrive()
        before = Gather(at, normed_two, all_two, send, recv, local.at[6], 10)
        before.begin()
        for reduce in reduces:
            reduce.second()

        def norm_three(rows, carry):
            incoming = scatter.total(rows)
            centred, factor = standard(after[rows])
            total = down[rows].astype(f32) + norm_back(incoming, centred, factor, vectors[4:5])
            grad_rows[rows] = total
            rounded_two[rows] = total.astype(bf16)
            return two_sums(incoming, centred, carry)

        gains, shifts = by_rows(BLOCK, 32, norm_three, no_sums())
        grad_vectors[4:5] = gains
        grad_vectors[5:6] = shifts

        def cross(b, carry):
            rows = pl.ds(pl.multiple_of(b * BLOCK, BLOCK), BLOCK)
            p = weights[b].astype(f32).T.reshape(HEADS, 64, BLOCK)
            dp = dot_flip(value_full[rows], rounded_two[...]).reshape(HEADS, 64, BLOCK)
            ds = p * (dp - jnp.sum(p * dp, axis=1, keepdims=True))
            ds = ds.reshape(BLOCK, BLOCK).T.astype(bf16)
            grad_scores[b] = ds
            part = dot(ds, key_full[rows])

            @pl.when(b == 0)
            def _():
                second[...] = part

            @pl.when(b > 0)
            def _():
                second[...] += part

            @pl.when(b == 3)
            def _():
                before.pass_on()
                before.pass_near()

            return carry

        lax.fori_loop(0, 8, cross, 0)

        for reduce in reduces:
            reduce.third()

        def norm_two(rows, carry):
            incoming = second[rows]
            centred, factor = standard(middle[rows])
            total = grad_rows[rows] + norm_back(incoming, centred, factor, vectors[2:3])
            grad_rows[rows] = total
            rounded[rows] = total.astype(bf16)
            return two_sums(incoming, centred, carry)

        gains, shifts = by_rows(BLOCK, 32, norm_two, no_sums())
        grad_vectors[2:3] = gains
        grad_vectors[3:4] = shifts
        gather = Gather(at, rounded, whole, send, recv, local.at[7], 21)
        gather.begin()
        for reduce in reduces:
            reduce.fourth()
        before.pass_far()
        keep = Keep(whole, all_rows, local, 8)

        def work(s, rows):
            keep.block(s, rows)
            grad_mixed[rows] = dot_flip(whole[rows], out_full[...]).astype(bf16)

        gather.each(work)
        before.got(4, 7, 8, 9, 10)
        before.end()
        keep.wait()
        scatter.end()
        for reduce in reduces:
            reduce.end()

    return call(
        body,
        number,
        [grad, *expand_w, after, middle, vectors, down, keys, values, weights, normed_two, *out_w, contract_sum, expand_sum],
        [
            shape(BLOCK, D, dtype=f32),
            shape(BLOCK, D),
            shape(8, BLOCK, BLOCK),
            shape(D, D),
            shape(D, D),
            shape(D, COLS),
            shape(8, D, dtype=f32),
            shape(4, 2, Reduce.deep, HALF),
            shape(4, 2, Reduce.deep, HALF),
        ],
        [
            *Scatter.scratch,
            *Reduce.scratch(False),
            *Reduce.scratch(True, True),
            VMEM((BLOCK, D), bf16),
            VMEM((D, D), bf16),
            VMEM((BLOCK, D), f32),
            VMEM((COLS, D), bf16),
            VMEM((D, HALF), bf16),
            VMEM((D, D), bf16),
            VMEM((D, D), bf16),
            *sems(52),
        ],
        beside,
        lambda at: ring_peers(at) + Reduce.peers(at),
        spaces=[VMEM, ANY, ANY, VMEM, VMEM, VMEM, VMEM, ANY, ANY, VMEM, VMEM, ANY, ANY, ANY, ANY],
        out_spaces=[VMEM, VMEM, VMEM, ANY, ANY, VMEM, VMEM, ANY, ANY],
    )


def causal_backward(number, joined, grad, logs, activated, contract, after, rounded_two, beside):
    at_once = 512

    def body(at, ins, outs, kept):
        (qkv, go, log_rows, activated, contract, after, block), (out, result, all_rows) = ins, outs
        *refs, parts, key_sum, value_sum, send, recv, local = kept
        scatter = Scatter(at, send, recv, refs)
        scatter.products(lambda rows: dot(activated[rows], contract[...]))
        gather = Gather(at, block, all_rows, send, recv, local.at[0], 10)
        for i in range(4):
            for h in range(HEADS):
                a = i * COLS + h * HDIM
                piece = qkv[:, a : a + HDIM] if i < 3 else go[:, h * HDIM : (h + 1) * HDIM]
                parts[i, h] = piece * EIGHTH if i == 0 else piece
        square = (at_once, at_once)
        seen = lax.broadcasted_iota(jnp.int32, square, 1) >= lax.broadcasted_iota(jnp.int32, square, 0)
        blocks = D // at_once

        def one(h, carry):
            turned = parts[1, h].T
            query_parts = []
            for i in reversed(range(blocks)):
                before, upto = i * at_once, (i + 1) * at_once
                rows = slice(before, upto)
                q, g = parts[0, h, rows], parts[3, h, rows]
                k, v = parts[1, h, 0:upto], parts[2, h, 0:upto]
                p = jnp.exp(dot_flip(k, q) - log_rows[pl.ds(h, 1), rows])
                last = jnp.where(seen, p[before:], 0.0)
                p = jnp.concatenate((p[:before], last), axis=0) if i else last
                dp = dot_flip(v, g)
                ds = (p * (dp - jnp.sum(p * dp, axis=0, keepdims=True))).astype(bf16)
                value_part, key_part = dot(p.astype(bf16), g), dot(ds, q)
                if i == blocks - 1:
                    key_sum[0:upto, :] = key_part
                    value_sum[0:upto, :] = value_part
                else:
                    key_sum[0:upto, :] += key_part
                    value_sum[0:upto, :] += value_part
                query_parts.append((dot(turned[:, 0:upto], ds) * EIGHTH).T)
            parts[0, h] = jnp.concatenate(query_parts[::-1], axis=0).astype(bf16)
            parts[1, h] = key_sum[...].astype(bf16)
            parts[2, h] = value_sum[...].astype(bf16)

            @pl.when(h == 0)
            def _():
                scatter.middle()
                gather.begin()

            @pl.when(h == 1)
            def _():
                gather.pass_on()
                gather.pass_near()

            return carry

        lax.fori_loop(0, HEADS, one, 0)
        gather.pass_far()
        for i in range(3):
            out[:, i * COLS : (i + 1) * COLS] = jnp.concatenate([parts[i, h] for h in range(HEADS)], axis=1)
        scatter.arrive()

        def finish(rows, carry):
            result[rows] = (after[rows] + scatter.total(rows)).astype(bf16)

        by_rows(BLOCK, 32, finish)
        gather.got(4, 7, 8, 9, 10)
        gather.end()
        scatter.end()

    return call(
        body,
        number,
        [joined, grad, logs, activated, contract, after, rounded_two],
        [shape(D, 3 * COLS), shape(BLOCK, D), shape(D, D)],
        [*Scatter.scratch, VMEM((4, HEADS, D, HDIM), bf16), VMEM((D, HDIM), f32), VMEM((D, HDIM), f32), *sems(21)],
        beside,
        ring_peers,
        out_spaces=[VMEM, VMEM, ANY],
    )


def leave(number, grad, joined, x, vectors, grad_rows, sums, late, text_part, beside):
    relay = Relay(jax.ShapeDtypeStruct((BLOCK, D), bf16), True)
    some = 64 // 8

    def ring(at):
        return [{"wide": lax.rem(at.w + k, 8)} for k in range(1, 8)]

    def clips(at):
        return [(k, b, {**at.at_dp(k), "narrow": lax.rem(at.n + b, 2)}) for k in range(8) for b in range(2)][1:]

    def group(at):
        return [(b, {"wide": lax.rem(at.w + k, 8), "narrow": lax.rem(at.n + b, 2)}) for k in range(8) for b in range(2)][1:]

    def peers(at):
        known = ring_peers(at) + relay.peers(at) + Reduce.peers(at)
        known += [(f"r{i}", peer) for i, peer in enumerate(ring(at))]
        known += [(f"c{i}", peer) for i, (_, _, peer) in enumerate(clips(at))]
        return known + [(f"g{i}", peer) for i, (_, peer) in enumerate(group(at))]

    def body(at, ins, outs, kept):
        grad, weight, x, vectors, before, late, text, one, two = ins
        result, out_one, out_two, vector_sums, text_out = outs
        refs, kept = kept[:7], kept[7:]
        reduces = [
            Reduce(at, one, out_one, kept[0:4], kept[-3], kept[-2], kept[-1], 12, 1, False),
            Reduce(at, two, out_two, kept[4:8], kept[-3], kept[-2], kept[-1], 22, 3, True),
        ]
        rounded, parts, ring_parts, ring_sum, clip_parts, text_parts, text_sum, send, recv, local = kept[8:]
        me = at.spot(at.y, at.c)

        def move(slot, source, target, peer):
            return remote(source, target, send.at[slot], recv.at[slot], peer)

        to_ring, to_clips, to_group = ring(at), clips(at), group(at)
        slot = 32
        trades = []
        for peer in to_ring:
            there = at.spot(lax.div(peer["wide"], 2), lax.rem(peer["wide"], 2))
            trades.append(move(slot, text.at[there], text_parts.at[me], peer))
            slot += 1
        text_own = pltpu.make_async_copy(text.at[me], text_parts.at[me], local.at[5])
        texts = []
        for b, peer in to_group:
            n = lax.rem(at.n + b, 2)
            texts.append(move(slot, text_sum.at[:, at.half(n)], text_out.at[at.n, me], peer))
            slot += 1
        text_stay = pltpu.make_async_copy(text_sum.at[:, at.half(at.n)], text_out.at[at.n, me], local.at[6])
        rings = []
        for peer in to_ring:
            rings.append(move(slot, parts, ring_parts.at[at.w], peer))
            slot += 1
        ring_own = pltpu.make_async_copy(parts, ring_parts.at[at.w], local.at[7])
        spreads = []
        for _, b, peer in to_clips:
            n = lax.rem(at.n + b, 2)
            spreads.append(move(slot, ring_sum.at[:, at.half(n)], clip_parts.at[at.dp, at.n], peer))
            slot += 1
        clip_own = pltpu.make_async_copy(ring_sum.at[:, at.half(at.n)], clip_parts.at[at.dp, at.n], local.at[8])

        for reduce in reduces:
            reduce.first()
        text_own.start()
        for copy in trades:
            copy.start()
        scatter = Scatter(at, send, recv, refs)
        scatter.products(lambda rows: dot(grad[rows], weight[...]))
        scatter.middle()
        text_own.wait()
        for copy in trades:
            copy.wait_recv()
        total = text_parts[0].astype(f32)
        for i in range(1, 8):
            total += text_parts[i].astype(f32)
        text_sum[...] = total.astype(bf16)
        text_stay.start()
        for copy in texts:
            copy.start()
        scatter.arrive()

        def norm(rows, carry):
            incoming = scatter.total(rows)
            centred, factor = standard(x[rows].astype(f32))
            total = before[rows] + norm_back(incoming, centred, factor, vectors[0:1])
            rounded[rows] = total.astype(bf16)
            return two_sums(incoming, centred, carry)

        gains, shifts = by_rows(BLOCK, 32, norm, no_sums())
        moving = functools.partial(relay_run, relay, at, rounded, result, send, recv, local.at[0], 10)
        moving(False)
        parts[0:1] = gains
        parts[1:2] = shifts
        parts[2:6] = late[2:6]
        parts[6:8] = jnp.zeros((2, D), f32)
        ring_own.start()
        for copy in rings:
            copy.start()
        for reduce in reduces:
            reduce.second()
        ring_own.wait()
        for copy in rings:
            copy.wait_recv()
        total = ring_parts[0]
        for i in range(1, 8):
            total += ring_parts[i]
        ring_sum[...] = total
        clip_own.start()
        for copy in spreads:
            copy.start()
        for reduce in reduces:
            reduce.third()
        for reduce in reduces:
            reduce.fourth()
        clip_own.wait()
        for copy in spreads:
            copy.wait_recv()
        total = clip_parts[0, 0] + clip_parts[0, 1]
        for i in range(1, 8):
            total += clip_parts[i, 0] + clip_parts[i, 1]
        vector_sums[...] = total
        moving(True)
        text_stay.wait()
        for copy in texts:
            copy.wait()
        for copy in trades + rings + spreads:
            copy.wait_send()
        scatter.end()
        for reduce in reduces:
            reduce.end()

    deep = Reduce.deep
    return call(
        body,
        number,
        [grad, joined, x, vectors, grad_rows, late, text_part, *sums],
        [
            shape(384, HALF),
            shape(4, 2, deep, HALF),
            shape(4, 2, deep, HALF),
            shape(8, HALF, dtype=f32),
            shape(2, 8, some, HALF),
        ],
        [
            *Scatter.scratch,
            *Reduce.scratch(False),
            *Reduce.scratch(True),
            VMEM((BLOCK, D), bf16),
            VMEM((8, D), f32),
            VMEM((8, 8, D), f32),
            VMEM((8, D), f32),
            VMEM((8, 2, 8, HALF), f32),
            VMEM((8, some, D), bf16),
            VMEM((some, D), bf16),
            *sems(32 + 7 + 15 + 7 + 15),
        ],
        beside,
        peers,
        spaces=[VMEM, VMEM, VMEM, VMEM, VMEM, VMEM, ANY, ANY, ANY],
        out_spaces=[ANY, ANY, ANY, VMEM, ANY],
    )


def on_device(
    layer_input,
    text_states,
    cotangent,
    first_gain,
    first_shift,
    query_weight,
    key_weight,
    value_weight,
    output_weight,
    second_gain,
    second_shift,
    cross_query,
    cross_key,
    cross_value,
    cross_output,
    third_gain,
    third_shift,
    expand_weight,
    contract_weight,
):
    vectors = (first_gain, first_shift, second_gain, second_shift, third_gain, third_shift)
    vectors = jnp.concatenate([jnp.stack(vectors).astype(f32), jnp.zeros((2, HALF), f32)], axis=0)
    weights = [query_weight.T, key_weight.T, value_weight.T]
    query_t = cross_query.T
    pair_t = jnp.concatenate((cross_key.T, cross_value.T), axis=0)
    n = lax.axis_index("narrow")

    text_parts = dot_flip(text_states.reshape(128, HALF), pair_t).reshape(2, 64, 2 * COLS)
    (x, vectors, joined, all_one, qkv), ((text_pair_got,), (query_got,), (cross_got,), (text_got,)) = enter(
        1, layer_input, vectors, weights, [GiveClip(text_parts), Give(query_t), Give(cross_output), GiveClip(text_states)]
    )
    text_pair = (lax.dynamic_index_in_dim(text_parts, n, 0, False) + text_pair_got).astype(bf16)
    (attended, logs, all_keys, all_values), ((down,), (out_got,), (expand_got,)) = causal_forward(
        2,
        qkv,
        (query_t, query_got),
        (cross_output, cross_got),
        text_pair,
        [Relay(cotangent), Give(output_weight), Give(expand_weight)],
    )
    out_w, expand_w = (output_weight, out_got), (expand_weight, expand_got)
    middle, after, normed_two, cross_p, all_three, all_down, activated, grad_expand, contract = forward_rest(
        3, attended, out_w, x, vectors, all_keys, all_values, down, expand_w, contract_weight
    )

    deep = Reduce.deep
    contract_part = outer(activated, all_down).astype(bf16).reshape(4, 2, deep, D)
    expand_part = outer(all_three, grad_expand).astype(bf16).reshape(2, 4, 2, deep, HALF)
    results, ((cross_p,),) = backward_rest(
        4,
        grad_expand,
        expand_w,
        after,
        middle,
        vectors,
        down,
        all_keys,
        all_values,
        cross_p,
        normed_two,
        out_w,
        contract_part,
        expand_part,
        [Trade(cross_p)],
    )
    grad_one, rounded_two, grad_scores, all_two, all_mid_one, grad_attended, late, contract_grad, expand_grad = results
    (grad_qkv, layer_output, all_mid_two), ((grad_scores,), (pair_got,)) = causal_backward(
        5, qkv, grad_attended, logs, activated, contract, after, rounded_two, [Trade(grad_scores), Give(pair_t)]
    )

    joined_part = jnp.concatenate((outer(grad_qkv, all_one), outer(attended, all_mid_one)), axis=0)
    grad_keys = outer(grad_scores.reshape(D, COLS), all_two).astype(bf16).reshape(HEADS, 64, D)
    grad_values = outer(cross_p.reshape(D, COLS), all_mid_two).astype(bf16).reshape(HEADS, 64, D)
    own_first = n == 0

    def whole(own, got):
        return jnp.concatenate((jnp.where(own_first, own, got), jnp.where(own_first, got, own)), axis=1)

    text = whole(lax.dynamic_index_in_dim(text_states, n, 0, False), text_got)
    heads_query = whole(query_t, query_got).reshape(HEADS, HDIM, D)
    heads_out = whole(cross_output, cross_got).reshape(HEADS, HDIM, D)
    text_heads = text_pair.reshape(64, 2, HEADS, HDIM)

    def heads(what, a, b):
        return jnp.einsum(what, a, b, preferred_element_type=f32)

    grad_text_keys = heads("hkf,hdf->khd", grad_keys, heads_query) * EIGHTH
    grad_text_values = heads("hkf,hdf->khd", grad_values, heads_out)
    grad_pair = jnp.stack((grad_text_keys, grad_text_values), axis=1).reshape(64, 2 * COLS).astype(bf16)
    grad_query = heads("khd,hkf->hdf", text_heads[:, 0], grad_keys).reshape(COLS, D) * EIGHTH
    grad_cross = heads("khd,hkf->hdf", text_heads[:, 1], grad_values).reshape(COLS, D)
    cross_part = jnp.concatenate((grad_query, outer(grad_pair, text), grad_cross), axis=0)
    text_part = dot(grad_pair, whole(pair_t, pair_got)).astype(bf16).reshape(8, 8, D)

    (input_grad, joined_grad, cross_grad, parts, text_grad), ((layer_output,),) = leave(
        6,
        grad_qkv,
        joined,
        x,
        vectors,
        grad_one,
        [part.astype(bf16).reshape(4, 2, deep, D) for part in (joined_part, cross_part)],
        late,
        text_part,
        [Relay(layer_output, True)],
    )
    joined_grad, cross_grad, expand_grad, contract_grad = (
        grad.reshape(HALF, HALF).astype(f32) for grad in (joined_grad, cross_grad, expand_grad, contract_grad)
    )
    return (
        layer_output,
        input_grad.astype(f32),
        text_grad.reshape(2, 64, HALF).astype(f32),
        parts[0],
        parts[1],
        joined_grad[:COLS].T,
        joined_grad[COLS : 2 * COLS].T,
        joined_grad[2 * COLS : 3 * COLS].T,
        joined_grad[3 * COLS :],
        parts[2],
        parts[3],
        cross_grad[:COLS].T,
        cross_grad[COLS : 2 * COLS].T,
        cross_grad[2 * COLS : 3 * COLS].T,
        cross_grad[3 * COLS :],
        parts[4],
        parts[5],
        expand_grad,
        contract_grad,
    )


def solution(mesh):
    return jax.shard_map(
        on_device,
        mesh=mesh,
        in_specs=(
            P(("dp", "wide"), "narrow"),
            P("dp", None, "narrow"),
            P(("dp", "wide"), "narrow"),
            P("narrow"),
            P("narrow"),
            P("narrow", "wide"),
            P("narrow", "wide"),
            P("narrow", "wide"),
            P("wide", "narrow"),
            P("narrow"),
            P("narrow"),
            P("narrow", "wide"),
            P("narrow", "wide"),
            P("narrow", "wide"),
            P("wide", "narrow"),
            P("narrow"),
            P("narrow"),
            P("narrow", "wide"),
            P("wide", "narrow"),
        ),
        out_specs=(
            P(("dp", "wide"), "narrow"),
            P(("dp", "wide"), "narrow"),
            P("dp", None, "narrow"),
            P("narrow"),
            P("narrow"),
            P("narrow", "wide"),
            P("narrow", "wide"),
            P("narrow", "wide"),
            P("wide", "narrow"),
            P("narrow"),
            P("narrow"),
            P("narrow", "wide"),
            P("narrow", "wide"),
            P("narrow", "wide"),
            P("wide", "narrow"),
            P("narrow"),
            P("narrow"),
            P("narrow", "wide"),
            P("wide", "narrow"),
        ),
        check_vma=False,
    )
```

```python
import functools
import math

import jax
import jax.numpy as jnp
from jax import lax
from jax.experimental import pallas as pl
from jax.experimental.pallas import tpu as pltpu
from jax.sharding import PartitionSpec as P

D = 1536
HALF = 768
HDIM = 64
HEADS = 3
COLS = HEADS * HDIM
BLOCK = 192
EPSILON = 1e-05
NEGATIVE = -1e30
ROOT_HALF = 0.7071067811865476
GAUSS_NORM = 0.3989422804014327
MESH = pl.DeviceIdType.MESH
VMEM = pltpu.VMEM
ANY = pl.ANY
bf16, f32 = jnp.bfloat16, jnp.float32


def dot(a, b):
    return lax.dot_general(a, b, (((1,), (0,)), ((), ())), preferred_element_type=f32)


def dot_flip(a, b):
    return lax.dot_general(a, b, (((1,), (1,)), ((), ())), preferred_element_type=f32)


def outer(a, b):
    return lax.dot_general(a, b, (((0,), (0,)), ((), ())), preferred_element_type=f32)


class Place:
    def __init__(self):
        self.dp, self.w, self.n = (lax.axis_index(a) for a in ("dp", "wide", "narrow"))
        self.y, self.c = lax.div(self.w, 2), lax.rem(self.w, 2)
        self.z, self.s = lax.div(self.dp, 2), lax.rem(self.dp, 2)
        self.up, self.down = lax.rem(self.y + 1, 4), lax.rem(self.y + 3, 4)
        self.across = 3 - self.y
        self.moved = lax.rem(lax.div(self.y, 2) + self.n, 2)
        self.clip = lax.div(self.y, 2)

    def spot(self, y, c):
        moved = lax.rem(lax.div(y, 2) + self.n, 2)
        return (lax.rem(y + moved, 2) * 2 + c) * 2 + moved

    def rows(self, y, c, start=0, size=BLOCK):
        return pl.ds(pl.multiple_of(self.spot(y, c) * BLOCK + start, 32), size)

    def half(self, n):
        return pl.ds(pl.multiple_of(n * HALF, HALF), HALF)

    def at_y(self, y):
        return {"wide": y * 2 + self.c}

    def core(self):
        return {"wide": self.y * 2 + 1 - self.c}

    def x(self):
        return {"narrow": 1 - self.n}

    def at_z(self, k):
        return {"dp": lax.rem(self.z + k, 4) * 2 + self.s}

    def at_dp(self, k):
        return {"dp": lax.rem(self.dp + k, 8)}

    def at_x(self, ds, dn):
        return {"dp": self.z * 2 + lax.rem(self.s + ds, 2), "narrow": lax.rem(self.n + dn, 2)}


def remote(src, dst, send, recv, peer):
    return pltpu.make_async_remote_copy(
        src_ref=src, dst_ref=dst, send_sem=send, recv_sem=recv, device_id=peer, device_id_type=MESH
    )


def greet(peers):
    barrier = pltpu.get_barrier_semaphore()
    for peer in peers:
        pl.semaphore_signal(barrier, inc=1, device_id=peer, device_id_type=MESH)
    pl.semaphore_wait(barrier, len(peers))


class Give:
    def __init__(self, array):
        self.ins, self.copies, self.locals = [array], 1, 0
        self.outs = [jax.ShapeDtypeStruct(array.shape, array.dtype)]

    def peers(self, at):
        return [("x", at.x())]

    def moves(self, at, ins, outs):
        return [(ins[0], outs[0], at.x())], []


class GiveClip(Give):
    def __init__(self, array):
        super().__init__(array)
        self.outs = [jax.ShapeDtypeStruct(array.shape[1:], array.dtype)]

    def moves(self, at, ins, outs):
        return [(ins[0].at[1 - at.n], outs[0], at.x())], []


class Trade:
    def __init__(self, array):
        self.ins, self.copies, self.locals = [array], 7, 1
        self.outs = [jax.ShapeDtypeStruct(array.shape, array.dtype)]

    def others(self, at):
        return [lax.rem(at.w + k, 8) for k in range(1, 8)]

    def peers(self, at):
        return [(f"w{k + 1}", {"wide": w}) for k, w in enumerate(self.others(at))]

    def moves(self, at, ins, outs):
        mine = at.spot(at.y, at.c)
        dst = outs[0].at[mine]
        far = [(ins[0].at[at.spot(lax.div(w, 2), lax.rem(w, 2))], dst, {"wide": w}) for w in self.others(at)]
        return far, [(ins[0].at[mine], dst)]


class ToSpots:
    def __init__(self, array):
        self.ins, self.copies, self.locals = [array], 7, 1
        self.outs = [jax.ShapeDtypeStruct((8, *array.shape), array.dtype)]

    def peers(self, at):
        return [(f"w{k}", {"wide": lax.rem(at.w + k, 8)}) for k in range(1, 8)]

    def moves(self, at, ins, outs):
        dst = outs[0].at[at.spot(at.y, at.c)]
        return [(ins[0], dst, peer) for _, peer in self.peers(at)], [(ins[0], dst)]


class Relay:
    def __init__(self, array, back=False):
        self.ins, self.back, self.copies, self.locals = [array], back, 2, 1
        shape = (384, HALF) if back else (BLOCK, D)
        self.outs = [jax.ShapeDtypeStruct(shape, array.dtype)]

    def peers(self, at):
        return [
            ("x", at.x()),
            ("a0", {"wide": at.across * 2 + at.c}),
            ("a1", {"wide": at.across * 2 + at.c, "narrow": 1 - at.n}),
        ]


def relay_run(relay, at, src, dst, send, recv, local, base, finish):
    mine, other = at.half(at.n), at.half(1 - at.n)
    over = at.across * 2 + at.c
    if relay.back:
        row = pl.ds(pl.multiple_of(at.moved * BLOCK, BLOCK), BLOCK)
        to = recv.at[base + at.moved]
        own = src.at[:, mine], src.at[:, other]
        land = dst.at[0:BLOCK], dst.at[BLOCK : 2 * BLOCK]
    else:
        row = mine
        to = recv.at[base + at.n]
        own = src.at[0:BLOCK], src.at[BLOCK : 2 * BLOCK]
        land = dst.at[:, at.half(0)], dst.at[:, at.half(1)]
    target = dst.at[row] if relay.back else dst.at[:, row]

    def arrive(slot, part):
        return remote(own[0], part, send.at[base], recv.at[base + slot], at.x())

    @pl.when(at.moved == 0)
    def _():
        stay = pltpu.make_async_copy(own[0], target, local)
        if relay.back:
            go = remote(own[1], target, send.at[base], to, at.x())
        else:
            go = remote(own[1], target, send.at[base], to, {"wide": over})
        if not finish:
            go.start()
            stay.start()
        else:
            stay.wait()
            go.wait_send()
            if relay.back:
                arrive(1, land[1]).wait_recv()
            else:
                arrive(1 - at.n, dst.at[:, other]).wait_recv()

    @pl.when(at.moved == 1)
    def _():
        if relay.back:
            first = remote(own[1], target, send.at[base], to, {"wide": over, "narrow": 1 - at.n})
            second = remote(own[0], target, send.at[base + 1], to, {"wide": over})
        else:
            first = remote(own[1], target, send.at[base], to, {"wide": over, "narrow": 1 - at.n})
            second = remote(own[0], target, send.at[base + 1], to, at.x())
        if not finish:
            first.start()
            second.start()
        else:
            first.wait_send()
            second.wait_send()
            arrive(0, land[0]).wait_recv()
            arrive(1, land[1]).wait_recv()


def call(body, number, ins, outs, scratch=(), beside=(), peers=None, spaces=None, out_spaces=None, late=False):
    spaces = spaces or [VMEM] * len(ins)
    out_spaces = out_spaces or [VMEM] * len(outs)
    copies = sum(b.copies for b in beside)
    locals_ = sum(b.locals for b in beside)
    side_ins = [a for b in beside for a in b.ins]
    side_outs = [a for b in beside for a in b.outs]
    n_in, n_out, n_scratch = len(ins), len(outs), len(scratch)

    def kernel(*refs):
        at = Place()
        refs = list(refs)

        def take(count):
            out = refs[:count]
            del refs[:count]
            return out

        main_in, side_in = take(n_in), take(len(side_ins))
        main_out, side_out, kept = take(n_out), take(len(side_outs)), take(n_scratch)
        send, recv, local = take(3)
        known = dict(peers(at)) if peers else {}
        for b in beside:
            known.update(dict(b.peers(at)))
        if known:
            greet(list(known.values()))
        side_refs = [([side_in.pop(0) for _ in b.ins], [side_out.pop(0) for _ in b.outs]) for b in beside]
        todo = []

        def start():
            slot, place = 0, 0
            for b, (i, o) in zip(beside, side_refs):
                if isinstance(b, Relay):
                    run = functools.partial(relay_run, b, at, i[0], o[0], send, recv, local.at[place], slot)
                    run(False)
                    todo.append(functools.partial(run, True))
                    slot, place = slot + 2, place + 1
                    continue
                far, near = b.moves(at, i, o)
                for src, dst, peer in far:
                    copy = remote(src, dst, send.at[slot], recv.at[slot], peer)
                    copy.start()
                    todo.append(copy.wait)
                    slot += 1
                for src, dst in near:
                    copy = pltpu.make_async_copy(src, dst, local.at[place])
                    copy.start()
                    todo.append(copy.wait)
                    place += 1

        at.start_beside = start
        if not late:
            start()
        if body:
            body(at, main_in, main_out, kept)
        for wait in todo:
            wait()

    results = pl.pallas_call(
        kernel,
        out_shape=tuple(outs) + tuple(side_outs),
        in_specs=[pl.BlockSpec(memory_space=s) for s in spaces] + [pl.BlockSpec(memory_space=ANY)] * len(side_ins),
        out_specs=tuple(pl.BlockSpec(memory_space=m) for m in out_spaces + [ANY] * len(side_outs)),
        scratch_shapes=[
            *scratch,
            pltpu.SemaphoreType.DMA((max(copies, 1),)),
            pltpu.SemaphoreType.DMA((max(copies, 1),)),
            pltpu.SemaphoreType.DMA((max(locals_, 1),)),
        ],
        compiler_params=pltpu.CompilerParams(
            collective_id=number, has_side_effects=True, vmem_limit_bytes=58 << 20
        ),
    )(*ins, *side_ins)
    results = list(results)
    main, rest = results[: len(outs)], results[len(outs) :]
    sides = []
    for b in beside:
        sides.append(rest[: len(b.outs)])
        del rest[: len(b.outs)]
    return main, sides


def ring_peers(at):
    return [("up", at.at_y(at.up)), ("down", at.at_y(at.down)), ("core", at.core())]


def sems(count):
    return [pltpu.SemaphoreType.DMA((count,)), pltpu.SemaphoreType.DMA((count,)), pltpu.SemaphoreType.DMA((count,))]


def by_rows(count, size, work, carry=None):
    def step(i, carry):
        return work(pl.ds(pl.multiple_of(i * size, size), size), carry)

    return lax.fori_loop(0, count // size, step, carry)


class Whole:
    def __init__(self, at, own, got, full, sem, axis):
        size = own.shape[axis]
        self.copies = []
        for i, (part, n) in enumerate(((own, at.n), (got, 1 - at.n))):
            where = pl.ds(pl.multiple_of(n * size, size), size)
            target = full.at[where] if axis == 0 else full.at[:, where]
            self.copies.append(pltpu.make_async_copy(part, target, sem.at[i]))
            self.copies[-1].start()

    def wait(self):
        for copy in self.copies:
            copy.wait()


class Reduce:
    @staticmethod
    def scratch(deep, x_first, by_rows=False):
        first = (4, deep, HALF) if x_first else (2, 2, deep, HALF) if by_rows else (2, deep, D)
        return [VMEM((3, *first), bf16), VMEM(first, bf16), VMEM((3, deep, HALF), bf16), VMEM((2, deep, HALF), bf16)]

    @staticmethod
    def peers(at):
        return [(f"z{k}", at.at_z(k)) for k in (1, 2, 3)] + [(f"x{a}{b}", at.at_x(a, b)) for a, b in ((0, 1), (1, 0), (1, 1))]

    def __init__(self, at, src, out, refs, send, recv, local, base, place, x_first, by_rows=False):
        self.at, self.src, self.out = at, src, out
        self.land, self.total, self.land_two, self.last = refs
        self.x_first, self.by_rows = x_first, by_rows
        self.deep = self.last.shape[1]
        self.chunk = 32 if self.deep % 32 == 0 else 24
        z_steps = [(at.at_z(k), lax.rem(at.z + k, 4)) for k in (1, 2, 3)]
        x_steps = [
            (at.at_x(a, b), (lax.rem(at.s + a, 2), lax.rem(at.n + b, 2))) for a, b in ((0, 1), (1, 0), (1, 1))
        ]
        first, second = (x_steps, z_steps) if x_first else (z_steps, x_steps)

        def move(slot, source, target, peer):
            return remote(source, target, send.at[base + slot], recv.at[base + slot], peer)

        self.one = [move(i, self.piece(where), self.land.at[i], peer) for i, (peer, where) in enumerate(first)]
        self.own = pltpu.make_async_copy(
            self.piece((at.s, at.n) if x_first else at.z), self.total, local.at[place]
        )
        self.two = [move(3 + i, self.part(where), self.land_two.at[i], peer) for i, (peer, where) in enumerate(second)]
        self.mine = at.z if x_first else (at.s, at.n)
        self.three = move(6, self.last.at[at.s], self.last.at[at.s], at.at_x(1, 0))
        target = out.at[at.z]
        self.four = [move(7 + i, self.last, target, peer) for i, (peer, _) in enumerate(z_steps)]
        self.stay = pltpu.make_async_copy(self.last, target, local.at[place + 1])

    def piece(self, where):
        if self.x_first:
            s, n = where
            return self.src.at[n, :, s] if self.by_rows else self.src.at[:, s, :, self.at.half(n)]
        return self.src.at[:, where] if self.by_rows else self.src.at[where]

    def part(self, where):
        if self.x_first:
            return self.total.at[where]
        s, n = where
        return self.total.at[n, s] if self.by_rows else self.total.at[s, :, self.at.half(n)]

    def first(self):
        for copy in self.one + [self.own]:
            copy.start()

    def second(self):
        self.own.wait()
        for copy in self.one:
            copy.wait_recv()
        lead = self.total.shape[:-2]
        count = math.prod(lead)

        def add(i, carry):
            at_lead = (i,) if len(lead) == 1 else (lax.div(i, lead[1]), lax.rem(i, lead[1]))
            for start in range(0, self.deep, self.chunk):
                where = (*at_lead, slice(start, start + self.chunk))
                got = self.total[where].astype(f32)
                for k in range(3):
                    got += self.land[(k, *where)].astype(f32)
                self.total[where] = got.astype(bf16)
            return carry

        lax.fori_loop(0, count, add, 0)
        for copy in self.two:
            copy.start()

    def third(self):
        for copy in self.two:
            copy.wait_recv()
        own = self.part(self.mine)
        s = self.at.s
        for start in range(0, self.deep, self.chunk):
            rows = slice(start, start + self.chunk)
            got = own[rows].astype(f32)
            for k in range(3):
                got += self.land_two[k, rows].astype(f32)
            self.last[s, rows] = got.astype(bf16)
        self.three.start()

    def fourth(self):
        self.three.wait_recv()
        for copy in self.four + [self.stay]:
            copy.start()

    def end(self):
        for copy in self.four:
            copy.wait()
        for copy in self.one + self.two + [self.three]:
            copy.wait_send()
        self.stay.wait()


class Gather:
    slots = 11

    def __init__(self, at, x, whole, send, recv, local, base=0):
        self.at, self.x, self.whole = at, x, whole
        y, c, up, down = at.y, at.c, at.up, at.down
        far = lax.rem(y + 2, 4)
        half = BLOCK // 2

        def move(slot, y_from, peer, start=0, size=BLOCK, first=False):
            rows = at.rows(y_from, c, start, size)
            src = whole.at[rows]
            if first:
                src = x if size == BLOCK else x.at[start : start + size]
            return remote(src, whole.at[rows], send.at[base + slot], recv.at[base + slot], peer)

        to_up, to_down, core = at.at_y(up), at.at_y(down), at.core()
        self.sends = [
            move(0, y, to_up, 0, half, first=True),
            move(1, y, to_up, half, half, first=True),
            move(2, y, to_down, half, half, first=True),
            move(3, y, to_down, 0, half, first=True),
            move(4, y, core, first=True),
            move(5, down, to_up, 0, half),
            move(6, up, to_down, half, half),
            move(7, down, core),
            move(8, up, core),
            move(9, far, core, 0, half),
            move(10, far, core, half, half),
        ]
        self.own = pltpu.make_async_copy(x, whole.at[at.rows(y, c)], local)

    def begin(self):
        for i in (0, 2, 1, 3, 4):
            self.sends[i].start()
        self.own.start()
        self.own.wait()

    def chain(self, *pairs):
        for arrived, leaving in pairs:
            self.sends[arrived].wait_recv()
            self.sends[leaving].start()

    def pass_on(self):
        self.chain((0, 5), (2, 6))

    def pass_near(self):
        self.chain((1, 7), (3, 8))

    def pass_far(self):
        self.chain((5, 9), (6, 10))

    def got(self, *slots):
        for i in slots:
            self.sends[i].wait_recv()

    def end(self):
        for copy in self.sends:
            copy.wait_send()

    def finish(self):
        self.pass_on()
        self.pass_near()
        self.pass_far()
        self.got(4, 7, 8, 9, 10)
        self.end()

    def each(self, work):
        at = self.at

        def step(s, carry):
            @pl.when(s == 1)
            def _():
                self.got(4)
                self.pass_on()

            @pl.when(s == 2)
            def _():
                self.pass_near()

            @pl.when(s == 3)
            def _():
                self.got(8)

            @pl.when(s == 5)
            def _():
                self.got(7)

            @pl.when(s == 6)
            def _():
                self.pass_far()

            @pl.when(s == 7)
            def _():
                self.got(9, 10)

            work(s, self.place(s))
            return carry

        lax.fori_loop(0, 8, step, 0)
        self.end()

    def place(self, s):
        g = lax.div(s, 2)
        off = g + lax.div(g, 2) - 2 * lax.div(g, 3)
        return self.at.rows(lax.rem(self.at.y + off, 4), lax.rem(self.at.c + s, 2))


QUARTER = 384


class GatherZ(Gather):
    def __init__(self, at, quarter, full, send, recv, local, base=0):
        self.at = at
        z, up, down, far = at.z, lax.rem(at.z + 1, 4), lax.rem(at.z + 3, 4), lax.rem(at.z + 2, 4)
        half = QUARTER

        def move(slot, z_from, peer, start=0, size=2 * QUARTER, first=False):
            rows = pl.ds(pl.multiple_of(at.c * 2 * QUARTER + start, QUARTER), size)
            target = full.at[rows, self.columns(z_from)]
            return remote(quarter.at[rows] if first else target, target, send.at[base + slot], recv.at[base + slot], peer)

        to_up, to_down, core = at.at_z(1), at.at_z(3), at.core()
        self.sends = {
            0: move(0, z, to_up, 0, half, first=True),
            1: move(1, z, to_up, half, half, first=True),
            2: move(2, z, to_down, half, half, first=True),
            3: move(3, z, to_down, 0, half, first=True),
            5: move(5, down, to_up, 0, half),
            6: move(6, up, to_down, half, half),
            7: move(7, down, core),
            8: move(8, up, core),
            9: move(9, far, core, 0, half),
            10: move(10, far, core, half, half),
        }
        self.own = pltpu.make_async_copy(quarter, full.at[:, self.columns(z)], local)

    @staticmethod
    def columns(z):
        return pl.ds(pl.multiple_of(z * QUARTER, QUARTER), QUARTER)

    @staticmethod
    def peers(at):
        return [("z1", at.at_z(1)), ("z3", at.at_z(3)), ("core", at.core())]

    def begin(self):
        for i in (0, 2, 1, 3):
            self.sends[i].start()
        self.own.start()

    def end(self):
        self.got(7, 8, 9, 10)
        self.own.wait()
        for copy in self.sends.values():
            copy.wait_send()


class Scatter:
    slots = 10
    scratch = [
        VMEM((4, BLOCK, D), bf16),
        VMEM((4, BLOCK, D), bf16),
        VMEM((4, BLOCK, D), f32),
        VMEM((2, BLOCK, D), bf16),
        VMEM((2, BLOCK, D), bf16),
        VMEM((2, BLOCK // 2, D), bf16),
        VMEM((2, BLOCK // 2, D), bf16),
    ]

    def __init__(self, at, send, recv, refs, base=0):
        self.at, self.send, self.recv, self.base = at, send, recv, base
        self.out_c, self.in_c, self.own, self.out_y, self.in_y, self.half_out, self.half_in = refs
        half = BLOCK // 2
        peers = at.at_y(at.up), at.at_y(at.down)

        def move(slot, src, dst, peer):
            return remote(src, dst, send.at[base + slot], recv.at[base + slot], peer)

        self.cores = [self.core(g) for g in range(4)]
        self.halves = [move(4 + i, self.half_out.at[i], self.half_in.at[i], peers[i]) for i in range(2)]
        free = [pl.ds((1 - i) * half, half) for i in range(2)]
        bound = [pl.ds(i * half, half) for i in range(2)]
        self.free = [move(6 + i, self.out_y.at[i, free[i]], self.in_y.at[i, free[i]], peers[i]) for i in range(2)]
        self.bound = [move(8 + i, self.out_y.at[i, bound[i]], self.in_y.at[i, bound[i]], peers[i]) for i in range(2)]

    def core(self, g):
        slot = self.base + g
        return remote(self.out_c.at[g], self.in_c.at[g], self.send.at[slot], self.recv.at[slot], self.at.core())

    def both(self, g, rows):
        return self.own[g, rows] + self.in_c[g, rows].astype(f32)

    def products(self, product):
        at = self.at
        half = BLOCK // 2

        def part_rows(rows, i):
            return pl.ds(pl.multiple_of(rows.start + i * half, 32), 32)

        def send_free(i):
            self.cores[1 + i].wait_recv()

            def add(rows, carry):
                there = part_rows(rows, 1 - i)
                self.out_y[i, there] = self.both(1 + i, there).astype(bf16)

            by_rows(half, 32, add)
            self.free[i].start()

        def step(s, carry):
            g = lax.div(s, 2)
            off = lax.rem(6 - g + 3 * lax.div(g, 2) + 2 * lax.div(g, 3), 4)
            part = product(at.rows(lax.rem(at.y + off, 4), lax.rem(at.c + 1 + s, 2)))

            @pl.when(lax.rem(s, 2) == 0)
            def _():
                self.out_c[g] = part.astype(bf16)
                self.core(g).start()

            @pl.when(lax.rem(s, 2) == 1)
            def _():
                self.own[g] = part

            @pl.when(s == 2)
            def _():
                self.cores[0].wait_recv()
                for i in range(2):

                    def add(rows, carry, i=i):
                        self.half_out[i, rows] = self.both(0, part_rows(rows, i)).astype(bf16)

                    by_rows(half, 32, add)
                    self.halves[i].start()

            @pl.when(s == 4)
            def _():
                send_free(0)

            @pl.when(s == 6)
            def _():
                send_free(1)

            return carry

        lax.fori_loop(0, 8, step, 0)

    def middle(self):
        half = BLOCK // 2
        for i in range(2):
            self.halves[i].wait_recv()

            def add(rows, carry, i=i):
                here = pl.ds(pl.multiple_of(rows.start + i * half, 32), 32)
                self.out_y[i, here] = (self.both(1 + i, here) + self.half_in[i, rows].astype(f32)).astype(bf16)

            by_rows(half, 32, add)
            self.bound[i].start()

    def arrive(self):
        self.cores[3].wait_recv()
        for copy in self.free + self.bound:
            copy.wait_recv()

    def total(self, rows):
        return self.both(3, rows) + self.in_y[0, rows].astype(f32) + self.in_y[1, rows].astype(f32)

    def end(self):
        for copy in self.cores + self.halves + self.free + self.bound:
            copy.wait_send()


def standard(values):
    average = jnp.mean(values, axis=1, keepdims=True)
    variance = jnp.mean(values * values, axis=1, keepdims=True) - average * average
    factor = lax.rsqrt(variance + EPSILON)
    return (values - average) * factor, factor


def norm_back(incoming, centred, factor, gain):
    scaled = incoming * gain
    first = jnp.mean(scaled, axis=1, keepdims=True)
    second = jnp.mean(scaled * centred, axis=1, keepdims=True)
    return factor * (scaled - first - centred * second)


def two_sums(incoming, centred, carry):
    gains, shifts = carry
    return gains + jnp.sum(incoming * centred, axis=0, keepdims=True), shifts + jnp.sum(incoming, axis=0, keepdims=True)


def no_sums():
    return jnp.zeros((1, D), f32), jnp.zeros((1, D), f32)


EIGHTH = 0.125


def shape(*dims, dtype=bf16):
    return jax.ShapeDtypeStruct(dims, dtype)


class Keep:
    def __init__(self, whole, out, sem, base):
        self.whole, self.out, self.sem, self.base = whole, out, sem, base

    def block(self, s, rows):
        pltpu.make_async_copy(self.whole.at[rows], self.out.at[rows], self.sem.at[self.base + s]).start()

    def wait(self):
        for s in range(8):
            some = pl.ds(0, BLOCK)
            pltpu.make_async_copy(self.whole.at[some], self.out.at[some], self.sem.at[self.base + s]).wait()


def enter(number, layer_input, vectors, weights, query_t, cross_out, beside):
    relay = Relay(layer_input)

    def body(at, ins, outs, kept):
        source, own_vectors, *own_weights, query_own, out_own = ins
        x, vectors, weight, all_rows, qkv, query_all, out_quarter = outs
        normed, whole, query_part, out_part, query_quarter, send, recv, local = kept
        half = at.half(at.n)
        moving = functools.partial(relay_run, relay, at, source, x, send, recv, local.at[0], 11)
        moving(False)
        columns = GatherZ.columns(lax.rem(at.z, 2))
        holds = at.n == lax.div(at.z, 2)
        quarters = []
        for i, (own, part) in enumerate(((query_own, query_part), (out_own, out_part))):
            quarters.append(
                (
                    pltpu.make_async_copy(own.at[:, columns], part, local.at[14 + i]),
                    remote(own.at[:, columns], part, send.at[17 + i], recv.at[17 + i], at.x()),
                )
            )

        @pl.when(holds)
        def _():
            for stay, go in quarters:
                go.start()
                stay.start()

        stay, go = [], []
        for i, (own, target) in enumerate(
            [(own_vectors, vectors.at[:, half])]
            + [(own, weight.at[j * COLS : (j + 1) * COLS, half]) for j, own in enumerate(own_weights)]
        ):
            stay.append(pltpu.make_async_copy(own, target, local.at[1 + i]))
            go.append(remote(own, target, send.at[13 + i], recv.at[13 + i], at.x()))
        stay[0].start()
        go[0].start()

        @pl.when(holds)
        def _():
            for near, far in quarters:
                near.wait()
                far.wait_send()

        @pl.when(jnp.logical_not(holds))
        def _():
            for near, far in quarters:
                far.wait_recv()

        queries = Gather(at, query_part, query_quarter, send, recv, local.at[16], 19)
        outputs = Gather(at, out_part, out_quarter, send, recv, local.at[17], 30)
        queries.begin()
        stay[0].wait()
        go[0].wait_recv()
        moving(True)
        for copy in stay[1:] + go[1:]:
            copy.start()
        queries.pass_on()
        queries.pass_near()

        def norm(rows, carry):
            centred, _ = standard(x[rows].astype(f32))
            normed[rows] = (centred * vectors[0:1] + vectors[1:2]).astype(bf16)

        by_rows(BLOCK, 32, norm)
        gather = Gather(at, normed, whole, send, recv, local.at[5])
        gather.begin()
        queries.pass_far()
        queries.got(4, 7, 8, 9, 10)
        around = GatherZ(at, query_quarter, query_all, send, recv, local.at[18], 41)
        around.begin()
        at.start_beside()
        keep = Keep(whole, all_rows, local, 6)

        def times(rows):
            qkv[rows] = dot_flip(whole[rows], weight[...]).astype(bf16)

        def work(s, rows):
            keep.block(s, rows)

            @pl.when(s == 4)
            def _():
                for copy in stay[1:]:
                    copy.wait()
                for copy in go[1:]:
                    copy.wait_recv()

            @pl.when(s >= 4)
            def _():
                times(rows)

            @pl.when(s == 6)
            def _():
                outputs.begin()
                around.pass_on()

        gather.each(work)
        around.pass_near()
        outputs.pass_on()
        outputs.pass_near()

        def rest(s, carry):
            times(gather.place(s))
            return carry

        lax.fori_loop(0, 4, rest, 0)
        outputs.pass_far()
        around.pass_far()
        outputs.got(4, 7, 8, 9, 10)
        keep.wait()
        for copy in go:
            copy.wait_send()
        outputs.end()
        queries.end()
        around.end()

    return call(
        body,
        number,
        [layer_input, vectors, *weights, query_t, cross_out],
        [
            shape(BLOCK, D),
            shape(8, D, dtype=f32),
            shape(3 * COLS, D),
            shape(D, D),
            shape(D, 3 * COLS),
            shape(D, D),
            shape(D, QUARTER),
        ],
        [
            VMEM((BLOCK, D), bf16),
            VMEM((D, D), bf16),
            VMEM((COLS, QUARTER), bf16),
            VMEM((COLS, QUARTER), bf16),
            VMEM((D, QUARTER), bf16),
            *sems(52),
        ],
        beside,
        lambda at: ring_peers(at) + relay.peers(at) + [("x", at.x())] + GatherZ.peers(at),
        out_spaces=[VMEM, VMEM, VMEM, ANY, VMEM, ANY, VMEM],
        late=True,
    )


def causal_forward(number, joined, down, out_quarter, beside):
    at_once = 512

    def body(at, ins, outs, kept):
        (qkv, block, quarter), (out, logs, all_down, out_all) = ins, outs
        parts, mixed, send, recv, local = kept
        first = Gather(at, block, all_down, send, recv, local.at[0])
        second = GatherZ(at, quarter, out_all, send, recv, local.at[1], 11)
        second.begin()
        first.begin()
        for i in range(3):
            for h in range(HEADS):
                a = i * COLS + h * HDIM
                piece = qkv[:, a : a + HDIM]
                parts[i, h] = piece * EIGHTH if i == 0 else piece
        square = (at_once, at_once)
        seen = lax.broadcasted_iota(jnp.int32, square, 0) >= lax.broadcasted_iota(jnp.int32, square, 1)

        def one(h, carry):
            for i in reversed(range(D // at_once)):
                before, upto = i * at_once, (i + 1) * at_once
                rows = slice(before, upto)
                scores = dot_flip(parts[0, h, rows], parts[1, h, 0:upto])
                last = jnp.where(seen, scores[:, before:], NEGATIVE)
                scores = jnp.concatenate((scores[:, :before], last), axis=1) if i else last
                peak = jnp.max(scores, axis=1, keepdims=True)
                raised = jnp.exp(scores - peak)
                total = jnp.sum(raised, axis=1, keepdims=True)
                mixed[h, rows] = (dot(raised.astype(bf16), parts[2, h, 0:upto]) / total).astype(bf16)
                column = jnp.broadcast_to(peak + jnp.log(total), (at_once, 128))
                logs[pl.ds(h, 1), rows] = column.T[0:1, :]

            @pl.when(h == 1)
            def _():
                first.pass_on()
                second.pass_on()

            return carry

        lax.fori_loop(0, HEADS, one, 0)
        first.pass_near()
        second.pass_near()
        out[...] = jnp.concatenate([mixed[h] for h in range(HEADS)], axis=1)
        first.pass_far()
        second.pass_far()
        first.got(4, 7, 8, 9, 10)
        first.end()
        second.end()

    return call(
        body,
        number,
        [joined, down, out_quarter],
        [shape(D, COLS), shape(8, D, dtype=f32), shape(D, D), shape(D, D)],
        [VMEM((3, HEADS, D, HDIM), bf16), VMEM((HEADS, D, HDIM), bf16), *sems(22)],
        beside,
        lambda at: ring_peers(at) + GatherZ.peers(at),
        out_spaces=[VMEM, VMEM, ANY, ANY],
    )


def forward_rest(number, attended, out_w, x, vectors, query_all, out_all, texts, all_down, expand_w, contract):
    def body(at, ins, outs, kept):
        mixed, out_own, out_got, x, vectors, query_all, out_all, texts, all_down, expand_own, expand_got, contract_own = ins
        middle, after, normed_two, weights, all_rows, activated, grad, contract_out, keys_out, values_out = outs
        *refs, normed, whole, downs, out_full, expand_full, contract_full, key_full, value_full, branch, send, recv, local = kept
        half = at.half(at.n)
        weight = Whole(at, out_own, out_got, out_full, local.at[pl.ds(0, 2)], 1)
        swap = remote(contract_own, contract_full.at[:, half], send.at[21], recv.at[21], at.x())
        swap.start()
        factors = [
            pltpu.make_async_copy(query_all, key_full, local.at[2]),
            pltpu.make_async_copy(out_all, value_full, local.at[3]),
        ]
        for copy in factors:
            copy.start()
        later = [
            pltpu.make_async_copy(contract_own, contract_full.at[:, half], local.at[4]),
            pltpu.make_async_copy(all_down, downs, local.at[7]),
        ]
        for copy in later:
            copy.start()
        later.append(Whole(at, expand_own, expand_got, expand_full, local.at[pl.ds(5, 2)], 0))
        weight.wait()
        scatter = Scatter(at, send, recv, refs)
        scatter.products(lambda rows: dot(mixed[rows], out_full[...]))
        for copy in factors:
            copy.wait()

        def make(b, carry):
            for h in range(HEADS):
                rows = pl.ds(pl.multiple_of(b * BLOCK + h * 64, 64), 64)
                text_keys = texts[b, :, h * HDIM : (h + 1) * HDIM]
                text_values = texts[b, :, COLS + h * HDIM : COLS + (h + 1) * HDIM]
                key_full[rows] = (dot(text_keys, key_full[rows]) * EIGHTH).astype(bf16)
                value_full[rows] = dot(text_values, value_full[rows]).astype(bf16)
            return carry

        lax.fori_loop(0, 8, make, 0)
        made = [
            pltpu.make_async_copy(key_full, keys_out, local.at[8]),
            pltpu.make_async_copy(value_full, values_out, local.at[9]),
        ]
        for copy in made:
            copy.start()
        scatter.middle()
        for copy in later:
            copy.wait()
        scatter.arrive()

        def norm_two(rows, carry):
            total = x[rows].astype(f32) + scatter.total(rows)
            middle[rows] = total
            centred, _ = standard(total)
            normed_two[rows] = (centred * vectors[2:3] + vectors[3:4]).astype(bf16)

        by_rows(BLOCK, 32, norm_two)

        def cross(b, carry):
            rows = pl.ds(pl.multiple_of(b * BLOCK, BLOCK), BLOCK)
            scores = dot_flip(key_full[rows], normed_two[...]).reshape(HEADS, 64, BLOCK)
            raised = jnp.exp(scores - jnp.max(scores, axis=1, keepdims=True))
            p = raised / jnp.sum(raised, axis=1, keepdims=True)
            p = p.reshape(BLOCK, BLOCK).T.astype(bf16)
            weights[b] = p
            part = dot(p, value_full[rows])

            @pl.when(b == 0)
            def _():
                branch[...] = part

            @pl.when(b > 0)
            def _():
                branch[...] += part

            return carry

        lax.fori_loop(0, 8, cross, 0)

        def norm_three(rows, carry):
            total = middle[rows] + branch[rows]
            after[rows] = total
            centred, _ = standard(total)
            normed[rows] = (centred * vectors[4:5] + vectors[5:6]).astype(bf16)

        by_rows(BLOCK, 32, norm_three)
        gather = Gather(at, normed, whole, send, recv, local.at[10], 10)
        gather.begin()
        swap.wait_recv()
        keep_contract = pltpu.make_async_copy(contract_full, contract_out, local.at[11])
        keep_contract.start()
        keep = Keep(whole, all_rows, local, 12)

        def ahead(rows, carry):
            grad[rows] = dot_flip(downs[rows], contract_full[...]).astype(bf16)

        by_rows(D, BLOCK, ahead)

        def work(s, rows):
            keep.block(s, rows)
            hidden = dot(whole[rows], expand_full[...])
            bell = 0.5 * (1.0 + lax.erf(hidden * ROOT_HALF))
            activated[rows] = (hidden * bell).astype(bf16)
            slope = bell + hidden * jnp.exp(-0.5 * hidden * hidden) * GAUSS_NORM
            grad[rows] = (grad[rows].astype(f32) * slope).astype(bf16)

        gather.each(work)
        keep.wait()
        keep_contract.wait()
        for copy in made:
            copy.wait()
        scatter.end()
        swap.wait_send()

    results, _ = call(
        body,
        number,
        [attended, *out_w, x, vectors, query_all, out_all, texts, all_down, *expand_w, contract],
        [
            shape(BLOCK, D, dtype=f32),
            shape(BLOCK, D, dtype=f32),
            shape(BLOCK, D),
            shape(8, BLOCK, BLOCK),
            shape(D, D),
            shape(D, HALF),
            shape(D, HALF),
            shape(HALF, D),
            shape(D, D),
            shape(D, D),
        ],
        [
            *Scatter.scratch,
            VMEM((BLOCK, D), bf16),
            VMEM((D, D), bf16),
            VMEM((D, D), bf16),
            VMEM((COLS, D), bf16),
            VMEM((D, HALF), bf16),
            VMEM((HALF, D), bf16),
            VMEM((D, D), bf16),
            VMEM((D, D), bf16),
            VMEM((BLOCK, D), f32),
            *sems(22),
        ],
        (),
        lambda at: ring_peers(at) + [("x", at.x())],
        spaces=[VMEM, ANY, ANY, VMEM, VMEM, ANY, ANY, VMEM, ANY, ANY, ANY, ANY],
        out_spaces=[VMEM, VMEM, VMEM, VMEM, ANY, VMEM, VMEM, ANY, ANY, ANY],
    )
    return results


def backward_rest(
    number, grad, expand_w, after, middle, vectors, down, keys, values, weights, out_w, contract_sum, expand_sum, beside
):
    def body(at, ins, outs, kept):
        grad, expand_own, expand_got, after, middle, vectors, down, keys, values, weights, out_own, out_got = ins[:12]
        grad_rows, rounded_two, grad_scores, all_two, all_rows, grad_mixed, grad_vectors = outs[:7]
        *refs, rounded, whole, second, out_full, expand_full, key_full, value_full, send, recv, local = kept
        reduces = [
            Reduce(at, ins[12], outs[7], refs[7:11], send, recv, local, 32, 16, False),
            Reduce(at, ins[13], outs[8], refs[11:15], send, recv, local, 42, 18, True, True),
        ]
        refs = refs[:7]
        for reduce in reduces:
            reduce.first()
        weight = Whole(at, expand_own, expand_got, expand_full, local.at[pl.ds(0, 2)], 0)
        later = [
            pltpu.make_async_copy(keys, key_full, local.at[2]),
            pltpu.make_async_copy(values, value_full, local.at[3]),
        ]
        for copy in later:
            copy.start()
        later.append(Whole(at, out_own, out_got, out_full, local.at[pl.ds(4, 2)], 1))
        weight.wait()
        scatter = Scatter(at, send, recv, refs)
        scatter.products(lambda rows: dot_flip(grad[rows], expand_full[...]))
        scatter.middle()
        for copy in later:
            copy.wait()
        scatter.arrive()

        def norm_three(rows, carry):
            incoming = scatter.total(rows)
            centred, factor = standard(after[rows])
            total = down[rows].astype(f32) + norm_back(incoming, centred, factor, vectors[4:5])
            grad_rows[rows] = total
            rounded_two[rows] = total.astype(bf16)
            return two_sums(incoming, centred, carry)

        gains, shifts = by_rows(BLOCK, 32, norm_three, no_sums())
        before = Gather(at, rounded_two, all_two, send, recv, local.at[6], 10)
        before.begin()
        for reduce in reduces:
            reduce.second()
        grad_vectors[4:5] = gains
        grad_vectors[5:6] = shifts

        def cross(b, carry):
            rows = pl.ds(pl.multiple_of(b * BLOCK, BLOCK), BLOCK)
            p = weights[b].astype(f32).T.reshape(HEADS, 64, BLOCK)
            dp = dot_flip(value_full[rows], rounded_two[...]).reshape(HEADS, 64, BLOCK)
            ds = p * (dp - jnp.sum(p * dp, axis=1, keepdims=True))
            ds = ds.reshape(BLOCK, BLOCK).T.astype(bf16)
            grad_scores[b] = ds
            part = dot(ds, key_full[rows])

            @pl.when(b == 0)
            def _():
                second[...] = part

            @pl.when(b > 0)
            def _():
                second[...] += part

            @pl.when(b == 3)
            def _():
                before.pass_on()
                before.pass_near()

            return carry

        lax.fori_loop(0, 8, cross, 0)

        for reduce in reduces:
            reduce.third()

        def norm_two(rows, carry):
            incoming = second[rows]
            centred, factor = standard(middle[rows])
            total = grad_rows[rows] + norm_back(incoming, centred, factor, vectors[2:3])
            grad_rows[rows] = total
            rounded[rows] = total.astype(bf16)
            return two_sums(incoming, centred, carry)

        gains, shifts = by_rows(BLOCK, 32, norm_two, no_sums())
        grad_vectors[2:3] = gains
        grad_vectors[3:4] = shifts
        gather = Gather(at, rounded, whole, send, recv, local.at[7], 21)
        gather.begin()
        for reduce in reduces:
            reduce.fourth()
        before.pass_far()
        keep = Keep(whole, all_rows, local, 8)

        def work(s, rows):
            keep.block(s, rows)
            grad_mixed[rows] = dot_flip(whole[rows], out_full[...]).astype(bf16)

        gather.each(work)
        before.got(4, 7, 8, 9, 10)
        before.end()
        keep.wait()
        scatter.end()
        for reduce in reduces:
            reduce.end()

    return call(
        body,
        number,
        [grad, *expand_w, after, middle, vectors, down, keys, values, weights, *out_w, contract_sum, expand_sum],
        [
            shape(BLOCK, D, dtype=f32),
            shape(BLOCK, D),
            shape(8, BLOCK, BLOCK),
            shape(D, D),
            shape(D, D),
            shape(D, COLS),
            shape(8, D, dtype=f32),
            shape(4, 2, 96, HALF),
            shape(4, 2, 96, HALF),
        ],
        [
            *Scatter.scratch,
            *Reduce.scratch(96, False),
            *Reduce.scratch(96, True, True),
            VMEM((BLOCK, D), bf16),
            VMEM((D, D), bf16),
            VMEM((BLOCK, D), f32),
            VMEM((COLS, D), bf16),
            VMEM((D, HALF), bf16),
            VMEM((D, D), bf16),
            VMEM((D, D), bf16),
            *sems(52),
        ],
        beside,
        lambda at: ring_peers(at) + Reduce.peers(at),
        spaces=[VMEM, ANY, ANY, VMEM, VMEM, VMEM, VMEM, ANY, ANY, VMEM, ANY, ANY, ANY, ANY],
        out_spaces=[VMEM, VMEM, VMEM, ANY, ANY, VMEM, VMEM, ANY, ANY],
    )


def causal_backward(number, joined, grad, logs, activated, contract, after, normed_two, part, beside):
    at_once = 512

    def body(at, ins, outs, kept):
        (qkv, go, log_rows, activated, contract, after, block, part), (out, result, all_rows, summed) = ins, outs
        *refs, parts, key_sum, value_sum, send, recv, local = kept
        reduce = Reduce(at, part, summed, refs[7:], send, recv, local, 21, 1, False)
        reduce.first()
        scatter = Scatter(at, send, recv, refs[:7])
        scatter.products(lambda rows: dot(activated[rows], contract[...]))
        gather = Gather(at, block, all_rows, send, recv, local.at[0], 10)
        for i in range(4):
            for h in range(HEADS):
                a = i * COLS + h * HDIM
                piece = qkv[:, a : a + HDIM] if i < 3 else go[:, h * HDIM : (h + 1) * HDIM]
                parts[i, h] = piece * EIGHTH if i == 0 else piece
        square = (at_once, at_once)
        seen = lax.broadcasted_iota(jnp.int32, square, 1) >= lax.broadcasted_iota(jnp.int32, square, 0)
        blocks = D // at_once

        def one(h, carry):
            turned = parts[1, h].T
            query_parts = []
            for i in reversed(range(blocks)):
                before, upto = i * at_once, (i + 1) * at_once
                rows = slice(before, upto)
                q, g = parts[0, h, rows], parts[3, h, rows]
                k, v = parts[1, h, 0:upto], parts[2, h, 0:upto]
                p = jnp.exp(dot_flip(k, q) - log_rows[pl.ds(h, 1), rows])
                last = jnp.where(seen, p[before:], 0.0)
                p = jnp.concatenate((p[:before], last), axis=0) if i else last
                dp = dot_flip(v, g)
                ds = (p * (dp - jnp.sum(p * dp, axis=0, keepdims=True))).astype(bf16)
                value_part, key_part = dot(p.astype(bf16), g), dot(ds, q)
                if i == blocks - 1:
                    key_sum[0:upto, :] = key_part
                    value_sum[0:upto, :] = value_part
                else:
                    key_sum[0:upto, :] += key_part
                    value_sum[0:upto, :] += value_part
                query_parts.append((dot(turned[:, 0:upto], ds) * EIGHTH).T)
            parts[0, h] = jnp.concatenate(query_parts[::-1], axis=0).astype(bf16)
            parts[1, h] = key_sum[...].astype(bf16)
            parts[2, h] = value_sum[...].astype(bf16)

            @pl.when(h == 0)
            def _():
                scatter.middle()
                gather.begin()
                reduce.second()

            @pl.when(h == 1)
            def _():
                gather.pass_on()
                gather.pass_near()
                reduce.third()

            return carry

        lax.fori_loop(0, HEADS, one, 0)
        reduce.fourth()
        gather.pass_far()
        for i in range(3):
            out[:, i * COLS : (i + 1) * COLS] = jnp.concatenate([parts[i, h] for h in range(HEADS)], axis=1)
        scatter.arrive()

        def finish(rows, carry):
            result[rows] = (after[rows] + scatter.total(rows)).astype(bf16)

        by_rows(BLOCK, 32, finish)
        gather.got(4, 7, 8, 9, 10)
        gather.end()
        scatter.end()
        reduce.end()

    return call(
        body,
        number,
        [joined, grad, logs, activated, contract, after, normed_two, part],
        [shape(D, 3 * COLS), shape(BLOCK, D), shape(D, D), shape(4, 2, 72, HALF)],
        [
            *Scatter.scratch,
            *Reduce.scratch(72, False),
            VMEM((4, HEADS, D, HDIM), bf16),
            VMEM((D, HDIM), f32),
            VMEM((D, HDIM), f32),
            *sems(31),
        ],
        beside,
        lambda at: ring_peers(at) + Reduce.peers(at),
        spaces=[VMEM] * 7 + [ANY],
        out_spaces=[VMEM, VMEM, ANY, ANY],
    )


def leave(number, grad, joined, x, vectors, grad_rows, sums, late, text_part, beside):
    relay = Relay(jax.ShapeDtypeStruct((BLOCK, D), bf16), True)
    some = 64 // 8

    def ring(at):
        return [{"wide": lax.rem(at.w + k, 8)} for k in range(1, 8)]

    def clips(at):
        return [(k, b, {**at.at_dp(k), "narrow": lax.rem(at.n + b, 2)}) for k in range(8) for b in range(2)][1:]

    def group(at):
        return [(b, {"wide": lax.rem(at.w + k, 8), "narrow": lax.rem(at.n + b, 2)}) for k in range(8) for b in range(2)][1:]

    def peers(at):
        known = ring_peers(at) + relay.peers(at) + Reduce.peers(at)
        known += [(f"r{i}", peer) for i, peer in enumerate(ring(at))]
        known += [(f"c{i}", peer) for i, (_, _, peer) in enumerate(clips(at))]
        return known + [(f"g{i}", peer) for i, (_, peer) in enumerate(group(at))]

    def body(at, ins, outs, kept):
        grad, weight, x, vectors, before, late, text, one, two = ins
        result, out_one, out_two, vector_sums, text_out = outs
        refs, kept = kept[:7], kept[7:]
        reduces = [
            Reduce(at, one, out_one, kept[0:4], kept[-3], kept[-2], kept[-1], 12, 1, False),
            Reduce(at, two, out_two, kept[4:8], kept[-3], kept[-2], kept[-1], 22, 3, True),
        ]
        rounded, parts, ring_parts, ring_sum, clip_parts, text_parts, text_sum, send, recv, local = kept[8:]
        me = at.spot(at.y, at.c)

        def move(slot, source, target, peer):
            return remote(source, target, send.at[slot], recv.at[slot], peer)

        to_ring, to_clips, to_group = ring(at), clips(at), group(at)
        slot = 32
        trades = []
        for peer in to_ring:
            there = at.spot(lax.div(peer["wide"], 2), lax.rem(peer["wide"], 2))
            trades.append(move(slot, text.at[there], text_parts.at[me], peer))
            slot += 1
        text_own = pltpu.make_async_copy(text.at[me], text_parts.at[me], local.at[5])
        texts = []
        for b, peer in to_group:
            n = lax.rem(at.n + b, 2)
            texts.append(move(slot, text_sum.at[:, at.half(n)], text_out.at[at.n, me], peer))
            slot += 1
        text_stay = pltpu.make_async_copy(text_sum.at[:, at.half(at.n)], text_out.at[at.n, me], local.at[6])
        rings = []
        for peer in to_ring:
            rings.append(move(slot, parts, ring_parts.at[at.w], peer))
            slot += 1
        ring_own = pltpu.make_async_copy(parts, ring_parts.at[at.w], local.at[7])
        spreads = []
        for _, b, peer in to_clips:
            n = lax.rem(at.n + b, 2)
            spreads.append(move(slot, ring_sum.at[:, at.half(n)], clip_parts.at[at.dp, at.n], peer))
            slot += 1
        clip_own = pltpu.make_async_copy(ring_sum.at[:, at.half(at.n)], clip_parts.at[at.dp, at.n], local.at[8])

        for reduce in reduces:
            reduce.first()
        text_own.start()
        for copy in trades:
            copy.start()
        scatter = Scatter(at, send, recv, refs)
        scatter.products(lambda rows: dot(grad[rows], weight[...]))
        scatter.middle()
        for reduce in reduces:
            reduce.second()
        at.start_beside()
        text_own.wait()
        for copy in trades:
            copy.wait_recv()
        total = text_parts[0].astype(f32)
        for i in range(1, 8):
            total += text_parts[i].astype(f32)
        text_sum[...] = total.astype(bf16)
        text_stay.start()
        for copy in texts:
            copy.start()
        scatter.arrive()

        def norm(rows, carry):
            incoming = scatter.total(rows)
            centred, factor = standard(x[rows].astype(f32))
            total = before[rows] + norm_back(incoming, centred, factor, vectors[0:1])
            rounded[rows] = total.astype(bf16)
            return two_sums(incoming, centred, carry)

        gains, shifts = by_rows(BLOCK, 32, norm, no_sums())
        moving = functools.partial(relay_run, relay, at, rounded, result, send, recv, local.at[0], 10)
        moving(False)
        parts[0:1] = gains
        parts[1:2] = shifts
        parts[2:6] = late[2:6]
        parts[6:8] = jnp.zeros((2, D), f32)
        ring_own.start()
        for copy in rings:
            copy.start()
        for reduce in reduces:
            reduce.third()
        ring_own.wait()
        for copy in rings:
            copy.wait_recv()
        total = ring_parts[0]
        for i in range(1, 8):
            total += ring_parts[i]
        ring_sum[...] = total
        clip_own.start()
        for copy in spreads:
            copy.start()
        for reduce in reduces:
            reduce.fourth()
        clip_own.wait()
        for copy in spreads:
            copy.wait_recv()
        total = clip_parts[0, 0] + clip_parts[0, 1]
        for i in range(1, 8):
            total += clip_parts[i, 0] + clip_parts[i, 1]
        vector_sums[...] = total
        moving(True)
        text_stay.wait()
        for copy in texts:
            copy.wait()
        for copy in trades + rings + spreads:
            copy.wait_send()
        scatter.end()
        for reduce in reduces:
            reduce.end()

    return call(
        body,
        number,
        [grad, joined, x, vectors, grad_rows, late, text_part, *sums],
        [
            shape(384, HALF),
            shape(4, 2, 72, HALF),
            shape(4, 2, 48, HALF),
            shape(8, HALF, dtype=f32),
            shape(2, 8, some, HALF),
        ],
        [
            *Scatter.scratch,
            *Reduce.scratch(72, False),
            *Reduce.scratch(48, True),
            VMEM((BLOCK, D), bf16),
            VMEM((8, D), f32),
            VMEM((8, 8, D), f32),
            VMEM((8, D), f32),
            VMEM((8, 2, 8, HALF), f32),
            VMEM((8, some, D), bf16),
            VMEM((some, D), bf16),
            *sems(32 + 7 + 15 + 7 + 15),
        ],
        beside,
        peers,
        spaces=[VMEM, VMEM, VMEM, VMEM, VMEM, VMEM, ANY, ANY, ANY],
        out_spaces=[ANY, ANY, ANY, VMEM, ANY],
        late=True,
    )


def on_device(
    layer_input,
    text_states,
    cotangent,
    first_gain,
    first_shift,
    query_weight,
    key_weight,
    value_weight,
    output_weight,
    second_gain,
    second_shift,
    cross_query,
    cross_key,
    cross_value,
    cross_output,
    third_gain,
    third_shift,
    expand_weight,
    contract_weight,
):
    vectors = (first_gain, first_shift, second_gain, second_shift, third_gain, third_shift)
    vectors = jnp.concatenate([jnp.stack(vectors).astype(f32), jnp.zeros((2, HALF), f32)], axis=0)
    weights = [query_weight.T, key_weight.T, value_weight.T]
    query_t = cross_query.T
    pair_t = jnp.concatenate((cross_key.T, cross_value.T), axis=0)
    n = lax.axis_index("narrow")

    text_parts = dot_flip(text_states.reshape(128, HALF), pair_t).reshape(2, 64, 2 * COLS)
    results, ((text_pair_got,), (down,), (query_got,), (cross_got,), (text_got,)) = enter(
        1,
        layer_input,
        vectors,
        weights,
        query_t,
        cross_output,
        [GiveClip(text_parts), Relay(cotangent), Give(query_t), Give(cross_output), GiveClip(text_states)],
    )
    x, vectors, joined, all_one, qkv, query_all, out_quarter = results
    text_pair = (lax.dynamic_index_in_dim(text_parts, n, 0, False) + text_pair_got).astype(bf16)
    (attended, logs, all_down, out_all), ((texts,), (out_got,), (expand_got,)) = causal_forward(
        2, qkv, down, out_quarter, [ToSpots(text_pair), Give(output_weight), Give(expand_weight)]
    )
    out_w, expand_w = (output_weight, out_got), (expand_weight, expand_got)
    middle, after, normed_two, cross_p, all_three, activated, grad_expand, contract, all_keys, all_values = forward_rest(
        3, attended, out_w, x, vectors, query_all, out_all, texts, all_down, expand_w, contract_weight
    )

    contract_part = outer(activated, all_down).astype(bf16).reshape(4, 2, 96, D)
    expand_part = outer(all_three, grad_expand).astype(bf16).reshape(2, 4, 2, 96, HALF)
    results, ((cross_p,),) = backward_rest(
        4,
        grad_expand,
        expand_w,
        after,
        middle,
        vectors,
        down,
        all_keys,
        all_values,
        cross_p,
        out_w,
        contract_part,
        expand_part,
        [Trade(cross_p)],
    )
    grad_one, _, grad_scores, all_mid_two, all_mid_one, grad_attended, late, contract_grad, expand_grad = results

    own_first = n == 0

    def whole(own, got):
        return jnp.concatenate((jnp.where(own_first, own, got), jnp.where(own_first, got, own)), axis=1)

    def heads(what, a, b):
        return jnp.einsum(what, a, b, preferred_element_type=f32)

    text = whole(lax.dynamic_index_in_dim(text_states, n, 0, False), text_got)
    text_heads = text_pair.reshape(64, 2, HEADS, HDIM)
    grad_values = outer(cross_p.reshape(D, COLS), all_mid_two).astype(bf16).reshape(HEADS, 64, D)
    heads_out = whole(cross_output, cross_got).reshape(HEADS, HDIM, D)
    grad_text_values = heads("hkf,hdf->khd", grad_values, heads_out).reshape(64, COLS).astype(bf16)
    grad_cross = heads("khd,hkf->hdf", text_heads[:, 1], grad_values).reshape(COLS, D)
    value_part = jnp.concatenate((grad_cross, outer(grad_text_values, text), outer(attended, all_mid_one)), axis=0)
    (grad_qkv, layer_output, all_two, value_grad), ((grad_scores,), (pair_got,)) = causal_backward(
        5,
        qkv,
        grad_attended,
        logs,
        activated,
        contract,
        after,
        normed_two,
        value_part.astype(bf16).reshape(4, 2, 72, D),
        [Trade(grad_scores), Give(pair_t)],
    )

    joined_part = outer(grad_qkv, all_one).astype(bf16).reshape(4, 2, 72, D)
    grad_keys = outer(grad_scores.reshape(D, COLS), all_two).astype(bf16).reshape(HEADS, 64, D)
    heads_query = whole(query_t, query_got).reshape(HEADS, HDIM, D)
    grad_text_keys = (heads("hkf,hdf->khd", grad_keys, heads_query) * EIGHTH).reshape(64, COLS).astype(bf16)
    grad_query = heads("khd,hkf->hdf", text_heads[:, 0], grad_keys).reshape(COLS, D) * EIGHTH
    key_part = jnp.concatenate((grad_query, outer(grad_text_keys, text)), axis=0).astype(bf16).reshape(4, 2, 48, D)
    grad_pair = jnp.concatenate((grad_text_keys, grad_text_values), axis=1)
    text_part = dot(grad_pair, whole(pair_t, pair_got)).astype(bf16).reshape(8, 8, D)

    (input_grad, joined_grad, key_grad, parts, text_grad), ((layer_output,),) = leave(
        6,
        grad_qkv,
        joined,
        x,
        vectors,
        grad_one,
        (joined_part, key_part),
        late,
        text_part,
        [Relay(layer_output, True)],
    )
    joined_grad, key_grad, value_grad, expand_grad, contract_grad = (
        grad.reshape(-1, HALF).astype(f32) for grad in (joined_grad, key_grad, value_grad, expand_grad, contract_grad)
    )
    return (
        layer_output,
        input_grad.astype(f32),
        text_grad.reshape(2, 64, HALF).astype(f32),
        parts[0],
        parts[1],
        joined_grad[:COLS].T,
        joined_grad[COLS : 2 * COLS].T,
        joined_grad[2 * COLS :].T,
        value_grad[2 * COLS :],
        parts[2],
        parts[3],
        key_grad[:COLS].T,
        key_grad[COLS:].T,
        value_grad[COLS : 2 * COLS].T,
        value_grad[:COLS],
        parts[4],
        parts[5],
        expand_grad,
        contract_grad,
    )


def solution(mesh):
    return jax.shard_map(
        on_device,
        mesh=mesh,
        in_specs=(
            P(("dp", "wide"), "narrow"),
            P("dp", None, "narrow"),
            P(("dp", "wide"), "narrow"),
            P("narrow"),
            P("narrow"),
            P("narrow", "wide"),
            P("narrow", "wide"),
            P("narrow", "wide"),
            P("wide", "narrow"),
            P("narrow"),
            P("narrow"),
            P("narrow", "wide"),
            P("narrow", "wide"),
            P("narrow", "wide"),
            P("wide", "narrow"),
            P("narrow"),
            P("narrow"),
            P("narrow", "wide"),
            P("wide", "narrow"),
        ),
        out_specs=(
            P(("dp", "wide"), "narrow"),
            P(("dp", "wide"), "narrow"),
            P("dp", None, "narrow"),
            P("narrow"),
            P("narrow"),
            P("narrow", "wide"),
            P("narrow", "wide"),
            P("narrow", "wide"),
            P("wide", "narrow"),
            P("narrow"),
            P("narrow"),
            P("narrow", "wide"),
            P("narrow", "wide"),
            P("narrow", "wide"),
            P("wide", "narrow"),
            P("narrow"),
            P("narrow"),
            P("narrow", "wide"),
            P("wide", "narrow"),
        ),
        check_vma=False,
    )
```

```python
import functools
import math

import jax
import jax.numpy as jnp
from jax import lax
from jax.experimental import pallas as pl
from jax.experimental.pallas import tpu as pltpu
from jax.sharding import PartitionSpec as P

D = 1536
HALF = 768
HDIM = 64
HEADS = 3
COLS = HEADS * HDIM
BLOCK = 192
EPSILON = 1e-05
NEGATIVE = -1e30
ROOT_HALF = 0.7071067811865476
GAUSS_NORM = 0.3989422804014327
MESH = pl.DeviceIdType.MESH
VMEM = pltpu.VMEM
ANY = pl.ANY
bf16, f32 = jnp.bfloat16, jnp.float32


def dot(a, b):
    return lax.dot_general(a, b, (((1,), (0,)), ((), ())), preferred_element_type=f32)


def dot_flip(a, b):
    return lax.dot_general(a, b, (((1,), (1,)), ((), ())), preferred_element_type=f32)


def outer(a, b):
    return lax.dot_general(a, b, (((0,), (0,)), ((), ())), preferred_element_type=f32)


class Place:
    def __init__(self):
        self.dp, self.w, self.n = (lax.axis_index(a) for a in ("dp", "wide", "narrow"))
        self.y, self.c = lax.div(self.w, 2), lax.rem(self.w, 2)
        self.z, self.s = lax.div(self.dp, 2), lax.rem(self.dp, 2)
        self.up, self.down = lax.rem(self.y + 1, 4), lax.rem(self.y + 3, 4)
        self.across = 3 - self.y
        self.moved = lax.rem(lax.div(self.y, 2) + self.n, 2)
        self.clip = lax.div(self.y, 2)

    def spot(self, y, c):
        moved = lax.rem(lax.div(y, 2) + self.n, 2)
        return (lax.rem(y + moved, 2) * 2 + c) * 2 + moved

    def rows(self, y, c, start=0, size=BLOCK):
        return pl.ds(pl.multiple_of(self.spot(y, c) * BLOCK + start, 32), size)

    def half(self, n):
        return pl.ds(pl.multiple_of(n * HALF, HALF), HALF)

    def at_y(self, y):
        return {"wide": y * 2 + self.c}

    def core(self):
        return {"wide": self.y * 2 + 1 - self.c}

    def x(self):
        return {"narrow": 1 - self.n}

    def at_z(self, k):
        return {"dp": lax.rem(self.z + k, 4) * 2 + self.s}

    def at_dp(self, k):
        return {"dp": lax.rem(self.dp + k, 8)}

    def at_x(self, ds, dn):
        return {"dp": self.z * 2 + lax.rem(self.s + ds, 2), "narrow": lax.rem(self.n + dn, 2)}


def remote(src, dst, send, recv, peer):
    return pltpu.make_async_remote_copy(
        src_ref=src, dst_ref=dst, send_sem=send, recv_sem=recv, device_id=peer, device_id_type=MESH
    )


def greet(peers):
    barrier = pltpu.get_barrier_semaphore()
    for peer in peers:
        pl.semaphore_signal(barrier, inc=1, device_id=peer, device_id_type=MESH)
    pl.semaphore_wait(barrier, len(peers))


class Give:
    def __init__(self, array):
        self.ins, self.copies, self.locals = [array], 1, 0
        self.outs = [jax.ShapeDtypeStruct(array.shape, array.dtype)]

    def peers(self, at):
        return [("x", at.x())]

    def moves(self, at, ins, outs):
        return [(ins[0], outs[0], at.x())], []


class GiveClip(Give):
    def __init__(self, array):
        super().__init__(array)
        self.outs = [jax.ShapeDtypeStruct(array.shape[1:], array.dtype)]

    def moves(self, at, ins, outs):
        return [(ins[0].at[1 - at.n], outs[0], at.x())], []


class Trade:
    def __init__(self, array):
        self.ins, self.copies, self.locals = [array], 7, 1
        self.outs = [jax.ShapeDtypeStruct(array.shape, array.dtype)]

    def others(self, at):
        return [lax.rem(at.w + k, 8) for k in range(1, 8)]

    def peers(self, at):
        return [(f"w{k + 1}", {"wide": w}) for k, w in enumerate(self.others(at))]

    def moves(self, at, ins, outs):
        mine = at.spot(at.y, at.c)
        dst = outs[0].at[mine]
        far = [(ins[0].at[at.spot(lax.div(w, 2), lax.rem(w, 2))], dst, {"wide": w}) for w in self.others(at)]
        return far, [(ins[0].at[mine], dst)]


class ToSpots:
    def __init__(self, array):
        self.ins, self.copies, self.locals = [array], 7, 1
        self.outs = [jax.ShapeDtypeStruct((8, *array.shape), array.dtype)]

    def peers(self, at):
        return [(f"w{k}", {"wide": lax.rem(at.w + k, 8)}) for k in range(1, 8)]

    def moves(self, at, ins, outs):
        dst = outs[0].at[at.spot(at.y, at.c)]
        return [(ins[0], dst, peer) for _, peer in self.peers(at)], [(ins[0], dst)]


class Relay:
    def __init__(self, array, back=False):
        self.ins, self.back, self.copies, self.locals = [array], back, 2, 1
        shape = (384, HALF) if back else (BLOCK, D)
        self.outs = [jax.ShapeDtypeStruct(shape, array.dtype)]

    def peers(self, at):
        return [
            ("x", at.x()),
            ("a0", {"wide": at.across * 2 + at.c}),
            ("a1", {"wide": at.across * 2 + at.c, "narrow": 1 - at.n}),
        ]


def relay_run(relay, at, src, dst, send, recv, local, base, finish):
    mine, other = at.half(at.n), at.half(1 - at.n)
    over = at.across * 2 + at.c
    if relay.back:
        row = pl.ds(pl.multiple_of(at.moved * BLOCK, BLOCK), BLOCK)
        to = recv.at[base + at.moved]
        own = src.at[:, mine], src.at[:, other]
        land = dst.at[0:BLOCK], dst.at[BLOCK : 2 * BLOCK]
    else:
        row = mine
        to = recv.at[base + at.n]
        own = src.at[0:BLOCK], src.at[BLOCK : 2 * BLOCK]
        land = dst.at[:, at.half(0)], dst.at[:, at.half(1)]
    target = dst.at[row] if relay.back else dst.at[:, row]

    def arrive(slot, part):
        return remote(own[0], part, send.at[base], recv.at[base + slot], at.x())

    @pl.when(at.moved == 0)
    def _():
        stay = pltpu.make_async_copy(own[0], target, local)
        if relay.back:
            go = remote(own[1], target, send.at[base], to, at.x())
        else:
            go = remote(own[1], target, send.at[base], to, {"wide": over})
        if not finish:
            go.start()
            stay.start()
        else:
            stay.wait()
            go.wait_send()
            if relay.back:
                arrive(1, land[1]).wait_recv()
            else:
                arrive(1 - at.n, dst.at[:, other]).wait_recv()

    @pl.when(at.moved == 1)
    def _():
        if relay.back:
            first = remote(own[1], target, send.at[base], to, {"wide": over, "narrow": 1 - at.n})
            second = remote(own[0], target, send.at[base + 1], to, {"wide": over})
        else:
            first = remote(own[1], target, send.at[base], to, {"wide": over, "narrow": 1 - at.n})
            second = remote(own[0], target, send.at[base + 1], to, at.x())
        if not finish:
            first.start()
            second.start()
        else:
            first.wait_send()
            second.wait_send()
            arrive(0, land[0]).wait_recv()
            arrive(1, land[1]).wait_recv()


def call(body, number, ins, outs, scratch=(), beside=(), peers=None, spaces=None, out_spaces=None, late=False):
    spaces = spaces or [VMEM] * len(ins)
    out_spaces = out_spaces or [VMEM] * len(outs)
    copies = sum(b.copies for b in beside)
    locals_ = sum(b.locals for b in beside)
    side_ins = [a for b in beside for a in b.ins]
    side_outs = [a for b in beside for a in b.outs]
    n_in, n_out, n_scratch = len(ins), len(outs), len(scratch)

    def kernel(*refs):
        at = Place()
        refs = list(refs)

        def take(count):
            out = refs[:count]
            del refs[:count]
            return out

        main_in, side_in = take(n_in), take(len(side_ins))
        main_out, side_out, kept = take(n_out), take(len(side_outs)), take(n_scratch)
        send, recv, local = take(3)
        known = dict(peers(at)) if peers else {}
        for b in beside:
            known.update(dict(b.peers(at)))
        if known:
            greet(list(known.values()))
        side_refs = [([side_in.pop(0) for _ in b.ins], [side_out.pop(0) for _ in b.outs]) for b in beside]
        begin, todo = [], []
        slot, place = 0, 0
        for b, (i, o) in zip(beside, side_refs):
            if isinstance(b, Relay):
                run = functools.partial(relay_run, b, at, i[0], o[0], send, recv, local.at[place], slot)
                begin.append(functools.partial(run, False))
                todo.append(functools.partial(run, True))
                slot, place = slot + 2, place + 1
                continue
            far, near = b.moves(at, i, o)
            for src, dst, peer in far:
                copy = remote(src, dst, send.at[slot], recv.at[slot], peer)
                begin.append(copy.start)
                todo.append(copy.wait)
                slot += 1
            for src, dst in near:
                copy = pltpu.make_async_copy(src, dst, local.at[place])
                begin.append(copy.start)
                todo.append(copy.wait)
                place += 1

        def start():
            for go in begin:
                go()

        at.start_beside = start
        if not late:
            start()
        if body:
            body(at, main_in, main_out, kept)
        for wait in todo:
            wait()

    results = pl.pallas_call(
        kernel,
        out_shape=tuple(outs) + tuple(side_outs),
        in_specs=[pl.BlockSpec(memory_space=s) for s in spaces] + [pl.BlockSpec(memory_space=ANY)] * len(side_ins),
        out_specs=tuple(pl.BlockSpec(memory_space=m) for m in out_spaces + [ANY] * len(side_outs)),
        scratch_shapes=[
            *scratch,
            pltpu.SemaphoreType.DMA((max(copies, 1),)),
            pltpu.SemaphoreType.DMA((max(copies, 1),)),
            pltpu.SemaphoreType.DMA((max(locals_, 1),)),
        ],
        compiler_params=pltpu.CompilerParams(
            collective_id=number, has_side_effects=True, vmem_limit_bytes=58 << 20
        ),
    )(*ins, *side_ins)
    results = list(results)
    main, rest = results[: len(outs)], results[len(outs) :]
    sides = []
    for b in beside:
        sides.append(rest[: len(b.outs)])
        del rest[: len(b.outs)]
    return main, sides


def ring_peers(at):
    return [("up", at.at_y(at.up)), ("down", at.at_y(at.down)), ("core", at.core())]


def sems(count):
    return [pltpu.SemaphoreType.DMA((count,)), pltpu.SemaphoreType.DMA((count,)), pltpu.SemaphoreType.DMA((count,))]


def by_rows(count, size, work, carry=None):
    def step(i, carry):
        return work(pl.ds(pl.multiple_of(i * size, size), size), carry)

    return lax.fori_loop(0, count // size, step, carry)


class Whole:
    def __init__(self, at, own, got, full, sem, axis):
        size = own.shape[axis]
        self.copies = []
        for i, (part, n) in enumerate(((own, at.n), (got, 1 - at.n))):
            where = pl.ds(pl.multiple_of(n * size, size), size)
            target = full.at[where] if axis == 0 else full.at[:, where]
            self.copies.append(pltpu.make_async_copy(part, target, sem.at[i]))
            self.copies[-1].start()

    def wait(self):
        for copy in self.copies:
            copy.wait()


class Reduce:
    @staticmethod
    def scratch(deep, x_first, by_rows=False):
        first = (4, deep, HALF) if x_first else (2, 2, deep, HALF) if by_rows else (2, deep, D)
        return [VMEM((3, *first), bf16), VMEM(first, bf16), VMEM((3, deep, HALF), bf16), VMEM((2, deep, HALF), bf16)]

    @staticmethod
    def peers(at):
        return [(f"z{k}", at.at_z(k)) for k in (1, 2, 3)] + [(f"x{a}{b}", at.at_x(a, b)) for a, b in ((0, 1), (1, 0), (1, 1))]

    def __init__(self, at, src, out, refs, send, recv, local, base, place, x_first, by_rows=False):
        self.at, self.src, self.out = at, src, out
        self.land, self.total, self.land_two, self.last = refs
        self.x_first, self.by_rows = x_first, by_rows
        self.deep = self.last.shape[1]
        self.chunk = 32 if self.deep % 32 == 0 else 24
        z_steps = [(at.at_z(k), lax.rem(at.z + k, 4)) for k in (1, 2, 3)]
        x_steps = [
            (at.at_x(a, b), (lax.rem(at.s + a, 2), lax.rem(at.n + b, 2))) for a, b in ((0, 1), (1, 0), (1, 1))
        ]
        first, second = (x_steps, z_steps) if x_first else (z_steps, x_steps)

        def move(slot, source, target, peer):
            return remote(source, target, send.at[base + slot], recv.at[base + slot], peer)

        self.one = [move(i, self.piece(where), self.land.at[i], peer) for i, (peer, where) in enumerate(first)]
        self.own = pltpu.make_async_copy(
            self.piece((at.s, at.n) if x_first else at.z), self.total, local.at[place]
        )
        self.two = [move(3 + i, self.part(where), self.land_two.at[i], peer) for i, (peer, where) in enumerate(second)]
        self.mine = at.z if x_first else (at.s, at.n)
        self.three = move(6, self.last.at[at.s], self.last.at[at.s], at.at_x(1, 0))
        target = out.at[at.z]
        self.four = [move(7 + i, self.last, target, peer) for i, (peer, _) in enumerate(z_steps)]
        self.stay = pltpu.make_async_copy(self.last, target, local.at[place + 1])

    def piece(self, where):
        if self.x_first:
            s, n = where
            return self.src.at[n, :, s] if self.by_rows else self.src.at[:, s, :, self.at.half(n)]
        return self.src.at[:, where] if self.by_rows else self.src.at[where]

    def part(self, where):
        if self.x_first:
            return self.total.at[where]
        s, n = where
        return self.total.at[n, s] if self.by_rows else self.total.at[s, :, self.at.half(n)]

    def first(self):
        for copy in self.one + [self.own]:
            copy.start()

    def second(self):
        self.own.wait()
        for copy in self.one:
            copy.wait_recv()
        lead = self.total.shape[:-2]
        count = math.prod(lead)

        def add(i, carry):
            at_lead = (i,) if len(lead) == 1 else (lax.div(i, lead[1]), lax.rem(i, lead[1]))
            for start in range(0, self.deep, self.chunk):
                where = (*at_lead, slice(start, start + self.chunk))
                got = self.total[where].astype(f32)
                for k in range(3):
                    got += self.land[(k, *where)].astype(f32)
                self.total[where] = got.astype(bf16)
            return carry

        lax.fori_loop(0, count, add, 0)
        for copy in self.two:
            copy.start()

    def third(self):
        for copy in self.two:
            copy.wait_recv()
        own = self.part(self.mine)
        s = self.at.s
        for start in range(0, self.deep, self.chunk):
            rows = slice(start, start + self.chunk)
            got = own[rows].astype(f32)
            for k in range(3):
                got += self.land_two[k, rows].astype(f32)
            self.last[s, rows] = got.astype(bf16)
        self.three.start()

    def fourth(self):
        self.three.wait_recv()
        for copy in self.four + [self.stay]:
            copy.start()

    def end(self):
        for copy in self.four:
            copy.wait()
        for copy in self.one + self.two + [self.three]:
            copy.wait_send()
        self.stay.wait()


class Gather:
    slots = 11

    def __init__(self, at, x, whole, send, recv, local, base=0):
        self.at, self.x, self.whole = at, x, whole
        y, c, up, down = at.y, at.c, at.up, at.down
        far = lax.rem(y + 2, 4)
        half = BLOCK // 2

        def move(slot, y_from, peer, start=0, size=BLOCK, first=False):
            rows = at.rows(y_from, c, start, size)
            src = whole.at[rows]
            if first:
                src = x if size == BLOCK else x.at[start : start + size]
            return remote(src, whole.at[rows], send.at[base + slot], recv.at[base + slot], peer)

        to_up, to_down, core = at.at_y(up), at.at_y(down), at.core()
        self.sends = [
            move(0, y, to_up, 0, half, first=True),
            move(1, y, to_up, half, half, first=True),
            move(2, y, to_down, half, half, first=True),
            move(3, y, to_down, 0, half, first=True),
            move(4, y, core, first=True),
            move(5, down, to_up, 0, half),
            move(6, up, to_down, half, half),
            move(7, down, core),
            move(8, up, core),
            move(9, far, core, 0, half),
            move(10, far, core, half, half),
        ]
        self.own = pltpu.make_async_copy(x, whole.at[at.rows(y, c)], local)

    def begin(self):
        for i in (0, 2, 1, 3, 4):
            self.sends[i].start()
        self.own.start()
        self.own.wait()

    def chain(self, *pairs):
        for arrived, leaving in pairs:
            self.sends[arrived].wait_recv()
            self.sends[leaving].start()

    def pass_on(self):
        self.chain((0, 5), (2, 6))

    def pass_near(self):
        self.chain((1, 7), (3, 8))

    def pass_far(self):
        self.chain((5, 9), (6, 10))

    def got(self, *slots):
        for i in slots:
            self.sends[i].wait_recv()

    def end(self):
        for copy in self.sends:
            copy.wait_send()

    def finish(self):
        self.pass_on()
        self.pass_near()
        self.pass_far()
        self.got(4, 7, 8, 9, 10)
        self.end()

    def each(self, work):
        at = self.at

        def step(s, carry):
            @pl.when(s == 1)
            def _():
                self.got(4)
                self.pass_on()

            @pl.when(s == 2)
            def _():
                self.pass_near()

            @pl.when(s == 3)
            def _():
                self.got(8)

            @pl.when(s == 5)
            def _():
                self.got(7)

            @pl.when(s == 6)
            def _():
                self.pass_far()

            @pl.when(s == 7)
            def _():
                self.got(9, 10)

            work(s, self.place(s))
            return carry

        lax.fori_loop(0, 8, step, 0)
        self.end()

    def place(self, s):
        g = lax.div(s, 2)
        off = g + lax.div(g, 2) - 2 * lax.div(g, 3)
        return self.at.rows(lax.rem(self.at.y + off, 4), lax.rem(self.at.c + s, 2))


QUARTER = 384


class GatherZ(Gather):
    def __init__(self, at, quarter, full, send, recv, local, base=0):
        self.at = at
        z, up, down, far = at.z, lax.rem(at.z + 1, 4), lax.rem(at.z + 3, 4), lax.rem(at.z + 2, 4)
        half = QUARTER

        def move(slot, z_from, peer, start=0, size=2 * QUARTER, first=False):
            rows = pl.ds(pl.multiple_of(at.c * 2 * QUARTER + start, QUARTER), size)
            target = full.at[rows, self.columns(z_from)]
            return remote(quarter.at[rows] if first else target, target, send.at[base + slot], recv.at[base + slot], peer)

        to_up, to_down, core = at.at_z(1), at.at_z(3), at.core()
        self.sends = {
            0: move(0, z, to_up, 0, half, first=True),
            1: move(1, z, to_up, half, half, first=True),
            2: move(2, z, to_down, half, half, first=True),
            3: move(3, z, to_down, 0, half, first=True),
            5: move(5, down, to_up, 0, half),
            6: move(6, up, to_down, half, half),
            7: move(7, down, core),
            8: move(8, up, core),
            9: move(9, far, core, 0, half),
            10: move(10, far, core, half, half),
        }
        self.own = pltpu.make_async_copy(quarter, full.at[:, self.columns(z)], local)

    @staticmethod
    def columns(z):
        return pl.ds(pl.multiple_of(z * QUARTER, QUARTER), QUARTER)

    @staticmethod
    def peers(at):
        return [("z1", at.at_z(1)), ("z3", at.at_z(3)), ("core", at.core())]

    def begin(self):
        for i in (0, 2, 1, 3):
            self.sends[i].start()
        self.own.start()

    def end(self):
        self.got(7, 8, 9, 10)
        self.own.wait()
        for copy in self.sends.values():
            copy.wait_send()


class Scatter:
    slots = 10
    scratch = [
        VMEM((4, BLOCK, D), bf16),
        VMEM((4, BLOCK, D), bf16),
        VMEM((4, BLOCK, D), f32),
        VMEM((2, BLOCK, D), bf16),
        VMEM((2, BLOCK, D), bf16),
        VMEM((2, BLOCK // 2, D), bf16),
        VMEM((2, BLOCK // 2, D), bf16),
    ]

    def __init__(self, at, send, recv, refs, base=0):
        self.at, self.send, self.recv, self.base = at, send, recv, base
        self.out_c, self.in_c, self.own, self.out_y, self.in_y, self.half_out, self.half_in = refs
        half = BLOCK // 2
        peers = at.at_y(at.up), at.at_y(at.down)

        def move(slot, src, dst, peer):
            return remote(src, dst, send.at[base + slot], recv.at[base + slot], peer)

        self.cores = [self.core(g) for g in range(4)]
        self.halves = [move(4 + i, self.half_out.at[i], self.half_in.at[i], peers[i]) for i in range(2)]
        free = [pl.ds((1 - i) * half, half) for i in range(2)]
        bound = [pl.ds(i * half, half) for i in range(2)]
        self.free = [move(6 + i, self.out_y.at[i, free[i]], self.in_y.at[i, free[i]], peers[i]) for i in range(2)]
        self.bound = [move(8 + i, self.out_y.at[i, bound[i]], self.in_y.at[i, bound[i]], peers[i]) for i in range(2)]

    def core(self, g):
        slot = self.base + g
        return remote(self.out_c.at[g], self.in_c.at[g], self.send.at[slot], self.recv.at[slot], self.at.core())

    def both(self, g, rows):
        return self.own[g, rows] + self.in_c[g, rows].astype(f32)

    def products(self, product):
        at = self.at
        half = BLOCK // 2

        def part_rows(rows, i):
            return pl.ds(pl.multiple_of(rows.start + i * half, 32), 32)

        def send_free(i):
            self.cores[1 + i].wait_recv()

            def add(rows, carry):
                there = part_rows(rows, 1 - i)
                self.out_y[i, there] = self.both(1 + i, there).astype(bf16)

            by_rows(half, 32, add)
            self.free[i].start()

        def step(s, carry):
            g = lax.div(s, 2)
            off = lax.rem(6 - g + 3 * lax.div(g, 2) + 2 * lax.div(g, 3), 4)
            part = product(at.rows(lax.rem(at.y + off, 4), lax.rem(at.c + 1 + s, 2)))

            @pl.when(lax.rem(s, 2) == 0)
            def _():
                self.out_c[g] = part.astype(bf16)
                self.core(g).start()

            @pl.when(lax.rem(s, 2) == 1)
            def _():
                self.own[g] = part

            @pl.when(s == 2)
            def _():
                self.cores[0].wait_recv()
                for i in range(2):

                    def add(rows, carry, i=i):
                        self.half_out[i, rows] = self.both(0, part_rows(rows, i)).astype(bf16)

                    by_rows(half, 32, add)
                    self.halves[i].start()

            @pl.when(s == 4)
            def _():
                send_free(0)

            @pl.when(s == 6)
            def _():
                send_free(1)

            return carry

        lax.fori_loop(0, 8, step, 0)

    def middle(self):
        half = BLOCK // 2
        for i in range(2):
            self.halves[i].wait_recv()

            def add(rows, carry, i=i):
                here = pl.ds(pl.multiple_of(rows.start + i * half, 32), 32)
                self.out_y[i, here] = (self.both(1 + i, here) + self.half_in[i, rows].astype(f32)).astype(bf16)

            by_rows(half, 32, add)
            self.bound[i].start()

    def arrive(self):
        self.cores[3].wait_recv()
        for copy in self.free + self.bound:
            copy.wait_recv()

    def total(self, rows):
        return self.both(3, rows) + self.in_y[0, rows].astype(f32) + self.in_y[1, rows].astype(f32)

    def end(self):
        for copy in self.cores + self.halves + self.free + self.bound:
            copy.wait_send()


def standard(values):
    average = jnp.mean(values, axis=1, keepdims=True)
    variance = jnp.mean(values * values, axis=1, keepdims=True) - average * average
    factor = lax.rsqrt(variance + EPSILON)
    return (values - average) * factor, factor


def norm_back(incoming, centred, factor, gain):
    scaled = incoming * gain
    first = jnp.mean(scaled, axis=1, keepdims=True)
    second = jnp.mean(scaled * centred, axis=1, keepdims=True)
    return factor * (scaled - first - centred * second)


def two_sums(incoming, centred, carry):
    gains, shifts = carry
    return gains + jnp.sum(incoming * centred, axis=0, keepdims=True), shifts + jnp.sum(incoming, axis=0, keepdims=True)


def no_sums():
    return jnp.zeros((1, D), f32), jnp.zeros((1, D), f32)


EIGHTH = 0.125


def shape(*dims, dtype=bf16):
    return jax.ShapeDtypeStruct(dims, dtype)


class Keep:
    def __init__(self, whole, out, sem, base):
        self.whole, self.out, self.sem, self.base = whole, out, sem, base

    def block(self, s, rows):
        pltpu.make_async_copy(self.whole.at[rows], self.out.at[rows], self.sem.at[self.base + s]).start()

    def wait(self):
        for s in range(8):
            some = pl.ds(0, BLOCK)
            pltpu.make_async_copy(self.whole.at[some], self.out.at[some], self.sem.at[self.base + s]).wait()


def enter(number, layer_input, gains, weights, query_t, cross_out, texts, pair_t, beside):
    relay = Relay(layer_input)

    def body(at, ins, outs, kept):
        source, *gains = ins[:7]
        *own_weights, query_own, out_own, own_texts, pair = ins[7:]
        x, vectors, weight, all_rows, qkv, query_all, out_quarter, text_pair = outs
        normed, whole, query_part, out_part, query_quarter, text_parts, text_got, own_vectors, send, recv, local = kept
        half = at.half(at.n)
        moving = functools.partial(relay_run, relay, at, source, x, send, recv, local.at[0], 11)
        moving(False)
        own_vectors[...] = jnp.zeros_like(own_vectors)
        for i, ref in enumerate(gains):
            own_vectors[i : i + 1] = ref[...].astype(f32).reshape(1, HALF)
        columns = GatherZ.columns(lax.rem(at.z, 2))
        holds = at.n == lax.div(at.z, 2)
        quarters = []
        for i, (own, part) in enumerate(((query_own, query_part), (out_own, out_part))):
            quarters.append(
                (
                    pltpu.make_async_copy(own.at[:, columns], part, local.at[14 + i]),
                    remote(own.at[:, columns], part, send.at[17 + i], recv.at[17 + i], at.x()),
                )
            )

        @pl.when(holds)
        def _():
            for stay, go in quarters:
                go.start()
                stay.start()

        stay, go = [], []
        for i, (own, target) in enumerate(
            [(own_vectors, vectors.at[:, half])]
            + [(own, weight.at[j * COLS : (j + 1) * COLS, half]) for j, own in enumerate(own_weights)]
        ):
            stay.append(pltpu.make_async_copy(own, target, local.at[1 + i]))
            go.append(remote(own, target, send.at[13 + i], recv.at[13 + i], at.x()))
        stay[0].start()
        go[0].start()

        @pl.when(holds)
        def _():
            for near, far in quarters:
                near.wait()
                far.wait_send()

        @pl.when(jnp.logical_not(holds))
        def _():
            for near, far in quarters:
                far.wait_recv()

        for clip in range(2):
            text_parts[clip] = dot_flip(own_texts[clip], pair[...])
        text_go = remote(text_parts.at[1 - at.n], text_got, send.at[52], recv.at[52], at.x())
        text_go.start()
        queries = Gather(at, query_part, query_quarter, send, recv, local.at[16], 19)
        outputs = Gather(at, out_part, out_quarter, send, recv, local.at[17], 30)
        queries.begin()
        stay[0].wait()
        go[0].wait_recv()
        moving(True)
        for copy in stay[1:] + go[1:]:
            copy.start()
        queries.pass_on()
        queries.pass_near()

        def norm(rows, carry):
            centred, _ = standard(x[rows].astype(f32))
            normed[rows] = (centred * vectors[0:1] + vectors[1:2]).astype(bf16)

        by_rows(BLOCK, 32, norm)
        gather = Gather(at, normed, whole, send, recv, local.at[5])
        gather.begin()
        queries.pass_far()
        queries.got(4, 7, 8, 9, 10)
        around = GatherZ(at, query_quarter, query_all, send, recv, local.at[18], 41)
        around.begin()
        keep = Keep(whole, all_rows, local, 6)

        def times(rows):
            qkv[rows] = dot_flip(whole[rows], weight[...]).astype(bf16)

        def work(s, rows):
            keep.block(s, rows)

            @pl.when(s == 4)
            def _():
                for copy in stay[1:]:
                    copy.wait()
                for copy in go[1:]:
                    copy.wait_recv()
                at.start_beside()

            @pl.when(s >= 4)
            def _():
                times(rows)

            @pl.when(s == 6)
            def _():
                outputs.begin()
                around.pass_on()

        gather.each(work)
        around.pass_near()
        outputs.pass_on()
        outputs.pass_near()

        def rest(s, carry):
            times(gather.place(s))
            return carry

        lax.fori_loop(0, 4, rest, 0)
        outputs.pass_far()
        around.pass_far()
        text_go.wait()
        text_pair[...] = (text_parts[at.n] + text_got[...]).astype(bf16)
        outputs.got(4, 7, 8, 9, 10)
        keep.wait()
        for copy in go:
            copy.wait_send()
        outputs.end()
        queries.end()
        around.end()

    return call(
        body,
        number,
        [layer_input, *gains, *weights, query_t, cross_out, texts, pair_t],
        [
            shape(BLOCK, D),
            shape(8, D, dtype=f32),
            shape(3 * COLS, D),
            shape(D, D),
            shape(D, 3 * COLS),
            shape(D, D),
            shape(D, QUARTER),
            shape(64, 2 * COLS),
        ],
        [
            VMEM((BLOCK, D), bf16),
            VMEM((D, D), bf16),
            VMEM((COLS, QUARTER), bf16),
            VMEM((COLS, QUARTER), bf16),
            VMEM((D, QUARTER), bf16),
            VMEM((2, 64, 2 * COLS), f32),
            VMEM((64, 2 * COLS), f32),
            VMEM((8, HALF), f32),
            *sems(53),
        ],
        beside,
        lambda at: ring_peers(at) + relay.peers(at) + [("x", at.x())] + GatherZ.peers(at),
        out_spaces=[VMEM, VMEM, VMEM, ANY, VMEM, ANY, VMEM, VMEM],
        late=True,
    )


def causal_forward(number, joined, down, out_quarter, beside):
    at_once = 512

    def body(at, ins, outs, kept):
        (qkv, block, quarter), (out, logs, all_down, out_all) = ins, outs
        parts, mixed, send, recv, local = kept
        first = Gather(at, block, all_down, send, recv, local.at[0])
        second = GatherZ(at, quarter, out_all, send, recv, local.at[1], 11)
        second.begin()
        first.begin()
        for i in range(3):
            for h in range(HEADS):
                a = i * COLS + h * HDIM
                piece = qkv[:, a : a + HDIM]
                parts[i, h] = piece * EIGHTH if i == 0 else piece
        square = (at_once, at_once)
        seen = lax.broadcasted_iota(jnp.int32, square, 0) >= lax.broadcasted_iota(jnp.int32, square, 1)

        def one(h, carry):
            for i in reversed(range(D // at_once)):
                before, upto = i * at_once, (i + 1) * at_once
                rows = slice(before, upto)
                scores = dot_flip(parts[0, h, rows], parts[1, h, 0:upto])
                last = jnp.where(seen, scores[:, before:], NEGATIVE)
                scores = jnp.concatenate((scores[:, :before], last), axis=1) if i else last
                peak = jnp.max(scores, axis=1, keepdims=True)
                raised = jnp.exp(scores - peak)
                total = jnp.sum(raised, axis=1, keepdims=True)
                mixed[h, rows] = (dot(raised.astype(bf16), parts[2, h, 0:upto]) / total).astype(bf16)
                column = jnp.broadcast_to(peak + jnp.log(total), (at_once, 128))
                logs[pl.ds(h, 1), rows] = column.T[0:1, :]

            @pl.when(h == 1)
            def _():
                first.pass_on()
                second.pass_on()

            return carry

        lax.fori_loop(0, HEADS, one, 0)
        first.pass_near()
        second.pass_near()
        out[...] = jnp.concatenate([mixed[h] for h in range(HEADS)], axis=1)
        first.pass_far()
        second.pass_far()
        first.got(4, 7, 8, 9, 10)
        first.end()
        second.end()

    return call(
        body,
        number,
        [joined, down, out_quarter],
        [shape(D, COLS), shape(8, D, dtype=f32), shape(D, D), shape(D, D)],
        [VMEM((3, HEADS, D, HDIM), bf16), VMEM((HEADS, D, HDIM), bf16), *sems(22)],
        beside,
        lambda at: ring_peers(at) + GatherZ.peers(at),
        out_spaces=[VMEM, VMEM, ANY, ANY],
    )


def forward_rest(number, attended, out_w, x, vectors, query_all, out_all, texts, all_down, expand_w, contract):
    def body(at, ins, outs, kept):
        mixed, out_own, out_got, x, vectors, query_all, out_all, texts, all_down, expand_own, expand_got, contract_own = ins
        middle, after, normed_two, weights, all_rows, activated, grad, contract_out, keys_out, values_out = outs
        *refs, normed, whole, downs, out_full, expand_full, contract_full, key_full, value_full, branch, send, recv, local = kept
        half = at.half(at.n)
        weight = Whole(at, out_own, out_got, out_full, local.at[pl.ds(0, 2)], 1)
        swap = remote(contract_own, contract_full.at[:, half], send.at[21], recv.at[21], at.x())
        swap.start()
        factors = [
            pltpu.make_async_copy(query_all, key_full, local.at[2]),
            pltpu.make_async_copy(out_all, value_full, local.at[3]),
        ]
        for copy in factors:
            copy.start()
        later = [
            pltpu.make_async_copy(contract_own, contract_full.at[:, half], local.at[4]),
            pltpu.make_async_copy(all_down, downs, local.at[7]),
        ]
        for copy in later:
            copy.start()
        later.append(Whole(at, expand_own, expand_got, expand_full, local.at[pl.ds(5, 2)], 0))
        weight.wait()
        scatter = Scatter(at, send, recv, refs)
        scatter.products(lambda rows: dot(mixed[rows], out_full[...]))
        for copy in factors:
            copy.wait()

        def make(b, carry):
            for h in range(HEADS):
                rows = pl.ds(pl.multiple_of(b * BLOCK + h * 64, 64), 64)
                text_keys = texts[b, :, h * HDIM : (h + 1) * HDIM]
                text_values = texts[b, :, COLS + h * HDIM : COLS + (h + 1) * HDIM]
                key_full[rows] = (dot(text_keys, key_full[rows]) * EIGHTH).astype(bf16)
                value_full[rows] = dot(text_values, value_full[rows]).astype(bf16)
            return carry

        lax.fori_loop(0, 8, make, 0)
        made = [
            pltpu.make_async_copy(key_full, keys_out, local.at[8]),
            pltpu.make_async_copy(value_full, values_out, local.at[9]),
        ]
        for copy in made:
            copy.start()
        scatter.middle()
        for copy in later:
            copy.wait()
        scatter.arrive()

        def norm_two(rows, carry):
            total = x[rows].astype(f32) + scatter.total(rows)
            middle[rows] = total
            centred, _ = standard(total)
            normed_two[rows] = (centred * vectors[2:3] + vectors[3:4]).astype(bf16)

        by_rows(BLOCK, 32, norm_two)

        def cross(b, carry):
            rows = pl.ds(pl.multiple_of(b * BLOCK, BLOCK), BLOCK)
            scores = dot_flip(key_full[rows], normed_two[...]).reshape(HEADS, 64, BLOCK)
            raised = jnp.exp(scores - jnp.max(scores, axis=1, keepdims=True))
            p = raised / jnp.sum(raised, axis=1, keepdims=True)
            p = p.reshape(BLOCK, BLOCK).T.astype(bf16)
            weights[b] = p
            part = dot(p, value_full[rows])

            @pl.when(b == 0)
            def _():
                branch[...] = part

            @pl.when(b > 0)
            def _():
                branch[...] += part

            return carry

        lax.fori_loop(0, 8, cross, 0)

        def norm_three(rows, carry):
            total = middle[rows] + branch[rows]
            after[rows] = total
            centred, _ = standard(total)
            normed[rows] = (centred * vectors[4:5] + vectors[5:6]).astype(bf16)

        by_rows(BLOCK, 32, norm_three)
        gather = Gather(at, normed, whole, send, recv, local.at[10], 10)
        gather.begin()
        swap.wait_recv()
        keep_contract = pltpu.make_async_copy(contract_full, contract_out, local.at[11])
        keep_contract.start()
        keep = Keep(whole, all_rows, local, 12)

        def ahead(rows, carry):
            grad[rows] = dot_flip(downs[rows], contract_full[...]).astype(bf16)

        by_rows(D, BLOCK, ahead)

        def work(s, rows):
            keep.block(s, rows)
            hidden = dot(whole[rows], expand_full[...])
            bell = 0.5 * (1.0 + lax.erf(hidden * ROOT_HALF))
            activated[rows] = (hidden * bell).astype(bf16)
            slope = bell + hidden * jnp.exp(-0.5 * hidden * hidden) * GAUSS_NORM
            grad[rows] = (grad[rows].astype(f32) * slope).astype(bf16)

        gather.each(work)
        keep.wait()
        keep_contract.wait()
        for copy in made:
            copy.wait()
        scatter.end()
        swap.wait_send()

    results, _ = call(
        body,
        number,
        [attended, *out_w, x, vectors, query_all, out_all, texts, all_down, *expand_w, contract],
        [
            shape(BLOCK, D, dtype=f32),
            shape(BLOCK, D, dtype=f32),
            shape(BLOCK, D),
            shape(8, BLOCK, BLOCK),
            shape(D, D),
            shape(D, HALF),
            shape(D, HALF),
            shape(HALF, D),
            shape(D, D),
            shape(D, D),
        ],
        [
            *Scatter.scratch,
            VMEM((BLOCK, D), bf16),
            VMEM((D, D), bf16),
            VMEM((D, D), bf16),
            VMEM((COLS, D), bf16),
            VMEM((D, HALF), bf16),
            VMEM((HALF, D), bf16),
            VMEM((D, D), bf16),
            VMEM((D, D), bf16),
            VMEM((BLOCK, D), f32),
            *sems(22),
        ],
        (),
        lambda at: ring_peers(at) + [("x", at.x())],
        spaces=[VMEM, ANY, ANY, VMEM, VMEM, ANY, ANY, VMEM, ANY, ANY, ANY, ANY],
        out_spaces=[VMEM, VMEM, VMEM, VMEM, ANY, VMEM, VMEM, ANY, ANY, ANY],
    )
    return results


def backward_rest(
    number, grad, expand_w, after, middle, vectors, down, keys, values, weights, out_w, contract_sum, expand_sum, beside
):
    def body(at, ins, outs, kept):
        grad, expand_own, expand_got, after, middle, vectors, down, keys, values, weights, out_own, out_got = ins[:12]
        grad_rows, rounded_two, grad_scores, all_two, all_rows, grad_mixed, grad_vectors = outs[:7]
        *refs, rounded, whole, second, out_full, expand_full, key_full, value_full, send, recv, local = kept
        reduces = [
            Reduce(at, ins[12], outs[7], refs[7:11], send, recv, local, 32, 16, False),
            Reduce(at, ins[13], outs[8], refs[11:15], send, recv, local, 42, 18, True, True),
        ]
        refs = refs[:7]
        for reduce in reduces:
            reduce.first()
        weight = Whole(at, expand_own, expand_got, expand_full, local.at[pl.ds(0, 2)], 0)
        later = [
            pltpu.make_async_copy(keys, key_full, local.at[2]),
            pltpu.make_async_copy(values, value_full, local.at[3]),
        ]
        for copy in later:
            copy.start()
        later.append(Whole(at, out_own, out_got, out_full, local.at[pl.ds(4, 2)], 1))
        weight.wait()
        scatter = Scatter(at, send, recv, refs)
        scatter.products(lambda rows: dot_flip(grad[rows], expand_full[...]))
        scatter.middle()
        for copy in later:
            copy.wait()
        scatter.arrive()

        def norm_three(rows, carry):
            incoming = scatter.total(rows)
            centred, factor = standard(after[rows])
            total = down[rows].astype(f32) + norm_back(incoming, centred, factor, vectors[4:5])
            grad_rows[rows] = total
            rounded_two[rows] = total.astype(bf16)
            return two_sums(incoming, centred, carry)

        gains, shifts = by_rows(BLOCK, 32, norm_three, no_sums())
        before = Gather(at, rounded_two, all_two, send, recv, local.at[6], 10)
        before.begin()
        for reduce in reduces:
            reduce.second()
        grad_vectors[4:5] = gains
        grad_vectors[5:6] = shifts

        def cross(b, carry):
            rows = pl.ds(pl.multiple_of(b * BLOCK, BLOCK), BLOCK)
            p = weights[b].astype(f32).T.reshape(HEADS, 64, BLOCK)
            dp = dot_flip(value_full[rows], rounded_two[...]).reshape(HEADS, 64, BLOCK)
            ds = p * (dp - jnp.sum(p * dp, axis=1, keepdims=True))
            ds = ds.reshape(BLOCK, BLOCK).T.astype(bf16)
            grad_scores[b] = ds
            part = dot(ds, key_full[rows])

            @pl.when(b == 0)
            def _():
                second[...] = part

            @pl.when(b > 0)
            def _():
                second[...] += part

            @pl.when(b == 3)
            def _():
                before.pass_on()
                before.pass_near()

            return carry

        lax.fori_loop(0, 8, cross, 0)

        for reduce in reduces:
            reduce.third()

        def norm_two(rows, carry):
            incoming = second[rows]
            centred, factor = standard(middle[rows])
            total = grad_rows[rows] + norm_back(incoming, centred, factor, vectors[2:3])
            grad_rows[rows] = total
            rounded[rows] = total.astype(bf16)
            return two_sums(incoming, centred, carry)

        gains, shifts = by_rows(BLOCK, 32, norm_two, no_sums())
        grad_vectors[2:3] = gains
        grad_vectors[3:4] = shifts
        gather = Gather(at, rounded, whole, send, recv, local.at[7], 21)
        gather.begin()
        for reduce in reduces:
            reduce.fourth()
        before.pass_far()
        keep = Keep(whole, all_rows, local, 8)

        def work(s, rows):
            keep.block(s, rows)
            grad_mixed[rows] = dot_flip(whole[rows], out_full[...]).astype(bf16)

        gather.each(work)
        before.got(4, 7, 8, 9, 10)
        before.end()
        keep.wait()
        scatter.end()
        for reduce in reduces:
            reduce.end()

    return call(
        body,
        number,
        [grad, *expand_w, after, middle, vectors, down, keys, values, weights, *out_w, contract_sum, expand_sum],
        [
            shape(BLOCK, D, dtype=f32),
            shape(BLOCK, D),
            shape(8, BLOCK, BLOCK),
            shape(D, D),
            shape(D, D),
            shape(D, COLS),
            shape(8, D, dtype=f32),
            shape(4, 2, 96, HALF),
            shape(4, 2, 96, HALF),
        ],
        [
            *Scatter.scratch,
            *Reduce.scratch(96, False),
            *Reduce.scratch(96, True, True),
            VMEM((BLOCK, D), bf16),
            VMEM((D, D), bf16),
            VMEM((BLOCK, D), f32),
            VMEM((COLS, D), bf16),
            VMEM((D, HALF), bf16),
            VMEM((D, D), bf16),
            VMEM((D, D), bf16),
            *sems(52),
        ],
        beside,
        lambda at: ring_peers(at) + Reduce.peers(at),
        spaces=[VMEM, ANY, ANY, VMEM, VMEM, VMEM, VMEM, ANY, ANY, VMEM, ANY, ANY, ANY, ANY],
        out_spaces=[VMEM, VMEM, VMEM, ANY, ANY, VMEM, VMEM, ANY, ANY],
    )


def causal_backward(number, joined, grad, logs, activated, contract, after, normed_two, part, beside):
    at_once = 512

    def body(at, ins, outs, kept):
        (qkv, go, log_rows, activated, contract, after, block, part), (out, result, all_rows, summed) = ins, outs
        *refs, parts, key_sum, value_sum, send, recv, local = kept
        reduce = Reduce(at, part, summed, refs[7:], send, recv, local, 21, 1, False)
        reduce.first()
        gather = Gather(at, block, all_rows, send, recv, local.at[0], 10)
        gather.begin()
        scatter = Scatter(at, send, recv, refs[:7])
        scatter.products(lambda rows: dot(activated[rows], contract[...]))
        gather.pass_on()
        for i in range(4):
            for h in range(HEADS):
                a = i * COLS + h * HDIM
                piece = qkv[:, a : a + HDIM] if i < 3 else go[:, h * HDIM : (h + 1) * HDIM]
                parts[i, h] = piece * EIGHTH if i == 0 else piece
        square = (at_once, at_once)
        seen = lax.broadcasted_iota(jnp.int32, square, 1) >= lax.broadcasted_iota(jnp.int32, square, 0)
        blocks = D // at_once

        def one(h, carry):
            turned = parts[1, h].T
            query_parts = []
            for i in reversed(range(blocks)):
                before, upto = i * at_once, (i + 1) * at_once
                rows = slice(before, upto)
                q, g = parts[0, h, rows], parts[3, h, rows]
                k, v = parts[1, h, 0:upto], parts[2, h, 0:upto]
                p = jnp.exp(dot_flip(k, q) - log_rows[pl.ds(h, 1), rows])
                last = jnp.where(seen, p[before:], 0.0)
                p = jnp.concatenate((p[:before], last), axis=0) if i else last
                dp = dot_flip(v, g)
                ds = (p * (dp - jnp.sum(p * dp, axis=0, keepdims=True))).astype(bf16)
                value_part, key_part = dot(p.astype(bf16), g), dot(ds, q)
                if i == blocks - 1:
                    key_sum[0:upto, :] = key_part
                    value_sum[0:upto, :] = value_part
                else:
                    key_sum[0:upto, :] += key_part
                    value_sum[0:upto, :] += value_part
                query_parts.append((dot(turned[:, 0:upto], ds) * EIGHTH).T)
                if i == blocks - 1:

                    @pl.when(h == 1)
                    def _():
                        reduce.second()

                    @pl.when(h == 2)
                    def _():
                        reduce.fourth()

            parts[0, h] = jnp.concatenate(query_parts[::-1], axis=0).astype(bf16)
            parts[1, h] = key_sum[...].astype(bf16)
            parts[2, h] = value_sum[...].astype(bf16)

            @pl.when(h == 0)
            def _():
                gather.pass_near()

            @pl.when(h == 1)
            def _():
                scatter.middle()
                gather.pass_far()
                reduce.third()

            return carry

        lax.fori_loop(0, HEADS, one, 0)
        for i in range(3):
            out[:, i * COLS : (i + 1) * COLS] = jnp.concatenate([parts[i, h] for h in range(HEADS)], axis=1)
        scatter.arrive()

        def finish(rows, carry):
            result[rows] = (after[rows] + scatter.total(rows)).astype(bf16)

        by_rows(BLOCK, 32, finish)
        gather.got(4, 7, 8, 9, 10)
        gather.end()
        scatter.end()
        reduce.end()

    return call(
        body,
        number,
        [joined, grad, logs, activated, contract, after, normed_two, part],
        [shape(D, 3 * COLS), shape(BLOCK, D), shape(D, D), shape(4, 2, 72, HALF)],
        [
            *Scatter.scratch,
            *Reduce.scratch(72, False),
            VMEM((4, HEADS, D, HDIM), bf16),
            VMEM((D, HDIM), f32),
            VMEM((D, HDIM), f32),
            *sems(31),
        ],
        beside,
        lambda at: ring_peers(at) + Reduce.peers(at),
        spaces=[VMEM] * 7 + [ANY],
        out_spaces=[VMEM, VMEM, ANY, ANY],
    )


def leave(number, grad, joined, x, vectors, grad_rows, sums, late, text_part, beside):
    relay = Relay(jax.ShapeDtypeStruct((BLOCK, D), bf16), True)
    some = 64 // 8

    def ring(at):
        return [{"wide": lax.rem(at.w + k, 8)} for k in range(1, 8)]

    def clips(at):
        return [(k, b, {**at.at_dp(k), "narrow": lax.rem(at.n + b, 2)}) for k in range(8) for b in range(2)][1:]

    def group(at):
        return [(b, {"wide": lax.rem(at.w + k, 8), "narrow": lax.rem(at.n + b, 2)}) for k in range(8) for b in range(2)][1:]

    def peers(at):
        known = ring_peers(at) + relay.peers(at) + Reduce.peers(at)
        known += [(f"r{i}", peer) for i, peer in enumerate(ring(at))]
        known += [(f"c{i}", peer) for i, (_, _, peer) in enumerate(clips(at))]
        return known + [(f"g{i}", peer) for i, (_, peer) in enumerate(group(at))]

    def body(at, ins, outs, kept):
        grad, weight, x, vectors, before, late, text, one, two = ins
        result, out_one, out_two, vector_sums, text_out = outs
        refs, kept = kept[:7], kept[7:]
        reduces = [
            Reduce(at, one, out_one, kept[0:4], kept[-3], kept[-2], kept[-1], 12, 1, False),
            Reduce(at, two, out_two, kept[4:8], kept[-3], kept[-2], kept[-1], 22, 3, True),
        ]
        rounded, parts, ring_parts, ring_sum, clip_parts, text_parts, text_sum, send, recv, local = kept[8:]
        me = at.spot(at.y, at.c)

        def move(slot, source, target, peer):
            return remote(source, target, send.at[slot], recv.at[slot], peer)

        to_ring, to_clips, to_group = ring(at), clips(at), group(at)
        slot = 32
        trades = []
        for peer in to_ring:
            there = at.spot(lax.div(peer["wide"], 2), lax.rem(peer["wide"], 2))
            trades.append(move(slot, text.at[there], text_parts.at[me], peer))
            slot += 1
        text_own = pltpu.make_async_copy(text.at[me], text_parts.at[me], local.at[5])
        texts = []
        for b, peer in to_group:
            n = lax.rem(at.n + b, 2)
            texts.append(move(slot, text_sum.at[:, at.half(n)], text_out.at[at.n, me], peer))
            slot += 1
        text_stay = pltpu.make_async_copy(text_sum.at[:, at.half(at.n)], text_out.at[at.n, me], local.at[6])
        rings = []
        for peer in to_ring:
            rings.append(move(slot, parts, ring_parts.at[at.w], peer))
            slot += 1
        ring_own = pltpu.make_async_copy(parts, ring_parts.at[at.w], local.at[7])
        spreads = []
        for _, b, peer in to_clips:
            n = lax.rem(at.n + b, 2)
            spreads.append(move(slot, ring_sum.at[:, at.half(n)], clip_parts.at[at.dp, at.n], peer))
            slot += 1
        clip_own = pltpu.make_async_copy(ring_sum.at[:, at.half(at.n)], clip_parts.at[at.dp, at.n], local.at[8])

        for reduce in reduces:
            reduce.first()
        text_own.start()
        for copy in trades:
            copy.start()
        scatter = Scatter(at, send, recv, refs)
        scatter.products(lambda rows: dot(grad[rows], weight[...]))
        at.start_beside()
        scatter.middle()
        for reduce in reduces:
            reduce.second()
        text_own.wait()
        for copy in trades:
            copy.wait_recv()
        total = text_parts[0].astype(f32)
        for i in range(1, 8):
            total += text_parts[i].astype(f32)
        text_sum[...] = total.astype(bf16)
        text_stay.start()
        for copy in texts:
            copy.start()
        scatter.arrive()

        def norm(rows, carry):
            incoming = scatter.total(rows)
            centred, factor = standard(x[rows].astype(f32))
            total = before[rows] + norm_back(incoming, centred, factor, vectors[0:1])
            rounded[rows] = total.astype(bf16)
            return two_sums(incoming, centred, carry)

        gains, shifts = by_rows(BLOCK, 32, norm, no_sums())
        moving = functools.partial(relay_run, relay, at, rounded, result, send, recv, local.at[0], 10)
        moving(False)
        parts[0:1] = gains
        parts[1:2] = shifts
        parts[2:6] = late[2:6]
        parts[6:8] = jnp.zeros((2, D), f32)
        ring_own.start()
        for copy in rings:
            copy.start()
        for reduce in reduces:
            reduce.third()
        ring_own.wait()
        for copy in rings:
            copy.wait_recv()
        total = ring_parts[0]
        for i in range(1, 8):
            total += ring_parts[i]
        ring_sum[...] = total
        clip_own.start()
        for copy in spreads:
            copy.start()
        for reduce in reduces:
            reduce.fourth()
        clip_own.wait()
        for copy in spreads:
            copy.wait_recv()
        total = clip_parts[0, 0] + clip_parts[0, 1]
        for i in range(1, 8):
            total += clip_parts[i, 0] + clip_parts[i, 1]
        vector_sums[...] = total
        moving(True)
        text_stay.wait()
        for copy in texts:
            copy.wait()
        for copy in trades + rings + spreads:
            copy.wait_send()
        scatter.end()
        for reduce in reduces:
            reduce.end()

    return call(
        body,
        number,
        [grad, joined, x, vectors, grad_rows, late, text_part, *sums],
        [
            shape(384, HALF),
            shape(4, 2, 72, HALF),
            shape(4, 2, 48, HALF),
            shape(8, HALF, dtype=f32),
            shape(2, 8, some, HALF),
        ],
        [
            *Scatter.scratch,
            *Reduce.scratch(72, False),
            *Reduce.scratch(48, True),
            VMEM((BLOCK, D), bf16),
            VMEM((8, D), f32),
            VMEM((8, 8, D), f32),
            VMEM((8, D), f32),
            VMEM((8, 2, 8, HALF), f32),
            VMEM((8, some, D), bf16),
            VMEM((some, D), bf16),
            *sems(32 + 7 + 15 + 7 + 15),
        ],
        beside,
        peers,
        spaces=[VMEM, VMEM, VMEM, VMEM, VMEM, VMEM, ANY, ANY, ANY],
        out_spaces=[ANY, ANY, ANY, VMEM, ANY],
        late=True,
    )


def on_device(
    layer_input,
    text_states,
    cotangent,
    first_gain,
    first_shift,
    query_weight,
    key_weight,
    value_weight,
    output_weight,
    second_gain,
    second_shift,
    cross_query,
    cross_key,
    cross_value,
    cross_output,
    third_gain,
    third_shift,
    expand_weight,
    contract_weight,
):
    gains = (first_gain, first_shift, second_gain, second_shift, third_gain, third_shift)
    weights = [query_weight.T, key_weight.T, value_weight.T]
    query_t = cross_query.T
    pair_t = jnp.concatenate((cross_key.T, cross_value.T), axis=0)
    n = lax.axis_index("narrow")

    results, ((down,), (text_got,)) = enter(
        1,
        layer_input,
        gains,
        weights,
        query_t,
        cross_output,
        text_states,
        pair_t,
        [Relay(cotangent), GiveClip(text_states)],
    )
    x, vectors, joined, all_one, qkv, query_all, out_quarter, text_pair = results
    (attended, logs, all_down, out_all), ((texts,), (out_got,), (expand_got,)) = causal_forward(
        2, qkv, down, out_quarter, [ToSpots(text_pair), Give(output_weight), Give(expand_weight)]
    )
    out_w, expand_w = (output_weight, out_got), (expand_weight, expand_got)
    middle, after, normed_two, cross_p, all_three, activated, grad_expand, contract, all_keys, all_values = forward_rest(
        3, attended, out_w, x, vectors, query_all, out_all, texts, all_down, expand_w, contract_weight
    )

    contract_part = outer(activated, all_down).astype(bf16).reshape(4, 2, 96, D)
    expand_part = outer(all_three, grad_expand).astype(bf16).reshape(2, 4, 2, 96, HALF)
    results, ((cross_p,), (query_got,), (cross_got,)) = backward_rest(
        4,
        grad_expand,
        expand_w,
        after,
        middle,
        vectors,
        down,
        all_keys,
        all_values,
        cross_p,
        out_w,
        contract_part,
        expand_part,
        [Trade(cross_p), Give(query_t), Give(cross_output)],
    )
    grad_one, _, grad_scores, all_mid_two, all_mid_one, grad_attended, late, contract_grad, expand_grad = results

    own_first = n == 0

    def whole(own, got):
        return jnp.concatenate((jnp.where(own_first, own, got), jnp.where(own_first, got, own)), axis=1)

    def heads(what, a, b):
        return jnp.einsum(what, a, b, preferred_element_type=f32)

    text = whole(lax.dynamic_index_in_dim(text_states, n, 0, False), text_got)
    text_heads = text_pair.reshape(64, 2, HEADS, HDIM)
    grad_values = outer(cross_p.reshape(D, COLS), all_mid_two).astype(bf16).reshape(HEADS, 64, D)
    heads_out = whole(cross_output, cross_got).reshape(HEADS, HDIM, D)
    grad_text_values = heads("hkf,hdf->khd", grad_values, heads_out).reshape(64, COLS).astype(bf16)
    grad_cross = heads("khd,hkf->hdf", text_heads[:, 1], grad_values).reshape(COLS, D)
    value_part = jnp.concatenate((grad_cross, outer(grad_text_values, text), outer(attended, all_mid_one)), axis=0)
    (grad_qkv, layer_output, all_two, value_grad), ((grad_scores,), (pair_got,)) = causal_backward(
        5,
        qkv,
        grad_attended,
        logs,
        activated,
        contract,
        after,
        normed_two,
        value_part.astype(bf16).reshape(4, 2, 72, D),
        [Trade(grad_scores), Give(pair_t)],
    )

    joined_part = outer(grad_qkv, all_one).astype(bf16).reshape(4, 2, 72, D)
    grad_keys = outer(grad_scores.reshape(D, COLS), all_two).astype(bf16).reshape(HEADS, 64, D)
    heads_query = whole(query_t, query_got).reshape(HEADS, HDIM, D)
    grad_text_keys = (heads("hkf,hdf->khd", grad_keys, heads_query) * EIGHTH).reshape(64, COLS).astype(bf16)
    grad_query = heads("khd,hkf->hdf", text_heads[:, 0], grad_keys).reshape(COLS, D) * EIGHTH
    key_part = jnp.concatenate((grad_query, outer(grad_text_keys, text)), axis=0).astype(bf16).reshape(4, 2, 48, D)
    grad_pair = jnp.concatenate((grad_text_keys, grad_text_values), axis=1)
    text_part = dot(grad_pair, whole(pair_t, pair_got)).astype(bf16).reshape(8, 8, D)

    (input_grad, joined_grad, key_grad, parts, text_grad), ((layer_output,),) = leave(
        6,
        grad_qkv,
        joined,
        x,
        vectors,
        grad_one,
        (joined_part, key_part),
        late,
        text_part,
        [Relay(layer_output, True)],
    )
    joined_grad, key_grad, value_grad, expand_grad, contract_grad = (
        grad.reshape(-1, HALF).astype(f32) for grad in (joined_grad, key_grad, value_grad, expand_grad, contract_grad)
    )
    return (
        layer_output,
        input_grad.astype(f32),
        text_grad.reshape(2, 64, HALF).astype(f32),
        parts[0],
        parts[1],
        joined_grad[:COLS].T,
        joined_grad[COLS : 2 * COLS].T,
        joined_grad[2 * COLS :].T,
        value_grad[2 * COLS :],
        parts[2],
        parts[3],
        key_grad[:COLS].T,
        key_grad[COLS:].T,
        value_grad[COLS : 2 * COLS].T,
        value_grad[:COLS],
        parts[4],
        parts[5],
        expand_grad,
        contract_grad,
    )


def solution(mesh):
    return jax.shard_map(
        on_device,
        mesh=mesh,
        in_specs=(
            P(("dp", "wide"), "narrow"),
            P("dp", None, "narrow"),
            P(("dp", "wide"), "narrow"),
            P("narrow"),
            P("narrow"),
            P("narrow", "wide"),
            P("narrow", "wide"),
            P("narrow", "wide"),
            P("wide", "narrow"),
            P("narrow"),
            P("narrow"),
            P("narrow", "wide"),
            P("narrow", "wide"),
            P("narrow", "wide"),
            P("wide", "narrow"),
            P("narrow"),
            P("narrow"),
            P("narrow", "wide"),
            P("wide", "narrow"),
        ),
        out_specs=(
            P(("dp", "wide"), "narrow"),
            P(("dp", "wide"), "narrow"),
            P("dp", None, "narrow"),
            P("narrow"),
            P("narrow"),
            P("narrow", "wide"),
            P("narrow", "wide"),
            P("narrow", "wide"),
            P("wide", "narrow"),
            P("narrow"),
            P("narrow"),
            P("narrow", "wide"),
            P("narrow", "wide"),
            P("narrow", "wide"),
            P("wide", "narrow"),
            P("narrow"),
            P("narrow"),
            P("narrow", "wide"),
            P("wide", "narrow"),
        ),
        check_vma=False,
    )
```

```python
import functools
import math

import jax
import jax.numpy as jnp
from jax import lax
from jax.experimental import pallas as pl
from jax.experimental.pallas import tpu as pltpu
from jax.sharding import PartitionSpec as P

D = 1536
HALF = 768
HDIM = 64
HEADS = 3
COLS = HEADS * HDIM
BLOCK = 192
EPSILON = 1e-05
NEGATIVE = -1e30
ROOT_HALF = 0.7071067811865476
GAUSS_NORM = 0.3989422804014327
MESH = pl.DeviceIdType.MESH
VMEM = pltpu.VMEM
ANY = pl.ANY
bf16, f32 = jnp.bfloat16, jnp.float32


def dot(a, b):
    return lax.dot_general(a, b, (((1,), (0,)), ((), ())), preferred_element_type=f32)


def dot_flip(a, b):
    return lax.dot_general(a, b, (((1,), (1,)), ((), ())), preferred_element_type=f32)


def outer(a, b):
    return lax.dot_general(a, b, (((0,), (0,)), ((), ())), preferred_element_type=f32)


class Place:
    def __init__(self):
        self.dp, self.w, self.n = (lax.axis_index(a) for a in ("dp", "wide", "narrow"))
        self.y, self.c = lax.div(self.w, 2), lax.rem(self.w, 2)
        self.z, self.s = lax.div(self.dp, 2), lax.rem(self.dp, 2)
        self.up, self.down = lax.rem(self.y + 1, 4), lax.rem(self.y + 3, 4)
        self.across = 3 - self.y
        self.moved = lax.rem(lax.div(self.y, 2) + self.n, 2)
        self.clip = lax.div(self.y, 2)

    def spot(self, y, c):
        moved = lax.rem(lax.div(y, 2) + self.n, 2)
        return (lax.rem(y + moved, 2) * 2 + c) * 2 + moved

    def rows(self, y, c, start=0, size=BLOCK):
        return pl.ds(pl.multiple_of(self.spot(y, c) * BLOCK + start, 32), size)

    def half(self, n):
        return pl.ds(pl.multiple_of(n * HALF, HALF), HALF)

    def at_y(self, y):
        return {"wide": y * 2 + self.c}

    def core(self):
        return {"wide": self.y * 2 + 1 - self.c}

    def x(self):
        return {"narrow": 1 - self.n}

    def at_z(self, k):
        return {"dp": lax.rem(self.z + k, 4) * 2 + self.s}

    def at_dp(self, k):
        return {"dp": lax.rem(self.dp + k, 8)}

    def at_x(self, ds, dn):
        return {"dp": self.z * 2 + lax.rem(self.s + ds, 2), "narrow": lax.rem(self.n + dn, 2)}


def remote(src, dst, send, recv, peer):
    return pltpu.make_async_remote_copy(
        src_ref=src, dst_ref=dst, send_sem=send, recv_sem=recv, device_id=peer, device_id_type=MESH
    )


def greet(peers):
    barrier = pltpu.get_barrier_semaphore()
    for peer in peers:
        pl.semaphore_signal(barrier, inc=1, device_id=peer, device_id_type=MESH)
    pl.semaphore_wait(barrier, len(peers))


class Give:
    def __init__(self, array):
        self.ins, self.copies, self.locals = [array], 1, 0
        self.outs = [jax.ShapeDtypeStruct(array.shape, array.dtype)]

    def peers(self, at):
        return [("x", at.x())]

    def moves(self, at, ins, outs):
        return [(ins[0], outs[0], at.x())], []


class GiveClip(Give):
    def __init__(self, array):
        super().__init__(array)
        self.outs = [jax.ShapeDtypeStruct(array.shape[1:], array.dtype)]

    def moves(self, at, ins, outs):
        return [(ins[0].at[1 - at.n], outs[0], at.x())], []


class Trade:
    def __init__(self, array):
        self.ins, self.copies, self.locals = [array], 7, 1
        self.outs = [jax.ShapeDtypeStruct(array.shape, array.dtype)]

    def others(self, at):
        return [lax.rem(at.w + k, 8) for k in range(1, 8)]

    def peers(self, at):
        return [(f"w{k}", {"wide": w}) for k, w in enumerate(self.others(at), 1)]

    def moves(self, at, ins, outs):
        mine = at.spot(at.y, at.c)
        dst = outs[0].at[mine]
        far = [(ins[0].at[at.spot(lax.div(w, 2), lax.rem(w, 2))], dst, {"wide": w}) for w in self.others(at)]
        return far, [(ins[0].at[mine], dst)]


class ToSpots:
    def __init__(self, array):
        self.ins, self.copies, self.locals = [array], 7, 1
        self.outs = [jax.ShapeDtypeStruct((8, *array.shape), array.dtype)]

    def peers(self, at):
        return [(f"w{k}", {"wide": lax.rem(at.w + k, 8)}) for k in range(1, 8)]

    def moves(self, at, ins, outs):
        dst = outs[0].at[at.spot(at.y, at.c)]
        return [(ins[0], dst, peer) for _, peer in self.peers(at)], [(ins[0], dst)]


class Relay:
    def __init__(self, array, back=False):
        self.ins, self.back, self.copies, self.locals = [array], back, 2, 1
        shape = (384, HALF) if back else (BLOCK, D)
        self.outs = [jax.ShapeDtypeStruct(shape, array.dtype)]

    def peers(self, at):
        return [
            ("x", at.x()),
            ("a0", {"wide": at.across * 2 + at.c}),
            ("a1", {"wide": at.across * 2 + at.c, "narrow": 1 - at.n}),
        ]


def relay_run(relay, at, src, dst, send, recv, local, base, finish):
    mine, other = at.half(at.n), at.half(1 - at.n)
    over = at.across * 2 + at.c
    if relay.back:
        row = pl.ds(pl.multiple_of(at.moved * BLOCK, BLOCK), BLOCK)
        to = recv.at[base + at.moved]
        own = src.at[:, mine], src.at[:, other]
        land = dst.at[0:BLOCK], dst.at[BLOCK : 2 * BLOCK]
    else:
        row = mine
        to = recv.at[base + at.n]
        own = src.at[0:BLOCK], src.at[BLOCK : 2 * BLOCK]
        land = dst.at[:, at.half(0)], dst.at[:, at.half(1)]
    target = dst.at[row] if relay.back else dst.at[:, row]

    def arrive(slot, part):
        return remote(own[0], part, send.at[base], recv.at[base + slot], at.x())

    @pl.when(at.moved == 0)
    def _():
        stay = pltpu.make_async_copy(own[0], target, local)
        if relay.back:
            go = remote(own[1], target, send.at[base], to, at.x())
        else:
            go = remote(own[1], target, send.at[base], to, {"wide": over})
        if not finish:
            go.start()
            stay.start()
        else:
            stay.wait()
            go.wait_send()
            if relay.back:
                arrive(1, land[1]).wait_recv()
            else:
                arrive(1 - at.n, dst.at[:, other]).wait_recv()

    @pl.when(at.moved == 1)
    def _():
        if relay.back:
            first = remote(own[1], target, send.at[base], to, {"wide": over, "narrow": 1 - at.n})
            second = remote(own[0], target, send.at[base + 1], to, {"wide": over})
        else:
            first = remote(own[1], target, send.at[base], to, {"wide": over, "narrow": 1 - at.n})
            second = remote(own[0], target, send.at[base + 1], to, at.x())
        if not finish:
            first.start()
            second.start()
        else:
            first.wait_send()
            second.wait_send()
            arrive(0, land[0]).wait_recv()
            arrive(1, land[1]).wait_recv()


def call(body, number, ins, outs, scratch=(), beside=(), peers=None, spaces=None, out_spaces=None, late=False):
    spaces = spaces or [VMEM] * len(ins)
    out_spaces = out_spaces or [VMEM] * len(outs)
    copies = sum(b.copies for b in beside)
    locals_ = sum(b.locals for b in beside)
    side_ins = [a for b in beside for a in b.ins]
    side_outs = [a for b in beside for a in b.outs]
    n_in, n_out, n_scratch = len(ins), len(outs), len(scratch)
    loaded = [i for i, m in enumerate(spaces) if m is VMEM]
    stored = [i for i, m in enumerate(out_spaces) if m is VMEM]
    buffers = [VMEM(ins[i].shape, ins[i].dtype) for i in loaded] + [VMEM(outs[i].shape, outs[i].dtype) for i in stored]

    def kernel(*refs):
        at = Place()
        refs = list(refs)

        def take(count):
            out = refs[:count]
            del refs[:count]
            return out

        main_in, side_in = take(n_in), take(len(side_ins))
        main_out, side_out, kept = take(n_out), take(len(side_outs)), take(n_scratch)
        in_buffers, out_buffers = take(len(loaded)), take(len(stored))
        send, recv, local, passing = take(4)
        loads, stores = [], {}
        for k, i in enumerate(loaded):
            loads.append(pltpu.make_async_copy(main_in[i], in_buffers[k], passing.at[k]))
            loads[-1].start()
            main_in[i] = in_buffers[k]
        for k, i in enumerate(stored):
            stores[i] = pltpu.make_async_copy(out_buffers[k], main_out[i], passing.at[len(loaded) + k])
            main_out[i] = out_buffers[k]
        waiting = dict(stores)

        def flush(*which):
            for i in which or list(waiting):
                waiting.pop(i).start()

        at.flush = flush
        known = dict(peers(at)) if peers else {}
        for b in beside:
            known.update(dict(b.peers(at)))
        if "w1" in known:
            for name in ("up", "down", "core", "a0"):
                known.pop(name, None)
        if "x01" in known:
            known.pop("x", None)
        if known:
            greet(list(known.values()))
        side_refs = [([side_in.pop(0) for _ in b.ins], [side_out.pop(0) for _ in b.outs]) for b in beside]
        begin, todo = [], []
        slot, place = 0, 0
        for b, (i, o) in zip(beside, side_refs):
            if isinstance(b, Relay):
                run = functools.partial(relay_run, b, at, i[0], o[0], send, recv, local.at[place], slot)
                begin.append(functools.partial(run, False))
                todo.append(functools.partial(run, True))
                slot, place = slot + 2, place + 1
                continue
            far, near = b.moves(at, i, o)
            for src, dst, peer in far:
                copy = remote(src, dst, send.at[slot], recv.at[slot], peer)
                begin.append(copy.start)
                todo.append(copy.wait)
                slot += 1
            for src, dst in near:
                copy = pltpu.make_async_copy(src, dst, local.at[place])
                begin.append(copy.start)
                todo.append(copy.wait)
                place += 1

        def start():
            for go in begin:
                go()

        at.start_beside = start
        if not late:
            start()
        for copy in loads:
            copy.wait()
        if body:
            body(at, main_in, main_out, kept)
        flush()
        for wait in todo:
            wait()
        for copy in stores.values():
            copy.wait()

    results = pl.pallas_call(
        kernel,
        out_shape=tuple(outs) + tuple(side_outs),
        in_specs=[pl.BlockSpec(memory_space=VMEM if m == PLAIN else ANY) for m in spaces]
        + [pl.BlockSpec(memory_space=ANY)] * len(side_ins),
        out_specs=(pl.BlockSpec(memory_space=ANY),) * (len(outs) + len(side_outs)),
        scratch_shapes=[
            *scratch,
            *buffers,
            pltpu.SemaphoreType.DMA((max(copies, 1),)),
            pltpu.SemaphoreType.DMA((max(copies, 1),)),
            pltpu.SemaphoreType.DMA((max(locals_, 1),)),
            pltpu.SemaphoreType.DMA((max(len(buffers), 1),)),
        ],
        compiler_params=pltpu.CompilerParams(
            collective_id=number, has_side_effects=True, vmem_limit_bytes=58 << 20
        ),
    )(*ins, *side_ins)
    results = list(results)
    main, rest = results[: len(outs)], results[len(outs) :]
    sides = []
    for b in beside:
        sides.append(rest[: len(b.outs)])
        del rest[: len(b.outs)]
    return main, sides


PLAIN = "plain"


def ring_peers(at):
    return [("up", at.at_y(at.up)), ("down", at.at_y(at.down)), ("core", at.core())]


def sems(count):
    return [pltpu.SemaphoreType.DMA((count,)), pltpu.SemaphoreType.DMA((count,)), pltpu.SemaphoreType.DMA((count,))]


def by_rows(count, size, work, carry=None):
    def step(i, carry):
        return work(pl.ds(pl.multiple_of(i * size, size), size), carry)

    return lax.fori_loop(0, count // size, step, carry)


class Whole:
    def __init__(self, at, own, got, full, sem, axis):
        size = own.shape[axis]
        self.copies = []
        for i, (part, n) in enumerate(((own, at.n), (got, 1 - at.n))):
            where = pl.ds(pl.multiple_of(n * size, size), size)
            target = full.at[where] if axis == 0 else full.at[:, where]
            self.copies.append(pltpu.make_async_copy(part, target, sem.at[i]))
            self.copies[-1].start()

    def wait(self):
        for copy in self.copies:
            copy.wait()


class Reduce:
    @staticmethod
    def scratch(deep, x_first, by_rows=False):
        first = (4, deep, HALF) if x_first else (2, 2, deep, HALF) if by_rows else (2, deep, D)
        return [VMEM((3, *first), bf16), VMEM(first, bf16), VMEM((3, deep, HALF), bf16), VMEM((2, deep, HALF), bf16)]

    @staticmethod
    def peers(at):
        return [(f"z{k}", at.at_z(k)) for k in (1, 2, 3)] + [(f"x{a}{b}", at.at_x(a, b)) for a, b in ((0, 1), (1, 0), (1, 1))]

    def __init__(self, at, src, out, refs, send, recv, local, base, place, x_first, by_rows=False):
        self.at, self.src, self.out = at, src, out
        self.land, self.total, self.land_two, self.last = refs
        self.x_first, self.by_rows = x_first, by_rows
        self.deep = self.last.shape[1]
        self.chunk = 32 if self.deep % 32 == 0 else 24
        z_steps = [(at.at_z(k), lax.rem(at.z + k, 4)) for k in (1, 2, 3)]
        x_steps = [
            (at.at_x(a, b), (lax.rem(at.s + a, 2), lax.rem(at.n + b, 2))) for a, b in ((0, 1), (1, 0), (1, 1))
        ]
        first, second = (x_steps, z_steps) if x_first else (z_steps, x_steps)

        def move(slot, source, target, peer):
            return remote(source, target, send.at[base + slot], recv.at[base + slot], peer)

        self.one = [move(i, self.piece(where), self.land.at[i], peer) for i, (peer, where) in enumerate(first)]
        self.own = pltpu.make_async_copy(
            self.piece((at.s, at.n) if x_first else at.z), self.total, local.at[place]
        )
        self.two = [move(3 + i, self.part(where), self.land_two.at[i], peer) for i, (peer, where) in enumerate(second)]
        self.mine = at.z if x_first else (at.s, at.n)
        self.three = move(6, self.last.at[at.s], self.last.at[at.s], at.at_x(1, 0))
        target = out.at[at.z]
        self.four = [move(7 + i, self.last, target, peer) for i, (peer, _) in enumerate(z_steps)]
        self.stay = pltpu.make_async_copy(self.last, target, local.at[place + 1])

    def piece(self, where):
        if self.x_first:
            s, n = where
            return self.src.at[n, :, s] if self.by_rows else self.src.at[:, s, :, self.at.half(n)]
        return self.src.at[:, where] if self.by_rows else self.src.at[where]

    def part(self, where):
        if self.x_first:
            return self.total.at[where]
        s, n = where
        return self.total.at[n, s] if self.by_rows else self.total.at[s, :, self.at.half(n)]

    def first(self):
        for copy in self.one + [self.own]:
            copy.start()

    def second(self):
        self.own.wait()
        for copy in self.one:
            copy.wait_recv()
        lead = self.total.shape[:-2]
        count = math.prod(lead)

        def add(i, carry):
            at_lead = (i,) if len(lead) == 1 else (lax.div(i, lead[1]), lax.rem(i, lead[1]))
            for start in range(0, self.deep, self.chunk):
                where = (*at_lead, slice(start, start + self.chunk))
                got = self.total[where].astype(f32)
                for k in range(3):
                    got += self.land[(k, *where)].astype(f32)
                self.total[where] = got.astype(bf16)
            return carry

        lax.fori_loop(0, count, add, 0)
        for copy in self.two:
            copy.start()

    def third(self):
        for copy in self.two:
            copy.wait_recv()
        own = self.part(self.mine)
        s = self.at.s
        for start in range(0, self.deep, self.chunk):
            rows = slice(start, start + self.chunk)
            got = own[rows].astype(f32)
            for k in range(3):
                got += self.land_two[k, rows].astype(f32)
            self.last[s, rows] = got.astype(bf16)
        self.three.start()

    def fourth(self):
        self.three.wait_recv()
        for copy in self.four + [self.stay]:
            copy.start()

    def end(self):
        for copy in self.four:
            copy.wait()
        for copy in self.one + self.two + [self.three]:
            copy.wait_send()
        self.stay.wait()


class Gather:
    slots = 11

    def __init__(self, at, x, whole, send, recv, local, base=0):
        self.at, self.x, self.whole = at, x, whole
        y, c, up, down = at.y, at.c, at.up, at.down
        far = lax.rem(y + 2, 4)
        half = BLOCK // 2

        def move(slot, y_from, peer, start=0, size=BLOCK, first=False):
            rows = at.rows(y_from, c, start, size)
            src = whole.at[rows]
            if first:
                src = x if size == BLOCK else x.at[start : start + size]
            return remote(src, whole.at[rows], send.at[base + slot], recv.at[base + slot], peer)

        to_up, to_down, core = at.at_y(up), at.at_y(down), at.core()
        self.sends = [
            move(0, y, to_up, 0, half, first=True),
            move(1, y, to_up, half, half, first=True),
            move(2, y, to_down, half, half, first=True),
            move(3, y, to_down, 0, half, first=True),
            move(4, y, core, first=True),
            move(5, down, to_up, 0, half),
            move(6, up, to_down, half, half),
            move(7, down, core),
            move(8, up, core),
            move(9, far, core, 0, half),
            move(10, far, core, half, half),
        ]
        self.own = pltpu.make_async_copy(x, whole.at[at.rows(y, c)], local)

    def begin(self):
        for i in (0, 2, 1, 3, 4):
            self.sends[i].start()
        self.own.start()
        self.own.wait()

    def chain(self, *pairs):
        for arrived, leaving in pairs:
            self.sends[arrived].wait_recv()
            self.sends[leaving].start()

    def pass_on(self):
        self.chain((0, 5), (2, 6))

    def pass_near(self):
        self.chain((1, 7), (3, 8))

    def pass_far(self):
        self.chain((5, 9), (6, 10))

    def got(self, *slots):
        for i in slots:
            self.sends[i].wait_recv()

    def end(self):
        for copy in self.sends:
            copy.wait_send()

    def finish(self):
        self.pass_on()
        self.pass_near()
        self.pass_far()
        self.got(4, 7, 8, 9, 10)
        self.end()

    def each(self, work):
        at = self.at

        def step(s, carry):
            @pl.when(s == 1)
            def _():
                self.got(4)
                self.pass_on()

            @pl.when(s == 2)
            def _():
                self.pass_near()

            @pl.when(s == 3)
            def _():
                self.got(8)

            @pl.when(s == 5)
            def _():
                self.got(7)

            @pl.when(s == 6)
            def _():
                self.pass_far()

            @pl.when(s == 7)
            def _():
                self.got(9, 10)

            work(s, self.place(s))
            return carry

        lax.fori_loop(0, 8, step, 0)
        self.end()

    def place(self, s):
        g = lax.div(s, 2)
        off = g + lax.div(g, 2) - 2 * lax.div(g, 3)
        return self.at.rows(lax.rem(self.at.y + off, 4), lax.rem(self.at.c + s, 2))


QUARTER = 384


class GatherZ(Gather):
    def __init__(self, at, quarter, full, send, recv, local, base=0):
        self.at = at
        z, up, down, far = at.z, lax.rem(at.z + 1, 4), lax.rem(at.z + 3, 4), lax.rem(at.z + 2, 4)
        half = QUARTER

        def move(slot, z_from, peer, start=0, size=2 * QUARTER, first=False):
            rows = pl.ds(pl.multiple_of(at.c * 2 * QUARTER + start, QUARTER), size)
            target = full.at[rows, self.columns(z_from)]
            return remote(quarter.at[rows] if first else target, target, send.at[base + slot], recv.at[base + slot], peer)

        to_up, to_down, core = at.at_z(1), at.at_z(3), at.core()
        self.sends = {
            0: move(0, z, to_up, 0, half, first=True),
            1: move(1, z, to_up, half, half, first=True),
            2: move(2, z, to_down, half, half, first=True),
            3: move(3, z, to_down, 0, half, first=True),
            5: move(5, down, to_up, 0, half),
            6: move(6, up, to_down, half, half),
            7: move(7, down, core),
            8: move(8, up, core),
            9: move(9, far, core, 0, half),
            10: move(10, far, core, half, half),
        }
        self.own = pltpu.make_async_copy(quarter, full.at[:, self.columns(z)], local)

    @staticmethod
    def columns(z):
        return pl.ds(pl.multiple_of(z * QUARTER, QUARTER), QUARTER)

    @staticmethod
    def peers(at):
        return [("z1", at.at_z(1)), ("z3", at.at_z(3)), ("core", at.core())]

    def begin(self):
        for i in (0, 2, 1, 3):
            self.sends[i].start()
        self.own.start()

    def end(self):
        self.got(7, 8, 9, 10)
        self.own.wait()
        for copy in self.sends.values():
            copy.wait_send()


class Scatter:
    slots = 10
    scratch = [
        VMEM((4, BLOCK, D), bf16),
        VMEM((4, BLOCK, D), bf16),
        VMEM((4, BLOCK, D), f32),
        VMEM((2, BLOCK, D), bf16),
        VMEM((2, BLOCK, D), bf16),
        VMEM((2, BLOCK // 2, D), bf16),
        VMEM((2, BLOCK // 2, D), bf16),
    ]

    def __init__(self, at, send, recv, refs, base=0):
        self.at, self.send, self.recv, self.base = at, send, recv, base
        self.out_c, self.in_c, self.own, self.out_y, self.in_y, self.half_out, self.half_in = refs
        half = BLOCK // 2
        peers = at.at_y(at.up), at.at_y(at.down)

        def move(slot, src, dst, peer):
            return remote(src, dst, send.at[base + slot], recv.at[base + slot], peer)

        self.cores = [self.core(g) for g in range(4)]
        self.halves = [move(4 + i, self.half_out.at[i], self.half_in.at[i], peers[i]) for i in range(2)]
        free = [pl.ds((1 - i) * half, half) for i in range(2)]
        bound = [pl.ds(i * half, half) for i in range(2)]
        self.free = [move(6 + i, self.out_y.at[i, free[i]], self.in_y.at[i, free[i]], peers[i]) for i in range(2)]
        self.bound = [move(8 + i, self.out_y.at[i, bound[i]], self.in_y.at[i, bound[i]], peers[i]) for i in range(2)]

    def core(self, g):
        slot = self.base + g
        return remote(self.out_c.at[g], self.in_c.at[g], self.send.at[slot], self.recv.at[slot], self.at.core())

    def both(self, g, rows):
        return self.own[g, rows] + self.in_c[g, rows].astype(f32)

    def products(self, product):
        at = self.at
        half = BLOCK // 2

        def part_rows(rows, i):
            return pl.ds(pl.multiple_of(rows.start + i * half, 32), 32)

        def send_free(i):
            self.cores[1 + i].wait_recv()

            def add(rows, carry):
                there = part_rows(rows, 1 - i)
                self.out_y[i, there] = self.both(1 + i, there).astype(bf16)

            by_rows(half, 32, add)
            self.free[i].start()

        def step(s, carry):
            g = lax.div(s, 2)
            off = lax.rem(6 - g + 3 * lax.div(g, 2) + 2 * lax.div(g, 3), 4)
            part = product(at.rows(lax.rem(at.y + off, 4), lax.rem(at.c + 1 + s, 2)))

            @pl.when(lax.rem(s, 2) == 0)
            def _():
                self.out_c[g] = part.astype(bf16)
                self.core(g).start()

            @pl.when(lax.rem(s, 2) == 1)
            def _():
                self.own[g] = part

            @pl.when(s == 2)
            def _():
                self.cores[0].wait_recv()
                for i in range(2):

                    def add(rows, carry, i=i):
                        self.half_out[i, rows] = self.both(0, part_rows(rows, i)).astype(bf16)

                    by_rows(half, 32, add)
                    self.halves[i].start()

            @pl.when(s == 4)
            def _():
                send_free(0)

            @pl.when(s == 6)
            def _():
                send_free(1)

            return carry

        lax.fori_loop(0, 8, step, 0)

    def middle(self):
        half = BLOCK // 2
        for i in range(2):
            self.halves[i].wait_recv()

            def add(rows, carry, i=i):
                here = pl.ds(pl.multiple_of(rows.start + i * half, 32), 32)
                self.out_y[i, here] = (self.both(1 + i, here) + self.half_in[i, rows].astype(f32)).astype(bf16)

            by_rows(half, 32, add)
            self.bound[i].start()

    def arrive(self):
        self.cores[3].wait_recv()
        for copy in self.free + self.bound:
            copy.wait_recv()

    def total(self, rows):
        return self.both(3, rows) + self.in_y[0, rows].astype(f32) + self.in_y[1, rows].astype(f32)

    def end(self):
        for copy in self.cores + self.halves + self.free + self.bound:
            copy.wait_send()


def standard(values):
    average = jnp.mean(values, axis=1, keepdims=True)
    variance = jnp.mean(values * values, axis=1, keepdims=True) - average * average
    factor = lax.rsqrt(variance + EPSILON)
    return (values - average) * factor, factor


def norm_back(incoming, centred, factor, gain):
    scaled = incoming * gain
    first = jnp.mean(scaled, axis=1, keepdims=True)
    second = jnp.mean(scaled * centred, axis=1, keepdims=True)
    return factor * (scaled - first - centred * second)


def two_sums(incoming, centred, carry):
    gains, shifts = carry
    return gains + jnp.sum(incoming * centred, axis=0, keepdims=True), shifts + jnp.sum(incoming, axis=0, keepdims=True)


def no_sums():
    return jnp.zeros((1, D), f32), jnp.zeros((1, D), f32)


EIGHTH = 0.125


def shape(*dims, dtype=bf16):
    return jax.ShapeDtypeStruct(dims, dtype)


class Keep:
    def __init__(self, whole, out, sem, base):
        self.whole, self.out, self.sem, self.base = whole, out, sem, base

    def block(self, s, rows):
        pltpu.make_async_copy(self.whole.at[rows], self.out.at[rows], self.sem.at[self.base + s]).start()

    def wait(self):
        for s in range(8):
            some = pl.ds(0, BLOCK)
            pltpu.make_async_copy(self.whole.at[some], self.out.at[some], self.sem.at[self.base + s]).wait()


def enter(number, layer_input, gains, weights, query_t, cross_out, texts, pair_t, beside):
    relay = Relay(layer_input)

    def body(at, ins, outs, kept):
        source, *gains = ins[:7]
        *own_weights, query_own, out_own, own_texts, pair = ins[7:]
        x, vectors, weight, all_rows, qkv, query_all, out_quarter, text_pair = outs
        normed, whole, query_part, out_part, query_quarter, text_parts, text_got, own_vectors, send, recv, local = kept
        half = at.half(at.n)
        moving = functools.partial(relay_run, relay, at, source, x, send, recv, local.at[0], 11)
        moving(False)
        own_vectors[...] = jnp.zeros_like(own_vectors)
        for i, ref in enumerate(gains):
            own_vectors[i : i + 1] = ref[...].astype(f32).reshape(1, HALF)
        columns = GatherZ.columns(lax.rem(at.z, 2))
        holds = at.n == lax.div(at.z, 2)
        quarters = []
        for i, (own, part) in enumerate(((query_own, query_part), (out_own, out_part))):
            quarters.append(
                (
                    pltpu.make_async_copy(own.at[:, columns], part, local.at[14 + i]),
                    remote(own.at[:, columns], part, send.at[17 + i], recv.at[17 + i], at.x()),
                )
            )

        @pl.when(holds)
        def _():
            for stay, go in quarters:
                go.start()
                stay.start()

        stay, go = [], []
        for i, (own, target) in enumerate(
            [(own_vectors, vectors.at[:, half])]
            + [(own, weight.at[j * COLS : (j + 1) * COLS, half]) for j, own in enumerate(own_weights)]
        ):
            stay.append(pltpu.make_async_copy(own, target, local.at[1 + i]))
            go.append(remote(own, target, send.at[13 + i], recv.at[13 + i], at.x()))
        stay[0].start()
        go[0].start()

        @pl.when(holds)
        def _():
            for near, far in quarters:
                near.wait()
                far.wait_send()

        @pl.when(jnp.logical_not(holds))
        def _():
            for near, far in quarters:
                far.wait_recv()

        for clip in range(2):
            text_parts[clip] = dot_flip(own_texts[clip], pair[...])
        text_go = remote(text_parts.at[1 - at.n], text_got, send.at[52], recv.at[52], at.x())
        text_go.start()
        queries = Gather(at, query_part, query_quarter, send, recv, local.at[16], 19)
        outputs = Gather(at, out_part, out_quarter, send, recv, local.at[17], 30)
        queries.begin()
        stay[0].wait()
        go[0].wait_recv()
        moving(True)
        for copy in stay[1:] + go[1:]:
            copy.start()
        queries.pass_on()
        queries.pass_near()

        def norm(rows, carry):
            centred, _ = standard(x[rows].astype(f32))
            normed[rows] = (centred * vectors[0:1] + vectors[1:2]).astype(bf16)

        by_rows(BLOCK, 32, norm)
        gather = Gather(at, normed, whole, send, recv, local.at[5])
        gather.begin()
        queries.pass_far()
        queries.got(4, 7, 8, 9, 10)
        around = GatherZ(at, query_quarter, query_all, send, recv, local.at[18], 41)
        around.begin()
        keep = Keep(whole, all_rows, local, 6)

        def times(rows):
            qkv[rows] = dot_flip(whole[rows], weight[...]).astype(bf16)

        def work(s, rows):
            keep.block(s, rows)

            @pl.when(s == 4)
            def _():
                for copy in stay[1:]:
                    copy.wait()
                for copy in go[1:]:
                    copy.wait_recv()
                at.start_beside()
                at.flush(0, 1, 2)

            @pl.when(s >= 4)
            def _():
                times(rows)

            @pl.when(s == 6)
            def _():
                outputs.begin()
                around.pass_on()

        gather.each(work)
        around.pass_near()
        outputs.pass_on()
        outputs.pass_near()

        def rest(s, carry):
            times(gather.place(s))
            return carry

        lax.fori_loop(0, 4, rest, 0)
        at.flush(4)
        outputs.pass_far()
        around.pass_far()
        text_go.wait()
        text_pair[...] = (text_parts[at.n] + text_got[...]).astype(bf16)
        outputs.got(4, 7, 8, 9, 10)
        keep.wait()
        for copy in go:
            copy.wait_send()
        outputs.end()
        queries.end()
        around.end()

    return call(
        body,
        number,
        [layer_input, *gains, *weights, query_t, cross_out, texts, pair_t],
        [
            shape(BLOCK, D),
            shape(8, D, dtype=f32),
            shape(3 * COLS, D),
            shape(D, D),
            shape(D, 3 * COLS),
            shape(D, D),
            shape(D, QUARTER),
            shape(64, 2 * COLS),
        ],
        [
            VMEM((BLOCK, D), bf16),
            VMEM((D, D), bf16),
            VMEM((COLS, QUARTER), bf16),
            VMEM((COLS, QUARTER), bf16),
            VMEM((D, QUARTER), bf16),
            VMEM((2, 64, 2 * COLS), f32),
            VMEM((64, 2 * COLS), f32),
            VMEM((8, HALF), f32),
            *sems(53),
        ],
        beside,
        lambda at: ring_peers(at) + relay.peers(at) + [("x", at.x())] + GatherZ.peers(at),
        spaces=[ANY] + [PLAIN] * 6 + [VMEM] * 7,
        out_spaces=[VMEM, VMEM, VMEM, ANY, VMEM, ANY, VMEM, VMEM],
        late=True,
    )


def causal_forward(number, joined, down, out_quarter, beside):
    at_once = 512

    def body(at, ins, outs, kept):
        (qkv, block, quarter), (out, logs, all_down, out_all) = ins, outs
        parts, mixed, send, recv, local = kept
        first = Gather(at, block, all_down, send, recv, local.at[0])
        second = GatherZ(at, quarter, out_all, send, recv, local.at[1], 11)
        second.begin()
        first.begin()
        for i in range(3):
            for h in range(HEADS):
                a = i * COLS + h * HDIM
                piece = qkv[:, a : a + HDIM]
                parts[i, h] = piece * EIGHTH if i == 0 else piece
        square = (at_once, at_once)
        seen = lax.broadcasted_iota(jnp.int32, square, 0) >= lax.broadcasted_iota(jnp.int32, square, 1)

        def one(h, carry):
            for i in reversed(range(D // at_once)):
                before, upto = i * at_once, (i + 1) * at_once
                rows = slice(before, upto)
                scores = dot_flip(parts[0, h, rows], parts[1, h, 0:upto])
                last = jnp.where(seen, scores[:, before:], NEGATIVE)
                scores = jnp.concatenate((scores[:, :before], last), axis=1) if i else last
                peak = jnp.max(scores, axis=1, keepdims=True)
                raised = jnp.exp(scores - peak)
                total = jnp.sum(raised, axis=1, keepdims=True)
                mixed[h, rows] = (dot(raised.astype(bf16), parts[2, h, 0:upto]) / total).astype(bf16)
                column = jnp.broadcast_to(peak + jnp.log(total), (at_once, 128))
                logs[pl.ds(h, 1), rows] = column.T[0:1, :]

            @pl.when(h == 1)
            def _():
                first.pass_on()
                second.pass_on()

            return carry

        lax.fori_loop(0, HEADS, one, 0)
        first.pass_near()
        second.pass_near()
        out[...] = jnp.concatenate([mixed[h] for h in range(HEADS)], axis=1)
        at.flush()
        first.pass_far()
        second.pass_far()
        first.got(4, 7, 8, 9, 10)
        first.end()
        second.end()

    return call(
        body,
        number,
        [joined, down, out_quarter],
        [shape(D, COLS), shape(8, D, dtype=f32), shape(D, D), shape(D, D)],
        [VMEM((3, HEADS, D, HDIM), bf16), VMEM((HEADS, D, HDIM), bf16), *sems(22)],
        beside,
        lambda at: ring_peers(at) + GatherZ.peers(at),
        out_spaces=[VMEM, VMEM, ANY, ANY],
    )


def forward_rest(number, attended, out_w, x, vectors, query_all, out_all, texts, all_down, expand_w, contract):
    def body(at, ins, outs, kept):
        mixed, out_own, out_got, x, vectors, query_all, out_all, texts, all_down, expand_own, expand_got, contract_own = ins
        middle, after, normed_two, weights, all_rows, activated, grad, contract_out, keys_out, values_out = outs
        *refs, normed, whole, downs, out_full, expand_full, contract_full, key_full, value_full, branch, send, recv, local = kept
        half = at.half(at.n)
        weight = Whole(at, out_own, out_got, out_full, local.at[pl.ds(0, 2)], 1)
        swap = remote(contract_own, contract_full.at[:, half], send.at[21], recv.at[21], at.x())
        swap.start()
        factors = [
            pltpu.make_async_copy(query_all, key_full, local.at[2]),
            pltpu.make_async_copy(out_all, value_full, local.at[3]),
        ]
        for copy in factors:
            copy.start()
        later = [
            pltpu.make_async_copy(contract_own, contract_full.at[:, half], local.at[4]),
            pltpu.make_async_copy(all_down, downs, local.at[7]),
        ]
        for copy in later:
            copy.start()
        later.append(Whole(at, expand_own, expand_got, expand_full, local.at[pl.ds(5, 2)], 0))
        weight.wait()
        scatter = Scatter(at, send, recv, refs)
        scatter.products(lambda rows: dot(mixed[rows], out_full[...]))
        for copy in factors:
            copy.wait()

        def make(b, carry):
            for h in range(HEADS):
                rows = pl.ds(pl.multiple_of(b * BLOCK + h * 64, 64), 64)
                text_keys = texts[b, :, h * HDIM : (h + 1) * HDIM]
                text_values = texts[b, :, COLS + h * HDIM : COLS + (h + 1) * HDIM]
                key_full[rows] = (dot(text_keys, key_full[rows]) * EIGHTH).astype(bf16)
                value_full[rows] = dot(text_values, value_full[rows]).astype(bf16)
            return carry

        lax.fori_loop(0, 8, make, 0)
        made = [
            pltpu.make_async_copy(key_full, keys_out, local.at[8]),
            pltpu.make_async_copy(value_full, values_out, local.at[9]),
        ]
        for copy in made:
            copy.start()
        scatter.middle()
        for copy in later:
            copy.wait()
        scatter.arrive()

        def norm_two(rows, carry):
            total = x[rows].astype(f32) + scatter.total(rows)
            middle[rows] = total
            centred, _ = standard(total)
            normed_two[rows] = (centred * vectors[2:3] + vectors[3:4]).astype(bf16)

        by_rows(BLOCK, 32, norm_two)

        def cross(b, carry):
            rows = pl.ds(pl.multiple_of(b * BLOCK, BLOCK), BLOCK)
            scores = dot_flip(key_full[rows], normed_two[...]).reshape(HEADS, 64, BLOCK)
            raised = jnp.exp(scores - jnp.max(scores, axis=1, keepdims=True))
            p = raised / jnp.sum(raised, axis=1, keepdims=True)
            p = p.reshape(BLOCK, BLOCK).T.astype(bf16)
            weights[b] = p
            part = dot(p, value_full[rows])

            @pl.when(b == 0)
            def _():
                branch[...] = part

            @pl.when(b > 0)
            def _():
                branch[...] += part

            return carry

        lax.fori_loop(0, 8, cross, 0)

        def norm_three(rows, carry):
            total = middle[rows] + branch[rows]
            after[rows] = total
            centred, _ = standard(total)
            normed[rows] = (centred * vectors[4:5] + vectors[5:6]).astype(bf16)

        by_rows(BLOCK, 32, norm_three)
        gather = Gather(at, normed, whole, send, recv, local.at[10], 10)
        gather.begin()
        at.flush(0, 1, 2, 3)
        swap.wait_recv()
        keep_contract = pltpu.make_async_copy(contract_full, contract_out, local.at[11])
        keep_contract.start()
        keep = Keep(whole, all_rows, local, 12)

        def ahead(rows, carry):
            grad[rows] = dot_flip(downs[rows], contract_full[...]).astype(bf16)

        by_rows(D, BLOCK, ahead)

        def work(s, rows):
            keep.block(s, rows)
            hidden = dot(whole[rows], expand_full[...])
            bell = 0.5 * (1.0 + lax.erf(hidden * ROOT_HALF))
            activated[rows] = (hidden * bell).astype(bf16)
            slope = bell + hidden * jnp.exp(-0.5 * hidden * hidden) * GAUSS_NORM
            grad[rows] = (grad[rows].astype(f32) * slope).astype(bf16)

        gather.each(work)
        at.flush()
        keep.wait()
        keep_contract.wait()
        for copy in made:
            copy.wait()
        scatter.end()
        swap.wait_send()

    results, _ = call(
        body,
        number,
        [attended, *out_w, x, vectors, query_all, out_all, texts, all_down, *expand_w, contract],
        [
            shape(BLOCK, D, dtype=f32),
            shape(BLOCK, D, dtype=f32),
            shape(BLOCK, D),
            shape(8, BLOCK, BLOCK),
            shape(D, D),
            shape(D, HALF),
            shape(D, HALF),
            shape(HALF, D),
            shape(D, D),
            shape(D, D),
        ],
        [
            *Scatter.scratch,
            VMEM((BLOCK, D), bf16),
            VMEM((D, D), bf16),
            VMEM((D, D), bf16),
            VMEM((COLS, D), bf16),
            VMEM((D, HALF), bf16),
            VMEM((HALF, D), bf16),
            VMEM((D, D), bf16),
            VMEM((D, D), bf16),
            VMEM((BLOCK, D), f32),
            *sems(22),
        ],
        (),
        lambda at: ring_peers(at) + [("x", at.x())],
        spaces=[VMEM, ANY, ANY, VMEM, VMEM, ANY, ANY, VMEM, ANY, ANY, ANY, ANY],
        out_spaces=[VMEM, VMEM, VMEM, VMEM, ANY, VMEM, VMEM, ANY, ANY, ANY],
    )
    return results


def backward_rest(
    number, grad, expand_w, after, middle, vectors, down, keys, values, weights, out_w, contract_sum, expand_sum, beside
):
    def body(at, ins, outs, kept):
        grad, expand_own, expand_got, after, middle, vectors, down, keys, values, weights, out_own, out_got = ins[:12]
        grad_rows, rounded_two, grad_scores, all_two, all_rows, grad_mixed, grad_vectors = outs[:7]
        *refs, rounded, whole, second, out_full, expand_full, key_full, value_full, send, recv, local = kept
        reduces = [
            Reduce(at, ins[12], outs[7], refs[7:11], send, recv, local, 32, 16, False),
            Reduce(at, ins[13], outs[8], refs[11:15], send, recv, local, 42, 18, True, True),
        ]
        refs = refs[:7]
        for reduce in reduces:
            reduce.first()
        weight = Whole(at, expand_own, expand_got, expand_full, local.at[pl.ds(0, 2)], 0)
        later = [
            pltpu.make_async_copy(keys, key_full, local.at[2]),
            pltpu.make_async_copy(values, value_full, local.at[3]),
        ]
        for copy in later:
            copy.start()
        later.append(Whole(at, out_own, out_got, out_full, local.at[pl.ds(4, 2)], 1))
        weight.wait()
        scatter = Scatter(at, send, recv, refs)
        scatter.products(lambda rows: dot_flip(grad[rows], expand_full[...]))
        scatter.middle()
        for copy in later:
            copy.wait()
        scatter.arrive()

        def norm_three(rows, carry):
            incoming = scatter.total(rows)
            centred, factor = standard(after[rows])
            total = down[rows].astype(f32) + norm_back(incoming, centred, factor, vectors[4:5])
            grad_rows[rows] = total
            rounded_two[rows] = total.astype(bf16)
            return two_sums(incoming, centred, carry)

        gains, shifts = by_rows(BLOCK, 32, norm_three, no_sums())
        before = Gather(at, rounded_two, all_two, send, recv, local.at[6], 10)
        before.begin()
        for reduce in reduces:
            reduce.second()
        grad_vectors[4:5] = gains
        grad_vectors[5:6] = shifts

        def cross(b, carry):
            rows = pl.ds(pl.multiple_of(b * BLOCK, BLOCK), BLOCK)
            p = weights[b].astype(f32).T.reshape(HEADS, 64, BLOCK)
            dp = dot_flip(value_full[rows], rounded_two[...]).reshape(HEADS, 64, BLOCK)
            ds = p * (dp - jnp.sum(p * dp, axis=1, keepdims=True))
            ds = ds.reshape(BLOCK, BLOCK).T.astype(bf16)
            grad_scores[b] = ds
            part = dot(ds, key_full[rows])

            @pl.when(b == 0)
            def _():
                second[...] = part

            @pl.when(b > 0)
            def _():
                second[...] += part

            @pl.when(b == 3)
            def _():
                before.pass_on()

            @pl.when(b == 5)
            def _():
                for reduce in reduces:
                    reduce.third()

            return carry

        lax.fori_loop(0, 8, cross, 0)
        at.flush(1, 2)
        for reduce in reduces:
            reduce.fourth()

        def norm_two(rows, carry):
            incoming = second[rows]
            centred, factor = standard(middle[rows])
            total = grad_rows[rows] + norm_back(incoming, centred, factor, vectors[2:3])
            grad_rows[rows] = total
            rounded[rows] = total.astype(bf16)
            return two_sums(incoming, centred, carry)

        gains, shifts = by_rows(BLOCK, 32, norm_two, no_sums())
        grad_vectors[2:3] = gains
        grad_vectors[3:4] = shifts
        gather = Gather(at, rounded, whole, send, recv, local.at[7], 21)
        before.pass_near()
        gather.begin()
        at.flush(0, 6)
        before.pass_far()
        keep = Keep(whole, all_rows, local, 8)

        def work(s, rows):
            keep.block(s, rows)
            grad_mixed[rows] = dot_flip(whole[rows], out_full[...]).astype(bf16)

        gather.each(work)
        at.flush()
        before.got(4, 7, 8, 9, 10)
        before.end()
        keep.wait()
        scatter.end()
        for reduce in reduces:
            reduce.end()

    return call(
        body,
        number,
        [grad, *expand_w, after, middle, vectors, down, keys, values, weights, *out_w, contract_sum, expand_sum],
        [
            shape(BLOCK, D, dtype=f32),
            shape(BLOCK, D),
            shape(8, BLOCK, BLOCK),
            shape(D, D),
            shape(D, D),
            shape(D, COLS),
            shape(8, D, dtype=f32),
            shape(4, 2, 96, HALF),
            shape(4, 2, 96, HALF),
        ],
        [
            *Scatter.scratch,
            *Reduce.scratch(96, False),
            *Reduce.scratch(96, True, True),
            VMEM((BLOCK, D), bf16),
            VMEM((D, D), bf16),
            VMEM((BLOCK, D), f32),
            VMEM((COLS, D), bf16),
            VMEM((D, HALF), bf16),
            VMEM((D, D), bf16),
            VMEM((D, D), bf16),
            *sems(52),
        ],
        beside,
        lambda at: ring_peers(at) + Reduce.peers(at),
        spaces=[VMEM, ANY, ANY, VMEM, VMEM, VMEM, VMEM, ANY, ANY, VMEM, ANY, ANY, ANY, ANY],
        out_spaces=[VMEM, VMEM, VMEM, ANY, ANY, VMEM, VMEM, ANY, ANY],
    )


def causal_backward(number, joined, grad, logs, activated, contract, after, normed_two, part, beside):
    at_once = 512

    def body(at, ins, outs, kept):
        (qkv, go, log_rows, activated, contract, after, block, part), (out, result, all_rows, summed) = ins, outs
        *refs, parts, key_sum, value_sum, send, recv, local = kept
        reduce = Reduce(at, part, summed, refs[7:], send, recv, local, 21, 1, False)
        reduce.first()
        gather = Gather(at, block, all_rows, send, recv, local.at[0], 10)
        gather.begin()
        scatter = Scatter(at, send, recv, refs[:7])
        scatter.products(lambda rows: dot(activated[rows], contract[...]))
        gather.pass_on()
        for i in range(4):
            for h in range(HEADS):
                a = i * COLS + h * HDIM
                piece = qkv[:, a : a + HDIM] if i < 3 else go[:, h * HDIM : (h + 1) * HDIM]
                parts[i, h] = piece * EIGHTH if i == 0 else piece
        square = (at_once, at_once)
        seen = lax.broadcasted_iota(jnp.int32, square, 1) >= lax.broadcasted_iota(jnp.int32, square, 0)
        blocks = D // at_once

        def one(h, carry):
            turned = parts[1, h].T
            query_parts = []
            for i in reversed(range(blocks)):
                before, upto = i * at_once, (i + 1) * at_once
                rows = slice(before, upto)
                q, g = parts[0, h, rows], parts[3, h, rows]
                k, v = parts[1, h, 0:upto], parts[2, h, 0:upto]
                p = jnp.exp(dot_flip(k, q) - log_rows[pl.ds(h, 1), rows])
                last = jnp.where(seen, p[before:], 0.0)
                p = jnp.concatenate((p[:before], last), axis=0) if i else last
                dp = dot_flip(v, g)
                ds = (p * (dp - jnp.sum(p * dp, axis=0, keepdims=True))).astype(bf16)
                value_part, key_part = dot(p.astype(bf16), g), dot(ds, q)
                if i == blocks - 1:
                    key_sum[0:upto, :] = key_part
                    value_sum[0:upto, :] = value_part
                else:
                    key_sum[0:upto, :] += key_part
                    value_sum[0:upto, :] += value_part
                query_parts.append((dot(turned[:, 0:upto], ds) * EIGHTH).T)
                if i == blocks - 1:

                    @pl.when(h == 1)
                    def _():
                        reduce.second()

                    @pl.when(h == 2)
                    def _():
                        reduce.fourth()

            parts[0, h] = jnp.concatenate(query_parts[::-1], axis=0).astype(bf16)
            parts[1, h] = key_sum[...].astype(bf16)
            parts[2, h] = value_sum[...].astype(bf16)

            @pl.when(h == 0)
            def _():
                gather.pass_near()

            @pl.when(h == 1)
            def _():
                scatter.middle()
                gather.pass_far()
                reduce.third()

            return carry

        lax.fori_loop(0, HEADS, one, 0)
        for i in range(3):
            out[:, i * COLS : (i + 1) * COLS] = jnp.concatenate([parts[i, h] for h in range(HEADS)], axis=1)
        scatter.arrive()

        def finish(rows, carry):
            result[rows] = (after[rows] + scatter.total(rows)).astype(bf16)

        at.flush(0)
        by_rows(BLOCK, 32, finish)
        at.flush(1)
        gather.got(4, 7, 8, 9, 10)
        gather.end()
        scatter.end()
        reduce.end()

    return call(
        body,
        number,
        [joined, grad, logs, activated, contract, after, normed_two, part],
        [shape(D, 3 * COLS), shape(BLOCK, D), shape(D, D), shape(4, 2, 72, HALF)],
        [
            *Scatter.scratch,
            *Reduce.scratch(72, False),
            VMEM((4, HEADS, D, HDIM), bf16),
            VMEM((D, HDIM), f32),
            VMEM((D, HDIM), f32),
            *sems(31),
        ],
        beside,
        lambda at: ring_peers(at) + Reduce.peers(at),
        spaces=[VMEM] * 7 + [ANY],
        out_spaces=[VMEM, VMEM, ANY, ANY],
    )


def leave(number, grad, joined, x, vectors, grad_rows, sums, late, text_part, beside):
    relay = Relay(jax.ShapeDtypeStruct((BLOCK, D), bf16), True)
    some = 64 // 8

    def ring(at):
        return [{"wide": lax.rem(at.w + k, 8)} for k in range(1, 8)]

    x_steps = ((0, 1), (1, 0), (1, 1))

    def group(at):
        return [(b, {"wide": lax.rem(at.w + k, 8), "narrow": lax.rem(at.n + b, 2)}) for k in range(8) for b in range(2)][1:]

    def peers(at):
        known = ring_peers(at) + relay.peers(at) + Reduce.peers(at)
        known += [(f"w{k}", peer) for k, peer in enumerate(ring(at), 1)]
        return known + [(f"g{i}", peer) for i, (b, peer) in enumerate(group(at)) if b]

    def body(at, ins, outs, kept):
        grad, weight, x, vectors, before, late, text, one, two = ins
        result, out_one, out_two, vector_sums, text_out = outs
        refs, kept = kept[:7], kept[7:]
        reduces = [
            Reduce(at, one, out_one, kept[0:4], kept[-3], kept[-2], kept[-1], 12, 1, False),
            Reduce(at, two, out_two, kept[4:8], kept[-3], kept[-2], kept[-1], 22, 3, True),
        ]
        rounded, parts, ring_parts, ring_sum, x_parts, x_sum, z_parts, text_parts, text_sum, send, recv, local = kept[8:]
        me = at.spot(at.y, at.c)

        def move(slot, source, target, peer):
            return remote(source, target, send.at[slot], recv.at[slot], peer)

        to_ring, to_group = ring(at), group(at)
        slot = 32
        trades = []
        for peer in to_ring:
            there = at.spot(lax.div(peer["wide"], 2), lax.rem(peer["wide"], 2))
            trades.append(move(slot, text.at[there], text_parts.at[me], peer))
            slot += 1
        text_own = pltpu.make_async_copy(text.at[me], text_parts.at[me], local.at[5])
        texts = []
        for b, peer in to_group:
            n = lax.rem(at.n + b, 2)
            texts.append(move(slot, text_sum.at[:, at.half(n)], text_out.at[at.n, me], peer))
            slot += 1
        text_stay = pltpu.make_async_copy(text_sum.at[:, at.half(at.n)], text_out.at[at.n, me], local.at[6])
        rings = []
        for peer in to_ring:
            rings.append(move(slot, parts, ring_parts.at[at.w], peer))
            slot += 1
        ring_own = pltpu.make_async_copy(parts, ring_parts.at[at.w], local.at[7])
        spreads = []
        for a, b in x_steps:
            half = ring_sum.at[:, at.half(lax.rem(at.n + b, 2))]
            spreads.append(move(slot, half, x_parts.at[at.s, at.n], at.at_x(a, b)))
            slot += 1
        x_own = pltpu.make_async_copy(ring_sum.at[:, at.half(at.n)], x_parts.at[at.s, at.n], local.at[8])
        lasts = []
        for k in (1, 2, 3):
            lasts.append(move(slot, x_sum, z_parts.at[at.z], at.at_z(k)))
            slot += 1

        for reduce in reduces:
            reduce.first()
        text_own.start()
        for copy in trades:
            copy.start()
        scatter = Scatter(at, send, recv, refs)
        scatter.products(lambda rows: dot(grad[rows], weight[...]))
        at.start_beside()
        scatter.middle()
        for reduce in reduces:
            reduce.second()
        text_own.wait()
        for copy in trades:
            copy.wait_recv()
        total = text_parts[0].astype(f32)
        for i in range(1, 8):
            total += text_parts[i].astype(f32)
        text_sum[...] = total.astype(bf16)
        text_stay.start()
        for copy in texts:
            copy.start()
        scatter.arrive()

        def norm(rows, carry):
            incoming = scatter.total(rows)
            centred, factor = standard(x[rows].astype(f32))
            total = before[rows] + norm_back(incoming, centred, factor, vectors[0:1])
            rounded[rows] = total.astype(bf16)
            return two_sums(incoming, centred, carry)

        gains, shifts = by_rows(BLOCK, 32, norm, no_sums())
        moving = functools.partial(relay_run, relay, at, rounded, result, send, recv, local.at[0], 10)
        moving(False)
        parts[0:1] = gains
        parts[1:2] = shifts
        parts[2:6] = late[2:6]
        parts[6:8] = jnp.zeros((2, D), f32)
        ring_own.start()
        for copy in rings:
            copy.start()
        for reduce in reduces:
            reduce.third()
        ring_own.wait()
        for copy in rings:
            copy.wait_recv()
        total = ring_parts[0]
        for i in range(1, 8):
            total += ring_parts[i]
        ring_sum[...] = total
        x_own.start()
        for copy in spreads:
            copy.start()
        for reduce in reduces:
            reduce.fourth()
        x_own.wait()
        for copy in spreads:
            copy.wait_recv()
        total = x_parts[0, 0] + x_parts[0, 1] + x_parts[1, 0] + x_parts[1, 1]
        x_sum[...] = total
        for copy in lasts:
            copy.start()
        z_parts[pl.ds(at.z, 1)] = total.reshape(1, 8, HALF)
        for copy in lasts:
            copy.wait_recv()
        vector_sums[...] = z_parts[0] + z_parts[1] + z_parts[2] + z_parts[3]
        at.flush()
        moving(True)
        text_stay.wait()
        for copy in texts:
            copy.wait()
        for copy in trades + rings + spreads + lasts:
            copy.wait_send()
        scatter.end()
        for reduce in reduces:
            reduce.end()

    return call(
        body,
        number,
        [grad, joined, x, vectors, grad_rows, late, text_part, *sums],
        [
            shape(384, HALF),
            shape(4, 2, 72, HALF),
            shape(4, 2, 48, HALF),
            shape(8, HALF, dtype=f32),
            shape(2, 8, some, HALF),
        ],
        [
            *Scatter.scratch,
            *Reduce.scratch(72, False),
            *Reduce.scratch(48, True),
            VMEM((BLOCK, D), bf16),
            VMEM((8, D), f32),
            VMEM((8, 8, D), f32),
            VMEM((8, D), f32),
            VMEM((2, 2, 8, HALF), f32),
            VMEM((8, HALF), f32),
            VMEM((4, 8, HALF), f32),
            VMEM((8, some, D), bf16),
            VMEM((some, D), bf16),
            *sems(32 + 7 + 15 + 7 + 6),
        ],
        beside,
        peers,
        spaces=[VMEM, VMEM, VMEM, VMEM, VMEM, VMEM, ANY, ANY, ANY],
        out_spaces=[ANY, ANY, ANY, VMEM, ANY],
        late=True,
    )


def on_device(
    layer_input,
    text_states,
    cotangent,
    first_gain,
    first_shift,
    query_weight,
    key_weight,
    value_weight,
    output_weight,
    second_gain,
    second_shift,
    cross_query,
    cross_key,
    cross_value,
    cross_output,
    third_gain,
    third_shift,
    expand_weight,
    contract_weight,
):
    gains = (first_gain, first_shift, second_gain, second_shift, third_gain, third_shift)
    weights = [query_weight.T, key_weight.T, value_weight.T]
    query_t = cross_query.T
    pair_t = jnp.concatenate((cross_key.T, cross_value.T), axis=0)
    n = lax.axis_index("narrow")

    results, ((down,), (text_got,)) = enter(
        1,
        layer_input,
        gains,
        weights,
        query_t,
        cross_output,
        text_states,
        pair_t,
        [Relay(cotangent), GiveClip(text_states)],
    )
    x, vectors, joined, all_one, qkv, query_all, out_quarter, text_pair = results
    (attended, logs, all_down, out_all), ((texts,), (out_got,), (expand_got,)) = causal_forward(
        2, qkv, down, out_quarter, [ToSpots(text_pair), Give(output_weight), Give(expand_weight)]
    )
    out_w, expand_w = (output_weight, out_got), (expand_weight, expand_got)
    middle, after, normed_two, cross_p, all_three, activated, grad_expand, contract, all_keys, all_values = forward_rest(
        3, attended, out_w, x, vectors, query_all, out_all, texts, all_down, expand_w, contract_weight
    )

    contract_part = outer(activated, all_down).astype(bf16).reshape(4, 2, 96, D)
    expand_part = outer(all_three, grad_expand).astype(bf16).reshape(2, 4, 2, 96, HALF)
    results, ((cross_p,), (query_got,), (cross_got,)) = backward_rest(
        4,
        grad_expand,
        expand_w,
        after,
        middle,
        vectors,
        down,
        all_keys,
        all_values,
        cross_p,
        out_w,
        contract_part,
        expand_part,
        [Trade(cross_p), Give(query_t), Give(cross_output)],
    )
    grad_one, _, grad_scores, all_mid_two, all_mid_one, grad_attended, late, contract_grad, expand_grad = results

    own_first = n == 0

    def whole(own, got):
        return jnp.concatenate((jnp.where(own_first, own, got), jnp.where(own_first, got, own)), axis=1)

    def heads(what, a, b):
        return jnp.einsum(what, a, b, preferred_element_type=f32)

    text = whole(lax.dynamic_index_in_dim(text_states, n, 0, False), text_got)
    text_heads = text_pair.reshape(64, 2, HEADS, HDIM)
    grad_values = outer(cross_p.reshape(D, COLS), all_mid_two).astype(bf16).reshape(HEADS, 64, D)
    heads_out = whole(cross_output, cross_got).reshape(HEADS, HDIM, D)
    grad_text_values = heads("hkf,hdf->khd", grad_values, heads_out).reshape(64, COLS).astype(bf16)
    grad_cross = heads("khd,hkf->hdf", text_heads[:, 1], grad_values).reshape(COLS, D)
    value_part = jnp.concatenate((grad_cross, outer(grad_text_values, text), outer(attended, all_mid_one)), axis=0)
    (grad_qkv, layer_output, all_two, value_grad), ((grad_scores,), (pair_got,)) = causal_backward(
        5,
        qkv,
        grad_attended,
        logs,
        activated,
        contract,
        after,
        normed_two,
        value_part.astype(bf16).reshape(4, 2, 72, D),
        [Trade(grad_scores), Give(pair_t)],
    )

    joined_part = outer(grad_qkv, all_one).astype(bf16).reshape(4, 2, 72, D)
    grad_keys = outer(grad_scores.reshape(D, COLS), all_two).astype(bf16).reshape(HEADS, 64, D)
    heads_query = whole(query_t, query_got).reshape(HEADS, HDIM, D)
    grad_text_keys = (heads("hkf,hdf->khd", grad_keys, heads_query) * EIGHTH).reshape(64, COLS).astype(bf16)
    grad_query = heads("khd,hkf->hdf", text_heads[:, 0], grad_keys).reshape(COLS, D) * EIGHTH
    key_part = jnp.concatenate((grad_query, outer(grad_text_keys, text)), axis=0).astype(bf16).reshape(4, 2, 48, D)
    grad_pair = jnp.concatenate((grad_text_keys, grad_text_values), axis=1)
    text_part = dot(grad_pair, whole(pair_t, pair_got)).astype(bf16).reshape(8, 8, D)

    (input_grad, joined_grad, key_grad, parts, text_grad), ((layer_output,),) = leave(
        6,
        grad_qkv,
        joined,
        x,
        vectors,
        grad_one,
        (joined_part, key_part),
        late,
        text_part,
        [Relay(layer_output, True)],
    )
    joined_grad, key_grad, value_grad, expand_grad, contract_grad = (
        grad.reshape(-1, HALF).astype(f32) for grad in (joined_grad, key_grad, value_grad, expand_grad, contract_grad)
    )
    return (
        layer_output,
        input_grad.astype(f32),
        text_grad.reshape(2, 64, HALF).astype(f32),
        parts[0],
        parts[1],
        joined_grad[:COLS].T,
        joined_grad[COLS : 2 * COLS].T,
        joined_grad[2 * COLS :].T,
        value_grad[2 * COLS :],
        parts[2],
        parts[3],
        key_grad[:COLS].T,
        key_grad[COLS:].T,
        value_grad[COLS : 2 * COLS].T,
        value_grad[:COLS],
        parts[4],
        parts[5],
        expand_grad,
        contract_grad,
    )


def solution(mesh):
    return jax.shard_map(
        on_device,
        mesh=mesh,
        in_specs=(
            P(("dp", "wide"), "narrow"),
            P("dp", None, "narrow"),
            P(("dp", "wide"), "narrow"),
            P("narrow"),
            P("narrow"),
            P("narrow", "wide"),
            P("narrow", "wide"),
            P("narrow", "wide"),
            P("wide", "narrow"),
            P("narrow"),
            P("narrow"),
            P("narrow", "wide"),
            P("narrow", "wide"),
            P("narrow", "wide"),
            P("wide", "narrow"),
            P("narrow"),
            P("narrow"),
            P("narrow", "wide"),
            P("wide", "narrow"),
        ),
        out_specs=(
            P(("dp", "wide"), "narrow"),
            P(("dp", "wide"), "narrow"),
            P("dp", None, "narrow"),
            P("narrow"),
            P("narrow"),
            P("narrow", "wide"),
            P("narrow", "wide"),
            P("narrow", "wide"),
            P("wide", "narrow"),
            P("narrow"),
            P("narrow"),
            P("narrow", "wide"),
            P("narrow", "wide"),
            P("narrow", "wide"),
            P("wide", "narrow"),
            P("narrow"),
            P("narrow"),
            P("narrow", "wide"),
            P("wide", "narrow"),
        ),
        check_vma=False,
    )
```

```python
import functools
import math

import jax
import jax.numpy as jnp
from jax import lax
from jax.experimental import pallas as pl
from jax.experimental.pallas import tpu as pltpu
from jax.sharding import PartitionSpec as P

D = 1536
HALF = 768
HDIM = 64
HEADS = 3
COLS = HEADS * HDIM
BLOCK = 192
EPSILON = 1e-05
NEGATIVE = -1e30
ROOT_HALF = 0.7071067811865476
GAUSS_NORM = 0.3989422804014327
MESH = pl.DeviceIdType.MESH
VMEM = pltpu.VMEM
ANY = pl.ANY
bf16, f32 = jnp.bfloat16, jnp.float32


def dot(a, b):
    return lax.dot_general(a, b, (((1,), (0,)), ((), ())), preferred_element_type=f32)


def dot_flip(a, b):
    return lax.dot_general(a, b, (((1,), (1,)), ((), ())), preferred_element_type=f32)


def outer(a, b):
    return lax.dot_general(a, b, (((0,), (0,)), ((), ())), preferred_element_type=f32)


class Place:
    def __init__(self):
        self.dp, self.w, self.n = (lax.axis_index(a) for a in ("dp", "wide", "narrow"))
        self.y, self.c = lax.div(self.w, 2), lax.rem(self.w, 2)
        self.z, self.s = lax.div(self.dp, 2), lax.rem(self.dp, 2)
        self.up, self.down = lax.rem(self.y + 1, 4), lax.rem(self.y + 3, 4)
        self.across = 3 - self.y
        self.moved = lax.rem(lax.div(self.y, 2) + self.n, 2)
        self.clip = lax.div(self.y, 2)

    def spot(self, y, c):
        moved = lax.rem(lax.div(y, 2) + self.n, 2)
        return (lax.rem(y + moved, 2) * 2 + c) * 2 + moved

    def rows(self, y, c, start=0, size=BLOCK):
        return pl.ds(pl.multiple_of(self.spot(y, c) * BLOCK + start, 32), size)

    def half(self, n):
        return pl.ds(pl.multiple_of(n * HALF, HALF), HALF)

    def at_y(self, y):
        return {"wide": y * 2 + self.c}

    def core(self):
        return {"wide": self.y * 2 + 1 - self.c}

    def x(self):
        return {"narrow": 1 - self.n}

    def at_z(self, k):
        return {"dp": lax.rem(self.z + k, 4) * 2 + self.s}

    def at_dp(self, k):
        return {"dp": lax.rem(self.dp + k, 8)}

    def at_x(self, ds, dn):
        return {"dp": self.z * 2 + lax.rem(self.s + ds, 2), "narrow": lax.rem(self.n + dn, 2)}


def remote(src, dst, send, recv, peer):
    return pltpu.make_async_remote_copy(
        src_ref=src, dst_ref=dst, send_sem=send, recv_sem=recv, device_id=peer, device_id_type=MESH
    )


def greet(peers):
    barrier = pltpu.get_barrier_semaphore()
    for peer in peers:
        pl.semaphore_signal(barrier, inc=1, device_id=peer, device_id_type=MESH)
    pl.semaphore_wait(barrier, len(peers))


class Give:
    def __init__(self, array):
        self.ins, self.copies, self.locals = [array], 1, 0
        self.outs = [jax.ShapeDtypeStruct(array.shape, array.dtype)]

    def peers(self, at):
        return [("x", at.x())]

    def moves(self, at, ins, outs):
        return [(ins[0], outs[0], at.x())], []


class GiveClip(Give):
    def __init__(self, array):
        super().__init__(array)
        self.outs = [jax.ShapeDtypeStruct(array.shape[1:], array.dtype)]

    def moves(self, at, ins, outs):
        return [(ins[0].at[1 - at.n], outs[0], at.x())], []


class ToSpots:
    def __init__(self, array):
        self.ins, self.copies, self.locals = [array], 7, 1
        self.outs = [jax.ShapeDtypeStruct((8, *array.shape), array.dtype)]

    def peers(self, at):
        return [(f"w{k}", {"wide": lax.rem(at.w + k, 8)}) for k in range(1, 8)]

    def moves(self, at, ins, outs):
        dst = outs[0].at[at.spot(at.y, at.c)]
        return [(ins[0], dst, peer) for _, peer in self.peers(at)], [(ins[0], dst)]


class Relay:
    def __init__(self, array, back=False):
        self.ins, self.back, self.copies, self.locals = [array], back, 2, 1
        shape = (384, HALF) if back else (BLOCK, D)
        self.outs = [jax.ShapeDtypeStruct(shape, array.dtype)]

    def peers(self, at):
        return [
            ("x", at.x()),
            ("a0", {"wide": at.across * 2 + at.c}),
            ("a1", {"wide": at.across * 2 + at.c, "narrow": 1 - at.n}),
        ]


def relay_run(relay, at, src, dst, send, recv, local, base, finish):
    mine, other = at.half(at.n), at.half(1 - at.n)
    over = at.across * 2 + at.c
    if relay.back:
        row = pl.ds(pl.multiple_of(at.moved * BLOCK, BLOCK), BLOCK)
        to = recv.at[base + at.moved]
        own = src.at[:, mine], src.at[:, other]
        land = dst.at[0:BLOCK], dst.at[BLOCK : 2 * BLOCK]
    else:
        row = mine
        to = recv.at[base + at.n]
        own = src.at[0:BLOCK], src.at[BLOCK : 2 * BLOCK]
        land = dst.at[:, at.half(0)], dst.at[:, at.half(1)]
    target = dst.at[row] if relay.back else dst.at[:, row]

    def arrive(slot, part):
        return remote(own[0], part, send.at[base], recv.at[base + slot], at.x())

    @pl.when(at.moved == 0)
    def _():
        stay = pltpu.make_async_copy(own[0], target, local)
        if relay.back:
            go = remote(own[1], target, send.at[base], to, at.x())
        else:
            go = remote(own[1], target, send.at[base], to, {"wide": over})
        if not finish:
            go.start()
            stay.start()
        else:
            stay.wait()
            go.wait_send()
            if relay.back:
                arrive(1, land[1]).wait_recv()
            else:
                arrive(1 - at.n, dst.at[:, other]).wait_recv()

    @pl.when(at.moved == 1)
    def _():
        if relay.back:
            first = remote(own[1], target, send.at[base], to, {"wide": over, "narrow": 1 - at.n})
            second = remote(own[0], target, send.at[base + 1], to, {"wide": over})
        else:
            first = remote(own[1], target, send.at[base], to, {"wide": over, "narrow": 1 - at.n})
            second = remote(own[0], target, send.at[base + 1], to, at.x())
        if not finish:
            first.start()
            second.start()
        else:
            first.wait_send()
            second.wait_send()
            arrive(0, land[0]).wait_recv()
            arrive(1, land[1]).wait_recv()


def call(body, number, ins, outs, scratch=(), beside=(), peers=None, spaces=None, out_spaces=None, late=False):
    spaces = spaces or [VMEM] * len(ins)
    out_spaces = out_spaces or [VMEM] * len(outs)
    copies = sum(b.copies for b in beside)
    locals_ = sum(b.locals for b in beside)
    side_ins = [a for b in beside for a in b.ins]
    side_outs = [a for b in beside for a in b.outs]
    n_in, n_out, n_scratch = len(ins), len(outs), len(scratch)
    loaded = [i for i, m in enumerate(spaces) if m is VMEM]
    stored = [i for i, m in enumerate(out_spaces) if m is VMEM]
    buffers = [VMEM(ins[i].shape, ins[i].dtype) for i in loaded] + [VMEM(outs[i].shape, outs[i].dtype) for i in stored]

    def kernel(*refs):
        at = Place()
        refs = list(refs)

        def take(count):
            out = refs[:count]
            del refs[:count]
            return out

        main_in, side_in = take(n_in), take(len(side_ins))
        main_out, side_out, kept = take(n_out), take(len(side_outs)), take(n_scratch)
        in_buffers, out_buffers = take(len(loaded)), take(len(stored))
        send, recv, local, passing = take(4)
        loads, stores = [], {}
        for k, i in enumerate(loaded):
            loads.append(pltpu.make_async_copy(main_in[i], in_buffers[k], passing.at[k]))
            loads[-1].start()
            main_in[i] = in_buffers[k]
        for k, i in enumerate(stored):
            stores[i] = pltpu.make_async_copy(out_buffers[k], main_out[i], passing.at[len(loaded) + k])
            main_out[i] = out_buffers[k]
        waiting = dict(stores)

        def flush(*which):
            for i in which or list(waiting):
                waiting.pop(i).start()

        at.flush = flush
        known = dict(peers(at)) if peers else {}
        for b in beside:
            known.update(dict(b.peers(at)))
        if "w1" in known:
            for name in ("up", "down", "core", "a0"):
                known.pop(name, None)
        if "x01" in known:
            known.pop("x", None)
        if known:
            greet(list(known.values()))
        side_refs = [([side_in.pop(0) for _ in b.ins], [side_out.pop(0) for _ in b.outs]) for b in beside]
        begin, todo = [], []
        slot, place = 0, 0
        for b, (i, o) in zip(beside, side_refs):
            if isinstance(b, Relay):
                run = functools.partial(relay_run, b, at, i[0], o[0], send, recv, local.at[place], slot)
                begin.append(functools.partial(run, False))
                todo.append(functools.partial(run, True))
                slot, place = slot + 2, place + 1
                continue
            far, near = b.moves(at, i, o)
            for src, dst, peer in far:
                copy = remote(src, dst, send.at[slot], recv.at[slot], peer)
                begin.append(copy.start)
                todo.append(copy.wait)
                slot += 1
            for src, dst in near:
                copy = pltpu.make_async_copy(src, dst, local.at[place])
                begin.append(copy.start)
                todo.append(copy.wait)
                place += 1

        def start():
            for go in begin:
                go()

        at.start_beside = start
        if not late:
            start()
        for copy in loads:
            copy.wait()
        if body:
            body(at, main_in, main_out, kept)
        flush()
        for wait in todo:
            wait()
        for copy in stores.values():
            copy.wait()

    results = pl.pallas_call(
        kernel,
        out_shape=tuple(outs) + tuple(side_outs),
        in_specs=[pl.BlockSpec(memory_space=VMEM if m == PLAIN else ANY) for m in spaces]
        + [pl.BlockSpec(memory_space=ANY)] * len(side_ins),
        out_specs=(pl.BlockSpec(memory_space=ANY),) * (len(outs) + len(side_outs)),
        scratch_shapes=[
            *scratch,
            *buffers,
            pltpu.SemaphoreType.DMA((max(copies, 1),)),
            pltpu.SemaphoreType.DMA((max(copies, 1),)),
            pltpu.SemaphoreType.DMA((max(locals_, 1),)),
            pltpu.SemaphoreType.DMA((max(len(buffers), 1),)),
        ],
        compiler_params=pltpu.CompilerParams(
            collective_id=number, has_side_effects=True, vmem_limit_bytes=58 << 20
        ),
    )(*ins, *side_ins)
    results = list(results)
    main, rest = results[: len(outs)], results[len(outs) :]
    sides = []
    for b in beside:
        sides.append(rest[: len(b.outs)])
        del rest[: len(b.outs)]
    return main, sides


PLAIN = "plain"


def ring_peers(at):
    return [("up", at.at_y(at.up)), ("down", at.at_y(at.down)), ("core", at.core())]


def sems(count):
    return [pltpu.SemaphoreType.DMA((count,)), pltpu.SemaphoreType.DMA((count,)), pltpu.SemaphoreType.DMA((count,))]


def by_rows(count, size, work, carry=None):
    def step(i, carry):
        return work(pl.ds(pl.multiple_of(i * size, size), size), carry)

    return lax.fori_loop(0, count // size, step, carry)


class Whole:
    def __init__(self, at, own, got, full, sem, axis):
        size = own.shape[axis]
        self.copies = []
        for i, (part, n) in enumerate(((own, at.n), (got, 1 - at.n))):
            where = pl.ds(pl.multiple_of(n * size, size), size)
            target = full.at[where] if axis == 0 else full.at[:, where]
            self.copies.append(pltpu.make_async_copy(part, target, sem.at[i]))
            self.copies[-1].start()

    def wait(self):
        for copy in self.copies:
            copy.wait()


class Trade:
    def __init__(self, at, parts, out, send, recv, local, base):
        self.at, self.parts, self.out, self.send, self.recv, self.base = at, parts, out, send, recv, base
        self.me = at.spot(at.y, at.c)
        self.own = pltpu.make_async_copy(parts.at[self.me], out.at[self.me], local)

    @staticmethod
    def peers(at):
        return [(f"w{k}", {"wide": lax.rem(at.w + k, 8)}) for k in range(1, 8)]

    def copy(self, b, place):
        m, core, a = lax.rem(b, 2), lax.rem(lax.div(b, 2), 2), lax.div(b, 4)
        y = 2 * lax.rem(m + self.at.n, 2) + lax.rem(a + m, 2)
        send, recv = self.send.at[self.base + b], self.recv.at[self.base + place]
        return remote(self.parts.at[b], self.out.at[place], send, recv, {"wide": y * 2 + core})

    def give(self, b):
        @pl.when(b == self.me)
        def _():
            self.own.start()

        @pl.when(b != self.me)
        def _():
            self.copy(b, self.me).start()

    def end(self):
        def wait(b, carry):
            @pl.when(b == self.me)
            def _():
                self.own.wait()

            @pl.when(b != self.me)
            def _():
                self.copy(b, b).wait()

            return carry

        lax.fori_loop(0, 8, wait, 0)


class Reduce:
    @staticmethod
    def scratch(deep, x_first, by_rows=False):
        first = (4, deep, HALF) if x_first else (2, 2, deep, HALF) if by_rows else (2, deep, D)
        return [VMEM((3, *first), bf16), VMEM(first, bf16), VMEM((3, deep, HALF), bf16), VMEM((2, deep, HALF), bf16)]

    @staticmethod
    def peers(at):
        return [(f"z{k}", at.at_z(k)) for k in (1, 2, 3)] + [(f"x{a}{b}", at.at_x(a, b)) for a, b in ((0, 1), (1, 0), (1, 1))]

    def __init__(self, at, src, out, refs, send, recv, local, base, place, x_first, by_rows=False):
        self.at, self.src, self.out = at, src, out
        self.land, self.total, self.land_two, self.last = refs
        self.x_first, self.by_rows = x_first, by_rows
        self.deep = self.last.shape[1]
        self.chunk = 32 if self.deep % 32 == 0 else 24
        z_steps = [(at.at_z(k), lax.rem(at.z + k, 4)) for k in (1, 2, 3)]
        x_steps = [
            (at.at_x(a, b), (lax.rem(at.s + a, 2), lax.rem(at.n + b, 2))) for a, b in ((0, 1), (1, 0), (1, 1))
        ]
        first, second = (x_steps, z_steps) if x_first else (z_steps, x_steps)

        def move(slot, source, target, peer):
            return remote(source, target, send.at[base + slot], recv.at[base + slot], peer)

        self.one = [move(i, self.piece(where), self.land.at[i], peer) for i, (peer, where) in enumerate(first)]
        self.own = pltpu.make_async_copy(
            self.piece((at.s, at.n) if x_first else at.z), self.total, local.at[place]
        )
        self.two = [move(3 + i, self.part(where), self.land_two.at[i], peer) for i, (peer, where) in enumerate(second)]
        self.mine = at.z if x_first else (at.s, at.n)
        self.three = move(6, self.last.at[at.s], self.last.at[at.s], at.at_x(1, 0))
        target = out.at[at.z]
        self.four = [move(7 + i, self.last, target, peer) for i, (peer, _) in enumerate(z_steps)]
        self.stay = pltpu.make_async_copy(self.last, target, local.at[place + 1])

    def piece(self, where):
        if self.x_first:
            s, n = where
            return self.src.at[n, :, s] if self.by_rows else self.src.at[:, s, :, self.at.half(n)]
        return self.src.at[:, where] if self.by_rows else self.src.at[where]

    def part(self, where):
        if self.x_first:
            return self.total.at[where]
        s, n = where
        return self.total.at[n, s] if self.by_rows else self.total.at[s, :, self.at.half(n)]

    def first(self):
        for copy in self.one + [self.own]:
            copy.start()

    def second(self):
        self.own.wait()
        for copy in self.one:
            copy.wait_recv()
        lead = self.total.shape[:-2]
        count = math.prod(lead)

        def add(i, carry):
            at_lead = (i,) if len(lead) == 1 else (lax.div(i, lead[1]), lax.rem(i, lead[1]))
            for start in range(0, self.deep, self.chunk):
                where = (*at_lead, slice(start, start + self.chunk))
                got = self.total[where].astype(f32)
                for k in range(3):
                    got += self.land[(k, *where)].astype(f32)
                self.total[where] = got.astype(bf16)
            return carry

        lax.fori_loop(0, count, add, 0)
        for copy in self.two:
            copy.start()

    def third(self):
        for copy in self.two:
            copy.wait_recv()
        own = self.part(self.mine)
        s = self.at.s
        for start in range(0, self.deep, self.chunk):
            rows = slice(start, start + self.chunk)
            got = own[rows].astype(f32)
            for k in range(3):
                got += self.land_two[k, rows].astype(f32)
            self.last[s, rows] = got.astype(bf16)
        self.three.start()

    def fourth(self):
        self.three.wait_recv()
        for copy in self.four + [self.stay]:
            copy.start()

    def end(self):
        for copy in self.four:
            copy.wait()
        for copy in self.one + self.two + [self.three]:
            copy.wait_send()
        self.stay.wait()


class Gather:
    slots = 11

    def __init__(self, at, x, whole, send, recv, local, base=0):
        self.at, self.x, self.whole = at, x, whole
        y, c, up, down = at.y, at.c, at.up, at.down
        far = lax.rem(y + 2, 4)
        half = BLOCK // 2

        def move(slot, y_from, peer, start=0, size=BLOCK, first=False):
            rows = at.rows(y_from, c, start, size)
            src = whole.at[rows]
            if first:
                src = x if size == BLOCK else x.at[start : start + size]
            return remote(src, whole.at[rows], send.at[base + slot], recv.at[base + slot], peer)

        to_up, to_down, core = at.at_y(up), at.at_y(down), at.core()
        self.sends = [
            move(0, y, to_up, 0, half, first=True),
            move(1, y, to_up, half, half, first=True),
            move(2, y, to_down, half, half, first=True),
            move(3, y, to_down, 0, half, first=True),
            move(4, y, core, first=True),
            move(5, down, to_up, 0, half),
            move(6, up, to_down, half, half),
            move(7, down, core),
            move(8, up, core),
            move(9, far, core, 0, half),
            move(10, far, core, half, half),
        ]
        self.own = pltpu.make_async_copy(x, whole.at[at.rows(y, c)], local)

    def begin(self):
        for i in (0, 2, 1, 3, 4):
            self.sends[i].start()
        self.own.start()
        self.own.wait()

    def chain(self, *pairs):
        for arrived, leaving in pairs:
            self.sends[arrived].wait_recv()
            self.sends[leaving].start()

    def pass_on(self):
        self.chain((0, 5), (2, 6))

    def pass_near(self):
        self.chain((1, 7), (3, 8))

    def pass_far(self):
        self.chain((5, 9), (6, 10))

    def got(self, *slots):
        for i in slots:
            self.sends[i].wait_recv()

    def end(self):
        for copy in self.sends:
            copy.wait_send()

    def finish(self):
        self.pass_on()
        self.pass_near()
        self.pass_far()
        self.got(4, 7, 8, 9, 10)
        self.end()

    def each(self, work):
        at = self.at

        def step(s, carry):
            @pl.when(s == 1)
            def _():
                self.got(4)
                self.pass_on()

            @pl.when(s == 2)
            def _():
                self.pass_near()

            @pl.when(s == 3)
            def _():
                self.got(8)

            @pl.when(s == 5)
            def _():
                self.got(7)

            @pl.when(s == 6)
            def _():
                self.pass_far()

            @pl.when(s == 7)
            def _():
                self.got(9, 10)

            work(s, self.place(s))
            return carry

        lax.fori_loop(0, 8, step, 0)
        self.end()

    def place(self, s):
        g = lax.div(s, 2)
        off = g + lax.div(g, 2) - 2 * lax.div(g, 3)
        return self.at.rows(lax.rem(self.at.y + off, 4), lax.rem(self.at.c + s, 2))


QUARTER = 384


class GatherZ(Gather):
    def __init__(self, at, quarter, full, send, recv, local, base=0):
        self.at = at
        z, up, down, far = at.z, lax.rem(at.z + 1, 4), lax.rem(at.z + 3, 4), lax.rem(at.z + 2, 4)
        half = QUARTER

        def move(slot, z_from, peer, start=0, size=2 * QUARTER, first=False):
            rows = pl.ds(pl.multiple_of(at.c * 2 * QUARTER + start, QUARTER), size)
            target = full.at[rows, self.columns(z_from)]
            return remote(quarter.at[rows] if first else target, target, send.at[base + slot], recv.at[base + slot], peer)

        to_up, to_down, core = at.at_z(1), at.at_z(3), at.core()
        self.sends = {
            0: move(0, z, to_up, 0, half, first=True),
            1: move(1, z, to_up, half, half, first=True),
            2: move(2, z, to_down, half, half, first=True),
            3: move(3, z, to_down, 0, half, first=True),
            5: move(5, down, to_up, 0, half),
            6: move(6, up, to_down, half, half),
            7: move(7, down, core),
            8: move(8, up, core),
            9: move(9, far, core, 0, half),
            10: move(10, far, core, half, half),
        }
        self.own = pltpu.make_async_copy(quarter, full.at[:, self.columns(z)], local)

    @staticmethod
    def columns(z):
        return pl.ds(pl.multiple_of(z * QUARTER, QUARTER), QUARTER)

    @staticmethod
    def peers(at):
        return [("z1", at.at_z(1)), ("z3", at.at_z(3)), ("core", at.core())]

    def begin(self):
        for i in (0, 2, 1, 3):
            self.sends[i].start()
        self.own.start()

    def end(self):
        self.got(7, 8, 9, 10)
        self.own.wait()
        for copy in self.sends.values():
            copy.wait_send()


class Scatter:
    slots = 10
    scratch = [
        VMEM((4, BLOCK, D), bf16),
        VMEM((4, BLOCK, D), bf16),
        VMEM((4, BLOCK, D), f32),
        VMEM((2, BLOCK, D), bf16),
        VMEM((2, BLOCK, D), bf16),
        VMEM((2, BLOCK // 2, D), bf16),
        VMEM((2, BLOCK // 2, D), bf16),
    ]

    def __init__(self, at, send, recv, refs, base=0):
        self.at, self.send, self.recv, self.base = at, send, recv, base
        self.out_c, self.in_c, self.own, self.out_y, self.in_y, self.half_out, self.half_in = refs
        half = BLOCK // 2
        peers = at.at_y(at.up), at.at_y(at.down)

        def move(slot, src, dst, peer):
            return remote(src, dst, send.at[base + slot], recv.at[base + slot], peer)

        self.cores = [self.core(g) for g in range(4)]
        self.halves = [move(4 + i, self.half_out.at[i], self.half_in.at[i], peers[i]) for i in range(2)]
        free = [pl.ds((1 - i) * half, half) for i in range(2)]
        bound = [pl.ds(i * half, half) for i in range(2)]
        self.free = [move(6 + i, self.out_y.at[i, free[i]], self.in_y.at[i, free[i]], peers[i]) for i in range(2)]
        self.bound = [move(8 + i, self.out_y.at[i, bound[i]], self.in_y.at[i, bound[i]], peers[i]) for i in range(2)]

    def core(self, g):
        slot = self.base + g
        return remote(self.out_c.at[g], self.in_c.at[g], self.send.at[slot], self.recv.at[slot], self.at.core())

    def both(self, g, rows):
        return self.own[g, rows] + self.in_c[g, rows].astype(f32)

    def products(self, product):
        at = self.at
        half = BLOCK // 2

        def part_rows(rows, i):
            return pl.ds(pl.multiple_of(rows.start + i * half, 32), 32)

        def send_free(i):
            self.cores[1 + i].wait_recv()

            def add(rows, carry):
                there = part_rows(rows, 1 - i)
                self.out_y[i, there] = self.both(1 + i, there).astype(bf16)

            by_rows(half, 32, add)
            self.free[i].start()

        def step(s, carry):
            g = lax.div(s, 2)
            off = lax.rem(6 - g + 3 * lax.div(g, 2) + 2 * lax.div(g, 3), 4)
            part = product(at.rows(lax.rem(at.y + off, 4), lax.rem(at.c + 1 + s, 2)))

            @pl.when(lax.rem(s, 2) == 0)
            def _():
                self.out_c[g] = part.astype(bf16)
                self.core(g).start()

            @pl.when(lax.rem(s, 2) == 1)
            def _():
                self.own[g] = part

            @pl.when(s == 2)
            def _():
                self.cores[0].wait_recv()
                for i in range(2):

                    def add(rows, carry, i=i):
                        self.half_out[i, rows] = self.both(0, part_rows(rows, i)).astype(bf16)

                    by_rows(half, 32, add)
                    self.halves[i].start()

            @pl.when(s == 4)
            def _():
                send_free(0)

            @pl.when(s == 6)
            def _():
                send_free(1)

            return carry

        lax.fori_loop(0, 8, step, 0)

    def middle(self):
        half = BLOCK // 2
        for i in range(2):
            self.halves[i].wait_recv()

            def add(rows, carry, i=i):
                here = pl.ds(pl.multiple_of(rows.start + i * half, 32), 32)
                self.out_y[i, here] = (self.both(1 + i, here) + self.half_in[i, rows].astype(f32)).astype(bf16)

            by_rows(half, 32, add)
            self.bound[i].start()

    def arrive(self):
        self.cores[3].wait_recv()
        for copy in self.free + self.bound:
            copy.wait_recv()

    def total(self, rows):
        return self.both(3, rows) + self.in_y[0, rows].astype(f32) + self.in_y[1, rows].astype(f32)

    def end(self):
        for copy in self.cores + self.halves + self.free + self.bound:
            copy.wait_send()


def standard(values):
    average = jnp.mean(values, axis=1, keepdims=True)
    variance = jnp.mean(values * values, axis=1, keepdims=True) - average * average
    factor = lax.rsqrt(variance + EPSILON)
    return (values - average) * factor, factor


def norm_back(incoming, centred, factor, gain):
    scaled = incoming * gain
    first = jnp.mean(scaled, axis=1, keepdims=True)
    second = jnp.mean(scaled * centred, axis=1, keepdims=True)
    return factor * (scaled - first - centred * second)


def two_sums(incoming, centred, carry):
    gains, shifts = carry
    return gains + jnp.sum(incoming * centred, axis=0, keepdims=True), shifts + jnp.sum(incoming, axis=0, keepdims=True)


def no_sums():
    return jnp.zeros((1, D), f32), jnp.zeros((1, D), f32)


EIGHTH = 0.125


def shape(*dims, dtype=bf16):
    return jax.ShapeDtypeStruct(dims, dtype)


class Keep:
    def __init__(self, whole, out, sem, base):
        self.whole, self.out, self.sem, self.base = whole, out, sem, base

    def block(self, s, rows):
        pltpu.make_async_copy(self.whole.at[rows], self.out.at[rows], self.sem.at[self.base + s]).start()

    def wait(self):
        for s in range(8):
            some = pl.ds(0, BLOCK)
            pltpu.make_async_copy(self.whole.at[some], self.out.at[some], self.sem.at[self.base + s]).wait()


def enter(number, layer_input, gains, weights, query_t, cross_out, texts, pair_t, beside):
    relay = Relay(layer_input)

    def body(at, ins, outs, kept):
        source, *gains = ins[:7]
        *own_weights, query_own, out_own, own_texts, pair = ins[7:]
        x, vectors, weight, all_rows, qkv, query_all, out_quarter, text_pair = outs
        normed, whole, query_part, out_part, query_quarter, text_parts, text_got, own_vectors, send, recv, local = kept
        half = at.half(at.n)
        moving = functools.partial(relay_run, relay, at, source, x, send, recv, local.at[0], 11)
        moving(False)
        own_vectors[...] = jnp.zeros_like(own_vectors)
        for i, ref in enumerate(gains):
            own_vectors[i : i + 1] = ref[...].astype(f32).reshape(1, HALF)
        columns = GatherZ.columns(lax.rem(at.z, 2))
        holds = at.n == lax.div(at.z, 2)
        quarters = []
        for i, (own, part) in enumerate(((query_own, query_part), (out_own, out_part))):
            quarters.append(
                (
                    pltpu.make_async_copy(own.at[:, columns], part, local.at[14 + i]),
                    remote(own.at[:, columns], part, send.at[17 + i], recv.at[17 + i], at.x()),
                )
            )

        @pl.when(holds)
        def _():
            for stay, go in quarters:
                go.start()
                stay.start()

        stay, go = [], []
        for i, (own, target) in enumerate(
            [(own_vectors, vectors.at[:, half])]
            + [(own, weight.at[j * COLS : (j + 1) * COLS, half]) for j, own in enumerate(own_weights)]
        ):
            stay.append(pltpu.make_async_copy(own, target, local.at[1 + i]))
            go.append(remote(own, target, send.at[13 + i], recv.at[13 + i], at.x()))
        stay[0].start()
        go[0].start()

        @pl.when(holds)
        def _():
            for near, far in quarters:
                near.wait()
                far.wait_send()

        @pl.when(jnp.logical_not(holds))
        def _():
            for near, far in quarters:
                far.wait_recv()

        for clip in range(2):
            text_parts[clip] = dot_flip(own_texts[clip], pair[...])
        text_go = remote(text_parts.at[1 - at.n], text_got, send.at[52], recv.at[52], at.x())
        text_go.start()
        queries = Gather(at, query_part, query_quarter, send, recv, local.at[16], 19)
        outputs = Gather(at, out_part, out_quarter, send, recv, local.at[17], 30)
        queries.begin()
        stay[0].wait()
        go[0].wait_recv()
        moving(True)
        for copy in stay[1:] + go[1:]:
            copy.start()
        queries.pass_on()
        queries.pass_near()

        def norm(rows, carry):
            centred, _ = standard(x[rows].astype(f32))
            normed[rows] = (centred * vectors[0:1] + vectors[1:2]).astype(bf16)

        by_rows(BLOCK, 32, norm)
        gather = Gather(at, normed, whole, send, recv, local.at[5])
        gather.begin()
        queries.pass_far()
        queries.got(4, 7, 8, 9, 10)
        around = GatherZ(at, query_quarter, query_all, send, recv, local.at[18], 41)
        around.begin()
        keep = Keep(whole, all_rows, local, 6)

        def times(rows):
            qkv[rows] = dot_flip(whole[rows], weight[...]).astype(bf16)

        def work(s, rows):
            keep.block(s, rows)

            @pl.when(s == 4)
            def _():
                for copy in stay[1:]:
                    copy.wait()
                for copy in go[1:]:
                    copy.wait_recv()
                at.start_beside()
                at.flush(0, 1, 2)

            @pl.when(s >= 4)
            def _():
                times(rows)

            @pl.when(s == 6)
            def _():
                outputs.begin()
                around.pass_on()

        gather.each(work)
        around.pass_near()
        outputs.pass_on()
        outputs.pass_near()

        def rest(s, carry):
            times(gather.place(s))
            return carry

        lax.fori_loop(0, 4, rest, 0)
        at.flush(4)
        outputs.pass_far()
        around.pass_far()
        text_go.wait()
        text_pair[...] = (text_parts[at.n] + text_got[...]).astype(bf16)
        outputs.got(4, 7, 8, 9, 10)
        keep.wait()
        for copy in go:
            copy.wait_send()
        outputs.end()
        queries.end()
        around.end()

    return call(
        body,
        number,
        [layer_input, *gains, *weights, query_t, cross_out, texts, pair_t],
        [
            shape(BLOCK, D),
            shape(8, D, dtype=f32),
            shape(3 * COLS, D),
            shape(D, D),
            shape(D, 3 * COLS),
            shape(D, D),
            shape(D, QUARTER),
            shape(64, 2 * COLS),
        ],
        [
            VMEM((BLOCK, D), bf16),
            VMEM((D, D), bf16),
            VMEM((COLS, QUARTER), bf16),
            VMEM((COLS, QUARTER), bf16),
            VMEM((D, QUARTER), bf16),
            VMEM((2, 64, 2 * COLS), f32),
            VMEM((64, 2 * COLS), f32),
            VMEM((8, HALF), f32),
            *sems(53),
        ],
        beside,
        lambda at: ring_peers(at) + relay.peers(at) + [("x", at.x())] + GatherZ.peers(at),
        spaces=[ANY] + [PLAIN] * 6 + [VMEM] * 7,
        out_spaces=[VMEM, VMEM, VMEM, ANY, VMEM, ANY, VMEM, VMEM],
        late=True,
    )


def causal_forward(number, joined, down, out_quarter, beside):
    at_once = 512

    def body(at, ins, outs, kept):
        (qkv, block, quarter), (out, logs, all_down, out_all) = ins, outs
        parts, mixed, send, recv, local = kept
        first = Gather(at, block, all_down, send, recv, local.at[0])
        second = GatherZ(at, quarter, out_all, send, recv, local.at[1], 11)
        second.begin()
        first.begin()
        for i in range(3):
            for h in range(HEADS):
                a = i * COLS + h * HDIM
                piece = qkv[:, a : a + HDIM]
                parts[i, h] = piece * EIGHTH if i == 0 else piece
        square = (at_once, at_once)
        seen = lax.broadcasted_iota(jnp.int32, square, 0) >= lax.broadcasted_iota(jnp.int32, square, 1)

        def one(h, carry):
            for i in reversed(range(D // at_once)):
                before, upto = i * at_once, (i + 1) * at_once
                rows = slice(before, upto)
                scores = dot_flip(parts[0, h, rows], parts[1, h, 0:upto])
                last = jnp.where(seen, scores[:, before:], NEGATIVE)
                scores = jnp.concatenate((scores[:, :before], last), axis=1) if i else last
                peak = jnp.max(scores, axis=1, keepdims=True)
                raised = jnp.exp(scores - peak)
                total = jnp.sum(raised, axis=1, keepdims=True)
                mixed[h, rows] = (dot(raised.astype(bf16), parts[2, h, 0:upto]) / total).astype(bf16)
                column = jnp.broadcast_to(peak + jnp.log(total), (at_once, 128))
                logs[pl.ds(h, 1), rows] = column.T[0:1, :]

            @pl.when(h == 1)
            def _():
                first.pass_on()
                second.pass_on()

            return carry

        lax.fori_loop(0, HEADS, one, 0)
        first.pass_near()
        second.pass_near()
        out[...] = jnp.concatenate([mixed[h] for h in range(HEADS)], axis=1)
        at.flush()
        first.pass_far()
        second.pass_far()
        first.got(4, 7, 8, 9, 10)
        first.end()
        second.end()

    return call(
        body,
        number,
        [joined, down, out_quarter],
        [shape(D, COLS), shape(8, D, dtype=f32), shape(D, D), shape(D, D)],
        [VMEM((3, HEADS, D, HDIM), bf16), VMEM((HEADS, D, HDIM), bf16), *sems(22)],
        beside,
        lambda at: ring_peers(at) + GatherZ.peers(at),
        out_spaces=[VMEM, VMEM, ANY, ANY],
    )


def forward_rest(number, attended, out_w, x, vectors, query_all, out_all, texts, all_down, expand_w, contract):
    def body(at, ins, outs, kept):
        mixed, out_own, out_got, x, vectors, query_all, out_all, texts, all_down, expand_own, expand_got, contract_own = ins
        middle, after, normed_two, weights, all_rows, activated, grad, contract_out, keys_out, values_out, traded = outs
        *refs, normed, whole, downs, out_full, expand_full, contract_full, key_full, value_full, branch, scores_all, send, recv, local = kept
        half = at.half(at.n)
        weight = Whole(at, out_own, out_got, out_full, local.at[pl.ds(0, 2)], 1)
        swap = remote(contract_own, contract_full.at[:, half], send.at[21], recv.at[21], at.x())
        swap.start()
        factors = [
            pltpu.make_async_copy(query_all, key_full, local.at[2]),
            pltpu.make_async_copy(out_all, value_full, local.at[3]),
        ]
        for copy in factors:
            copy.start()
        later = [
            pltpu.make_async_copy(contract_own, contract_full.at[:, half], local.at[4]),
            pltpu.make_async_copy(all_down, downs, local.at[7]),
        ]
        for copy in later:
            copy.start()
        later.append(Whole(at, expand_own, expand_got, expand_full, local.at[pl.ds(5, 2)], 0))
        weight.wait()
        scatter = Scatter(at, send, recv, refs)
        scatter.products(lambda rows: dot(mixed[rows], out_full[...]))
        for copy in factors:
            copy.wait()

        def make(b, carry):
            for h in range(HEADS):
                rows = pl.ds(pl.multiple_of(b * BLOCK + h * 64, 64), 64)
                text_keys = texts[b, :, h * HDIM : (h + 1) * HDIM]
                text_values = texts[b, :, COLS + h * HDIM : COLS + (h + 1) * HDIM]
                key_full[rows] = (dot(text_keys, key_full[rows]) * EIGHTH).astype(bf16)
                value_full[rows] = dot(text_values, value_full[rows]).astype(bf16)
            return carry

        lax.fori_loop(0, 8, make, 0)
        made = [
            pltpu.make_async_copy(key_full, keys_out, local.at[8]),
            pltpu.make_async_copy(value_full, values_out, local.at[9]),
        ]
        for copy in made:
            copy.start()
        scatter.middle()
        for copy in later:
            copy.wait()
        scatter.arrive()

        def norm_two(rows, carry):
            total = x[rows].astype(f32) + scatter.total(rows)
            middle[rows] = total
            centred, _ = standard(total)
            normed_two[rows] = (centred * vectors[2:3] + vectors[3:4]).astype(bf16)

        by_rows(BLOCK, 32, norm_two)

        trade = Trade(at, weights, traded, send, recv, local.at[20], 22)

        def score(rows, carry):
            scores_all[rows] = dot_flip(key_full[rows], normed_two[...])

        by_rows(D, QUARTER, score)

        def cross(b, carry):
            rows = pl.ds(pl.multiple_of(b * BLOCK, BLOCK), BLOCK)
            scores = scores_all[rows].reshape(HEADS, 64, BLOCK)
            raised = jnp.exp(scores - jnp.max(scores, axis=1, keepdims=True))
            p = raised / jnp.sum(raised, axis=1, keepdims=True)
            p = p.reshape(BLOCK, BLOCK).T.astype(bf16)
            weights[b] = p
            trade.give(b)
            part = dot(p, value_full[rows])

            @pl.when(b == 0)
            def _():
                branch[...] = part

            @pl.when(b > 0)
            def _():
                branch[...] += part

            return carry

        lax.fori_loop(0, 8, cross, 0)

        def norm_three(rows, carry):
            total = middle[rows] + branch[rows]
            after[rows] = total
            centred, _ = standard(total)
            normed[rows] = (centred * vectors[4:5] + vectors[5:6]).astype(bf16)

        by_rows(BLOCK, 32, norm_three)
        gather = Gather(at, normed, whole, send, recv, local.at[10], 10)
        gather.begin()
        at.flush(0, 1, 2, 3)
        swap.wait_recv()
        keep_contract = pltpu.make_async_copy(contract_full, contract_out, local.at[11])
        keep_contract.start()
        keep = Keep(whole, all_rows, local, 12)

        def ahead(rows, carry):
            grad[rows] = dot_flip(downs[rows], contract_full[...]).astype(bf16)

        by_rows(D, BLOCK, ahead)

        def work(s, rows):
            keep.block(s, rows)
            hidden = dot(whole[rows], expand_full[...])
            bell = 0.5 * (1.0 + lax.erf(hidden * ROOT_HALF))
            activated[rows] = (hidden * bell).astype(bf16)
            slope = bell + hidden * jnp.exp(-0.5 * hidden * hidden) * GAUSS_NORM
            grad[rows] = (grad[rows].astype(f32) * slope).astype(bf16)

        gather.each(work)
        at.flush()
        keep.wait()
        keep_contract.wait()
        trade.end()
        for copy in made:
            copy.wait()
        scatter.end()
        swap.wait_send()

    results, _ = call(
        body,
        number,
        [attended, *out_w, x, vectors, query_all, out_all, texts, all_down, *expand_w, contract],
        [
            shape(BLOCK, D, dtype=f32),
            shape(BLOCK, D, dtype=f32),
            shape(BLOCK, D),
            shape(8, BLOCK, BLOCK),
            shape(D, D),
            shape(D, HALF),
            shape(D, HALF),
            shape(HALF, D),
            shape(D, D),
            shape(D, D),
            shape(8, BLOCK, BLOCK),
        ],
        [
            *Scatter.scratch,
            VMEM((BLOCK, D), bf16),
            VMEM((D, D), bf16),
            VMEM((D, D), bf16),
            VMEM((COLS, D), bf16),
            VMEM((D, HALF), bf16),
            VMEM((HALF, D), bf16),
            VMEM((D, D), bf16),
            VMEM((D, D), bf16),
            VMEM((BLOCK, D), f32),
            VMEM((D, BLOCK), f32),
            *sems(30),
        ],
        (),
        lambda at: Trade.peers(at) + [("x", at.x())],
        spaces=[VMEM, ANY, ANY, VMEM, VMEM, ANY, ANY, VMEM, ANY, ANY, ANY, ANY],
        out_spaces=[VMEM, VMEM, VMEM, VMEM, ANY, VMEM, VMEM, ANY, ANY, ANY, ANY],
    )
    return results


def backward_rest(
    number, grad, expand_w, after, middle, vectors, down, keys, values, weights, out_w, contract_sum, expand_sum, beside
):
    def body(at, ins, outs, kept):
        grad, expand_own, expand_got, after, middle, vectors, down, keys, values, weights, out_own, out_got = ins[:12]
        grad_rows, rounded_two, traded, all_two, all_rows, grad_mixed, grad_vectors = outs[:7]
        *refs, rounded, whole, second, out_full, expand_full, key_full, value_full, grad_scores, grads_all, send, recv, local = kept
        reduces = [
            Reduce(at, ins[12], outs[7], refs[7:11], send, recv, local, 32, 16, False),
            Reduce(at, ins[13], outs[8], refs[11:15], send, recv, local, 42, 18, True),
        ]
        refs = refs[:7]
        for reduce in reduces:
            reduce.first()
        weight = Whole(at, expand_own, expand_got, expand_full, local.at[pl.ds(0, 2)], 0)
        later = [
            pltpu.make_async_copy(keys, key_full, local.at[2]),
            pltpu.make_async_copy(values, value_full, local.at[3]),
        ]
        for copy in later:
            copy.start()
        later.append(Whole(at, out_own, out_got, out_full, local.at[pl.ds(4, 2)], 1))
        weight.wait()
        scatter = Scatter(at, send, recv, refs)
        scatter.products(lambda rows: dot_flip(grad[rows], expand_full[...]))
        scatter.middle()
        for copy in later:
            copy.wait()
        scatter.arrive()

        def norm_three(rows, carry):
            incoming = scatter.total(rows)
            centred, factor = standard(after[rows])
            total = down[rows].astype(f32) + norm_back(incoming, centred, factor, vectors[4:5])
            grad_rows[rows] = total
            rounded_two[rows] = total.astype(bf16)
            return two_sums(incoming, centred, carry)

        gains, shifts = by_rows(BLOCK, 32, norm_three, no_sums())
        before = Gather(at, rounded_two, all_two, send, recv, local.at[6], 10)
        before.begin()
        for reduce in reduces:
            reduce.second()
        grad_vectors[4:5] = gains
        grad_vectors[5:6] = shifts

        trade = Trade(at, grad_scores, traded, send, recv, local.at[20], 52)

        def score(rows, carry):
            grads_all[rows] = dot_flip(value_full[rows], rounded_two[...])

        by_rows(D, QUARTER, score)

        def cross(b, carry):
            rows = pl.ds(pl.multiple_of(b * BLOCK, BLOCK), BLOCK)
            p = weights[b].astype(f32).T.reshape(HEADS, 64, BLOCK)
            dp = grads_all[rows].reshape(HEADS, 64, BLOCK)
            ds = p * (dp - jnp.sum(p * dp, axis=1, keepdims=True))
            ds = ds.reshape(BLOCK, BLOCK).T.astype(bf16)
            grad_scores[b] = ds
            trade.give(b)
            part = dot(ds, key_full[rows])

            @pl.when(b == 0)
            def _():
                second[...] = part

            @pl.when(b > 0)
            def _():
                second[...] += part

            @pl.when(b == 3)
            def _():
                before.pass_on()

            @pl.when(b == 5)
            def _():
                for reduce in reduces:
                    reduce.third()

            return carry

        lax.fori_loop(0, 8, cross, 0)
        at.flush(1)
        for reduce in reduces:
            reduce.fourth()

        def norm_two(rows, carry):
            incoming = second[rows]
            centred, factor = standard(middle[rows])
            total = grad_rows[rows] + norm_back(incoming, centred, factor, vectors[2:3])
            grad_rows[rows] = total
            rounded[rows] = total.astype(bf16)
            return two_sums(incoming, centred, carry)

        gains, shifts = by_rows(BLOCK, 32, norm_two, no_sums())
        grad_vectors[2:3] = gains
        grad_vectors[3:4] = shifts
        gather = Gather(at, rounded, whole, send, recv, local.at[7], 21)
        before.pass_near()
        gather.begin()
        at.flush(0, 6)
        before.pass_far()
        keep = Keep(whole, all_rows, local, 8)

        def work(s, rows):
            keep.block(s, rows)
            grad_mixed[rows] = dot_flip(whole[rows], out_full[...]).astype(bf16)

        gather.each(work)
        at.flush()
        before.got(4, 7, 8, 9, 10)
        before.end()
        trade.end()
        keep.wait()
        scatter.end()
        for reduce in reduces:
            reduce.end()

    return call(
        body,
        number,
        [grad, *expand_w, after, middle, vectors, down, keys, values, weights, *out_w, contract_sum, expand_sum],
        [
            shape(BLOCK, D, dtype=f32),
            shape(BLOCK, D),
            shape(8, BLOCK, BLOCK),
            shape(D, D),
            shape(D, D),
            shape(D, COLS),
            shape(8, D, dtype=f32),
            shape(4, 2, 96, HALF),
            shape(4, 2, 96, HALF),
        ],
        [
            *Scatter.scratch,
            *Reduce.scratch(96, False),
            *Reduce.scratch(96, True),
            VMEM((BLOCK, D), bf16),
            VMEM((D, D), bf16),
            VMEM((BLOCK, D), f32),
            VMEM((COLS, D), bf16),
            VMEM((D, HALF), bf16),
            VMEM((D, D), bf16),
            VMEM((D, D), bf16),
            VMEM((8, BLOCK, BLOCK), bf16),
            VMEM((D, BLOCK), f32),
            *sems(60),
        ],
        beside,
        lambda at: Trade.peers(at) + Reduce.peers(at),
        spaces=[VMEM, ANY, ANY, VMEM, VMEM, VMEM, VMEM, ANY, ANY, VMEM, ANY, ANY, ANY, ANY],
        out_spaces=[VMEM, VMEM, ANY, ANY, ANY, VMEM, VMEM, ANY, ANY],
    )


def causal_backward(number, joined, grad, logs, activated, contract, after, normed_two, part, beside):
    at_once = 512

    def body(at, ins, outs, kept):
        (qkv, go, log_rows, activated, contract, after, block, part), (out, result, all_rows, summed) = ins, outs
        *refs, parts, key_sum, value_sum, send, recv, local = kept
        reduce = Reduce(at, part, summed, refs[7:], send, recv, local, 21, 1, False)
        reduce.first()
        gather = Gather(at, block, all_rows, send, recv, local.at[0], 10)
        gather.begin()
        scatter = Scatter(at, send, recv, refs[:7])
        scatter.products(lambda rows: dot(activated[rows], contract[...]))
        gather.pass_on()
        for i in range(4):
            for h in range(HEADS):
                a = i * COLS + h * HDIM
                piece = qkv[:, a : a + HDIM] if i < 3 else go[:, h * HDIM : (h + 1) * HDIM]
                parts[i, h] = piece * EIGHTH if i == 0 else piece
        square = (at_once, at_once)
        seen = lax.broadcasted_iota(jnp.int32, square, 1) >= lax.broadcasted_iota(jnp.int32, square, 0)
        blocks = D // at_once

        def one(h, carry):
            turned = parts[1, h].T
            query_parts = []
            for i in reversed(range(blocks)):
                before, upto = i * at_once, (i + 1) * at_once
                rows = slice(before, upto)
                q, g = parts[0, h, rows], parts[3, h, rows]
                k, v = parts[1, h, 0:upto], parts[2, h, 0:upto]
                p = jnp.exp(dot_flip(k, q) - log_rows[pl.ds(h, 1), rows])
                last = jnp.where(seen, p[before:], 0.0)
                p = jnp.concatenate((p[:before], last), axis=0) if i else last
                dp = dot_flip(v, g)
                ds = (p * (dp - jnp.sum(p * dp, axis=0, keepdims=True))).astype(bf16)
                value_part, key_part = dot(p.astype(bf16), g), dot(ds, q)
                if i == blocks - 1:
                    key_sum[0:upto, :] = key_part
                    value_sum[0:upto, :] = value_part
                else:
                    key_sum[0:upto, :] += key_part
                    value_sum[0:upto, :] += value_part
                query_parts.append((dot(turned[:, 0:upto], ds) * EIGHTH).T)
                if i == blocks - 1:

                    @pl.when(h == 1)
                    def _():
                        reduce.second()

                    @pl.when(h == 2)
                    def _():
                        reduce.fourth()

            parts[0, h] = jnp.concatenate(query_parts[::-1], axis=0).astype(bf16)
            parts[1, h] = key_sum[...].astype(bf16)
            parts[2, h] = value_sum[...].astype(bf16)

            @pl.when(h == 0)
            def _():
                gather.pass_near()

            @pl.when(h == 1)
            def _():
                scatter.middle()
                gather.pass_far()
                reduce.third()

            return carry

        lax.fori_loop(0, HEADS, one, 0)
        for i in range(3):
            out[:, i * COLS : (i + 1) * COLS] = jnp.concatenate([parts[i, h] for h in range(HEADS)], axis=1)
        scatter.arrive()

        def finish(rows, carry):
            result[rows] = (after[rows] + scatter.total(rows)).astype(bf16)

        at.flush(0)
        by_rows(BLOCK, 32, finish)
        at.flush(1)
        gather.got(4, 7, 8, 9, 10)
        gather.end()
        scatter.end()
        reduce.end()

    return call(
        body,
        number,
        [joined, grad, logs, activated, contract, after, normed_two, part],
        [shape(D, 3 * COLS), shape(BLOCK, D), shape(D, D), shape(4, 2, 72, HALF)],
        [
            *Scatter.scratch,
            *Reduce.scratch(72, False),
            VMEM((4, HEADS, D, HDIM), bf16),
            VMEM((D, HDIM), f32),
            VMEM((D, HDIM), f32),
            *sems(31),
        ],
        beside,
        lambda at: ring_peers(at) + Reduce.peers(at),
        spaces=[VMEM] * 7 + [ANY],
        out_spaces=[VMEM, VMEM, ANY, ANY],
    )


def leave(number, grad, joined, x, vectors, grad_rows, sums, late, text_part, beside):
    relay = Relay(jax.ShapeDtypeStruct((BLOCK, D), bf16), True)
    some = 64 // 8

    def ring(at):
        return [{"wide": lax.rem(at.w + k, 8)} for k in range(1, 8)]

    x_steps = ((0, 1), (1, 0), (1, 1))

    def group(at):
        return [(b, {"wide": lax.rem(at.w + k, 8), "narrow": lax.rem(at.n + b, 2)}) for k in range(8) for b in range(2)][1:]

    def peers(at):
        known = ring_peers(at) + relay.peers(at) + Reduce.peers(at)
        known += [(f"w{k}", peer) for k, peer in enumerate(ring(at), 1)]
        return known + [(f"g{i}", peer) for i, (b, peer) in enumerate(group(at)) if b]

    def body(at, ins, outs, kept):
        grad, weight, x, vectors, before, late, text, one, two = ins
        result, out_one, out_two, vector_sums, text_out = outs
        refs, kept = kept[:7], kept[7:]
        reduces = [
            Reduce(at, one, out_one, kept[0:4], kept[-3], kept[-2], kept[-1], 12, 1, False),
            Reduce(at, two, out_two, kept[4:8], kept[-3], kept[-2], kept[-1], 22, 3, True),
        ]
        rounded, parts, ring_parts, ring_sum, x_parts, x_sum, z_parts, text_parts, text_sum, send, recv, local = kept[8:]
        me = at.spot(at.y, at.c)

        def move(slot, source, target, peer):
            return remote(source, target, send.at[slot], recv.at[slot], peer)

        to_ring, to_group = ring(at), group(at)
        slot = 32
        trades = []
        for peer in to_ring:
            there = at.spot(lax.div(peer["wide"], 2), lax.rem(peer["wide"], 2))
            trades.append(move(slot, text.at[there], text_parts.at[me], peer))
            slot += 1
        text_own = pltpu.make_async_copy(text.at[me], text_parts.at[me], local.at[5])
        texts = []
        for b, peer in to_group:
            n = lax.rem(at.n + b, 2)
            texts.append(move(slot, text_sum.at[:, at.half(n)], text_out.at[at.n, me], peer))
            slot += 1
        text_stay = pltpu.make_async_copy(text_sum.at[:, at.half(at.n)], text_out.at[at.n, me], local.at[6])
        rings = []
        for peer in to_ring:
            rings.append(move(slot, parts, ring_parts.at[at.w], peer))
            slot += 1
        ring_own = pltpu.make_async_copy(parts, ring_parts.at[at.w], local.at[7])
        spreads = []
        for a, b in x_steps:
            half = ring_sum.at[:, at.half(lax.rem(at.n + b, 2))]
            spreads.append(move(slot, half, x_parts.at[at.s, at.n], at.at_x(a, b)))
            slot += 1
        x_own = pltpu.make_async_copy(ring_sum.at[:, at.half(at.n)], x_parts.at[at.s, at.n], local.at[8])
        lasts = []
        for k in (1, 2, 3):
            lasts.append(move(slot, x_sum, z_parts.at[at.z], at.at_z(k)))
            slot += 1

        for reduce in reduces:
            reduce.first()
        text_own.start()
        for copy in trades:
            copy.start()
        scatter = Scatter(at, send, recv, refs)
        scatter.products(lambda rows: dot(grad[rows], weight[...]))
        at.start_beside()
        scatter.middle()
        for reduce in reduces:
            reduce.second()
        text_own.wait()
        for copy in trades:
            copy.wait_recv()
        total = text_parts[0].astype(f32)
        for i in range(1, 8):
            total += text_parts[i].astype(f32)
        text_sum[...] = total.astype(bf16)
        text_stay.start()
        for copy in texts:
            copy.start()
        scatter.arrive()

        def norm(rows, carry):
            incoming = scatter.total(rows)
            centred, factor = standard(x[rows].astype(f32))
            total = before[rows] + norm_back(incoming, centred, factor, vectors[0:1])
            rounded[rows] = total.astype(bf16)
            return two_sums(incoming, centred, carry)

        gains, shifts = by_rows(BLOCK, 32, norm, no_sums())
        moving = functools.partial(relay_run, relay, at, rounded, result, send, recv, local.at[0], 10)
        moving(False)
        parts[0:1] = gains
        parts[1:2] = shifts
        parts[2:6] = late[2:6]
        parts[6:8] = jnp.zeros((2, D), f32)
        ring_own.start()
        for copy in rings:
            copy.start()
        for reduce in reduces:
            reduce.third()
        ring_own.wait()
        for copy in rings:
            copy.wait_recv()
        total = ring_parts[0]
        for i in range(1, 8):
            total += ring_parts[i]
        ring_sum[...] = total
        x_own.start()
        for copy in spreads:
            copy.start()
        for reduce in reduces:
            reduce.fourth()
        x_own.wait()
        for copy in spreads:
            copy.wait_recv()
        total = x_parts[0, 0] + x_parts[0, 1] + x_parts[1, 0] + x_parts[1, 1]
        x_sum[...] = total
        for copy in lasts:
            copy.start()
        z_parts[pl.ds(at.z, 1)] = total.reshape(1, 8, HALF)
        for copy in lasts:
            copy.wait_recv()
        vector_sums[...] = z_parts[0] + z_parts[1] + z_parts[2] + z_parts[3]
        at.flush()
        moving(True)
        text_stay.wait()
        for copy in texts:
            copy.wait()
        for copy in trades + rings + spreads + lasts:
            copy.wait_send()
        scatter.end()
        for reduce in reduces:
            reduce.end()

    return call(
        body,
        number,
        [grad, joined, x, vectors, grad_rows, late, text_part, *sums],
        [
            shape(384, HALF),
            shape(4, 2, 72, HALF),
            shape(4, 2, 48, HALF),
            shape(8, HALF, dtype=f32),
            shape(2, 8, some, HALF),
        ],
        [
            *Scatter.scratch,
            *Reduce.scratch(72, False),
            *Reduce.scratch(48, True),
            VMEM((BLOCK, D), bf16),
            VMEM((8, D), f32),
            VMEM((8, 8, D), f32),
            VMEM((8, D), f32),
            VMEM((2, 2, 8, HALF), f32),
            VMEM((8, HALF), f32),
            VMEM((4, 8, HALF), f32),
            VMEM((8, some, D), bf16),
            VMEM((some, D), bf16),
            *sems(32 + 7 + 15 + 7 + 6),
        ],
        beside,
        peers,
        spaces=[VMEM, VMEM, VMEM, VMEM, VMEM, VMEM, ANY, ANY, ANY],
        out_spaces=[ANY, ANY, ANY, VMEM, ANY],
        late=True,
    )


def on_device(
    layer_input,
    text_states,
    cotangent,
    first_gain,
    first_shift,
    query_weight,
    key_weight,
    value_weight,
    output_weight,
    second_gain,
    second_shift,
    cross_query,
    cross_key,
    cross_value,
    cross_output,
    third_gain,
    third_shift,
    expand_weight,
    contract_weight,
):
    gains = (first_gain, first_shift, second_gain, second_shift, third_gain, third_shift)
    weights = [query_weight.T, key_weight.T, value_weight.T]
    query_t = cross_query.T
    pair_t = jnp.concatenate((cross_key.T, cross_value.T), axis=0)
    n = lax.axis_index("narrow")

    results, ((down,), (out_got,), (text_got,)) = enter(
        1,
        layer_input,
        gains,
        weights,
        query_t,
        cross_output,
        text_states,
        pair_t,
        [Relay(cotangent), Give(output_weight), GiveClip(text_states)],
    )
    x, vectors, joined, all_one, qkv, query_all, out_quarter, text_pair = results
    (attended, logs, all_down, out_all), ((texts,), (expand_got,)) = causal_forward(
        2, qkv, down, out_quarter, [ToSpots(text_pair), Give(expand_weight)]
    )
    out_w, expand_w = (output_weight, out_got), (expand_weight, expand_got)
    results = forward_rest(3, attended, out_w, x, vectors, query_all, out_all, texts, all_down, expand_w, contract_weight)
    middle, after, normed_two, cross_p, all_three, activated, grad_expand, contract, all_keys, all_values, traded_p = results

    contract_part = outer(activated, all_down).astype(bf16).reshape(4, 2, 96, D)
    expand_part = outer(grad_expand, all_three).astype(bf16).reshape(4, 2, 96, D)
    results, ((query_got,), (cross_got,)) = backward_rest(
        4,
        grad_expand,
        expand_w,
        after,
        middle,
        vectors,
        down,
        all_keys,
        all_values,
        cross_p,
        out_w,
        contract_part,
        expand_part,
        [Give(query_t), Give(cross_output)],
    )
    grad_one, _, grad_scores, all_mid_two, all_mid_one, grad_attended, late, contract_grad, expand_grad = results

    own_first = n == 0

    def whole(own, got):
        return jnp.concatenate((jnp.where(own_first, own, got), jnp.where(own_first, got, own)), axis=1)

    def heads(what, a, b):
        return jnp.einsum(what, a, b, preferred_element_type=f32)

    text = whole(lax.dynamic_index_in_dim(text_states, n, 0, False), text_got)
    text_heads = text_pair.reshape(64, 2, HEADS, HDIM)
    grad_values = outer(traded_p.reshape(D, COLS), all_mid_two).astype(bf16).reshape(HEADS, 64, D)
    heads_out = whole(cross_output, cross_got).reshape(HEADS, HDIM, D)
    grad_text_values = heads("hkf,hdf->khd", grad_values, heads_out).reshape(64, COLS).astype(bf16)
    grad_cross = heads("khd,hkf->hdf", text_heads[:, 1], grad_values).reshape(COLS, D)
    value_part = jnp.concatenate((grad_cross, outer(grad_text_values, text), outer(attended, all_mid_one)), axis=0)
    (grad_qkv, layer_output, all_two, value_grad), ((pair_got,),) = causal_backward(
        5,
        qkv,
        grad_attended,
        logs,
        activated,
        contract,
        after,
        normed_two,
        value_part.astype(bf16).reshape(4, 2, 72, D),
        [Give(pair_t)],
    )

    joined_part = outer(grad_qkv, all_one).astype(bf16).reshape(4, 2, 72, D)
    grad_keys = outer(grad_scores.reshape(D, COLS), all_two).astype(bf16).reshape(HEADS, 64, D)
    heads_query = whole(query_t, query_got).reshape(HEADS, HDIM, D)
    grad_text_keys = (heads("hkf,hdf->khd", grad_keys, heads_query) * EIGHTH).reshape(64, COLS).astype(bf16)
    grad_query = heads("khd,hkf->hdf", text_heads[:, 0], grad_keys).reshape(COLS, D) * EIGHTH
    key_part = jnp.concatenate((grad_query, outer(grad_text_keys, text)), axis=0).astype(bf16).reshape(4, 2, 48, D)
    grad_pair = jnp.concatenate((grad_text_keys, grad_text_values), axis=1)
    text_part = dot(grad_pair, whole(pair_t, pair_got)).astype(bf16).reshape(8, 8, D)

    (input_grad, joined_grad, key_grad, parts, text_grad), ((layer_output,),) = leave(
        6,
        grad_qkv,
        joined,
        x,
        vectors,
        grad_one,
        (joined_part, key_part),
        late,
        text_part,
        [Relay(layer_output, True)],
    )
    joined_grad, key_grad, value_grad, expand_grad, contract_grad = (
        grad.reshape(-1, HALF).astype(f32) for grad in (joined_grad, key_grad, value_grad, expand_grad, contract_grad)
    )
    return (
        layer_output,
        input_grad.astype(f32),
        text_grad.reshape(2, 64, HALF).astype(f32),
        parts[0],
        parts[1],
        joined_grad[:COLS].T,
        joined_grad[COLS : 2 * COLS].T,
        joined_grad[2 * COLS :].T,
        value_grad[2 * COLS :],
        parts[2],
        parts[3],
        key_grad[:COLS].T,
        key_grad[COLS:].T,
        value_grad[COLS : 2 * COLS].T,
        value_grad[:COLS],
        parts[4],
        parts[5],
        expand_grad.T,
        contract_grad,
    )


def solution(mesh):
    return jax.shard_map(
        on_device,
        mesh=mesh,
        in_specs=(
            P(("dp", "wide"), "narrow"),
            P("dp", None, "narrow"),
            P(("dp", "wide"), "narrow"),
            P("narrow"),
            P("narrow"),
            P("narrow", "wide"),
            P("narrow", "wide"),
            P("narrow", "wide"),
            P("wide", "narrow"),
            P("narrow"),
            P("narrow"),
            P("narrow", "wide"),
            P("narrow", "wide"),
            P("narrow", "wide"),
            P("wide", "narrow"),
            P("narrow"),
            P("narrow"),
            P("narrow", "wide"),
            P("wide", "narrow"),
        ),
        out_specs=(
            P(("dp", "wide"), "narrow"),
            P(("dp", "wide"), "narrow"),
            P("dp", None, "narrow"),
            P("narrow"),
            P("narrow"),
            P("narrow", "wide"),
            P("narrow", "wide"),
            P("narrow", "wide"),
            P("wide", "narrow"),
            P("narrow"),
            P("narrow"),
            P("narrow", "wide"),
            P("narrow", "wide"),
            P("narrow", "wide"),
            P("wide", "narrow"),
            P("narrow"),
            P("narrow"),
            P("narrow", "wide"),
            P("wide", "narrow"),
        ),
        check_vma=False,
    )
```

```python
import functools
import math

import jax
import jax.numpy as jnp
from jax import lax
from jax.experimental import pallas as pl
from jax.experimental.pallas import tpu as pltpu
from jax.sharding import PartitionSpec as P

D = 1536
HALF = 768
HDIM = 64
HEADS = 3
COLS = HEADS * HDIM
BLOCK = 192
EPSILON = 1e-05
NEGATIVE = -1e30
ROOT_HALF = 0.7071067811865476
GAUSS_NORM = 0.3989422804014327
MESH = pl.DeviceIdType.MESH
VMEM = pltpu.VMEM
ANY = pl.ANY
bf16, f32 = jnp.bfloat16, jnp.float32


def dot(a, b):
    return lax.dot_general(a, b, (((1,), (0,)), ((), ())), preferred_element_type=f32)


def dot_flip(a, b):
    return lax.dot_general(a, b, (((1,), (1,)), ((), ())), preferred_element_type=f32)


def outer(a, b):
    return lax.dot_general(a, b, (((0,), (0,)), ((), ())), preferred_element_type=f32)


class Place:
    def __init__(self):
        self.dp, self.w, self.n = (lax.axis_index(a) for a in ("dp", "wide", "narrow"))
        self.y, self.c = lax.div(self.w, 2), lax.rem(self.w, 2)
        self.z, self.s = lax.div(self.dp, 2), lax.rem(self.dp, 2)
        self.up, self.down = lax.rem(self.y + 1, 4), lax.rem(self.y + 3, 4)
        self.across = 3 - self.y
        self.moved = lax.rem(lax.div(self.y, 2) + self.n, 2)
        self.clip = lax.div(self.y, 2)

    def spot(self, y, c):
        moved = lax.rem(lax.div(y, 2) + self.n, 2)
        return (lax.rem(y + moved, 2) * 2 + c) * 2 + moved

    def rows(self, y, c, start=0, size=BLOCK):
        return pl.ds(pl.multiple_of(self.spot(y, c) * BLOCK + start, 32), size)

    def half(self, n):
        return pl.ds(pl.multiple_of(n * HALF, HALF), HALF)

    def at_y(self, y):
        return {"wide": y * 2 + self.c}

    def core(self):
        return {"wide": self.y * 2 + 1 - self.c}

    def x(self):
        return {"narrow": 1 - self.n}

    def at_z(self, k):
        return {"dp": lax.rem(self.z + k, 4) * 2 + self.s}

    def at_dp(self, k):
        return {"dp": lax.rem(self.dp + k, 8)}

    def at_x(self, ds, dn):
        return {"dp": self.z * 2 + lax.rem(self.s + ds, 2), "narrow": lax.rem(self.n + dn, 2)}


def remote(src, dst, send, recv, peer):
    return pltpu.make_async_remote_copy(
        src_ref=src, dst_ref=dst, send_sem=send, recv_sem=recv, device_id=peer, device_id_type=MESH
    )


def greet(peers):
    barrier = pltpu.get_barrier_semaphore()
    for peer in peers:
        pl.semaphore_signal(barrier, inc=1, device_id=peer, device_id_type=MESH)
    pl.semaphore_wait(barrier, len(peers))


class Give:
    def __init__(self, array):
        self.ins, self.copies, self.locals = [array], 1, 0
        self.outs = [jax.ShapeDtypeStruct(array.shape, array.dtype)]

    def peers(self, at):
        return [("x", at.x())]

    def moves(self, at, ins, outs):
        return [(ins[0], outs[0], at.x())], []


class GiveClip(Give):
    def __init__(self, array):
        super().__init__(array)
        self.outs = [jax.ShapeDtypeStruct(array.shape[1:], array.dtype)]

    def moves(self, at, ins, outs):
        return [(ins[0].at[1 - at.n], outs[0], at.x())], []


class ToSpots:
    def __init__(self, array):
        self.ins, self.copies, self.locals = [array], 7, 1
        self.outs = [jax.ShapeDtypeStruct((8, *array.shape), array.dtype)]

    def peers(self, at):
        return [(f"w{k}", {"wide": lax.rem(at.w + k, 8)}) for k in range(1, 8)]

    def moves(self, at, ins, outs):
        dst = outs[0].at[at.spot(at.y, at.c)]
        return [(ins[0], dst, peer) for _, peer in self.peers(at)], [(ins[0], dst)]


class Relay:
    def __init__(self, array, back=False):
        self.ins, self.back, self.copies, self.locals = [array], back, 2, 1
        shape = (384, HALF) if back else (BLOCK, D)
        self.outs = [jax.ShapeDtypeStruct(shape, array.dtype)]

    def peers(self, at):
        return [
            ("x", at.x()),
            ("a0", {"wide": at.across * 2 + at.c}),
            ("a1", {"wide": at.across * 2 + at.c, "narrow": 1 - at.n}),
        ]


def relay_run(relay, at, src, dst, send, recv, local, base, finish):
    mine, other = at.half(at.n), at.half(1 - at.n)
    over = at.across * 2 + at.c
    if relay.back:
        row = pl.ds(pl.multiple_of(at.moved * BLOCK, BLOCK), BLOCK)
        to = recv.at[base + at.moved]
        own = src.at[:, mine], src.at[:, other]
        land = dst.at[0:BLOCK], dst.at[BLOCK : 2 * BLOCK]
    else:
        row = mine
        to = recv.at[base + at.n]
        own = src.at[0:BLOCK], src.at[BLOCK : 2 * BLOCK]
        land = dst.at[:, at.half(0)], dst.at[:, at.half(1)]
    target = dst.at[row] if relay.back else dst.at[:, row]

    def arrive(slot, part):
        return remote(own[0], part, send.at[base], recv.at[base + slot], at.x())

    @pl.when(at.moved == 0)
    def _():
        stay = pltpu.make_async_copy(own[0], target, local)
        if relay.back:
            go = remote(own[1], target, send.at[base], to, at.x())
        else:
            go = remote(own[1], target, send.at[base], to, {"wide": over})
        if not finish:
            go.start()
            stay.start()
        else:
            stay.wait()
            go.wait_send()
            if relay.back:
                arrive(1, land[1]).wait_recv()
            else:
                arrive(1 - at.n, dst.at[:, other]).wait_recv()

    @pl.when(at.moved == 1)
    def _():
        if relay.back:
            first = remote(own[1], target, send.at[base], to, {"wide": over, "narrow": 1 - at.n})
            second = remote(own[0], target, send.at[base + 1], to, {"wide": over})
        else:
            first = remote(own[1], target, send.at[base], to, {"wide": over, "narrow": 1 - at.n})
            second = remote(own[0], target, send.at[base + 1], to, at.x())
        if not finish:
            first.start()
            second.start()
        else:
            first.wait_send()
            second.wait_send()
            arrive(0, land[0]).wait_recv()
            arrive(1, land[1]).wait_recv()


def call(body, number, ins, outs, scratch=(), beside=(), peers=None, spaces=None, out_spaces=None, late=False):
    spaces = spaces or [VMEM] * len(ins)
    out_spaces = out_spaces or [VMEM] * len(outs)
    copies = sum(b.copies for b in beside)
    locals_ = sum(b.locals for b in beside)
    side_ins = [a for b in beside for a in b.ins]
    side_outs = [a for b in beside for a in b.outs]
    n_in, n_out, n_scratch = len(ins), len(outs), len(scratch)
    loaded = [i for i, m in enumerate(spaces) if m is VMEM]
    stored = [i for i, m in enumerate(out_spaces) if m is VMEM]
    buffers = [VMEM(ins[i].shape, ins[i].dtype) for i in loaded] + [VMEM(outs[i].shape, outs[i].dtype) for i in stored]

    def kernel(*refs):
        at = Place()
        refs = list(refs)

        def take(count):
            out = refs[:count]
            del refs[:count]
            return out

        main_in, side_in = take(n_in), take(len(side_ins))
        main_out, side_out, kept = take(n_out), take(len(side_outs)), take(n_scratch)
        in_buffers, out_buffers = take(len(loaded)), take(len(stored))
        send, recv, local, passing = take(4)
        loads, stores = [], {}
        for k, i in enumerate(loaded):
            loads.append(pltpu.make_async_copy(main_in[i], in_buffers[k], passing.at[k]))
            loads[-1].start()
            main_in[i] = in_buffers[k]
        for k, i in enumerate(stored):
            stores[i] = pltpu.make_async_copy(out_buffers[k], main_out[i], passing.at[len(loaded) + k])
            main_out[i] = out_buffers[k]
        waiting = dict(stores)

        def flush(*which):
            for i in which or list(waiting):
                waiting.pop(i).start()

        at.flush = flush
        known = dict(peers(at)) if peers else {}
        for b in beside:
            known.update(dict(b.peers(at)))
        if "w1" in known:
            for name in ("up", "down", "core", "a0"):
                known.pop(name, None)
        if "x01" in known:
            known.pop("x", None)
        if known:
            greet(list(known.values()))
        side_refs = [([side_in.pop(0) for _ in b.ins], [side_out.pop(0) for _ in b.outs]) for b in beside]
        begin, todo = [], []
        slot, place = 0, 0
        for b, (i, o) in zip(beside, side_refs):
            if isinstance(b, Relay):
                run = functools.partial(relay_run, b, at, i[0], o[0], send, recv, local.at[place], slot)
                begin.append([functools.partial(run, False)])
                todo.append(functools.partial(run, True))
                slot, place = slot + 2, place + 1
                continue
            far, near = b.moves(at, i, o)
            begin.append([])
            for src, dst, peer in far:
                copy = remote(src, dst, send.at[slot], recv.at[slot], peer)
                begin[-1].append(copy.start)
                todo.append(copy.wait)
                slot += 1
            for src, dst in near:
                copy = pltpu.make_async_copy(src, dst, local.at[place])
                begin[-1].append(copy.start)
                todo.append(copy.wait)
                place += 1

        def start(*which):
            for i in which or range(len(begin)):
                for go in begin[i]:
                    go()

        at.start_beside = start
        if not late:
            start()
        for copy in loads:
            copy.wait()
        if body:
            body(at, main_in, main_out, kept)
        flush()
        for wait in todo:
            wait()
        for copy in stores.values():
            copy.wait()

    results = pl.pallas_call(
        kernel,
        out_shape=tuple(outs) + tuple(side_outs),
        in_specs=[pl.BlockSpec(memory_space=VMEM if m == PLAIN else ANY) for m in spaces]
        + [pl.BlockSpec(memory_space=ANY)] * len(side_ins),
        out_specs=(pl.BlockSpec(memory_space=ANY),) * (len(outs) + len(side_outs)),
        scratch_shapes=[
            *scratch,
            *buffers,
            pltpu.SemaphoreType.DMA((max(copies, 1),)),
            pltpu.SemaphoreType.DMA((max(copies, 1),)),
            pltpu.SemaphoreType.DMA((max(locals_, 1),)),
            pltpu.SemaphoreType.DMA((max(len(buffers), 1),)),
        ],
        compiler_params=pltpu.CompilerParams(
            collective_id=number, has_side_effects=True, vmem_limit_bytes=58 << 20
        ),
    )(*ins, *side_ins)
    results = list(results)
    main, rest = results[: len(outs)], results[len(outs) :]
    sides = []
    for b in beside:
        sides.append(rest[: len(b.outs)])
        del rest[: len(b.outs)]
    return main, sides


PLAIN = "plain"


def ring_peers(at):
    return [("up", at.at_y(at.up)), ("down", at.at_y(at.down)), ("core", at.core())]


def sems(count):
    return [pltpu.SemaphoreType.DMA((count,)), pltpu.SemaphoreType.DMA((count,)), pltpu.SemaphoreType.DMA((count,))]


def by_rows(count, size, work, carry=None):
    def step(i, carry):
        return work(pl.ds(pl.multiple_of(i * size, size), size), carry)

    return lax.fori_loop(0, count // size, step, carry)


class Whole:
    def __init__(self, at, own, got, full, sem, axis):
        size = own.shape[axis]
        self.copies = []
        for i, (part, n) in enumerate(((own, at.n), (got, 1 - at.n))):
            where = pl.ds(pl.multiple_of(n * size, size), size)
            target = full.at[where] if axis == 0 else full.at[:, where]
            self.copies.append(pltpu.make_async_copy(part, target, sem.at[i]))
            self.copies[-1].start()

    def wait(self):
        for copy in self.copies:
            copy.wait()


class Trade:
    def __init__(self, at, parts, out, send, recv, local, base):
        self.at, self.parts, self.out, self.send, self.recv, self.base = at, parts, out, send, recv, base
        self.me = at.spot(at.y, at.c)
        self.own = pltpu.make_async_copy(parts.at[self.me], out.at[self.me], local)

    @staticmethod
    def peers(at):
        return [(f"w{k}", {"wide": lax.rem(at.w + k, 8)}) for k in range(1, 8)]

    def copy(self, b, place):
        m, core, a = lax.rem(b, 2), lax.rem(lax.div(b, 2), 2), lax.div(b, 4)
        y = 2 * lax.rem(m + self.at.n, 2) + lax.rem(a + m, 2)
        send, recv = self.send.at[self.base + b], self.recv.at[self.base + place]
        return remote(self.parts.at[b], self.out.at[place], send, recv, {"wide": y * 2 + core})

    def give(self, b):
        @pl.when(b == self.me)
        def _():
            self.own.start()

        @pl.when(b != self.me)
        def _():
            self.copy(b, self.me).start()

    def end(self):
        def wait(b, carry):
            @pl.when(b == self.me)
            def _():
                self.own.wait()

            @pl.when(b != self.me)
            def _():
                self.copy(b, b).wait()

            return carry

        lax.fori_loop(0, 8, wait, 0)


class Reduce:
    @staticmethod
    def scratch(deep, x_first, by_rows=False):
        first = (4, deep, HALF) if x_first else (2, 2, deep, HALF) if by_rows else (2, deep, D)
        return [VMEM((3, *first), bf16), VMEM(first, bf16), VMEM((3, deep, HALF), bf16), VMEM((2, deep, HALF), bf16)]

    @staticmethod
    def peers(at):
        return [(f"z{k}", at.at_z(k)) for k in (1, 2, 3)] + [(f"x{a}{b}", at.at_x(a, b)) for a, b in ((0, 1), (1, 0), (1, 1))]

    def __init__(self, at, src, out, refs, send, recv, local, base, place, x_first, by_rows=False):
        self.at, self.src, self.out = at, src, out
        self.land, self.total, self.land_two, self.last = refs
        self.x_first, self.by_rows = x_first, by_rows
        self.deep = self.last.shape[1]
        self.chunk = 32 if self.deep % 32 == 0 else 24
        z_steps = [(at.at_z(k), lax.rem(at.z + k, 4)) for k in (1, 2, 3)]
        x_steps = [
            (at.at_x(a, b), (lax.rem(at.s + a, 2), lax.rem(at.n + b, 2))) for a, b in ((0, 1), (1, 0), (1, 1))
        ]
        first, second = (x_steps, z_steps) if x_first else (z_steps, x_steps)

        def move(slot, source, target, peer):
            return remote(source, target, send.at[base + slot], recv.at[base + slot], peer)

        self.one = [move(i, self.piece(where), self.land.at[i], peer) for i, (peer, where) in enumerate(first)]
        self.own = pltpu.make_async_copy(
            self.piece((at.s, at.n) if x_first else at.z), self.total, local.at[place]
        )
        self.two = [move(3 + i, self.part(where), self.land_two.at[i], peer) for i, (peer, where) in enumerate(second)]
        self.mine = at.z if x_first else (at.s, at.n)
        self.three = move(6, self.last.at[at.s], self.last.at[at.s], at.at_x(1, 0))
        target = out.at[at.z]
        self.four = [move(7 + i, self.last, target, peer) for i, (peer, _) in enumerate(z_steps)]
        self.stay = pltpu.make_async_copy(self.last, target, local.at[place + 1])

    def piece(self, where):
        if self.x_first:
            s, n = where
            return self.src.at[n, :, s] if self.by_rows else self.src.at[:, s, :, self.at.half(n)]
        return self.src.at[:, where] if self.by_rows else self.src.at[where]

    def part(self, where):
        if self.x_first:
            return self.total.at[where]
        s, n = where
        return self.total.at[n, s] if self.by_rows else self.total.at[s, :, self.at.half(n)]

    def first(self):
        for copy in self.one + [self.own]:
            copy.start()

    def second(self):
        self.own.wait()
        for copy in self.one:
            copy.wait_recv()
        lead = self.total.shape[:-2]
        count = math.prod(lead)

        def add(i, carry):
            at_lead = (i,) if len(lead) == 1 else (lax.div(i, lead[1]), lax.rem(i, lead[1]))
            for start in range(0, self.deep, self.chunk):
                where = (*at_lead, slice(start, start + self.chunk))
                got = self.total[where].astype(f32)
                for k in range(3):
                    got += self.land[(k, *where)].astype(f32)
                self.total[where] = got.astype(bf16)
            return carry

        lax.fori_loop(0, count, add, 0)
        for copy in self.two:
            copy.start()

    def third(self):
        for copy in self.two:
            copy.wait_recv()
        own = self.part(self.mine)
        s = self.at.s
        for start in range(0, self.deep, self.chunk):
            rows = slice(start, start + self.chunk)
            got = own[rows].astype(f32)
            for k in range(3):
                got += self.land_two[k, rows].astype(f32)
            self.last[s, rows] = got.astype(bf16)
        self.three.start()

    def fourth(self):
        self.three.wait_recv()
        for copy in self.four + [self.stay]:
            copy.start()

    def end(self):
        for copy in self.four:
            copy.wait()
        for copy in self.one + self.two + [self.three]:
            copy.wait_send()
        self.stay.wait()


class Gather:
    slots = 11

    def __init__(self, at, x, whole, send, recv, local, base=0):
        self.at, self.x, self.whole = at, x, whole
        y, c, up, down = at.y, at.c, at.up, at.down
        far = lax.rem(y + 2, 4)
        half = BLOCK // 2

        def move(slot, y_from, peer, start=0, size=BLOCK, first=False):
            rows = at.rows(y_from, c, start, size)
            src = whole.at[rows]
            if first:
                src = x if size == BLOCK else x.at[start : start + size]
            return remote(src, whole.at[rows], send.at[base + slot], recv.at[base + slot], peer)

        to_up, to_down, core = at.at_y(up), at.at_y(down), at.core()
        self.sends = [
            move(0, y, to_up, 0, half, first=True),
            move(1, y, to_up, half, half, first=True),
            move(2, y, to_down, half, half, first=True),
            move(3, y, to_down, 0, half, first=True),
            move(4, y, core, first=True),
            move(5, down, to_up, 0, half),
            move(6, up, to_down, half, half),
            move(7, down, core),
            move(8, up, core),
            move(9, far, core, 0, half),
            move(10, far, core, half, half),
        ]
        self.own = pltpu.make_async_copy(x, whole.at[at.rows(y, c)], local)

    def begin(self):
        for i in (0, 2, 1, 3, 4):
            self.sends[i].start()
        self.own.start()
        self.own.wait()

    def chain(self, *pairs):
        for arrived, leaving in pairs:
            self.sends[arrived].wait_recv()
            self.sends[leaving].start()

    def pass_on(self):
        self.chain((0, 5), (2, 6))

    def pass_near(self):
        self.chain((1, 7), (3, 8))

    def pass_far(self):
        self.chain((5, 9), (6, 10))

    def got(self, *slots):
        for i in slots:
            self.sends[i].wait_recv()

    def end(self):
        for copy in self.sends:
            copy.wait_send()

    def finish(self):
        self.pass_on()
        self.pass_near()
        self.pass_far()
        self.got(4, 7, 8, 9, 10)
        self.end()

    def each(self, work):
        at = self.at

        def step(s, carry):
            @pl.when(s == 1)
            def _():
                self.got(4)
                self.pass_on()

            @pl.when(s == 2)
            def _():
                self.pass_near()

            @pl.when(s == 3)
            def _():
                self.got(8)

            @pl.when(s == 5)
            def _():
                self.got(7)

            @pl.when(s == 6)
            def _():
                self.pass_far()

            @pl.when(s == 7)
            def _():
                self.got(9, 10)

            work(s, self.place(s))
            return carry

        lax.fori_loop(0, 8, step, 0)
        self.end()

    def place(self, s):
        g = lax.div(s, 2)
        off = g + lax.div(g, 2) - 2 * lax.div(g, 3)
        return self.at.rows(lax.rem(self.at.y + off, 4), lax.rem(self.at.c + s, 2))


QUARTER = 384


class GatherZ(Gather):
    def __init__(self, at, quarter, full, send, recv, local, base=0):
        self.at = at
        z, up, down, far = at.z, lax.rem(at.z + 1, 4), lax.rem(at.z + 3, 4), lax.rem(at.z + 2, 4)
        half = QUARTER

        def move(slot, z_from, peer, start=0, size=2 * QUARTER, first=False):
            rows = pl.ds(pl.multiple_of(at.c * 2 * QUARTER + start, QUARTER), size)
            target = full.at[rows, self.columns(z_from)]
            return remote(quarter.at[rows] if first else target, target, send.at[base + slot], recv.at[base + slot], peer)

        to_up, to_down, core = at.at_z(1), at.at_z(3), at.core()
        self.sends = {
            0: move(0, z, to_up, 0, half, first=True),
            1: move(1, z, to_up, half, half, first=True),
            2: move(2, z, to_down, half, half, first=True),
            3: move(3, z, to_down, 0, half, first=True),
            5: move(5, down, to_up, 0, half),
            6: move(6, up, to_down, half, half),
            7: move(7, down, core),
            8: move(8, up, core),
            9: move(9, far, core, 0, half),
            10: move(10, far, core, half, half),
        }
        self.own = pltpu.make_async_copy(quarter, full.at[:, self.columns(z)], local)

    @staticmethod
    def columns(z):
        return pl.ds(pl.multiple_of(z * QUARTER, QUARTER), QUARTER)

    @staticmethod
    def peers(at):
        return [("z1", at.at_z(1)), ("z3", at.at_z(3)), ("core", at.core())]

    def begin(self):
        for i in (0, 2, 1, 3):
            self.sends[i].start()
        self.own.start()

    def end(self):
        self.got(7, 8, 9, 10)
        self.own.wait()
        for copy in self.sends.values():
            copy.wait_send()


class Scatter:
    slots = 10
    scratch = [
        VMEM((4, BLOCK, D), bf16),
        VMEM((4, BLOCK, D), bf16),
        VMEM((4, BLOCK, D), f32),
        VMEM((2, BLOCK, D), bf16),
        VMEM((2, BLOCK, D), bf16),
        VMEM((2, BLOCK // 2, D), bf16),
        VMEM((2, BLOCK // 2, D), bf16),
    ]

    def __init__(self, at, send, recv, refs, base=0):
        self.at, self.send, self.recv, self.base = at, send, recv, base
        self.out_c, self.in_c, self.own, self.out_y, self.in_y, self.half_out, self.half_in = refs
        half = BLOCK // 2
        peers = at.at_y(at.up), at.at_y(at.down)

        def move(slot, src, dst, peer):
            return remote(src, dst, send.at[base + slot], recv.at[base + slot], peer)

        self.cores = [self.core(g) for g in range(4)]
        self.halves = [move(4 + i, self.half_out.at[i], self.half_in.at[i], peers[i]) for i in range(2)]
        free = [pl.ds((1 - i) * half, half) for i in range(2)]
        bound = [pl.ds(i * half, half) for i in range(2)]
        self.free = [move(6 + i, self.out_y.at[i, free[i]], self.in_y.at[i, free[i]], peers[i]) for i in range(2)]
        self.bound = [move(8 + i, self.out_y.at[i, bound[i]], self.in_y.at[i, bound[i]], peers[i]) for i in range(2)]

    def core(self, g):
        slot = self.base + g
        return remote(self.out_c.at[g], self.in_c.at[g], self.send.at[slot], self.recv.at[slot], self.at.core())

    def both(self, g, rows):
        return self.own[g, rows] + self.in_c[g, rows].astype(f32)

    def products(self, product):
        at = self.at
        half = BLOCK // 2

        def part_rows(rows, i):
            return pl.ds(pl.multiple_of(rows.start + i * half, 32), 32)

        def send_free(i):
            self.cores[1 + i].wait_recv()

            def add(rows, carry):
                there = part_rows(rows, 1 - i)
                self.out_y[i, there] = self.both(1 + i, there).astype(bf16)

            by_rows(half, 32, add)
            self.free[i].start()

        def step(s, carry):
            g = lax.div(s, 2)
            off = lax.rem(6 - g + 3 * lax.div(g, 2) + 2 * lax.div(g, 3), 4)
            part = product(at.rows(lax.rem(at.y + off, 4), lax.rem(at.c + 1 + s, 2)))

            @pl.when(lax.rem(s, 2) == 0)
            def _():
                self.out_c[g] = part.astype(bf16)
                self.core(g).start()

            @pl.when(lax.rem(s, 2) == 1)
            def _():
                self.own[g] = part

            @pl.when(s == 2)
            def _():
                self.cores[0].wait_recv()
                for i in range(2):

                    def add(rows, carry, i=i):
                        self.half_out[i, rows] = self.both(0, part_rows(rows, i)).astype(bf16)

                    by_rows(half, 32, add)
                    self.halves[i].start()

            @pl.when(s == 4)
            def _():
                send_free(0)

            @pl.when(s == 6)
            def _():
                send_free(1)

            return carry

        lax.fori_loop(0, 8, step, 0)

    def middle(self):
        half = BLOCK // 2
        for i in range(2):
            self.halves[i].wait_recv()

            def add(rows, carry, i=i):
                here = pl.ds(pl.multiple_of(rows.start + i * half, 32), 32)
                self.out_y[i, here] = (self.both(1 + i, here) + self.half_in[i, rows].astype(f32)).astype(bf16)

            by_rows(half, 32, add)
            self.bound[i].start()

    def arrive(self):
        self.cores[3].wait_recv()
        for copy in self.free + self.bound:
            copy.wait_recv()

    def total(self, rows):
        return self.both(3, rows) + self.in_y[0, rows].astype(f32) + self.in_y[1, rows].astype(f32)

    def end(self):
        for copy in self.cores + self.halves + self.free + self.bound:
            copy.wait_send()


def standard(values):
    average = jnp.mean(values, axis=1, keepdims=True)
    variance = jnp.mean(values * values, axis=1, keepdims=True) - average * average
    factor = lax.rsqrt(variance + EPSILON)
    return (values - average) * factor, factor


def norm_back(incoming, centred, factor, gain):
    scaled = incoming * gain
    first = jnp.mean(scaled, axis=1, keepdims=True)
    second = jnp.mean(scaled * centred, axis=1, keepdims=True)
    return factor * (scaled - first - centred * second)


def two_sums(incoming, centred, carry):
    gains, shifts = carry
    return gains + jnp.sum(incoming * centred, axis=0, keepdims=True), shifts + jnp.sum(incoming, axis=0, keepdims=True)


def no_sums():
    return jnp.zeros((1, D), f32), jnp.zeros((1, D), f32)


EIGHTH = 0.125


def shape(*dims, dtype=bf16):
    return jax.ShapeDtypeStruct(dims, dtype)


class Keep:
    def __init__(self, whole, out, sem, base):
        self.whole, self.out, self.sem, self.base = whole, out, sem, base

    def block(self, s, rows):
        pltpu.make_async_copy(self.whole.at[rows], self.out.at[rows], self.sem.at[self.base + s]).start()

    def wait(self):
        for s in range(8):
            some = pl.ds(0, BLOCK)
            pltpu.make_async_copy(self.whole.at[some], self.out.at[some], self.sem.at[self.base + s]).wait()


def enter(number, layer_input, gains, weights, query_t, cross_out, texts, pair_t, beside):
    relay = Relay(layer_input)

    def body(at, ins, outs, kept):
        source, *gains = ins[:7]
        *own_weights, query_own, out_own, own_texts, pair = ins[7:]
        x, vectors, weight, all_rows, qkv, query_all, out_quarter, text_pair = outs
        normed, whole, query_part, out_part, query_quarter, text_parts, text_got, own_vectors, send, recv, local = kept
        half = at.half(at.n)
        moving = functools.partial(relay_run, relay, at, source, x, send, recv, local.at[0], 11)
        moving(False)
        own_vectors[...] = jnp.zeros_like(own_vectors)
        for i, ref in enumerate(gains):
            own_vectors[i : i + 1] = ref[...].astype(f32).reshape(1, HALF)
        columns = GatherZ.columns(lax.rem(at.z, 2))
        holds = at.n == lax.div(at.z, 2)
        quarters = []
        for i, (own, part) in enumerate(((query_own, query_part), (out_own, out_part))):
            quarters.append(
                (
                    pltpu.make_async_copy(own.at[:, columns], part, local.at[14 + i]),
                    remote(own.at[:, columns], part, send.at[17 + i], recv.at[17 + i], at.x()),
                )
            )

        @pl.when(holds)
        def _():
            for stay, go in quarters:
                go.start()
                stay.start()

        stay = [
            pltpu.make_async_copy(own, target, local.at[1 + i])
            for i, (own, target) in enumerate(
                [(own_vectors, vectors.at[:, half])]
                + [(own, weight.at[j * COLS : (j + 1) * COLS, half]) for j, own in enumerate(own_weights)]
            )
        ]
        for copy in stay:
            copy.start()
        vectors_go = remote(own_vectors, vectors.at[:, half], send.at[13], recv.at[13], at.x())
        vectors_go.start()
        rows = pl.ds(pl.multiple_of(at.z * 144, 16), 144)
        over = remote(weight.at[rows, half], weight.at[rows, half], send.at[14], recv.at[14], at.x())
        other = weight.at[rows, at.half(1 - at.n)]
        others = [
            remote(other, other, send.at[slot], recv.at[slot], at.at_z(k)) for k, slot in ((1, 15), (2, 16), (3, 53))
        ]
        for copy in stay:
            copy.wait()
        over.start()

        @pl.when(holds)
        def _():
            for near, far in quarters:
                near.wait()
                far.wait_send()

        @pl.when(jnp.logical_not(holds))
        def _():
            for near, far in quarters:
                far.wait_recv()

        for clip in range(2):
            text_parts[clip] = dot_flip(own_texts[clip], pair[...])
        text_go = remote(text_parts.at[1 - at.n], text_got, send.at[52], recv.at[52], at.x())
        text_go.start()
        queries = Gather(at, query_part, query_quarter, send, recv, local.at[16], 19)
        outputs = Gather(at, out_part, out_quarter, send, recv, local.at[17], 30)
        queries.begin()
        vectors_go.wait_recv()
        moving(True)
        over.wait_recv()
        for copy in others:
            copy.start()
        at.start_beside(1, 2)
        queries.pass_on()
        queries.pass_near()

        def norm(rows, carry):
            centred, _ = standard(x[rows].astype(f32))
            normed[rows] = (centred * vectors[0:1] + vectors[1:2]).astype(bf16)

        by_rows(BLOCK, 32, norm)
        gather = Gather(at, normed, whole, send, recv, local.at[5])
        gather.begin()
        queries.pass_far()
        queries.got(4, 7, 8, 9, 10)
        around = GatherZ(at, query_quarter, query_all, send, recv, local.at[18], 41)
        around.begin()
        keep = Keep(whole, all_rows, local, 6)

        def times(rows):
            qkv[rows] = dot_flip(whole[rows], weight[...]).astype(bf16)

        def work(s, rows):
            keep.block(s, rows)

            @pl.when(s == 4)
            def _():
                for copy in others:
                    copy.wait_recv()
                at.start_beside(0)
                at.flush(0, 1, 2)

            @pl.when(s >= 4)
            def _():
                times(rows)

            @pl.when(s == 6)
            def _():
                outputs.begin()
                around.pass_on()

        gather.each(work)
        around.pass_near()
        outputs.pass_on()
        outputs.pass_near()

        def rest(s, carry):
            times(gather.place(s))
            return carry

        lax.fori_loop(0, 4, rest, 0)
        at.flush(4)
        outputs.pass_far()
        around.pass_far()
        text_go.wait()
        text_pair[...] = (text_parts[at.n] + text_got[...]).astype(bf16)
        outputs.got(4, 7, 8, 9, 10)
        keep.wait()
        for copy in [vectors_go, over] + others:
            copy.wait_send()
        outputs.end()
        queries.end()
        around.end()

    return call(
        body,
        number,
        [layer_input, *gains, *weights, query_t, cross_out, texts, pair_t],
        [
            shape(BLOCK, D),
            shape(8, D, dtype=f32),
            shape(3 * COLS, D),
            shape(D, D),
            shape(D, 3 * COLS),
            shape(D, D),
            shape(D, QUARTER),
            shape(64, 2 * COLS),
        ],
        [
            VMEM((BLOCK, D), bf16),
            VMEM((D, D), bf16),
            VMEM((COLS, QUARTER), bf16),
            VMEM((COLS, QUARTER), bf16),
            VMEM((D, QUARTER), bf16),
            VMEM((2, 64, 2 * COLS), f32),
            VMEM((64, 2 * COLS), f32),
            VMEM((8, HALF), f32),
            *sems(54),
        ],
        beside,
        lambda at: ring_peers(at) + relay.peers(at) + [("x", at.x()), ("z2", at.at_z(2))] + GatherZ.peers(at),
        spaces=[ANY] + [PLAIN] * 6 + [VMEM] * 7,
        out_spaces=[VMEM, VMEM, VMEM, ANY, VMEM, ANY, VMEM, VMEM],
        late=True,
    )


def causal_forward(number, joined, down, out_quarter, beside):
    at_once = 512

    def body(at, ins, outs, kept):
        (qkv, block, quarter), (out, logs, all_down, out_all) = ins, outs
        parts, mixed, send, recv, local = kept
        first = Gather(at, block, all_down, send, recv, local.at[0])
        second = GatherZ(at, quarter, out_all, send, recv, local.at[1], 11)
        second.begin()
        first.begin()
        for i in range(3):
            for h in range(HEADS):
                a = i * COLS + h * HDIM
                piece = qkv[:, a : a + HDIM]
                parts[i, h] = piece * EIGHTH if i == 0 else piece
        square = (at_once, at_once)
        seen = lax.broadcasted_iota(jnp.int32, square, 0) >= lax.broadcasted_iota(jnp.int32, square, 1)

        def one(h, carry):
            for i in reversed(range(D // at_once)):
                before, upto = i * at_once, (i + 1) * at_once
                rows = slice(before, upto)
                scores = dot_flip(parts[0, h, rows], parts[1, h, 0:upto])
                last = jnp.where(seen, scores[:, before:], NEGATIVE)
                scores = jnp.concatenate((scores[:, :before], last), axis=1) if i else last
                peak = jnp.max(scores, axis=1, keepdims=True)
                raised = jnp.exp(scores - peak)
                total = jnp.sum(raised, axis=1, keepdims=True)
                mixed[h, rows] = (dot(raised.astype(bf16), parts[2, h, 0:upto]) / total).astype(bf16)
                column = jnp.broadcast_to(peak + jnp.log(total), (at_once, 128))
                logs[pl.ds(h, 1), rows] = column.T[0:1, :]

            @pl.when(h == 1)
            def _():
                first.pass_on()
                second.pass_on()

            return carry

        lax.fori_loop(0, HEADS, one, 0)
        first.pass_near()
        second.pass_near()
        out[...] = jnp.concatenate([mixed[h] for h in range(HEADS)], axis=1)
        at.flush()
        first.pass_far()
        second.pass_far()
        first.got(4, 7, 8, 9, 10)
        first.end()
        second.end()

    return call(
        body,
        number,
        [joined, down, out_quarter],
        [shape(D, COLS), shape(8, D, dtype=f32), shape(D, D), shape(D, D)],
        [VMEM((3, HEADS, D, HDIM), bf16), VMEM((HEADS, D, HDIM), bf16), *sems(22)],
        beside,
        lambda at: ring_peers(at) + GatherZ.peers(at),
        out_spaces=[VMEM, VMEM, ANY, ANY],
    )


def forward_rest(number, attended, out_w, x, vectors, query_all, out_all, texts, all_down, expand_w, contract):
    def body(at, ins, outs, kept):
        mixed, out_own, out_got, x, vectors, query_all, out_all, texts, all_down, expand_own, expand_got, contract_own = ins
        middle, after, normed_two, weights, all_rows, activated, grad, contract_out, keys_out, values_out, traded = outs
        *refs, normed, whole, downs, out_full, expand_full, contract_full, key_full, value_full, branch, scores_all, send, recv, local = kept
        half = at.half(at.n)
        weight = Whole(at, out_own, out_got, out_full, local.at[pl.ds(0, 2)], 1)
        swap = remote(contract_own, contract_full.at[:, half], send.at[21], recv.at[21], at.x())
        swap.start()
        factors = [
            pltpu.make_async_copy(query_all, key_full, local.at[2]),
            pltpu.make_async_copy(out_all, value_full, local.at[3]),
        ]
        for copy in factors:
            copy.start()
        later = [
            pltpu.make_async_copy(contract_own, contract_full.at[:, half], local.at[4]),
            pltpu.make_async_copy(all_down, downs, local.at[7]),
        ]
        for copy in later:
            copy.start()
        later.append(Whole(at, expand_own, expand_got, expand_full, local.at[pl.ds(5, 2)], 0))
        weight.wait()
        scatter = Scatter(at, send, recv, refs)
        scatter.products(lambda rows: dot(mixed[rows], out_full[...]))
        for copy in factors:
            copy.wait()

        def make(b, carry):
            for h in range(HEADS):
                rows = pl.ds(pl.multiple_of(b * BLOCK + h * 64, 64), 64)
                text_keys = texts[b, :, h * HDIM : (h + 1) * HDIM]
                text_values = texts[b, :, COLS + h * HDIM : COLS + (h + 1) * HDIM]
                key_full[rows] = (dot(text_keys, key_full[rows]) * EIGHTH).astype(bf16)
                value_full[rows] = dot(text_values, value_full[rows]).astype(bf16)
            return carry

        lax.fori_loop(0, 8, make, 0)
        made = [
            pltpu.make_async_copy(key_full, keys_out, local.at[8]),
            pltpu.make_async_copy(value_full, values_out, local.at[9]),
        ]
        for copy in made:
            copy.start()
        scatter.middle()
        for copy in later:
            copy.wait()
        scatter.arrive()

        def norm_two(rows, carry):
            total = x[rows].astype(f32) + scatter.total(rows)
            middle[rows] = total
            centred, _ = standard(total)
            normed_two[rows] = (centred * vectors[2:3] + vectors[3:4]).astype(bf16)

        by_rows(BLOCK, 32, norm_two)

        trade = Trade(at, weights, traded, send, recv, local.at[20], 22)

        def score(rows, carry):
            scores_all[rows] = dot_flip(key_full[rows], normed_two[...])

        by_rows(D, QUARTER, score)

        def cross(b, carry):
            rows = pl.ds(pl.multiple_of(b * BLOCK, BLOCK), BLOCK)
            scores = scores_all[rows].reshape(HEADS, 64, BLOCK)
            raised = jnp.exp(scores - jnp.max(scores, axis=1, keepdims=True))
            p = raised / jnp.sum(raised, axis=1, keepdims=True)
            p = p.reshape(BLOCK, BLOCK).T.astype(bf16)
            weights[b] = p
            trade.give(b)
            part = dot(p, value_full[rows])

            @pl.when(b == 0)
            def _():
                branch[...] = part

            @pl.when(b > 0)
            def _():
                branch[...] += part

            return carry

        lax.fori_loop(0, 8, cross, 0)

        def norm_three(rows, carry):
            total = middle[rows] + branch[rows]
            after[rows] = total
            centred, _ = standard(total)
            normed[rows] = (centred * vectors[4:5] + vectors[5:6]).astype(bf16)

        by_rows(BLOCK, 32, norm_three)
        gather = Gather(at, normed, whole, send, recv, local.at[10], 10)
        gather.begin()
        at.flush(0, 1, 2, 3)
        swap.wait_recv()
        keep_contract = pltpu.make_async_copy(contract_full, contract_out, local.at[11])
        keep_contract.start()
        keep = Keep(whole, all_rows, local, 12)

        def ahead(rows, carry):
            grad[rows] = dot_flip(downs[rows], contract_full[...]).astype(bf16)

        by_rows(D, BLOCK, ahead)

        def work(s, rows):
            keep.block(s, rows)
            hidden = dot(whole[rows], expand_full[...])
            bell = 0.5 * (1.0 + lax.erf(hidden * ROOT_HALF))
            activated[rows] = (hidden * bell).astype(bf16)
            slope = bell + hidden * jnp.exp(-0.5 * hidden * hidden) * GAUSS_NORM
            grad[rows] = (grad[rows].astype(f32) * slope).astype(bf16)

        gather.each(work)
        at.flush()
        keep.wait()
        keep_contract.wait()
        trade.end()
        for copy in made:
            copy.wait()
        scatter.end()
        swap.wait_send()

    results, _ = call(
        body,
        number,
        [attended, *out_w, x, vectors, query_all, out_all, texts, all_down, *expand_w, contract],
        [
            shape(BLOCK, D, dtype=f32),
            shape(BLOCK, D, dtype=f32),
            shape(BLOCK, D),
            shape(8, BLOCK, BLOCK),
            shape(D, D),
            shape(D, HALF),
            shape(D, HALF),
            shape(HALF, D),
            shape(D, D),
            shape(D, D),
            shape(8, BLOCK, BLOCK),
        ],
        [
            *Scatter.scratch,
            VMEM((BLOCK, D), bf16),
            VMEM((D, D), bf16),
            VMEM((D, D), bf16),
            VMEM((COLS, D), bf16),
            VMEM((D, HALF), bf16),
            VMEM((HALF, D), bf16),
            VMEM((D, D), bf16),
            VMEM((D, D), bf16),
            VMEM((BLOCK, D), f32),
            VMEM((D, BLOCK), f32),
            *sems(30),
        ],
        (),
        lambda at: Trade.peers(at) + [("x", at.x())],
        spaces=[VMEM, ANY, ANY, VMEM, VMEM, ANY, ANY, VMEM, ANY, ANY, ANY, ANY],
        out_spaces=[VMEM, VMEM, VMEM, VMEM, ANY, VMEM, VMEM, ANY, ANY, ANY, ANY],
    )
    return results


def backward_rest(
    number, grad, expand_w, after, middle, vectors, down, keys, values, weights, out_w, contract_sum, expand_sum, beside
):
    def body(at, ins, outs, kept):
        grad, expand_own, expand_got, after, middle, vectors, down, keys, values, weights, out_own, out_got = ins[:12]
        grad_rows, rounded_two, traded, all_two, all_rows, grad_mixed, grad_vectors = outs[:7]
        *refs, rounded, whole, second, out_full, expand_full, key_full, value_full, grad_scores, grads_all, send, recv, local = kept
        reduces = [
            Reduce(at, ins[12], outs[7], refs[7:11], send, recv, local, 32, 16, False),
            Reduce(at, ins[13], outs[8], refs[11:15], send, recv, local, 42, 18, True, True),
        ]
        refs = refs[:7]
        for reduce in reduces:
            reduce.first()
        weight = Whole(at, expand_own, expand_got, expand_full, local.at[pl.ds(0, 2)], 0)
        later = [
            pltpu.make_async_copy(keys, key_full, local.at[2]),
            pltpu.make_async_copy(values, value_full, local.at[3]),
        ]
        for copy in later:
            copy.start()
        later.append(Whole(at, out_own, out_got, out_full, local.at[pl.ds(4, 2)], 1))
        weight.wait()
        scatter = Scatter(at, send, recv, refs)
        scatter.products(lambda rows: dot_flip(grad[rows], expand_full[...]))
        scatter.middle()
        for copy in later:
            copy.wait()
        scatter.arrive()

        def norm_three(rows, carry):
            incoming = scatter.total(rows)
            centred, factor = standard(after[rows])
            total = down[rows].astype(f32) + norm_back(incoming, centred, factor, vectors[4:5])
            grad_rows[rows] = total
            rounded_two[rows] = total.astype(bf16)
            return two_sums(incoming, centred, carry)

        gains, shifts = by_rows(BLOCK, 32, norm_three, no_sums())
        before = Gather(at, rounded_two, all_two, send, recv, local.at[6], 10)
        before.begin()
        for reduce in reduces:
            reduce.second()
        at.start_beside()
        grad_vectors[4:5] = gains
        grad_vectors[5:6] = shifts

        trade = Trade(at, grad_scores, traded, send, recv, local.at[20], 52)

        def score(rows, carry):
            grads_all[rows] = dot_flip(value_full[rows], rounded_two[...])

        by_rows(D, QUARTER, score)

        def cross(b, carry):
            rows = pl.ds(pl.multiple_of(b * BLOCK, BLOCK), BLOCK)
            p = weights[b].astype(f32).T.reshape(HEADS, 64, BLOCK)
            dp = grads_all[rows].reshape(HEADS, 64, BLOCK)
            ds = p * (dp - jnp.sum(p * dp, axis=1, keepdims=True))
            ds = ds.reshape(BLOCK, BLOCK).T.astype(bf16)
            grad_scores[b] = ds
            trade.give(b)
            part = dot(ds, key_full[rows])

            @pl.when(b == 0)
            def _():
                second[...] = part

            @pl.when(b > 0)
            def _():
                second[...] += part

            @pl.when(b == 3)
            def _():
                before.pass_on()

            @pl.when(b == 5)
            def _():
                for reduce in reduces:
                    reduce.third()

            return carry

        lax.fori_loop(0, 8, cross, 0)
        at.flush(1)
        for reduce in reduces:
            reduce.fourth()

        def norm_two(rows, carry):
            incoming = second[rows]
            centred, factor = standard(middle[rows])
            total = grad_rows[rows] + norm_back(incoming, centred, factor, vectors[2:3])
            grad_rows[rows] = total
            rounded[rows] = total.astype(bf16)
            return two_sums(incoming, centred, carry)

        gains, shifts = by_rows(BLOCK, 32, norm_two, no_sums())
        grad_vectors[2:3] = gains
        grad_vectors[3:4] = shifts
        gather = Gather(at, rounded, whole, send, recv, local.at[7], 21)
        before.pass_near()
        gather.begin()
        at.flush(0, 6)
        before.pass_far()
        keep = Keep(whole, all_rows, local, 8)

        def work(s, rows):
            keep.block(s, rows)
            grad_mixed[rows] = dot_flip(whole[rows], out_full[...]).astype(bf16)

        gather.each(work)
        at.flush()
        before.got(4, 7, 8, 9, 10)
        before.end()
        trade.end()
        keep.wait()
        scatter.end()
        for reduce in reduces:
            reduce.end()

    return call(
        body,
        number,
        [grad, *expand_w, after, middle, vectors, down, keys, values, weights, *out_w, contract_sum, expand_sum],
        [
            shape(BLOCK, D, dtype=f32),
            shape(BLOCK, D),
            shape(8, BLOCK, BLOCK),
            shape(D, D),
            shape(D, D),
            shape(D, COLS),
            shape(8, D, dtype=f32),
            shape(4, 2, 96, HALF),
            shape(4, 2, 96, HALF),
        ],
        [
            *Scatter.scratch,
            *Reduce.scratch(96, False),
            *Reduce.scratch(96, True, True),
            VMEM((BLOCK, D), bf16),
            VMEM((D, D), bf16),
            VMEM((BLOCK, D), f32),
            VMEM((COLS, D), bf16),
            VMEM((D, HALF), bf16),
            VMEM((D, D), bf16),
            VMEM((D, D), bf16),
            VMEM((8, BLOCK, BLOCK), bf16),
            VMEM((D, BLOCK), f32),
            *sems(60),
        ],
        beside,
        lambda at: Trade.peers(at) + Reduce.peers(at),
        spaces=[VMEM, ANY, ANY, VMEM, VMEM, VMEM, VMEM, ANY, ANY, VMEM, ANY, ANY, ANY, ANY],
        out_spaces=[VMEM, VMEM, ANY, ANY, ANY, VMEM, VMEM, ANY, ANY],
        late=True,
    )


def causal_backward(number, joined, grad, logs, activated, contract, after, normed_two, part, beside):
    at_once = 512

    def body(at, ins, outs, kept):
        (qkv, go, log_rows, activated, contract, after, block, part), (out, result, all_rows, summed) = ins, outs
        *refs, parts, key_sum, value_sum, send, recv, local = kept
        reduce = Reduce(at, part, summed, refs[7:], send, recv, local, 21, 1, False)
        reduce.first()
        gather = Gather(at, block, all_rows, send, recv, local.at[0], 10)
        gather.begin()
        scatter = Scatter(at, send, recv, refs[:7])
        scatter.products(lambda rows: dot(activated[rows], contract[...]))
        gather.pass_on()
        for i in range(4):
            for h in range(HEADS):
                a = i * COLS + h * HDIM
                piece = qkv[:, a : a + HDIM] if i < 3 else go[:, h * HDIM : (h + 1) * HDIM]
                parts[i, h] = piece * EIGHTH if i == 0 else piece
        square = (at_once, at_once)
        seen = lax.broadcasted_iota(jnp.int32, square, 1) >= lax.broadcasted_iota(jnp.int32, square, 0)
        blocks = D // at_once

        def one(h, carry):
            turned = parts[1, h].T
            query_parts = []
            for i in reversed(range(blocks)):
                before, upto = i * at_once, (i + 1) * at_once
                rows = slice(before, upto)
                q, g = parts[0, h, rows], parts[3, h, rows]
                k, v = parts[1, h, 0:upto], parts[2, h, 0:upto]
                p = jnp.exp(dot_flip(k, q) - log_rows[pl.ds(h, 1), rows])
                last = jnp.where(seen, p[before:], 0.0)
                p = jnp.concatenate((p[:before], last), axis=0) if i else last
                dp = dot_flip(v, g)
                ds = (p * (dp - jnp.sum(p * dp, axis=0, keepdims=True))).astype(bf16)
                value_part, key_part = dot(p.astype(bf16), g), dot(ds, q)
                if i == blocks - 1:
                    key_sum[0:upto, :] = key_part
                    value_sum[0:upto, :] = value_part
                else:
                    key_sum[0:upto, :] += key_part
                    value_sum[0:upto, :] += value_part
                query_parts.append((dot(turned[:, 0:upto], ds) * EIGHTH).T)
                if i == blocks - 1:

                    @pl.when(h == 1)
                    def _():
                        reduce.second()

                    @pl.when(h == 2)
                    def _():
                        reduce.fourth()

            parts[0, h] = jnp.concatenate(query_parts[::-1], axis=0).astype(bf16)
            parts[1, h] = key_sum[...].astype(bf16)
            parts[2, h] = value_sum[...].astype(bf16)

            @pl.when(h == 0)
            def _():
                gather.pass_near()

            @pl.when(h == 1)
            def _():
                scatter.middle()
                gather.pass_far()
                reduce.third()

            return carry

        lax.fori_loop(0, HEADS, one, 0)
        for i in range(3):
            out[:, i * COLS : (i + 1) * COLS] = jnp.concatenate([parts[i, h] for h in range(HEADS)], axis=1)
        scatter.arrive()

        def finish(rows, carry):
            result[rows] = (after[rows] + scatter.total(rows)).astype(bf16)

        at.flush(0)
        by_rows(BLOCK, 32, finish)
        at.flush(1)
        gather.got(4, 7, 8, 9, 10)
        gather.end()
        scatter.end()
        reduce.end()

    return call(
        body,
        number,
        [joined, grad, logs, activated, contract, after, normed_two, part],
        [shape(D, 3 * COLS), shape(BLOCK, D), shape(D, D), shape(4, 2, 72, HALF)],
        [
            *Scatter.scratch,
            *Reduce.scratch(72, False),
            VMEM((4, HEADS, D, HDIM), bf16),
            VMEM((D, HDIM), f32),
            VMEM((D, HDIM), f32),
            *sems(31),
        ],
        beside,
        lambda at: ring_peers(at) + Reduce.peers(at),
        spaces=[VMEM] * 7 + [ANY],
        out_spaces=[VMEM, VMEM, ANY, ANY],
    )


def leave(number, grad, joined, x, vectors, grad_rows, sums, late, text_part, beside):
    relay = Relay(jax.ShapeDtypeStruct((BLOCK, D), bf16), True)
    some = 64 // 8

    def ring(at):
        return [{"wide": lax.rem(at.w + k, 8)} for k in range(1, 8)]

    x_steps = ((0, 1), (1, 0), (1, 1))

    def group(at):
        return [(b, {"wide": lax.rem(at.w + k, 8), "narrow": lax.rem(at.n + b, 2)}) for k in range(8) for b in range(2)][1:]

    def peers(at):
        known = ring_peers(at) + relay.peers(at) + Reduce.peers(at)
        known += [(f"w{k}", peer) for k, peer in enumerate(ring(at), 1)]
        return known + [(f"g{i}", peer) for i, (b, peer) in enumerate(group(at)) if b]

    def body(at, ins, outs, kept):
        grad, weight, x, vectors, before, late, text, one, two = ins
        result, out_one, out_two, vector_sums, text_out = outs
        refs, kept = kept[:7], kept[7:]
        reduces = [
            Reduce(at, one, out_one, kept[0:4], kept[-3], kept[-2], kept[-1], 12, 1, False),
            Reduce(at, two, out_two, kept[4:8], kept[-3], kept[-2], kept[-1], 22, 3, True),
        ]
        rounded, parts, ring_parts, ring_sum, x_parts, x_sum, z_parts, text_parts, text_sum, send, recv, local = kept[8:]
        me = at.spot(at.y, at.c)

        def move(slot, source, target, peer):
            return remote(source, target, send.at[slot], recv.at[slot], peer)

        to_ring, to_group = ring(at), group(at)
        slot = 32
        trades = []
        for peer in to_ring:
            there = at.spot(lax.div(peer["wide"], 2), lax.rem(peer["wide"], 2))
            trades.append(move(slot, text.at[there], text_parts.at[me], peer))
            slot += 1
        text_own = pltpu.make_async_copy(text.at[me], text_parts.at[me], local.at[5])
        texts = []
        for b, peer in to_group:
            n = lax.rem(at.n + b, 2)
            texts.append(move(slot, text_sum.at[:, at.half(n)], text_out.at[at.n, me], peer))
            slot += 1
        text_stay = pltpu.make_async_copy(text_sum.at[:, at.half(at.n)], text_out.at[at.n, me], local.at[6])
        rings = []
        for peer in to_ring:
            rings.append(move(slot, parts, ring_parts.at[at.w], peer))
            slot += 1
        ring_own = pltpu.make_async_copy(parts, ring_parts.at[at.w], local.at[7])
        spreads = []
        for a, b in x_steps:
            half = ring_sum.at[:, at.half(lax.rem(at.n + b, 2))]
            spreads.append(move(slot, half, x_parts.at[at.s, at.n], at.at_x(a, b)))
            slot += 1
        x_own = pltpu.make_async_copy(ring_sum.at[:, at.half(at.n)], x_parts.at[at.s, at.n], local.at[8])
        lasts = []
        for k in (1, 2, 3):
            lasts.append(move(slot, x_sum, z_parts.at[at.z], at.at_z(k)))
            slot += 1

        for reduce in reduces:
            reduce.first()
        text_own.start()
        for copy in trades:
            copy.start()
        scatter = Scatter(at, send, recv, refs)
        scatter.products(lambda rows: dot(grad[rows], weight[...]))
        scatter.middle()
        for reduce in reduces:
            reduce.second()
        text_own.wait()
        for copy in trades:
            copy.wait_recv()
        total = text_parts[0].astype(f32)
        for i in range(1, 8):
            total += text_parts[i].astype(f32)
        text_sum[...] = total.astype(bf16)
        text_stay.start()
        for copy in texts:
            copy.start()
        scatter.arrive()
        at.start_beside()

        def norm(rows, carry):
            incoming = scatter.total(rows)
            centred, factor = standard(x[rows].astype(f32))
            total = before[rows] + norm_back(incoming, centred, factor, vectors[0:1])
            rounded[rows] = total.astype(bf16)
            return two_sums(incoming, centred, carry)

        gains, shifts = by_rows(BLOCK, 32, norm, no_sums())
        moving = functools.partial(relay_run, relay, at, rounded, result, send, recv, local.at[0], 10)
        moving(False)
        parts[0:1] = gains
        parts[1:2] = shifts
        parts[2:6] = late[2:6]
        parts[6:8] = jnp.zeros((2, D), f32)
        ring_own.start()
        for copy in rings:
            copy.start()
        for reduce in reduces:
            reduce.third()
        ring_own.wait()
        for copy in rings:
            copy.wait_recv()
        total = ring_parts[0]
        for i in range(1, 8):
            total += ring_parts[i]
        ring_sum[...] = total
        x_own.start()
        for copy in spreads:
            copy.start()
        for reduce in reduces:
            reduce.fourth()
        x_own.wait()
        for copy in spreads:
            copy.wait_recv()
        total = x_parts[0, 0] + x_parts[0, 1] + x_parts[1, 0] + x_parts[1, 1]
        x_sum[...] = total
        for copy in lasts:
            copy.start()
        z_parts[pl.ds(at.z, 1)] = total.reshape(1, 8, HALF)
        for copy in lasts:
            copy.wait_recv()
        vector_sums[...] = z_parts[0] + z_parts[1] + z_parts[2] + z_parts[3]
        at.flush()
        moving(True)
        text_stay.wait()
        for copy in texts:
            copy.wait()
        for copy in trades + rings + spreads + lasts:
            copy.wait_send()
        scatter.end()
        for reduce in reduces:
            reduce.end()

    return call(
        body,
        number,
        [grad, joined, x, vectors, grad_rows, late, text_part, *sums],
        [
            shape(384, HALF),
            shape(4, 2, 72, HALF),
            shape(4, 2, 48, HALF),
            shape(8, HALF, dtype=f32),
            shape(2, 8, some, HALF),
        ],
        [
            *Scatter.scratch,
            *Reduce.scratch(72, False),
            *Reduce.scratch(48, True),
            VMEM((BLOCK, D), bf16),
            VMEM((8, D), f32),
            VMEM((8, 8, D), f32),
            VMEM((8, D), f32),
            VMEM((2, 2, 8, HALF), f32),
            VMEM((8, HALF), f32),
            VMEM((4, 8, HALF), f32),
            VMEM((8, some, D), bf16),
            VMEM((some, D), bf16),
            *sems(32 + 7 + 15 + 7 + 6),
        ],
        beside,
        peers,
        spaces=[VMEM, VMEM, VMEM, VMEM, VMEM, VMEM, ANY, ANY, ANY],
        out_spaces=[ANY, ANY, ANY, VMEM, ANY],
        late=True,
    )


def on_device(
    layer_input,
    text_states,
    cotangent,
    first_gain,
    first_shift,
    query_weight,
    key_weight,
    value_weight,
    output_weight,
    second_gain,
    second_shift,
    cross_query,
    cross_key,
    cross_value,
    cross_output,
    third_gain,
    third_shift,
    expand_weight,
    contract_weight,
):
    gains = (first_gain, first_shift, second_gain, second_shift, third_gain, third_shift)
    weights = [query_weight.T, key_weight.T, value_weight.T]
    query_t = cross_query.T
    pair_t = jnp.concatenate((cross_key.T, cross_value.T), axis=0)
    n = lax.axis_index("narrow")

    results, ((down,), (out_got,), (text_got,)) = enter(
        1,
        layer_input,
        gains,
        weights,
        query_t,
        cross_output,
        text_states,
        pair_t,
        [Relay(cotangent), Give(output_weight), GiveClip(text_states)],
    )
    x, vectors, joined, all_one, qkv, query_all, out_quarter, text_pair = results
    (attended, logs, all_down, out_all), ((texts,), (expand_got,)) = causal_forward(
        2, qkv, down, out_quarter, [ToSpots(text_pair), Give(expand_weight)]
    )
    out_w, expand_w = (output_weight, out_got), (expand_weight, expand_got)
    results = forward_rest(3, attended, out_w, x, vectors, query_all, out_all, texts, all_down, expand_w, contract_weight)
    middle, after, normed_two, cross_p, all_three, activated, grad_expand, contract, all_keys, all_values, traded_p = results

    contract_part = outer(activated, all_down).astype(bf16).reshape(4, 2, 96, D)
    expand_part = outer(all_three, grad_expand).astype(bf16).reshape(2, 4, 2, 96, HALF)
    results, ((query_got,), (cross_got,)) = backward_rest(
        4,
        grad_expand,
        expand_w,
        after,
        middle,
        vectors,
        down,
        all_keys,
        all_values,
        cross_p,
        out_w,
        contract_part,
        expand_part,
        [Give(query_t), Give(cross_output)],
    )
    grad_one, _, grad_scores, all_mid_two, all_mid_one, grad_attended, late, contract_grad, expand_grad = results

    own_first = n == 0

    def whole(own, got):
        return jnp.concatenate((jnp.where(own_first, own, got), jnp.where(own_first, got, own)), axis=1)

    def heads(what, a, b):
        return jnp.einsum(what, a, b, preferred_element_type=f32)

    text = whole(lax.dynamic_index_in_dim(text_states, n, 0, False), text_got)
    text_heads = text_pair.reshape(64, 2, HEADS, HDIM)
    grad_values = outer(traded_p.reshape(D, COLS), all_mid_two).astype(bf16).reshape(HEADS, 64, D)
    heads_out = whole(cross_output, cross_got).reshape(HEADS, HDIM, D)
    grad_text_values = heads("hkf,hdf->khd", grad_values, heads_out).reshape(64, COLS).astype(bf16)
    grad_cross = heads("khd,hkf->hdf", text_heads[:, 1], grad_values).reshape(COLS, D)
    value_part = jnp.concatenate((grad_cross, outer(grad_text_values, text), outer(attended, all_mid_one)), axis=0)
    (grad_qkv, layer_output, all_two, value_grad), ((pair_got,),) = causal_backward(
        5,
        qkv,
        grad_attended,
        logs,
        activated,
        contract,
        after,
        normed_two,
        value_part.astype(bf16).reshape(4, 2, 72, D),
        [Give(pair_t)],
    )

    joined_part = outer(grad_qkv, all_one).astype(bf16).reshape(4, 2, 72, D)
    grad_keys = outer(grad_scores.reshape(D, COLS), all_two).astype(bf16).reshape(HEADS, 64, D)
    heads_query = whole(query_t, query_got).reshape(HEADS, HDIM, D)
    grad_text_keys = (heads("hkf,hdf->khd", grad_keys, heads_query) * EIGHTH).reshape(64, COLS).astype(bf16)
    grad_query = heads("khd,hkf->hdf", text_heads[:, 0], grad_keys).reshape(COLS, D) * EIGHTH
    key_part = jnp.concatenate((grad_query, outer(grad_text_keys, text)), axis=0).astype(bf16).reshape(4, 2, 48, D)
    grad_pair = jnp.concatenate((grad_text_keys, grad_text_values), axis=1)
    text_part = dot(grad_pair, whole(pair_t, pair_got)).astype(bf16).reshape(8, 8, D)

    (input_grad, joined_grad, key_grad, parts, text_grad), ((layer_output,),) = leave(
        6,
        grad_qkv,
        joined,
        x,
        vectors,
        grad_one,
        (joined_part, key_part),
        late,
        text_part,
        [Relay(layer_output, True)],
    )
    joined_grad, key_grad, value_grad, expand_grad, contract_grad = (
        grad.reshape(-1, HALF).astype(f32) for grad in (joined_grad, key_grad, value_grad, expand_grad, contract_grad)
    )
    return (
        layer_output,
        input_grad.astype(f32),
        text_grad.reshape(2, 64, HALF).astype(f32),
        parts[0],
        parts[1],
        joined_grad[:COLS].T,
        joined_grad[COLS : 2 * COLS].T,
        joined_grad[2 * COLS :].T,
        value_grad[2 * COLS :],
        parts[2],
        parts[3],
        key_grad[:COLS].T,
        key_grad[COLS:].T,
        value_grad[COLS : 2 * COLS].T,
        value_grad[:COLS],
        parts[4],
        parts[5],
        expand_grad,
        contract_grad,
    )


def solution(mesh):
    return jax.shard_map(
        on_device,
        mesh=mesh,
        in_specs=(
            P(("dp", "wide"), "narrow"),
            P("dp", None, "narrow"),
            P(("dp", "wide"), "narrow"),
            P("narrow"),
            P("narrow"),
            P("narrow", "wide"),
            P("narrow", "wide"),
            P("narrow", "wide"),
            P("wide", "narrow"),
            P("narrow"),
            P("narrow"),
            P("narrow", "wide"),
            P("narrow", "wide"),
            P("narrow", "wide"),
            P("wide", "narrow"),
            P("narrow"),
            P("narrow"),
            P("narrow", "wide"),
            P("wide", "narrow"),
        ),
        out_specs=(
            P(("dp", "wide"), "narrow"),
            P(("dp", "wide"), "narrow"),
            P("dp", None, "narrow"),
            P("narrow"),
            P("narrow"),
            P("narrow", "wide"),
            P("narrow", "wide"),
            P("narrow", "wide"),
            P("wide", "narrow"),
            P("narrow"),
            P("narrow"),
            P("narrow", "wide"),
            P("narrow", "wide"),
            P("narrow", "wide"),
            P("wide", "narrow"),
            P("narrow"),
            P("narrow"),
            P("narrow", "wide"),
            P("wide", "narrow"),
        ),
        check_vma=False,
    )
```

```python
import functools
import math

import jax
import jax.numpy as jnp
from jax import lax
from jax.experimental import pallas as pl
from jax.experimental.pallas import tpu as pltpu
from jax.sharding import PartitionSpec as P

D = 1536
HALF = 768
HDIM = 64
HEADS = 3
COLS = HEADS * HDIM
BLOCK = 192
EPSILON = 1e-05
NEGATIVE = -1e30
ROOT_HALF = 0.7071067811865476
GAUSS_NORM = 0.3989422804014327
MESH = pl.DeviceIdType.MESH
VMEM = pltpu.VMEM
ANY = pl.ANY
bf16, f32 = jnp.bfloat16, jnp.float32


def dot(a, b):
    return lax.dot_general(a, b, (((1,), (0,)), ((), ())), preferred_element_type=f32)


def dot_flip(a, b):
    return lax.dot_general(a, b, (((1,), (1,)), ((), ())), preferred_element_type=f32)


def outer(a, b):
    return lax.dot_general(a, b, (((0,), (0,)), ((), ())), preferred_element_type=f32)


class Place:
    def __init__(self):
        self.dp, self.w, self.n = (lax.axis_index(a) for a in ("dp", "wide", "narrow"))
        self.y, self.c = lax.div(self.w, 2), lax.rem(self.w, 2)
        self.z, self.s = lax.div(self.dp, 2), lax.rem(self.dp, 2)
        self.up, self.down = lax.rem(self.y + 1, 4), lax.rem(self.y + 3, 4)
        self.across = 3 - self.y
        self.moved = lax.rem(lax.div(self.y, 2) + self.n, 2)
        self.clip = lax.div(self.y, 2)

    def spot(self, y, c):
        moved = lax.rem(lax.div(y, 2) + self.n, 2)
        return (lax.rem(y + moved, 2) * 2 + c) * 2 + moved

    def rows(self, y, c, start=0, size=BLOCK):
        return pl.ds(pl.multiple_of(self.spot(y, c) * BLOCK + start, 32), size)

    def half(self, n):
        return pl.ds(pl.multiple_of(n * HALF, HALF), HALF)

    def at_y(self, y):
        return {"wide": y * 2 + self.c}

    def core(self):
        return {"wide": self.y * 2 + 1 - self.c}

    def x(self):
        return {"narrow": 1 - self.n}

    def at_z(self, k):
        return {"dp": lax.rem(self.z + k, 4) * 2 + self.s}

    def at_dp(self, k):
        return {"dp": lax.rem(self.dp + k, 8)}

    def at_x(self, ds, dn):
        return {"dp": self.z * 2 + lax.rem(self.s + ds, 2), "narrow": lax.rem(self.n + dn, 2)}


def remote(src, dst, send, recv, peer):
    return pltpu.make_async_remote_copy(
        src_ref=src, dst_ref=dst, send_sem=send, recv_sem=recv, device_id=peer, device_id_type=MESH
    )


def greet(peers):
    barrier = pltpu.get_barrier_semaphore()
    for peer in peers:
        pl.semaphore_signal(barrier, inc=1, device_id=peer, device_id_type=MESH)
    pl.semaphore_wait(barrier, len(peers))


class Give:
    def __init__(self, array):
        self.ins, self.copies, self.locals = [array], 1, 0
        self.outs = [jax.ShapeDtypeStruct(array.shape, array.dtype)]

    def peers(self, at):
        return [("x", at.x())]

    def moves(self, at, ins, outs):
        return [(ins[0], outs[0], at.x())], []


class GiveClip(Give):
    def __init__(self, array):
        super().__init__(array)
        self.outs = [jax.ShapeDtypeStruct(array.shape[1:], array.dtype)]

    def moves(self, at, ins, outs):
        return [(ins[0].at[1 - at.n], outs[0], at.x())], []


class ToSpots:
    def __init__(self, array):
        self.ins, self.copies, self.locals = [array], 7, 1
        self.outs = [jax.ShapeDtypeStruct((8, *array.shape), array.dtype)]

    def peers(self, at):
        return [(f"w{k}", {"wide": lax.rem(at.w + k, 8)}) for k in range(1, 8)]

    def moves(self, at, ins, outs):
        dst = outs[0].at[at.spot(at.y, at.c)]
        return [(ins[0], dst, peer) for _, peer in self.peers(at)], [(ins[0], dst)]


class Relay:
    def __init__(self, array, back=False):
        self.ins, self.back, self.copies, self.locals = [array], back, 2, 1
        shape = (384, HALF) if back else (BLOCK, D)
        self.outs = [jax.ShapeDtypeStruct(shape, array.dtype)]

    def peers(self, at):
        return [
            ("x", at.x()),
            ("a0", {"wide": at.across * 2 + at.c}),
            ("a1", {"wide": at.across * 2 + at.c, "narrow": 1 - at.n}),
        ]


def relay_run(relay, at, src, dst, send, recv, local, base, finish):
    mine, other = at.half(at.n), at.half(1 - at.n)
    over = at.across * 2 + at.c
    if relay.back:
        row = pl.ds(pl.multiple_of(at.moved * BLOCK, BLOCK), BLOCK)
        to = recv.at[base + at.moved]
        own = src.at[:, mine], src.at[:, other]
        land = dst.at[0:BLOCK], dst.at[BLOCK : 2 * BLOCK]
    else:
        row = mine
        to = recv.at[base + at.n]
        own = src.at[0:BLOCK], src.at[BLOCK : 2 * BLOCK]
        land = dst.at[:, at.half(0)], dst.at[:, at.half(1)]
    target = dst.at[row] if relay.back else dst.at[:, row]

    def arrive(slot, part):
        return remote(own[0], part, send.at[base], recv.at[base + slot], at.x())

    @pl.when(at.moved == 0)
    def _():
        stay = pltpu.make_async_copy(own[0], target, local)
        if relay.back:
            go = remote(own[1], target, send.at[base], to, at.x())
        else:
            go = remote(own[1], target, send.at[base], to, {"wide": over})
        if not finish:
            go.start()
            stay.start()
        else:
            stay.wait()
            go.wait_send()
            if relay.back:
                arrive(1, land[1]).wait_recv()
            else:
                arrive(1 - at.n, dst.at[:, other]).wait_recv()

    @pl.when(at.moved == 1)
    def _():
        if relay.back:
            first = remote(own[1], target, send.at[base], to, {"wide": over, "narrow": 1 - at.n})
            second = remote(own[0], target, send.at[base + 1], to, {"wide": over})
        else:
            first = remote(own[1], target, send.at[base], to, {"wide": over, "narrow": 1 - at.n})
            second = remote(own[0], target, send.at[base + 1], to, at.x())
        if not finish:
            first.start()
            second.start()
        else:
            first.wait_send()
            second.wait_send()
            arrive(0, land[0]).wait_recv()
            arrive(1, land[1]).wait_recv()


def call(body, number, ins, outs, scratch=(), beside=(), peers=None, spaces=None, out_spaces=None, late=False, early=None):
    spaces = spaces or [VMEM] * len(ins)
    out_spaces = out_spaces or [VMEM] * len(outs)
    copies = sum(b.copies for b in beside)
    locals_ = sum(b.locals for b in beside)
    side_ins = [a for b in beside for a in b.ins]
    side_outs = [a for b in beside for a in b.outs]
    n_in, n_out, n_scratch = len(ins), len(outs), len(scratch)
    loaded = [i for i, m in enumerate(spaces) if m is VMEM]
    stored = [i for i, m in enumerate(out_spaces) if m is VMEM]
    buffers = [VMEM(ins[i].shape, ins[i].dtype) for i in loaded] + [VMEM(outs[i].shape, outs[i].dtype) for i in stored]

    def kernel(*refs):
        at = Place()
        refs = list(refs)

        def take(count):
            out = refs[:count]
            del refs[:count]
            return out

        main_in, side_in = take(n_in), take(len(side_ins))
        main_out, side_out, kept = take(n_out), take(len(side_outs)), take(n_scratch)
        in_buffers, out_buffers = take(len(loaded)), take(len(stored))
        send, recv, local, passing = take(4)
        loads, stores = [], {}
        for k, i in enumerate(loaded):
            loads.append(pltpu.make_async_copy(main_in[i], in_buffers[k], passing.at[k]))
            loads[-1].start()
            main_in[i] = in_buffers[k]
        for k, i in enumerate(stored):
            stores[i] = pltpu.make_async_copy(out_buffers[k], main_out[i], passing.at[len(loaded) + k])
            main_out[i] = out_buffers[k]
        waiting = dict(stores)

        def flush(*which):
            for i in which or list(waiting):
                waiting.pop(i).start()

        at.flush = flush
        if early:
            at.early = early(at, main_in, kept)
        known = dict(peers(at)) if peers else {}
        for b in beside:
            known.update(dict(b.peers(at)))
        if "w1" in known:
            for name in ("up", "down", "core", "a0"):
                known.pop(name, None)
        if "x01" in known:
            known.pop("x", None)
        if known:
            greet(list(known.values()))
        side_refs = [([side_in.pop(0) for _ in b.ins], [side_out.pop(0) for _ in b.outs]) for b in beside]
        begin, todo = [], []
        slot, place = 0, 0
        for b, (i, o) in zip(beside, side_refs):
            if isinstance(b, Relay):
                run = functools.partial(relay_run, b, at, i[0], o[0], send, recv, local.at[place], slot)
                begin.append([functools.partial(run, False)])
                todo.append(functools.partial(run, True))
                slot, place = slot + 2, place + 1
                continue
            far, near = b.moves(at, i, o)
            begin.append([])
            for src, dst, peer in far:
                copy = remote(src, dst, send.at[slot], recv.at[slot], peer)
                begin[-1].append(copy.start)
                todo.append(copy.wait)
                slot += 1
            for src, dst in near:
                copy = pltpu.make_async_copy(src, dst, local.at[place])
                begin[-1].append(copy.start)
                todo.append(copy.wait)
                place += 1

        def start(*which):
            for i in which or range(len(begin)):
                for go in begin[i]:
                    go()

        at.start_beside = start
        if not late:
            start()
        for copy in loads:
            copy.wait()
        if body:
            body(at, main_in, main_out, kept)
        flush()
        for wait in todo:
            wait()
        for copy in stores.values():
            copy.wait()

    results = pl.pallas_call(
        kernel,
        out_shape=tuple(outs) + tuple(side_outs),
        in_specs=[pl.BlockSpec(memory_space=VMEM if m == PLAIN else ANY) for m in spaces]
        + [pl.BlockSpec(memory_space=ANY)] * len(side_ins),
        out_specs=(pl.BlockSpec(memory_space=ANY),) * (len(outs) + len(side_outs)),
        scratch_shapes=[
            *scratch,
            *buffers,
            pltpu.SemaphoreType.DMA((max(copies, 1),)),
            pltpu.SemaphoreType.DMA((max(copies, 1),)),
            pltpu.SemaphoreType.DMA((max(locals_, 1),)),
            pltpu.SemaphoreType.DMA((max(len(buffers), 1),)),
        ],
        compiler_params=pltpu.CompilerParams(
            collective_id=number, has_side_effects=True, vmem_limit_bytes=58 << 20
        ),
    )(*ins, *side_ins)
    results = list(results)
    main, rest = results[: len(outs)], results[len(outs) :]
    sides = []
    for b in beside:
        sides.append(rest[: len(b.outs)])
        del rest[: len(b.outs)]
    return main, sides


PLAIN = "plain"


def ring_peers(at):
    return [("up", at.at_y(at.up)), ("down", at.at_y(at.down)), ("core", at.core())]


def sems(count):
    return [pltpu.SemaphoreType.DMA((count,)), pltpu.SemaphoreType.DMA((count,)), pltpu.SemaphoreType.DMA((count,))]


def by_rows(count, size, work, carry=None):
    def step(i, carry):
        return work(pl.ds(pl.multiple_of(i * size, size), size), carry)

    return lax.fori_loop(0, count // size, step, carry)


class Whole:
    def __init__(self, at, own, got, full, sem, axis):
        size = own.shape[axis]
        self.copies = []
        for i, (part, n) in enumerate(((own, at.n), (got, 1 - at.n))):
            where = pl.ds(pl.multiple_of(n * size, size), size)
            target = full.at[where] if axis == 0 else full.at[:, where]
            self.copies.append(pltpu.make_async_copy(part, target, sem.at[i]))
            self.copies[-1].start()

    def wait(self):
        for copy in self.copies:
            copy.wait()


class Trade:
    def __init__(self, at, parts, out, send, recv, local, base):
        self.at, self.parts, self.out, self.send, self.recv, self.base = at, parts, out, send, recv, base
        self.me = at.spot(at.y, at.c)
        self.own = pltpu.make_async_copy(parts.at[self.me], out.at[self.me], local)

    @staticmethod
    def peers(at):
        return [(f"w{k}", {"wide": lax.rem(at.w + k, 8)}) for k in range(1, 8)]

    def copy(self, b, place):
        m, core, a = lax.rem(b, 2), lax.rem(lax.div(b, 2), 2), lax.div(b, 4)
        y = 2 * lax.rem(m + self.at.n, 2) + lax.rem(a + m, 2)
        send, recv = self.send.at[self.base + b], self.recv.at[self.base + place]
        return remote(self.parts.at[b], self.out.at[place], send, recv, {"wide": y * 2 + core})

    def give(self, b):
        @pl.when(b == self.me)
        def _():
            self.own.start()

        @pl.when(b != self.me)
        def _():
            self.copy(b, self.me).start()

    def end(self):
        def wait(b, carry):
            @pl.when(b == self.me)
            def _():
                self.own.wait()

            @pl.when(b != self.me)
            def _():
                self.copy(b, b).wait()

            return carry

        lax.fori_loop(0, 8, wait, 0)


class Reduce:
    @staticmethod
    def scratch(deep, x_first, by_rows=False):
        first = (4, deep, HALF) if x_first else (2, 2, deep, HALF) if by_rows else (2, deep, D)
        return [VMEM((3, *first), bf16), VMEM(first, bf16), VMEM((3, deep, HALF), bf16), VMEM((2, deep, HALF), bf16)]

    @staticmethod
    def peers(at):
        return [(f"z{k}", at.at_z(k)) for k in (1, 2, 3)] + [(f"x{a}{b}", at.at_x(a, b)) for a, b in ((0, 1), (1, 0), (1, 1))]

    def __init__(self, at, src, out, refs, send, recv, local, base, place, x_first, by_rows=False):
        self.at, self.src, self.out = at, src, out
        self.land, self.total, self.land_two, self.last = refs
        self.x_first, self.by_rows = x_first, by_rows
        self.deep = self.last.shape[1]
        self.chunk = 32 if self.deep % 32 == 0 else 24
        z_steps = [(at.at_z(k), lax.rem(at.z + k, 4)) for k in (1, 2, 3)]
        x_steps = [
            (at.at_x(a, b), (lax.rem(at.s + a, 2), lax.rem(at.n + b, 2))) for a, b in ((0, 1), (1, 0), (1, 1))
        ]
        first, second = (x_steps, z_steps) if x_first else (z_steps, x_steps)

        def move(slot, source, target, peer):
            return remote(source, target, send.at[base + slot], recv.at[base + slot], peer)

        self.one = [move(i, self.piece(where), self.land.at[i], peer) for i, (peer, where) in enumerate(first)]
        self.own = pltpu.make_async_copy(
            self.piece((at.s, at.n) if x_first else at.z), self.total, local.at[place]
        )
        self.two = [move(3 + i, self.part(where), self.land_two.at[i], peer) for i, (peer, where) in enumerate(second)]
        self.mine = at.z if x_first else (at.s, at.n)
        self.three = move(6, self.last.at[at.s], self.last.at[at.s], at.at_x(1, 0))
        target = out.at[at.z]
        self.four = [move(7 + i, self.last, target, peer) for i, (peer, _) in enumerate(z_steps)]
        self.stay = pltpu.make_async_copy(self.last, target, local.at[place + 1])

    def piece(self, where):
        if self.x_first:
            s, n = where
            return self.src.at[n, :, s] if self.by_rows else self.src.at[:, s, :, self.at.half(n)]
        return self.src.at[:, where] if self.by_rows else self.src.at[where]

    def part(self, where):
        if self.x_first:
            return self.total.at[where]
        s, n = where
        return self.total.at[n, s] if self.by_rows else self.total.at[s, :, self.at.half(n)]

    def first(self):
        for copy in self.one + [self.own]:
            copy.start()

    def second(self):
        self.own.wait()
        for copy in self.one:
            copy.wait_recv()
        lead = self.total.shape[:-2]
        count = math.prod(lead)

        def add(i, carry):
            at_lead = (i,) if len(lead) == 1 else (lax.div(i, lead[1]), lax.rem(i, lead[1]))
            for start in range(0, self.deep, self.chunk):
                where = (*at_lead, slice(start, start + self.chunk))
                got = self.total[where].astype(f32)
                for k in range(3):
                    got += self.land[(k, *where)].astype(f32)
                self.total[where] = got.astype(bf16)
            return carry

        lax.fori_loop(0, count, add, 0)
        for copy in self.two:
            copy.start()

    def third(self):
        for copy in self.two:
            copy.wait_recv()
        own = self.part(self.mine)
        s = self.at.s
        for start in range(0, self.deep, self.chunk):
            rows = slice(start, start + self.chunk)
            got = own[rows].astype(f32)
            for k in range(3):
                got += self.land_two[k, rows].astype(f32)
            self.last[s, rows] = got.astype(bf16)
        self.three.start()

    def fourth(self):
        self.three.wait_recv()
        for copy in self.four + [self.stay]:
            copy.start()

    def end(self):
        for copy in self.four:
            copy.wait()
        for copy in self.one + self.two + [self.three]:
            copy.wait_send()
        self.stay.wait()


class Gather:
    slots = 11

    def __init__(self, at, x, whole, send, recv, local, base=0):
        self.at, self.x, self.whole = at, x, whole
        y, c, up, down = at.y, at.c, at.up, at.down
        far = lax.rem(y + 2, 4)
        half = BLOCK // 2

        def move(slot, y_from, peer, start=0, size=BLOCK, first=False):
            rows = at.rows(y_from, c, start, size)
            src = whole.at[rows]
            if first:
                src = x if size == BLOCK else x.at[start : start + size]
            return remote(src, whole.at[rows], send.at[base + slot], recv.at[base + slot], peer)

        to_up, to_down, core = at.at_y(up), at.at_y(down), at.core()
        self.sends = [
            move(0, y, to_up, 0, half, first=True),
            move(1, y, to_up, half, half, first=True),
            move(2, y, to_down, half, half, first=True),
            move(3, y, to_down, 0, half, first=True),
            move(4, y, core, first=True),
            move(5, down, to_up, 0, half),
            move(6, up, to_down, half, half),
            move(7, down, core),
            move(8, up, core),
            move(9, far, core, 0, half),
            move(10, far, core, half, half),
        ]
        self.own = pltpu.make_async_copy(x, whole.at[at.rows(y, c)], local)

    def begin(self):
        for i in (0, 2, 1, 3, 4):
            self.sends[i].start()
        self.own.start()
        self.own.wait()

    def chain(self, *pairs):
        for arrived, leaving in pairs:
            self.sends[arrived].wait_recv()
            self.sends[leaving].start()

    def pass_on(self):
        self.chain((0, 5), (2, 6))

    def pass_near(self):
        self.chain((1, 7), (3, 8))

    def pass_far(self):
        self.chain((5, 9), (6, 10))

    def got(self, *slots):
        for i in slots:
            self.sends[i].wait_recv()

    def end(self):
        for copy in self.sends:
            copy.wait_send()

    def finish(self):
        self.pass_on()
        self.pass_near()
        self.pass_far()
        self.got(4, 7, 8, 9, 10)
        self.end()

    def each(self, work):
        at = self.at

        def step(s, carry):
            @pl.when(s == 1)
            def _():
                self.got(4)
                self.pass_on()

            @pl.when(s == 2)
            def _():
                self.pass_near()

            @pl.when(s == 3)
            def _():
                self.got(8)

            @pl.when(s == 5)
            def _():
                self.got(7)

            @pl.when(s == 6)
            def _():
                self.pass_far()

            @pl.when(s == 7)
            def _():
                self.got(9, 10)

            work(s, self.place(s))
            return carry

        lax.fori_loop(0, 8, step, 0)
        self.end()

    def place(self, s):
        g = lax.div(s, 2)
        off = g + lax.div(g, 2) - 2 * lax.div(g, 3)
        return self.at.rows(lax.rem(self.at.y + off, 4), lax.rem(self.at.c + s, 2))


QUARTER = 384


class GatherZ(Gather):
    def __init__(self, at, quarter, full, send, recv, local, base=0):
        self.at = at
        z, up, down, far = at.z, lax.rem(at.z + 1, 4), lax.rem(at.z + 3, 4), lax.rem(at.z + 2, 4)
        half = QUARTER

        def move(slot, z_from, peer, start=0, size=2 * QUARTER, first=False):
            rows = pl.ds(pl.multiple_of(at.c * 2 * QUARTER + start, QUARTER), size)
            target = full.at[rows, self.columns(z_from)]
            return remote(quarter.at[rows] if first else target, target, send.at[base + slot], recv.at[base + slot], peer)

        to_up, to_down, core = at.at_z(1), at.at_z(3), at.core()
        self.sends = {
            0: move(0, z, to_up, 0, half, first=True),
            1: move(1, z, to_up, half, half, first=True),
            2: move(2, z, to_down, half, half, first=True),
            3: move(3, z, to_down, 0, half, first=True),
            5: move(5, down, to_up, 0, half),
            6: move(6, up, to_down, half, half),
            7: move(7, down, core),
            8: move(8, up, core),
            9: move(9, far, core, 0, half),
            10: move(10, far, core, half, half),
        }
        self.own = pltpu.make_async_copy(quarter, full.at[:, self.columns(z)], local)

    @staticmethod
    def columns(z):
        return pl.ds(pl.multiple_of(z * QUARTER, QUARTER), QUARTER)

    @staticmethod
    def peers(at):
        return [("z1", at.at_z(1)), ("z3", at.at_z(3)), ("core", at.core())]

    def begin(self):
        for i in (0, 2, 1, 3):
            self.sends[i].start()
        self.own.start()

    def end(self):
        self.got(7, 8, 9, 10)
        self.own.wait()
        for copy in self.sends.values():
            copy.wait_send()


class Scatter:
    slots = 10
    scratch = [
        VMEM((4, BLOCK, D), bf16),
        VMEM((4, BLOCK, D), bf16),
        VMEM((4, BLOCK, D), f32),
        VMEM((2, BLOCK, D), bf16),
        VMEM((2, BLOCK, D), bf16),
        VMEM((2, BLOCK // 2, D), bf16),
        VMEM((2, BLOCK // 2, D), bf16),
    ]

    def __init__(self, at, send, recv, refs, base=0):
        self.at, self.send, self.recv, self.base = at, send, recv, base
        self.out_c, self.in_c, self.own, self.out_y, self.in_y, self.half_out, self.half_in = refs
        half = BLOCK // 2
        peers = at.at_y(at.up), at.at_y(at.down)

        def move(slot, src, dst, peer):
            return remote(src, dst, send.at[base + slot], recv.at[base + slot], peer)

        self.cores = [self.core(g) for g in range(4)]
        self.halves = [move(4 + i, self.half_out.at[i], self.half_in.at[i], peers[i]) for i in range(2)]
        free = [pl.ds((1 - i) * half, half) for i in range(2)]
        bound = [pl.ds(i * half, half) for i in range(2)]
        self.free = [move(6 + i, self.out_y.at[i, free[i]], self.in_y.at[i, free[i]], peers[i]) for i in range(2)]
        self.bound = [move(8 + i, self.out_y.at[i, bound[i]], self.in_y.at[i, bound[i]], peers[i]) for i in range(2)]

    def core(self, g):
        slot = self.base + g
        return remote(self.out_c.at[g], self.in_c.at[g], self.send.at[slot], self.recv.at[slot], self.at.core())

    def both(self, g, rows):
        return self.own[g, rows] + self.in_c[g, rows].astype(f32)

    def products(self, product):
        at = self.at
        half = BLOCK // 2

        def part_rows(rows, i):
            return pl.ds(pl.multiple_of(rows.start + i * half, 32), 32)

        def send_free(i):
            self.cores[1 + i].wait_recv()

            def add(rows, carry):
                there = part_rows(rows, 1 - i)
                self.out_y[i, there] = self.both(1 + i, there).astype(bf16)

            by_rows(half, 32, add)
            self.free[i].start()

        def step(s, carry):
            g = lax.div(s, 2)
            off = lax.rem(6 - g + 3 * lax.div(g, 2) + 2 * lax.div(g, 3), 4)
            part = product(at.rows(lax.rem(at.y + off, 4), lax.rem(at.c + 1 + s, 2)))

            @pl.when(lax.rem(s, 2) == 0)
            def _():
                self.out_c[g] = part.astype(bf16)
                self.core(g).start()

            @pl.when(lax.rem(s, 2) == 1)
            def _():
                self.own[g] = part

            @pl.when(s == 2)
            def _():
                self.cores[0].wait_recv()
                for i in range(2):

                    def add(rows, carry, i=i):
                        self.half_out[i, rows] = self.both(0, part_rows(rows, i)).astype(bf16)

                    by_rows(half, 32, add)
                    self.halves[i].start()

            @pl.when(s == 4)
            def _():
                send_free(0)

            @pl.when(s == 6)
            def _():
                send_free(1)

            return carry

        lax.fori_loop(0, 8, step, 0)

    def middle(self):
        half = BLOCK // 2
        for i in range(2):
            self.halves[i].wait_recv()

            def add(rows, carry, i=i):
                here = pl.ds(pl.multiple_of(rows.start + i * half, 32), 32)
                self.out_y[i, here] = (self.both(1 + i, here) + self.half_in[i, rows].astype(f32)).astype(bf16)

            by_rows(half, 32, add)
            self.bound[i].start()

    def arrive(self):
        self.cores[3].wait_recv()
        for copy in self.free + self.bound:
            copy.wait_recv()

    def total(self, rows):
        return self.both(3, rows) + self.in_y[0, rows].astype(f32) + self.in_y[1, rows].astype(f32)

    def end(self):
        for copy in self.cores + self.halves + self.free + self.bound:
            copy.wait_send()


def standard(values):
    average = jnp.mean(values, axis=1, keepdims=True)
    variance = jnp.mean(values * values, axis=1, keepdims=True) - average * average
    factor = lax.rsqrt(variance + EPSILON)
    return (values - average) * factor, factor


def norm_back(incoming, centred, factor, gain):
    scaled = incoming * gain
    first = jnp.mean(scaled, axis=1, keepdims=True)
    second = jnp.mean(scaled * centred, axis=1, keepdims=True)
    return factor * (scaled - first - centred * second)


def two_sums(incoming, centred, carry):
    gains, shifts = carry
    return gains + jnp.sum(incoming * centred, axis=0, keepdims=True), shifts + jnp.sum(incoming, axis=0, keepdims=True)


def no_sums():
    return jnp.zeros((1, D), f32), jnp.zeros((1, D), f32)


EIGHTH = 0.125


def shape(*dims, dtype=bf16):
    return jax.ShapeDtypeStruct(dims, dtype)


class Keep:
    def __init__(self, whole, out, sem, base):
        self.whole, self.out, self.sem, self.base = whole, out, sem, base

    def block(self, s, rows):
        pltpu.make_async_copy(self.whole.at[rows], self.out.at[rows], self.sem.at[self.base + s]).start()

    def wait(self):
        for s in range(8):
            some = pl.ds(0, BLOCK)
            pltpu.make_async_copy(self.whole.at[some], self.out.at[some], self.sem.at[self.base + s]).wait()


def enter(number, layer_input, gains, weights, query_t, cross_out, texts, pair_t, beside):
    relay = Relay(layer_input)

    def body(at, ins, outs, kept):
        source, *gains = ins[:7]
        *own_weights, query_own, out_own, own_texts, pair = ins[7:]
        x, vectors, weight, all_rows, qkv, query_all, out_quarter, text_pair = outs
        normed, whole, query_part, out_part, query_quarter, text_parts, text_got, own_vectors, send, recv, local = kept
        half = at.half(at.n)
        moving = functools.partial(relay_run, relay, at, source, x, send, recv, local.at[0], 11)
        moving(False)
        own_vectors[...] = jnp.zeros_like(own_vectors)
        for i, ref in enumerate(gains):
            own_vectors[i : i + 1] = ref[...].astype(f32).reshape(1, HALF)
        columns = GatherZ.columns(lax.rem(at.z, 2))
        holds = at.n == lax.div(at.z, 2)
        quarters = []
        for i, (own, part) in enumerate(((query_own, query_part), (out_own, out_part))):
            quarters.append(
                (
                    pltpu.make_async_copy(own.at[:, columns], part, local.at[14 + i]),
                    remote(own.at[:, columns], part, send.at[17 + i], recv.at[17 + i], at.x()),
                )
            )

        @pl.when(holds)
        def _():
            for stay, go in quarters:
                go.start()
                stay.start()

        stay = [
            pltpu.make_async_copy(own, target, local.at[1 + i])
            for i, (own, target) in enumerate(
                [(own_vectors, vectors.at[:, half])]
                + [(own, weight.at[j * COLS : (j + 1) * COLS, half]) for j, own in enumerate(own_weights)]
            )
        ]
        for copy in stay:
            copy.start()
        vectors_go = remote(own_vectors, vectors.at[:, half], send.at[13], recv.at[13], at.x())
        vectors_go.start()
        rows = pl.ds(pl.multiple_of(at.z * 144, 16), 144)
        over = remote(weight.at[rows, half], weight.at[rows, half], send.at[14], recv.at[14], at.x())
        other = weight.at[rows, at.half(1 - at.n)]
        others = [
            remote(other, other, send.at[slot], recv.at[slot], at.at_z(k)) for k, slot in ((1, 15), (2, 16), (3, 53))
        ]
        for copy in stay:
            copy.wait()
        over.start()

        @pl.when(holds)
        def _():
            for near, far in quarters:
                near.wait()
                far.wait_send()

        @pl.when(jnp.logical_not(holds))
        def _():
            for near, far in quarters:
                far.wait_recv()

        for clip in range(2):
            text_parts[clip] = dot_flip(own_texts[clip], pair[...])
        text_go = remote(text_parts.at[1 - at.n], text_got, send.at[52], recv.at[52], at.x())
        text_go.start()
        queries = Gather(at, query_part, query_quarter, send, recv, local.at[16], 19)
        outputs = Gather(at, out_part, out_quarter, send, recv, local.at[17], 30)
        queries.begin()
        vectors_go.wait_recv()
        moving(True)
        over.wait_recv()
        for copy in others:
            copy.start()
        at.start_beside(1, 2)
        queries.pass_on()
        queries.pass_near()

        def norm(rows, carry):
            centred, _ = standard(x[rows].astype(f32))
            normed[rows] = (centred * vectors[0:1] + vectors[1:2]).astype(bf16)

        by_rows(BLOCK, 32, norm)
        gather = Gather(at, normed, whole, send, recv, local.at[5])
        gather.begin()
        queries.pass_far()
        queries.got(4, 7, 8, 9, 10)
        around = GatherZ(at, query_quarter, query_all, send, recv, local.at[18], 41)
        around.begin()
        keep = Keep(whole, all_rows, local, 6)

        def times(rows):
            qkv[rows] = dot_flip(whole[rows], weight[...]).astype(bf16)

        def work(s, rows):
            keep.block(s, rows)

            @pl.when(s == 4)
            def _():
                for copy in others:
                    copy.wait_recv()
                at.start_beside(0)
                at.flush(0, 1, 2)

            @pl.when(s >= 4)
            def _():
                times(rows)

            @pl.when(s == 6)
            def _():
                outputs.begin()
                around.pass_on()

        gather.each(work)
        around.pass_near()
        outputs.pass_on()
        outputs.pass_near()

        def rest(s, carry):
            times(gather.place(s))
            return carry

        lax.fori_loop(0, 4, rest, 0)
        at.flush(4)
        outputs.pass_far()
        around.pass_far()
        text_go.wait()
        text_pair[...] = (text_parts[at.n] + text_got[...]).astype(bf16)
        outputs.got(4, 7, 8, 9, 10)
        keep.wait()
        for copy in [vectors_go, over] + others:
            copy.wait_send()
        outputs.end()
        queries.end()
        around.end()

    return call(
        body,
        number,
        [layer_input, *gains, *weights, query_t, cross_out, texts, pair_t],
        [
            shape(BLOCK, D),
            shape(8, D, dtype=f32),
            shape(3 * COLS, D),
            shape(D, D),
            shape(D, 3 * COLS),
            shape(D, D),
            shape(D, QUARTER),
            shape(64, 2 * COLS),
        ],
        [
            VMEM((BLOCK, D), bf16),
            VMEM((D, D), bf16),
            VMEM((COLS, QUARTER), bf16),
            VMEM((COLS, QUARTER), bf16),
            VMEM((D, QUARTER), bf16),
            VMEM((2, 64, 2 * COLS), f32),
            VMEM((64, 2 * COLS), f32),
            VMEM((8, HALF), f32),
            *sems(54),
        ],
        beside,
        lambda at: ring_peers(at) + relay.peers(at) + [("x", at.x()), ("z2", at.at_z(2))] + GatherZ.peers(at),
        spaces=[ANY] + [PLAIN] * 6 + [VMEM] * 7,
        out_spaces=[VMEM, VMEM, VMEM, ANY, VMEM, ANY, VMEM, VMEM],
        late=True,
    )


def causal_forward(number, joined, down, out_quarter, beside):
    at_once = 512

    def body(at, ins, outs, kept):
        (qkv, block, quarter), (out, logs, all_down, out_all) = ins, outs
        parts, mixed, send, recv, local = kept
        first = Gather(at, block, all_down, send, recv, local.at[0])
        second = GatherZ(at, quarter, out_all, send, recv, local.at[1], 11)
        second.begin()
        first.begin()
        for i in range(3):
            for h in range(HEADS):
                a = i * COLS + h * HDIM
                piece = qkv[:, a : a + HDIM]
                parts[i, h] = piece * EIGHTH if i == 0 else piece
        square = (at_once, at_once)
        seen = lax.broadcasted_iota(jnp.int32, square, 0) >= lax.broadcasted_iota(jnp.int32, square, 1)

        def one(h, carry):
            for i in reversed(range(D // at_once)):
                before, upto = i * at_once, (i + 1) * at_once
                rows = slice(before, upto)
                scores = dot_flip(parts[0, h, rows], parts[1, h, 0:upto])
                last = jnp.where(seen, scores[:, before:], NEGATIVE)
                scores = jnp.concatenate((scores[:, :before], last), axis=1) if i else last
                peak = jnp.max(scores, axis=1, keepdims=True)
                raised = jnp.exp(scores - peak)
                total = jnp.sum(raised, axis=1, keepdims=True)
                mixed[h, rows] = (dot(raised.astype(bf16), parts[2, h, 0:upto]) / total).astype(bf16)
                column = jnp.broadcast_to(peak + jnp.log(total), (at_once, 128))
                logs[pl.ds(h, 1), rows] = column.T[0:1, :]

            @pl.when(h == 1)
            def _():
                first.pass_on()
                second.pass_on()

            return carry

        lax.fori_loop(0, HEADS, one, 0)
        first.pass_near()
        second.pass_near()
        out[...] = jnp.concatenate([mixed[h] for h in range(HEADS)], axis=1)
        at.flush()
        first.pass_far()
        second.pass_far()
        first.got(4, 7, 8, 9, 10)
        first.end()
        second.end()

    return call(
        body,
        number,
        [joined, down, out_quarter],
        [shape(D, COLS), shape(8, D, dtype=f32), shape(D, D), shape(D, D)],
        [VMEM((3, HEADS, D, HDIM), bf16), VMEM((HEADS, D, HDIM), bf16), *sems(22)],
        beside,
        lambda at: ring_peers(at) + GatherZ.peers(at),
        out_spaces=[VMEM, VMEM, ANY, ANY],
    )


def forward_rest(number, attended, out_w, x, vectors, query_all, out_all, texts, all_down, expand_w, contract):
    def body(at, ins, outs, kept):
        mixed, out_own, out_got, x, vectors, query_all, out_all, texts, all_down, expand_own, expand_got, contract_own = ins
        middle, after, normed_two, weights, all_rows, activated, grad, contract_out, keys_out, values_out, traded = outs
        *refs, normed, whole, downs, out_full, expand_full, contract_full, key_full, value_full, branch, scores_all, send, recv, local = kept
        half = at.half(at.n)
        weight = at.early
        swap = remote(contract_own, contract_full.at[:, half], send.at[21], recv.at[21], at.x())
        swap.start()
        factors = [
            pltpu.make_async_copy(query_all, key_full, local.at[2]),
            pltpu.make_async_copy(out_all, value_full, local.at[3]),
        ]
        for copy in factors:
            copy.start()
        later = [
            pltpu.make_async_copy(contract_own, contract_full.at[:, half], local.at[4]),
            pltpu.make_async_copy(all_down, downs, local.at[7]),
        ]
        for copy in later:
            copy.start()
        later.append(Whole(at, expand_own, expand_got, expand_full, local.at[pl.ds(5, 2)], 0))
        weight.wait()
        scatter = Scatter(at, send, recv, refs)
        scatter.products(lambda rows: dot(mixed[rows], out_full[...]))
        for copy in factors:
            copy.wait()

        def make(b, carry):
            for h in range(HEADS):
                rows = pl.ds(pl.multiple_of(b * BLOCK + h * 64, 64), 64)
                text_keys = texts[b, :, h * HDIM : (h + 1) * HDIM]
                text_values = texts[b, :, COLS + h * HDIM : COLS + (h + 1) * HDIM]
                key_full[rows] = (dot(text_keys, key_full[rows]) * EIGHTH).astype(bf16)
                value_full[rows] = dot(text_values, value_full[rows]).astype(bf16)
            return carry

        lax.fori_loop(0, 8, make, 0)
        made = [
            pltpu.make_async_copy(key_full, keys_out, local.at[8]),
            pltpu.make_async_copy(value_full, values_out, local.at[9]),
        ]
        for copy in made:
            copy.start()
        scatter.middle()
        for copy in later:
            copy.wait()
        scatter.arrive()

        def norm_two(rows, carry):
            total = x[rows].astype(f32) + scatter.total(rows)
            middle[rows] = total
            centred, _ = standard(total)
            normed_two[rows] = (centred * vectors[2:3] + vectors[3:4]).astype(bf16)

        by_rows(BLOCK, 32, norm_two)

        trade = Trade(at, weights, traded, send, recv, local.at[20], 22)

        def score(rows, carry):
            scores_all[rows] = dot_flip(key_full[rows], normed_two[...])

        by_rows(D, QUARTER, score)

        def cross(b, carry):
            rows = pl.ds(pl.multiple_of(b * BLOCK, BLOCK), BLOCK)
            scores = scores_all[rows].reshape(HEADS, 64, BLOCK)
            raised = jnp.exp(scores - jnp.max(scores, axis=1, keepdims=True))
            p = raised / jnp.sum(raised, axis=1, keepdims=True)
            p = p.reshape(BLOCK, BLOCK).T.astype(bf16)
            weights[b] = p
            trade.give(b)
            part = dot(p, value_full[rows])

            @pl.when(b == 0)
            def _():
                branch[...] = part

            @pl.when(b > 0)
            def _():
                branch[...] += part

            return carry

        lax.fori_loop(0, 8, cross, 0)

        def norm_three(rows, carry):
            total = middle[rows] + branch[rows]
            after[rows] = total
            centred, _ = standard(total)
            normed[rows] = (centred * vectors[4:5] + vectors[5:6]).astype(bf16)

        by_rows(BLOCK, 32, norm_three)
        gather = Gather(at, normed, whole, send, recv, local.at[10], 10)
        gather.begin()
        at.flush(0, 1, 2, 3)
        swap.wait_recv()
        keep_contract = pltpu.make_async_copy(contract_full, contract_out, local.at[11])
        keep_contract.start()
        keep = Keep(whole, all_rows, local, 12)

        def ahead(rows, carry):
            grad[rows] = dot_flip(downs[rows], contract_full[...]).astype(bf16)

        by_rows(D, BLOCK, ahead)

        def work(s, rows):
            keep.block(s, rows)
            hidden = dot(whole[rows], expand_full[...])
            bell = 0.5 * (1.0 + lax.erf(hidden * ROOT_HALF))
            activated[rows] = (hidden * bell).astype(bf16)
            slope = bell + hidden * jnp.exp(-0.5 * hidden * hidden) * GAUSS_NORM
            grad[rows] = (grad[rows].astype(f32) * slope).astype(bf16)

        gather.each(work)
        at.flush()
        keep.wait()
        keep_contract.wait()
        trade.end()
        for copy in made:
            copy.wait()
        scatter.end()
        swap.wait_send()

    results, _ = call(
        body,
        number,
        [attended, *out_w, x, vectors, query_all, out_all, texts, all_down, *expand_w, contract],
        [
            shape(BLOCK, D, dtype=f32),
            shape(BLOCK, D, dtype=f32),
            shape(BLOCK, D),
            shape(8, BLOCK, BLOCK),
            shape(D, D),
            shape(D, HALF),
            shape(D, HALF),
            shape(HALF, D),
            shape(D, D),
            shape(D, D),
            shape(8, BLOCK, BLOCK),
        ],
        [
            *Scatter.scratch,
            VMEM((BLOCK, D), bf16),
            VMEM((D, D), bf16),
            VMEM((D, D), bf16),
            VMEM((COLS, D), bf16),
            VMEM((D, HALF), bf16),
            VMEM((HALF, D), bf16),
            VMEM((D, D), bf16),
            VMEM((D, D), bf16),
            VMEM((BLOCK, D), f32),
            VMEM((D, BLOCK), f32),
            *sems(30),
        ],
        (),
        lambda at: Trade.peers(at) + [("x", at.x())],
        early=lambda at, ins, kept: Whole(at, ins[1], ins[2], kept[len(Scatter.scratch) + 3], kept[-1].at[pl.ds(0, 2)], 1),
        spaces=[VMEM, ANY, ANY, VMEM, VMEM, ANY, ANY, VMEM, ANY, ANY, ANY, ANY],
        out_spaces=[VMEM, VMEM, VMEM, VMEM, ANY, VMEM, VMEM, ANY, ANY, ANY, ANY],
    )
    return results


def backward_rest(
    number, grad, expand_w, after, middle, vectors, down, keys, values, weights, out_w, contract_sum, expand_sum, beside
):
    def body(at, ins, outs, kept):
        grad, expand_own, expand_got, after, middle, vectors, down, keys, values, weights, out_own, out_got = ins[:12]
        grad_rows, rounded_two, traded, all_two, all_rows, grad_mixed, grad_vectors = outs[:7]
        *refs, rounded, whole, second, out_full, expand_full, key_full, value_full, grad_scores, grads_all, send, recv, local = kept
        reduces = [
            Reduce(at, ins[12], outs[7], refs[7:11], send, recv, local, 32, 16, False),
            Reduce(at, ins[13], outs[8], refs[11:15], send, recv, local, 42, 18, True, True),
        ]
        refs = refs[:7]
        for reduce in reduces:
            reduce.first()
        weight = at.early
        later = [
            pltpu.make_async_copy(keys, key_full, local.at[2]),
            pltpu.make_async_copy(values, value_full, local.at[3]),
        ]
        for copy in later:
            copy.start()
        later.append(Whole(at, out_own, out_got, out_full, local.at[pl.ds(4, 2)], 1))
        weight.wait()
        scatter = Scatter(at, send, recv, refs)
        scatter.products(lambda rows: dot_flip(grad[rows], expand_full[...]))
        scatter.middle()
        for copy in later:
            copy.wait()
        scatter.arrive()

        def norm_three(rows, carry):
            incoming = scatter.total(rows)
            centred, factor = standard(after[rows])
            total = down[rows].astype(f32) + norm_back(incoming, centred, factor, vectors[4:5])
            grad_rows[rows] = total
            rounded_two[rows] = total.astype(bf16)
            return two_sums(incoming, centred, carry)

        gains, shifts = by_rows(BLOCK, 32, norm_three, no_sums())
        before = Gather(at, rounded_two, all_two, send, recv, local.at[6], 10)
        before.begin()
        for reduce in reduces:
            reduce.second()
        grad_vectors[4:5] = gains
        grad_vectors[5:6] = shifts

        trade = Trade(at, grad_scores, traded, send, recv, local.at[20], 52)

        def score(rows, carry):
            grads_all[rows] = dot_flip(value_full[rows], rounded_two[...])

        by_rows(D, QUARTER, score)

        def cross(b, carry):
            rows = pl.ds(pl.multiple_of(b * BLOCK, BLOCK), BLOCK)
            p = weights[b].astype(f32).T.reshape(HEADS, 64, BLOCK)
            dp = grads_all[rows].reshape(HEADS, 64, BLOCK)
            ds = p * (dp - jnp.sum(p * dp, axis=1, keepdims=True))
            ds = ds.reshape(BLOCK, BLOCK).T.astype(bf16)
            grad_scores[b] = ds
            trade.give(b)
            part = dot(ds, key_full[rows])

            @pl.when(b == 0)
            def _():
                second[...] = part

            @pl.when(b > 0)
            def _():
                second[...] += part

            @pl.when(b == 3)
            def _():
                before.pass_on()

            @pl.when(b == 5)
            def _():
                for reduce in reduces:
                    reduce.third()

            return carry

        lax.fori_loop(0, 8, cross, 0)
        at.flush(1)
        for reduce in reduces:
            reduce.fourth()
        at.start_beside()

        def norm_two(rows, carry):
            incoming = second[rows]
            centred, factor = standard(middle[rows])
            total = grad_rows[rows] + norm_back(incoming, centred, factor, vectors[2:3])
            grad_rows[rows] = total
            rounded[rows] = total.astype(bf16)
            return two_sums(incoming, centred, carry)

        gains, shifts = by_rows(BLOCK, 32, norm_two, no_sums())
        grad_vectors[2:3] = gains
        grad_vectors[3:4] = shifts
        gather = Gather(at, rounded, whole, send, recv, local.at[7], 21)
        before.pass_near()
        gather.begin()
        at.flush(0, 6)
        before.pass_far()
        keep = Keep(whole, all_rows, local, 8)

        def work(s, rows):
            keep.block(s, rows)
            grad_mixed[rows] = dot_flip(whole[rows], out_full[...]).astype(bf16)

        gather.each(work)
        at.flush()
        before.got(4, 7, 8, 9, 10)
        before.end()
        trade.end()
        keep.wait()
        scatter.end()
        for reduce in reduces:
            reduce.end()

    return call(
        body,
        number,
        [grad, *expand_w, after, middle, vectors, down, keys, values, weights, *out_w, contract_sum, expand_sum],
        [
            shape(BLOCK, D, dtype=f32),
            shape(BLOCK, D),
            shape(8, BLOCK, BLOCK),
            shape(D, D),
            shape(D, D),
            shape(D, COLS),
            shape(8, D, dtype=f32),
            shape(4, 2, 96, HALF),
            shape(4, 2, 96, HALF),
        ],
        [
            *Scatter.scratch,
            *Reduce.scratch(96, False),
            *Reduce.scratch(96, True, True),
            VMEM((BLOCK, D), bf16),
            VMEM((D, D), bf16),
            VMEM((BLOCK, D), f32),
            VMEM((COLS, D), bf16),
            VMEM((D, HALF), bf16),
            VMEM((D, D), bf16),
            VMEM((D, D), bf16),
            VMEM((8, BLOCK, BLOCK), bf16),
            VMEM((D, BLOCK), f32),
            *sems(60),
        ],
        beside,
        lambda at: Trade.peers(at) + Reduce.peers(at),
        early=lambda at, ins, kept: Whole(at, ins[1], ins[2], kept[len(Scatter.scratch) + 12], kept[-1].at[pl.ds(0, 2)], 0),
        spaces=[VMEM, ANY, ANY, VMEM, VMEM, VMEM, VMEM, ANY, ANY, VMEM, ANY, ANY, ANY, ANY],
        out_spaces=[VMEM, VMEM, ANY, ANY, ANY, VMEM, VMEM, ANY, ANY],
        late=True,
    )


def causal_backward(number, joined, grad, logs, activated, contract, after, normed_two, part, beside):
    at_once = 512

    def body(at, ins, outs, kept):
        (qkv, go, log_rows, activated, contract, after, block, part), (out, result, all_rows, summed) = ins, outs
        *refs, parts, key_sum, value_sum, send, recv, local = kept
        reduce = Reduce(at, part, summed, refs[7:], send, recv, local, 21, 1, False)
        reduce.first()
        gather = Gather(at, block, all_rows, send, recv, local.at[0], 10)
        gather.begin()
        scatter = Scatter(at, send, recv, refs[:7])
        scatter.products(lambda rows: dot(activated[rows], contract[...]))
        gather.pass_on()
        for i in range(4):
            for h in range(HEADS):
                a = i * COLS + h * HDIM
                piece = qkv[:, a : a + HDIM] if i < 3 else go[:, h * HDIM : (h + 1) * HDIM]
                parts[i, h] = piece * EIGHTH if i == 0 else piece
        square = (at_once, at_once)
        seen = lax.broadcasted_iota(jnp.int32, square, 1) >= lax.broadcasted_iota(jnp.int32, square, 0)
        blocks = D // at_once

        def one(h, carry):
            turned = parts[1, h].T
            query_parts = []
            for i in reversed(range(blocks)):
                before, upto = i * at_once, (i + 1) * at_once
                rows = slice(before, upto)
                q, g = parts[0, h, rows], parts[3, h, rows]
                k, v = parts[1, h, 0:upto], parts[2, h, 0:upto]
                p = jnp.exp(dot_flip(k, q) - log_rows[pl.ds(h, 1), rows])
                last = jnp.where(seen, p[before:], 0.0)
                p = jnp.concatenate((p[:before], last), axis=0) if i else last
                dp = dot_flip(v, g)
                ds = (p * (dp - jnp.sum(p * dp, axis=0, keepdims=True))).astype(bf16)
                value_part, key_part = dot(p.astype(bf16), g), dot(ds, q)
                if i == blocks - 1:
                    key_sum[0:upto, :] = key_part
                    value_sum[0:upto, :] = value_part
                else:
                    key_sum[0:upto, :] += key_part
                    value_sum[0:upto, :] += value_part
                query_parts.append((dot(turned[:, 0:upto], ds) * EIGHTH).T)
                if i == blocks - 1:

                    @pl.when(h == 1)
                    def _():
                        reduce.second()

                    @pl.when(h == 2)
                    def _():
                        reduce.fourth()

            parts[0, h] = jnp.concatenate(query_parts[::-1], axis=0).astype(bf16)
            parts[1, h] = key_sum[...].astype(bf16)
            parts[2, h] = value_sum[...].astype(bf16)

            @pl.when(h == 0)
            def _():
                gather.pass_near()

            @pl.when(h == 1)
            def _():
                scatter.middle()
                gather.pass_far()
                reduce.third()

            return carry

        lax.fori_loop(0, HEADS, one, 0)
        for i in range(3):
            out[:, i * COLS : (i + 1) * COLS] = jnp.concatenate([parts[i, h] for h in range(HEADS)], axis=1)
        scatter.arrive()

        def finish(rows, carry):
            result[rows] = (after[rows] + scatter.total(rows)).astype(bf16)

        at.flush(0)
        by_rows(BLOCK, 32, finish)
        at.flush(1)
        gather.got(4, 7, 8, 9, 10)
        gather.end()
        scatter.end()
        reduce.end()

    return call(
        body,
        number,
        [joined, grad, logs, activated, contract, after, normed_two, part],
        [shape(D, 3 * COLS), shape(BLOCK, D), shape(D, D), shape(4, 2, 72, HALF)],
        [
            *Scatter.scratch,
            *Reduce.scratch(72, False),
            VMEM((4, HEADS, D, HDIM), bf16),
            VMEM((D, HDIM), f32),
            VMEM((D, HDIM), f32),
            *sems(31),
        ],
        beside,
        lambda at: ring_peers(at) + Reduce.peers(at),
        spaces=[VMEM] * 7 + [ANY],
        out_spaces=[VMEM, VMEM, ANY, ANY],
    )


def leave(number, grad, joined, x, vectors, grad_rows, sums, late, text_part, beside):
    relay = Relay(jax.ShapeDtypeStruct((BLOCK, D), bf16), True)
    some = 64 // 8

    def ring(at):
        return [{"wide": lax.rem(at.w + k, 8)} for k in range(1, 8)]

    x_steps = ((0, 1), (1, 0), (1, 1))

    def group(at):
        return [(b, {"wide": lax.rem(at.w + k, 8), "narrow": lax.rem(at.n + b, 2)}) for k in range(8) for b in range(2)][1:]

    def peers(at):
        known = ring_peers(at) + relay.peers(at) + Reduce.peers(at)
        known += [(f"w{k}", peer) for k, peer in enumerate(ring(at), 1)]
        return known + [(f"g{i}", peer) for i, (b, peer) in enumerate(group(at)) if b]

    def body(at, ins, outs, kept):
        grad, weight, x, vectors, before, late, text, one, two = ins
        result, out_one, out_two, vector_sums, text_out = outs
        refs, kept = kept[:7], kept[7:]
        reduces = [
            Reduce(at, one, out_one, kept[0:4], kept[-3], kept[-2], kept[-1], 12, 1, False),
            Reduce(at, two, out_two, kept[4:8], kept[-3], kept[-2], kept[-1], 22, 3, True),
        ]
        rounded, parts, ring_parts, ring_sum, x_parts, x_sum, z_parts, text_parts, text_sum, send, recv, local = kept[8:]
        me = at.spot(at.y, at.c)

        def move(slot, source, target, peer):
            return remote(source, target, send.at[slot], recv.at[slot], peer)

        to_ring, to_group = ring(at), group(at)
        slot = 32
        trades = []
        for peer in to_ring:
            there = at.spot(lax.div(peer["wide"], 2), lax.rem(peer["wide"], 2))
            trades.append(move(slot, text.at[there], text_parts.at[me], peer))
            slot += 1
        text_own = pltpu.make_async_copy(text.at[me], text_parts.at[me], local.at[5])
        texts = []
        for b, peer in to_group:
            n = lax.rem(at.n + b, 2)
            texts.append(move(slot, text_sum.at[:, at.half(n)], text_out.at[at.n, me], peer))
            slot += 1
        text_stay = pltpu.make_async_copy(text_sum.at[:, at.half(at.n)], text_out.at[at.n, me], local.at[6])
        rings = []
        for peer in to_ring:
            rings.append(move(slot, parts, ring_parts.at[at.w], peer))
            slot += 1
        ring_own = pltpu.make_async_copy(parts, ring_parts.at[at.w], local.at[7])
        spreads = []
        for a, b in x_steps:
            half = ring_sum.at[:, at.half(lax.rem(at.n + b, 2))]
            spreads.append(move(slot, half, x_parts.at[at.s, at.n], at.at_x(a, b)))
            slot += 1
        x_own = pltpu.make_async_copy(ring_sum.at[:, at.half(at.n)], x_parts.at[at.s, at.n], local.at[8])
        lasts = []
        for k in (1, 2, 3):
            lasts.append(move(slot, x_sum, z_parts.at[at.z], at.at_z(k)))
            slot += 1

        for reduce in reduces:
            reduce.first()
        text_own.start()
        for copy in trades:
            copy.start()
        scatter = Scatter(at, send, recv, refs)
        scatter.products(lambda rows: dot(grad[rows], weight[...]))
        scatter.middle()
        for reduce in reduces:
            reduce.second()
        text_own.wait()
        for copy in trades:
            copy.wait_recv()
        total = text_parts[0].astype(f32)
        for i in range(1, 8):
            total += text_parts[i].astype(f32)
        text_sum[...] = total.astype(bf16)
        text_stay.start()
        for copy in texts:
            copy.start()
        scatter.arrive()

        def norm(rows, carry):
            incoming = scatter.total(rows)
            centred, factor = standard(x[rows].astype(f32))
            total = before[rows] + norm_back(incoming, centred, factor, vectors[0:1])
            rounded[rows] = total.astype(bf16)
            return two_sums(incoming, centred, carry)

        gains, shifts = by_rows(BLOCK, 32, norm, no_sums())
        moving = functools.partial(relay_run, relay, at, rounded, result, send, recv, local.at[0], 10)
        moving(False)
        parts[0:1] = gains
        parts[1:2] = shifts
        parts[2:6] = late[2:6]
        parts[6:8] = jnp.zeros((2, D), f32)
        ring_own.start()
        for copy in rings:
            copy.start()
        for reduce in reduces:
            reduce.third()
        ring_own.wait()
        for copy in rings:
            copy.wait_recv()
        total = ring_parts[0]
        for i in range(1, 8):
            total += ring_parts[i]
        ring_sum[...] = total
        x_own.start()
        for copy in spreads:
            copy.start()
        for reduce in reduces:
            reduce.fourth()
        at.start_beside()
        x_own.wait()
        for copy in spreads:
            copy.wait_recv()
        total = x_parts[0, 0] + x_parts[0, 1] + x_parts[1, 0] + x_parts[1, 1]
        x_sum[...] = total
        for copy in lasts:
            copy.start()
        z_parts[pl.ds(at.z, 1)] = total.reshape(1, 8, HALF)
        for copy in lasts:
            copy.wait_recv()
        vector_sums[...] = z_parts[0] + z_parts[1] + z_parts[2] + z_parts[3]
        at.flush()
        moving(True)
        text_stay.wait()
        for copy in texts:
            copy.wait()
        for copy in trades + rings + spreads + lasts:
            copy.wait_send()
        scatter.end()
        for reduce in reduces:
            reduce.end()

    return call(
        body,
        number,
        [grad, joined, x, vectors, grad_rows, late, text_part, *sums],
        [
            shape(384, HALF),
            shape(4, 2, 72, HALF),
            shape(4, 2, 48, HALF),
            shape(8, HALF, dtype=f32),
            shape(2, 8, some, HALF),
        ],
        [
            *Scatter.scratch,
            *Reduce.scratch(72, False),
            *Reduce.scratch(48, True),
            VMEM((BLOCK, D), bf16),
            VMEM((8, D), f32),
            VMEM((8, 8, D), f32),
            VMEM((8, D), f32),
            VMEM((2, 2, 8, HALF), f32),
            VMEM((8, HALF), f32),
            VMEM((4, 8, HALF), f32),
            VMEM((8, some, D), bf16),
            VMEM((some, D), bf16),
            *sems(32 + 7 + 15 + 7 + 6),
        ],
        beside,
        peers,
        spaces=[VMEM, VMEM, VMEM, VMEM, VMEM, VMEM, ANY, ANY, ANY],
        out_spaces=[ANY, ANY, ANY, VMEM, ANY],
        late=True,
    )


def on_device(
    layer_input,
    text_states,
    cotangent,
    first_gain,
    first_shift,
    query_weight,
    key_weight,
    value_weight,
    output_weight,
    second_gain,
    second_shift,
    cross_query,
    cross_key,
    cross_value,
    cross_output,
    third_gain,
    third_shift,
    expand_weight,
    contract_weight,
):
    gains = (first_gain, first_shift, second_gain, second_shift, third_gain, third_shift)
    weights = [query_weight.T, key_weight.T, value_weight.T]
    query_t = cross_query.T
    pair_t = jnp.concatenate((cross_key.T, cross_value.T), axis=0)
    n = lax.axis_index("narrow")

    results, ((down,), (out_got,), (text_got,)) = enter(
        1,
        layer_input,
        gains,
        weights,
        query_t,
        cross_output,
        text_states,
        pair_t,
        [Relay(cotangent), Give(output_weight), GiveClip(text_states)],
    )
    x, vectors, joined, all_one, qkv, query_all, out_quarter, text_pair = results
    (attended, logs, all_down, out_all), ((texts,), (expand_got,)) = causal_forward(
        2, qkv, down, out_quarter, [ToSpots(text_pair), Give(expand_weight)]
    )
    out_w, expand_w = (output_weight, out_got), (expand_weight, expand_got)
    results = forward_rest(3, attended, out_w, x, vectors, query_all, out_all, texts, all_down, expand_w, contract_weight)
    middle, after, normed_two, cross_p, all_three, activated, grad_expand, contract, all_keys, all_values, traded_p = results

    contract_part = outer(activated, all_down).astype(bf16).reshape(4, 2, 96, D)
    expand_part = outer(all_three, grad_expand).astype(bf16).reshape(2, 4, 2, 96, HALF)
    results, ((query_got,), (cross_got,)) = backward_rest(
        4,
        grad_expand,
        expand_w,
        after,
        middle,
        vectors,
        down,
        all_keys,
        all_values,
        cross_p,
        out_w,
        contract_part,
        expand_part,
        [Give(query_t), Give(cross_output)],
    )
    grad_one, _, grad_scores, all_mid_two, all_mid_one, grad_attended, late, contract_grad, expand_grad = results

    own_first = n == 0

    def whole(own, got):
        return jnp.concatenate((jnp.where(own_first, own, got), jnp.where(own_first, got, own)), axis=1)

    def heads(what, a, b):
        return jnp.einsum(what, a, b, preferred_element_type=f32)

    text = whole(lax.dynamic_index_in_dim(text_states, n, 0, False), text_got)
    text_heads = text_pair.reshape(64, 2, HEADS, HDIM)
    grad_values = outer(traded_p.reshape(D, COLS), all_mid_two).astype(bf16).reshape(HEADS, 64, D)
    heads_out = whole(cross_output, cross_got).reshape(HEADS, HDIM, D)
    grad_text_values = heads("hkf,hdf->khd", grad_values, heads_out).reshape(64, COLS).astype(bf16)
    grad_cross = heads("khd,hkf->hdf", text_heads[:, 1], grad_values).reshape(COLS, D)
    value_part = jnp.concatenate((grad_cross, outer(grad_text_values, text), outer(attended, all_mid_one)), axis=0)
    (grad_qkv, layer_output, all_two, value_grad), ((pair_got,),) = causal_backward(
        5,
        qkv,
        grad_attended,
        logs,
        activated,
        contract,
        after,
        normed_two,
        value_part.astype(bf16).reshape(4, 2, 72, D),
        [Give(pair_t)],
    )

    joined_part = outer(grad_qkv, all_one).astype(bf16).reshape(4, 2, 72, D)
    grad_keys = outer(grad_scores.reshape(D, COLS), all_two).astype(bf16).reshape(HEADS, 64, D)
    heads_query = whole(query_t, query_got).reshape(HEADS, HDIM, D)
    grad_text_keys = (heads("hkf,hdf->khd", grad_keys, heads_query) * EIGHTH).reshape(64, COLS).astype(bf16)
    grad_query = heads("khd,hkf->hdf", text_heads[:, 0], grad_keys).reshape(COLS, D) * EIGHTH
    key_part = jnp.concatenate((grad_query, outer(grad_text_keys, text)), axis=0).astype(bf16).reshape(4, 2, 48, D)
    grad_pair = jnp.concatenate((grad_text_keys, grad_text_values), axis=1)
    text_part = dot(grad_pair, whole(pair_t, pair_got)).astype(bf16).reshape(8, 8, D)

    (input_grad, joined_grad, key_grad, parts, text_grad), ((layer_output,),) = leave(
        6,
        grad_qkv,
        joined,
        x,
        vectors,
        grad_one,
        (joined_part, key_part),
        late,
        text_part,
        [Relay(layer_output, True)],
    )
    joined_grad, key_grad, value_grad, expand_grad, contract_grad = (
        grad.reshape(-1, HALF).astype(f32) for grad in (joined_grad, key_grad, value_grad, expand_grad, contract_grad)
    )
    return (
        layer_output,
        input_grad.astype(f32),
        text_grad.reshape(2, 64, HALF).astype(f32),
        parts[0],
        parts[1],
        joined_grad[:COLS].T,
        joined_grad[COLS : 2 * COLS].T,
        joined_grad[2 * COLS :].T,
        value_grad[2 * COLS :],
        parts[2],
        parts[3],
        key_grad[:COLS].T,
        key_grad[COLS:].T,
        value_grad[COLS : 2 * COLS].T,
        value_grad[:COLS],
        parts[4],
        parts[5],
        expand_grad,
        contract_grad,
    )


def solution(mesh):
    return jax.shard_map(
        on_device,
        mesh=mesh,
        in_specs=(
            P(("dp", "wide"), "narrow"),
            P("dp", None, "narrow"),
            P(("dp", "wide"), "narrow"),
            P("narrow"),
            P("narrow"),
            P("narrow", "wide"),
            P("narrow", "wide"),
            P("narrow", "wide"),
            P("wide", "narrow"),
            P("narrow"),
            P("narrow"),
            P("narrow", "wide"),
            P("narrow", "wide"),
            P("narrow", "wide"),
            P("wide", "narrow"),
            P("narrow"),
            P("narrow"),
            P("narrow", "wide"),
            P("wide", "narrow"),
        ),
        out_specs=(
            P(("dp", "wide"), "narrow"),
            P(("dp", "wide"), "narrow"),
            P("dp", None, "narrow"),
            P("narrow"),
            P("narrow"),
            P("narrow", "wide"),
            P("narrow", "wide"),
            P("narrow", "wide"),
            P("wide", "narrow"),
            P("narrow"),
            P("narrow"),
            P("narrow", "wide"),
            P("narrow", "wide"),
            P("narrow", "wide"),
            P("wide", "narrow"),
            P("narrow"),
            P("narrow"),
            P("narrow", "wide"),
            P("wide", "narrow"),
        ),
        check_vma=False,
    )
```

```python
import functools
import math

import jax
import jax.numpy as jnp
from jax import lax
from jax.experimental import pallas as pl
from jax.experimental.pallas import tpu as pltpu
from jax.sharding import PartitionSpec as P

D = 1536
HALF = 768
HDIM = 64
HEADS = 3
COLS = HEADS * HDIM
BLOCK = 192
EPSILON = 1e-05
NEGATIVE = -1e30
ROOT_HALF = 0.7071067811865476
GAUSS_NORM = 0.3989422804014327
MESH = pl.DeviceIdType.MESH
VMEM = pltpu.VMEM
ANY = pl.ANY
bf16, f32 = jnp.bfloat16, jnp.float32


def dot(a, b):
    return lax.dot_general(a, b, (((1,), (0,)), ((), ())), preferred_element_type=f32)


def dot_flip(a, b):
    return lax.dot_general(a, b, (((1,), (1,)), ((), ())), preferred_element_type=f32)


def outer(a, b):
    return lax.dot_general(a, b, (((0,), (0,)), ((), ())), preferred_element_type=f32)


class Place:
    def __init__(self):
        self.dp, self.w, self.n = (lax.axis_index(a) for a in ("dp", "wide", "narrow"))
        self.y, self.c = lax.div(self.w, 2), lax.rem(self.w, 2)
        self.z, self.s = lax.div(self.dp, 2), lax.rem(self.dp, 2)
        self.up, self.down = lax.rem(self.y + 1, 4), lax.rem(self.y + 3, 4)
        self.across = 3 - self.y
        self.moved = lax.rem(lax.div(self.y, 2) + self.n, 2)
        self.clip = lax.div(self.y, 2)

    def spot(self, y, c):
        moved = lax.rem(lax.div(y, 2) + self.n, 2)
        return (lax.rem(y + moved, 2) * 2 + c) * 2 + moved

    def rows(self, y, c, start=0, size=BLOCK):
        return pl.ds(pl.multiple_of(self.spot(y, c) * BLOCK + start, 32), size)

    def half(self, n):
        return pl.ds(pl.multiple_of(n * HALF, HALF), HALF)

    def at_y(self, y):
        return {"wide": y * 2 + self.c}

    def core(self):
        return {"wide": self.y * 2 + 1 - self.c}

    def x(self):
        return {"narrow": 1 - self.n}

    def at_z(self, k):
        return {"dp": lax.rem(self.z + k, 4) * 2 + self.s}

    def at_dp(self, k):
        return {"dp": lax.rem(self.dp + k, 8)}

    def at_x(self, ds, dn):
        return {"dp": self.z * 2 + lax.rem(self.s + ds, 2), "narrow": lax.rem(self.n + dn, 2)}


def remote(src, dst, send, recv, peer):
    return pltpu.make_async_remote_copy(
        src_ref=src, dst_ref=dst, send_sem=send, recv_sem=recv, device_id=peer, device_id_type=MESH
    )


def greet(peers):
    barrier = pltpu.get_barrier_semaphore()
    for peer in peers:
        pl.semaphore_signal(barrier, inc=1, device_id=peer, device_id_type=MESH)
    pl.semaphore_wait(barrier, len(peers))


class Give:
    def __init__(self, array):
        self.ins, self.copies, self.locals = [array], 1, 0
        self.outs = [jax.ShapeDtypeStruct(array.shape, array.dtype)]

    def peers(self, at):
        return [("x", at.x())]

    def moves(self, at, ins, outs):
        return [(ins[0], outs[0], at.x())], []


class GiveClip(Give):
    def __init__(self, array):
        super().__init__(array)
        self.outs = [jax.ShapeDtypeStruct(array.shape[1:], array.dtype)]

    def moves(self, at, ins, outs):
        return [(ins[0].at[1 - at.n], outs[0], at.x())], []


class ToSpots:
    def __init__(self, array):
        self.ins, self.copies, self.locals = [array], 7, 1
        self.outs = [jax.ShapeDtypeStruct((8, *array.shape), array.dtype)]

    def peers(self, at):
        return [(f"w{k}", {"wide": lax.rem(at.w + k, 8)}) for k in range(1, 8)]

    def moves(self, at, ins, outs):
        dst = outs[0].at[at.spot(at.y, at.c)]
        return [(ins[0], dst, peer) for _, peer in self.peers(at)], [(ins[0], dst)]


class Relay:
    def __init__(self, array, back=False):
        self.ins, self.back, self.copies, self.locals = [array], back, 2, 1
        shape = (384, HALF) if back else (BLOCK, D)
        self.outs = [jax.ShapeDtypeStruct(shape, array.dtype)]

    def peers(self, at):
        return [
            ("x", at.x()),
            ("a0", {"wide": at.across * 2 + at.c}),
            ("a1", {"wide": at.across * 2 + at.c, "narrow": 1 - at.n}),
        ]


def relay_run(relay, at, src, dst, send, recv, local, base, finish):
    mine, other = at.half(at.n), at.half(1 - at.n)
    over = at.across * 2 + at.c
    if relay.back:
        row = pl.ds(pl.multiple_of(at.moved * BLOCK, BLOCK), BLOCK)
        to = recv.at[base + at.moved]
        own = src.at[:, mine], src.at[:, other]
        land = dst.at[0:BLOCK], dst.at[BLOCK : 2 * BLOCK]
    else:
        row = mine
        to = recv.at[base + at.n]
        own = src.at[0:BLOCK], src.at[BLOCK : 2 * BLOCK]
        land = dst.at[:, at.half(0)], dst.at[:, at.half(1)]
    target = dst.at[row] if relay.back else dst.at[:, row]

    def arrive(slot, part):
        return remote(own[0], part, send.at[base], recv.at[base + slot], at.x())

    @pl.when(at.moved == 0)
    def _():
        stay = pltpu.make_async_copy(own[0], target, local)
        if relay.back:
            go = remote(own[1], target, send.at[base], to, at.x())
        else:
            go = remote(own[1], target, send.at[base], to, {"wide": over})
        if not finish:
            go.start()
            stay.start()
        else:
            stay.wait()
            go.wait_send()
            if relay.back:
                arrive(1, land[1]).wait_recv()
            else:
                arrive(1 - at.n, dst.at[:, other]).wait_recv()

    @pl.when(at.moved == 1)
    def _():
        if relay.back:
            first = remote(own[1], target, send.at[base], to, {"wide": over, "narrow": 1 - at.n})
            second = remote(own[0], target, send.at[base + 1], to, {"wide": over})
        else:
            first = remote(own[1], target, send.at[base], to, {"wide": over, "narrow": 1 - at.n})
            second = remote(own[0], target, send.at[base + 1], to, at.x())
        if not finish:
            first.start()
            second.start()
        else:
            first.wait_send()
            second.wait_send()
            arrive(0, land[0]).wait_recv()
            arrive(1, land[1]).wait_recv()


def call(body, number, ins, outs, scratch=(), beside=(), peers=None, spaces=None, out_spaces=None, late=False, early=None):
    spaces = spaces or [VMEM] * len(ins)
    out_spaces = out_spaces or [VMEM] * len(outs)
    copies = sum(b.copies for b in beside)
    locals_ = sum(b.locals for b in beside)
    side_ins = [a for b in beside for a in b.ins]
    side_outs = [a for b in beside for a in b.outs]
    n_in, n_out, n_scratch = len(ins), len(outs), len(scratch)
    loaded = [i for i, m in enumerate(spaces) if m is VMEM]
    stored = [i for i, m in enumerate(out_spaces) if m is VMEM]
    buffers = [VMEM(ins[i].shape, ins[i].dtype) for i in loaded] + [VMEM(outs[i].shape, outs[i].dtype) for i in stored]

    def kernel(*refs):
        at = Place()
        refs = list(refs)

        def take(count):
            out = refs[:count]
            del refs[:count]
            return out

        main_in, side_in = take(n_in), take(len(side_ins))
        main_out, side_out, kept = take(n_out), take(len(side_outs)), take(n_scratch)
        in_buffers, out_buffers = take(len(loaded)), take(len(stored))
        send, recv, local, passing = take(4)
        loads, stores = [], {}
        for k, i in enumerate(loaded):
            loads.append(pltpu.make_async_copy(main_in[i], in_buffers[k], passing.at[k]))
            loads[-1].start()
            main_in[i] = in_buffers[k]
        for k, i in enumerate(stored):
            stores[i] = pltpu.make_async_copy(out_buffers[k], main_out[i], passing.at[len(loaded) + k])
            main_out[i] = out_buffers[k]
        waiting = dict(stores)

        def flush(*which):
            for i in which or list(waiting):
                waiting.pop(i).start()

        at.flush = flush
        if early:
            at.early = early(at, main_in, kept)
        known = dict(peers(at)) if peers else {}
        for b in beside:
            known.update(dict(b.peers(at)))
        if "w1" in known:
            for name in ("up", "down", "core", "a0"):
                known.pop(name, None)
        if "x01" in known:
            known.pop("x", None)
        if known:
            greet(list(known.values()))
        side_refs = [([side_in.pop(0) for _ in b.ins], [side_out.pop(0) for _ in b.outs]) for b in beside]
        begin, todo = [], []
        slot, place = 0, 0
        for b, (i, o) in zip(beside, side_refs):
            if isinstance(b, Relay):
                run = functools.partial(relay_run, b, at, i[0], o[0], send, recv, local.at[place], slot)
                begin.append([functools.partial(run, False)])
                todo.append(functools.partial(run, True))
                slot, place = slot + 2, place + 1
                continue
            far, near = b.moves(at, i, o)
            begin.append([])
            for src, dst, peer in far:
                copy = remote(src, dst, send.at[slot], recv.at[slot], peer)
                begin[-1].append(copy.start)
                todo.append(copy.wait)
                slot += 1
            for src, dst in near:
                copy = pltpu.make_async_copy(src, dst, local.at[place])
                begin[-1].append(copy.start)
                todo.append(copy.wait)
                place += 1

        def start(*which):
            for i in which or range(len(begin)):
                for go in begin[i]:
                    go()

        at.start_beside = start
        if not late:
            start()
        for copy in loads:
            copy.wait()
        if body:
            body(at, main_in, main_out, kept)
        flush()
        for wait in todo:
            wait()
        for copy in stores.values():
            copy.wait()

    results = pl.pallas_call(
        kernel,
        out_shape=tuple(outs) + tuple(side_outs),
        in_specs=[pl.BlockSpec(memory_space=VMEM if m == PLAIN else ANY) for m in spaces]
        + [pl.BlockSpec(memory_space=ANY)] * len(side_ins),
        out_specs=(pl.BlockSpec(memory_space=ANY),) * (len(outs) + len(side_outs)),
        scratch_shapes=[
            *scratch,
            *buffers,
            pltpu.SemaphoreType.DMA((max(copies, 1),)),
            pltpu.SemaphoreType.DMA((max(copies, 1),)),
            pltpu.SemaphoreType.DMA((max(locals_, 1),)),
            pltpu.SemaphoreType.DMA((max(len(buffers), 1),)),
        ],
        compiler_params=pltpu.CompilerParams(
            collective_id=number, has_side_effects=True, vmem_limit_bytes=58 << 20
        ),
    )(*ins, *side_ins)
    results = list(results)
    main, rest = results[: len(outs)], results[len(outs) :]
    sides = []
    for b in beside:
        sides.append(rest[: len(b.outs)])
        del rest[: len(b.outs)]
    return main, sides


PLAIN = "plain"


def ring_peers(at):
    return [("up", at.at_y(at.up)), ("down", at.at_y(at.down)), ("core", at.core())]


def sems(count):
    return [pltpu.SemaphoreType.DMA((count,)), pltpu.SemaphoreType.DMA((count,)), pltpu.SemaphoreType.DMA((count,))]


def by_rows(count, size, work, carry=None):
    def step(i, carry):
        return work(pl.ds(pl.multiple_of(i * size, size), size), carry)

    return lax.fori_loop(0, count // size, step, carry)


class Whole:
    def __init__(self, at, own, got, full, sem, axis):
        size = own.shape[axis]
        self.copies = []
        for i, (part, n) in enumerate(((own, at.n), (got, 1 - at.n))):
            where = pl.ds(pl.multiple_of(n * size, size), size)
            target = full.at[where] if axis == 0 else full.at[:, where]
            self.copies.append(pltpu.make_async_copy(part, target, sem.at[i]))
            self.copies[-1].start()

    def wait(self):
        for copy in self.copies:
            copy.wait()


class Trade:
    def __init__(self, at, parts, out, send, recv, local, base):
        self.at, self.parts, self.out, self.send, self.recv, self.base = at, parts, out, send, recv, base
        self.me = at.spot(at.y, at.c)
        self.own = pltpu.make_async_copy(parts.at[self.me], out.at[self.me], local)

    @staticmethod
    def peers(at):
        return [(f"w{k}", {"wide": lax.rem(at.w + k, 8)}) for k in range(1, 8)]

    def copy(self, b, place):
        m, core, a = lax.rem(b, 2), lax.rem(lax.div(b, 2), 2), lax.div(b, 4)
        y = 2 * lax.rem(m + self.at.n, 2) + lax.rem(a + m, 2)
        send, recv = self.send.at[self.base + b], self.recv.at[self.base + place]
        return remote(self.parts.at[b], self.out.at[place], send, recv, {"wide": y * 2 + core})

    def give(self, b):
        @pl.when(b == self.me)
        def _():
            self.own.start()

        @pl.when(b != self.me)
        def _():
            self.copy(b, self.me).start()

    def end(self):
        def wait(b, carry):
            @pl.when(b == self.me)
            def _():
                self.own.wait()

            @pl.when(b != self.me)
            def _():
                self.copy(b, b).wait()

            return carry

        lax.fori_loop(0, 8, wait, 0)


class Reduce:
    @staticmethod
    def scratch(deep, x_first, by_rows=False):
        first = (4, deep, HALF) if x_first else (2, 2, deep, HALF) if by_rows else (2, deep, D)
        return [VMEM((3, *first), bf16), VMEM(first, bf16), VMEM((3, deep, HALF), bf16), VMEM((2, deep, HALF), bf16)]

    @staticmethod
    def peers(at):
        return [(f"z{k}", at.at_z(k)) for k in (1, 2, 3)] + [(f"x{a}{b}", at.at_x(a, b)) for a, b in ((0, 1), (1, 0), (1, 1))]

    def __init__(self, at, src, out, refs, send, recv, local, base, place, x_first, by_rows=False):
        self.at, self.src, self.out = at, src, out
        self.land, self.total, self.land_two, self.last = refs
        self.x_first, self.by_rows = x_first, by_rows
        self.deep = self.last.shape[1]
        self.chunk = 32 if self.deep % 32 == 0 else 24
        z_steps = [(at.at_z(k), lax.rem(at.z + k, 4)) for k in (1, 2, 3)]
        x_steps = [
            (at.at_x(a, b), (lax.rem(at.s + a, 2), lax.rem(at.n + b, 2))) for a, b in ((0, 1), (1, 0), (1, 1))
        ]
        first, second = (x_steps, z_steps) if x_first else (z_steps, x_steps)

        def move(slot, source, target, peer):
            return remote(source, target, send.at[base + slot], recv.at[base + slot], peer)

        self.one = [move(i, self.piece(where), self.land.at[i], peer) for i, (peer, where) in enumerate(first)]
        self.own = pltpu.make_async_copy(
            self.piece((at.s, at.n) if x_first else at.z), self.total, local.at[place]
        )
        self.two = [move(3 + i, self.part(where), self.land_two.at[i], peer) for i, (peer, where) in enumerate(second)]
        self.mine = at.z if x_first else (at.s, at.n)
        self.three = move(6, self.last.at[at.s], self.last.at[at.s], at.at_x(1, 0))
        target = out.at[at.z]
        self.four = [move(7 + i, self.last, target, peer) for i, (peer, _) in enumerate(z_steps)]
        self.stay = pltpu.make_async_copy(self.last, target, local.at[place + 1])

    def piece(self, where):
        if self.x_first:
            s, n = where
            return self.src.at[n, :, s] if self.by_rows else self.src.at[:, s, :, self.at.half(n)]
        return self.src.at[:, where] if self.by_rows else self.src.at[where]

    def part(self, where):
        if self.x_first:
            return self.total.at[where]
        s, n = where
        return self.total.at[n, s] if self.by_rows else self.total.at[s, :, self.at.half(n)]

    def first(self):
        for copy in self.one + [self.own]:
            copy.start()

    def second(self):
        self.own.wait()
        for copy in self.one:
            copy.wait_recv()
        lead = self.total.shape[:-2]
        count = math.prod(lead)

        def add(i, carry):
            at_lead = (i,) if len(lead) == 1 else (lax.div(i, lead[1]), lax.rem(i, lead[1]))
            for start in range(0, self.deep, self.chunk):
                where = (*at_lead, slice(start, start + self.chunk))
                got = self.total[where].astype(f32)
                for k in range(3):
                    got += self.land[(k, *where)].astype(f32)
                self.total[where] = got.astype(bf16)
            return carry

        lax.fori_loop(0, count, add, 0)
        for copy in self.two:
            copy.start()

    def third(self):
        for copy in self.two:
            copy.wait_recv()
        own = self.part(self.mine)
        s = self.at.s
        for start in range(0, self.deep, self.chunk):
            rows = slice(start, start + self.chunk)
            got = own[rows].astype(f32)
            for k in range(3):
                got += self.land_two[k, rows].astype(f32)
            self.last[s, rows] = got.astype(bf16)
        self.three.start()

    def fourth(self):
        self.three.wait_recv()
        for copy in self.four + [self.stay]:
            copy.start()

    def end(self):
        for copy in self.four:
            copy.wait()
        for copy in self.one + self.two + [self.three]:
            copy.wait_send()
        self.stay.wait()


class Gather:
    slots = 11

    def __init__(self, at, x, whole, send, recv, local, base=0):
        self.at, self.x, self.whole = at, x, whole
        y, c, up, down = at.y, at.c, at.up, at.down
        far = lax.rem(y + 2, 4)
        half = BLOCK // 2

        def move(slot, y_from, peer, start=0, size=BLOCK, first=False):
            rows = at.rows(y_from, c, start, size)
            src = whole.at[rows]
            if first:
                src = x if size == BLOCK else x.at[start : start + size]
            return remote(src, whole.at[rows], send.at[base + slot], recv.at[base + slot], peer)

        to_up, to_down, core = at.at_y(up), at.at_y(down), at.core()
        self.sends = [
            move(0, y, to_up, 0, half, first=True),
            move(1, y, to_up, half, half, first=True),
            move(2, y, to_down, half, half, first=True),
            move(3, y, to_down, 0, half, first=True),
            move(4, y, core, first=True),
            move(5, down, to_up, 0, half),
            move(6, up, to_down, half, half),
            move(7, down, core),
            move(8, up, core),
            move(9, far, core, 0, half),
            move(10, far, core, half, half),
        ]
        self.own = pltpu.make_async_copy(x, whole.at[at.rows(y, c)], local)

    def begin(self):
        for i in (0, 2, 1, 3, 4):
            self.sends[i].start()
        self.own.start()
        self.own.wait()

    def chain(self, *pairs):
        for arrived, leaving in pairs:
            self.sends[arrived].wait_recv()
            self.sends[leaving].start()

    def pass_on(self):
        self.chain((0, 5), (2, 6))

    def pass_near(self):
        self.chain((1, 7), (3, 8))

    def pass_far(self):
        self.chain((5, 9), (6, 10))

    def got(self, *slots):
        for i in slots:
            self.sends[i].wait_recv()

    def end(self):
        for copy in self.sends:
            copy.wait_send()

    def finish(self):
        self.pass_on()
        self.pass_near()
        self.pass_far()
        self.got(4, 7, 8, 9, 10)
        self.end()

    def each(self, work):
        at = self.at

        def step(s, carry):
            @pl.when(s == 1)
            def _():
                self.got(4)
                self.pass_on()

            @pl.when(s == 2)
            def _():
                self.pass_near()

            @pl.when(s == 3)
            def _():
                self.got(8)

            @pl.when(s == 5)
            def _():
                self.got(7)

            @pl.when(s == 6)
            def _():
                self.pass_far()

            @pl.when(s == 7)
            def _():
                self.got(9, 10)

            work(s, self.place(s))
            return carry

        lax.fori_loop(0, 8, step, 0)
        self.end()

    def place(self, s):
        g = lax.div(s, 2)
        off = g + lax.div(g, 2) - 2 * lax.div(g, 3)
        return self.at.rows(lax.rem(self.at.y + off, 4), lax.rem(self.at.c + s, 2))


QUARTER = 384


class GatherZ(Gather):
    def __init__(self, at, quarter, full, send, recv, local, base=0):
        self.at = at
        z, up, down, far = at.z, lax.rem(at.z + 1, 4), lax.rem(at.z + 3, 4), lax.rem(at.z + 2, 4)
        half = QUARTER

        def move(slot, z_from, peer, start=0, size=2 * QUARTER, first=False):
            rows = pl.ds(pl.multiple_of(at.c * 2 * QUARTER + start, QUARTER), size)
            target = full.at[rows, self.columns(z_from)]
            return remote(quarter.at[rows] if first else target, target, send.at[base + slot], recv.at[base + slot], peer)

        to_up, to_down, core = at.at_z(1), at.at_z(3), at.core()
        self.sends = {
            0: move(0, z, to_up, 0, half, first=True),
            1: move(1, z, to_up, half, half, first=True),
            2: move(2, z, to_down, half, half, first=True),
            3: move(3, z, to_down, 0, half, first=True),
            5: move(5, down, to_up, 0, half),
            6: move(6, up, to_down, half, half),
            7: move(7, down, core),
            8: move(8, up, core),
            9: move(9, far, core, 0, half),
            10: move(10, far, core, half, half),
        }
        self.own = pltpu.make_async_copy(quarter, full.at[:, self.columns(z)], local)

    @staticmethod
    def columns(z):
        return pl.ds(pl.multiple_of(z * QUARTER, QUARTER), QUARTER)

    @staticmethod
    def peers(at):
        return [("z1", at.at_z(1)), ("z3", at.at_z(3)), ("core", at.core())]

    def begin(self):
        for i in (0, 2, 1, 3):
            self.sends[i].start()
        self.own.start()

    def end(self):
        self.got(7, 8, 9, 10)
        self.own.wait()
        for copy in self.sends.values():
            copy.wait_send()


class Scatter:
    slots = 10
    scratch = [
        VMEM((4, BLOCK, D), bf16),
        VMEM((4, BLOCK, D), bf16),
        VMEM((4, BLOCK, D), f32),
        VMEM((2, BLOCK, D), bf16),
        VMEM((2, BLOCK, D), bf16),
        VMEM((2, BLOCK // 2, D), bf16),
        VMEM((2, BLOCK // 2, D), bf16),
    ]

    def __init__(self, at, send, recv, refs, base=0):
        self.at, self.send, self.recv, self.base = at, send, recv, base
        self.out_c, self.in_c, self.own, self.out_y, self.in_y, self.half_out, self.half_in = refs
        half = BLOCK // 2
        peers = at.at_y(at.up), at.at_y(at.down)

        def move(slot, src, dst, peer):
            return remote(src, dst, send.at[base + slot], recv.at[base + slot], peer)

        self.cores = [self.core(g) for g in range(4)]
        self.halves = [move(4 + i, self.half_out.at[i], self.half_in.at[i], peers[i]) for i in range(2)]
        free = [pl.ds((1 - i) * half, half) for i in range(2)]
        bound = [pl.ds(i * half, half) for i in range(2)]
        self.free = [move(6 + i, self.out_y.at[i, free[i]], self.in_y.at[i, free[i]], peers[i]) for i in range(2)]
        self.bound = [move(8 + i, self.out_y.at[i, bound[i]], self.in_y.at[i, bound[i]], peers[i]) for i in range(2)]

    def core(self, g):
        slot = self.base + g
        return remote(self.out_c.at[g], self.in_c.at[g], self.send.at[slot], self.recv.at[slot], self.at.core())

    def both(self, g, rows):
        return self.own[g, rows] + self.in_c[g, rows].astype(f32)

    def products(self, product):
        at = self.at
        half = BLOCK // 2

        def part_rows(rows, i):
            return pl.ds(pl.multiple_of(rows.start + i * half, 32), 32)

        def send_free(i):
            self.cores[1 + i].wait_recv()

            def add(rows, carry):
                there = part_rows(rows, 1 - i)
                self.out_y[i, there] = self.both(1 + i, there).astype(bf16)

            by_rows(half, 32, add)
            self.free[i].start()

        def step(s, carry):
            g = lax.div(s, 2)
            off = lax.rem(6 - g + 3 * lax.div(g, 2) + 2 * lax.div(g, 3), 4)
            part = product(at.rows(lax.rem(at.y + off, 4), lax.rem(at.c + 1 + s, 2)))

            @pl.when(lax.rem(s, 2) == 0)
            def _():
                self.out_c[g] = part.astype(bf16)
                self.core(g).start()

            @pl.when(lax.rem(s, 2) == 1)
            def _():
                self.own[g] = part

            @pl.when(s == 2)
            def _():
                self.cores[0].wait_recv()
                for i in range(2):

                    def add(rows, carry, i=i):
                        self.half_out[i, rows] = self.both(0, part_rows(rows, i)).astype(bf16)

                    by_rows(half, 32, add)
                    self.halves[i].start()

            @pl.when(s == 4)
            def _():
                send_free(0)

            @pl.when(s == 6)
            def _():
                send_free(1)

            return carry

        lax.fori_loop(0, 8, step, 0)

    def middle(self):
        half = BLOCK // 2
        for i in range(2):
            self.halves[i].wait_recv()

            def add(rows, carry, i=i):
                here = pl.ds(pl.multiple_of(rows.start + i * half, 32), 32)
                self.out_y[i, here] = (self.both(1 + i, here) + self.half_in[i, rows].astype(f32)).astype(bf16)

            by_rows(half, 32, add)
            self.bound[i].start()

    def arrive(self):
        self.cores[3].wait_recv()
        for copy in self.free + self.bound:
            copy.wait_recv()

    def total(self, rows):
        return self.both(3, rows) + self.in_y[0, rows].astype(f32) + self.in_y[1, rows].astype(f32)

    def end(self):
        for copy in self.cores + self.halves + self.free + self.bound:
            copy.wait_send()


def standard(values):
    average = jnp.mean(values, axis=1, keepdims=True)
    variance = jnp.mean(values * values, axis=1, keepdims=True) - average * average
    factor = lax.rsqrt(variance + EPSILON)
    return (values - average) * factor, factor


def norm_back(incoming, centred, factor, gain):
    scaled = incoming * gain
    first = jnp.mean(scaled, axis=1, keepdims=True)
    second = jnp.mean(scaled * centred, axis=1, keepdims=True)
    return factor * (scaled - first - centred * second)


def two_sums(incoming, centred, carry):
    gains, shifts = carry
    return gains + jnp.sum(incoming * centred, axis=0, keepdims=True), shifts + jnp.sum(incoming, axis=0, keepdims=True)


def no_sums():
    return jnp.zeros((1, D), f32), jnp.zeros((1, D), f32)


EIGHTH = 0.125


def shape(*dims, dtype=bf16):
    return jax.ShapeDtypeStruct(dims, dtype)


class Keep:
    def __init__(self, whole, out, sem, base):
        self.whole, self.out, self.sem, self.base = whole, out, sem, base

    def block(self, s, rows):
        pltpu.make_async_copy(self.whole.at[rows], self.out.at[rows], self.sem.at[self.base + s]).start()

    def wait(self):
        for s in range(8):
            some = pl.ds(0, BLOCK)
            pltpu.make_async_copy(self.whole.at[some], self.out.at[some], self.sem.at[self.base + s]).wait()


def enter(number, layer_input, gains, weights, query_t, cross_out, texts, pairs_t, beside):
    relay = Relay(layer_input)

    def body(at, ins, outs, kept):
        source, *gains = ins[:7]
        *own_weights, query_own, out_own, own_texts, text_key, text_value = ins[7:]
        x, vectors, weight, all_rows, qkv, query_all, out_quarter, text_pair = outs
        normed, whole, query_part, out_part, query_quarter, text_parts, text_got, own_vectors, send, recv, local = kept
        half = at.half(at.n)
        moving = functools.partial(relay_run, relay, at, source, x, send, recv, local.at[0], 11)
        moving(False)
        own_vectors[...] = jnp.zeros_like(own_vectors)
        for i, ref in enumerate(gains):
            own_vectors[i : i + 1] = ref[...].astype(f32).reshape(1, HALF)
        columns = GatherZ.columns(lax.rem(at.z, 2))
        holds = at.n == lax.div(at.z, 2)
        quarters = []
        for i, (own, part) in enumerate(((query_own, query_part), (out_own, out_part))):
            quarters.append(
                (
                    pltpu.make_async_copy(own.at[:, columns], part, local.at[14 + i]),
                    remote(own.at[:, columns], part, send.at[17 + i], recv.at[17 + i], at.x()),
                )
            )

        @pl.when(holds)
        def _():
            for stay, go in quarters:
                go.start()
                stay.start()

        stay = [
            pltpu.make_async_copy(own, target, local.at[1 + i])
            for i, (own, target) in enumerate(
                [(own_vectors, vectors.at[:, half])]
                + [(own, weight.at[j * COLS : (j + 1) * COLS, half]) for j, own in enumerate(own_weights)]
            )
        ]
        for copy in stay:
            copy.start()
        vectors_go = remote(own_vectors, vectors.at[:, half], send.at[13], recv.at[13], at.x())
        vectors_go.start()
        rows = pl.ds(pl.multiple_of(at.z * 144, 16), 144)
        over = remote(weight.at[rows, half], weight.at[rows, half], send.at[14], recv.at[14], at.x())
        other = weight.at[rows, at.half(1 - at.n)]
        others = [
            remote(other, other, send.at[slot], recv.at[slot], at.at_z(k)) for k, slot in ((1, 15), (2, 16), (3, 53))
        ]
        for copy in stay:
            copy.wait()
        over.start()

        @pl.when(holds)
        def _():
            for near, far in quarters:
                near.wait()
                far.wait_send()

        @pl.when(jnp.logical_not(holds))
        def _():
            for near, far in quarters:
                far.wait_recv()

        for clip in range(2):
            text_parts[clip, :, :COLS] = dot_flip(own_texts[clip], text_key[...])
            text_parts[clip, :, COLS:] = dot_flip(own_texts[clip], text_value[...])
        text_go = remote(text_parts.at[1 - at.n], text_got, send.at[52], recv.at[52], at.x())
        text_go.start()
        queries = Gather(at, query_part, query_quarter, send, recv, local.at[16], 19)
        outputs = Gather(at, out_part, out_quarter, send, recv, local.at[17], 30)
        queries.begin()
        vectors_go.wait_recv()
        moving(True)
        over.wait_recv()
        for copy in others:
            copy.start()
        at.start_beside(1, 2)
        queries.pass_on()
        queries.pass_near()

        def norm(rows, carry):
            centred, _ = standard(x[rows].astype(f32))
            normed[rows] = (centred * vectors[0:1] + vectors[1:2]).astype(bf16)

        by_rows(BLOCK, 32, norm)
        gather = Gather(at, normed, whole, send, recv, local.at[5])
        gather.begin()
        queries.pass_far()
        queries.got(4, 7, 8, 9, 10)
        around = GatherZ(at, query_quarter, query_all, send, recv, local.at[18], 41)
        around.begin()
        keep = Keep(whole, all_rows, local, 6)

        def times(rows):
            qkv[rows] = dot_flip(whole[rows], weight[...]).astype(bf16)

        def work(s, rows):
            keep.block(s, rows)

            @pl.when(s == 4)
            def _():
                for copy in others:
                    copy.wait_recv()
                at.start_beside(0)
                at.flush(0, 1, 2)

            @pl.when(s >= 4)
            def _():
                times(rows)

            @pl.when(s == 6)
            def _():
                outputs.begin()
                around.pass_on()

        gather.each(work)
        around.pass_near()
        outputs.pass_on()
        outputs.pass_near()

        def rest(s, carry):
            times(gather.place(s))
            return carry

        lax.fori_loop(0, 4, rest, 0)
        at.flush(4)
        outputs.pass_far()
        around.pass_far()
        text_go.wait()
        text_pair[...] = (text_parts[at.n] + text_got[...]).astype(bf16)
        outputs.got(4, 7, 8, 9, 10)
        keep.wait()
        for copy in [vectors_go, over] + others:
            copy.wait_send()
        outputs.end()
        queries.end()
        around.end()

    return call(
        body,
        number,
        [layer_input, *gains, *weights, query_t, cross_out, texts, *pairs_t],
        [
            shape(BLOCK, D),
            shape(8, D, dtype=f32),
            shape(3 * COLS, D),
            shape(D, D),
            shape(D, 3 * COLS),
            shape(D, D),
            shape(D, QUARTER),
            shape(64, 2 * COLS),
        ],
        [
            VMEM((BLOCK, D), bf16),
            VMEM((D, D), bf16),
            VMEM((COLS, QUARTER), bf16),
            VMEM((COLS, QUARTER), bf16),
            VMEM((D, QUARTER), bf16),
            VMEM((2, 64, 2 * COLS), f32),
            VMEM((64, 2 * COLS), f32),
            VMEM((8, HALF), f32),
            *sems(54),
        ],
        beside,
        lambda at: ring_peers(at) + relay.peers(at) + [("x", at.x()), ("z2", at.at_z(2))] + GatherZ.peers(at),
        spaces=[ANY] + [PLAIN] * 6 + [VMEM] * 8,
        out_spaces=[VMEM, VMEM, VMEM, ANY, VMEM, ANY, VMEM, VMEM],
        late=True,
    )


def causal_forward(number, joined, down, out_quarter, beside):
    at_once = 512

    def body(at, ins, outs, kept):
        (qkv, block, quarter), (out, logs, all_down, out_all) = ins, outs
        parts, mixed, send, recv, local = kept
        first = Gather(at, block, all_down, send, recv, local.at[0])
        second = GatherZ(at, quarter, out_all, send, recv, local.at[1], 11)
        second.begin()
        first.begin()
        for i in range(3):
            for h in range(HEADS):
                a = i * COLS + h * HDIM
                piece = qkv[:, a : a + HDIM]
                parts[i, h] = piece * EIGHTH if i == 0 else piece
        square = (at_once, at_once)
        seen = lax.broadcasted_iota(jnp.int32, square, 0) >= lax.broadcasted_iota(jnp.int32, square, 1)

        def one(h, carry):
            for i in reversed(range(D // at_once)):
                before, upto = i * at_once, (i + 1) * at_once
                rows = slice(before, upto)
                scores = dot_flip(parts[0, h, rows], parts[1, h, 0:upto])
                last = jnp.where(seen, scores[:, before:], NEGATIVE)
                scores = jnp.concatenate((scores[:, :before], last), axis=1) if i else last
                peak = jnp.max(scores, axis=1, keepdims=True)
                raised = jnp.exp(scores - peak)
                total = jnp.sum(raised, axis=1, keepdims=True)
                mixed[h, rows] = (dot(raised.astype(bf16), parts[2, h, 0:upto]) / total).astype(bf16)
                column = jnp.broadcast_to(peak + jnp.log(total), (at_once, 128))
                logs[pl.ds(h, 1), rows] = column.T[0:1, :]

            @pl.when(h == 1)
            def _():
                first.pass_on()
                second.pass_on()

            return carry

        lax.fori_loop(0, HEADS, one, 0)
        first.pass_near()
        second.pass_near()
        out[...] = jnp.concatenate([mixed[h] for h in range(HEADS)], axis=1)
        at.flush()
        first.pass_far()
        second.pass_far()
        first.got(4, 7, 8, 9, 10)
        first.end()
        second.end()

    return call(
        body,
        number,
        [joined, down, out_quarter],
        [shape(D, COLS), shape(8, D, dtype=f32), shape(D, D), shape(D, D)],
        [VMEM((3, HEADS, D, HDIM), bf16), VMEM((HEADS, D, HDIM), bf16), *sems(22)],
        beside,
        lambda at: ring_peers(at) + GatherZ.peers(at),
        out_spaces=[VMEM, VMEM, ANY, ANY],
    )


def forward_rest(number, attended, out_w, x, vectors, query_all, out_all, texts, all_down, expand_w, contract):
    def body(at, ins, outs, kept):
        mixed, out_own, out_got, x, vectors, query_all, out_all, texts, all_down, expand_own, expand_got, contract_own = ins
        middle, after, normed_two, weights, all_rows, activated, grad, contract_out, keys_out, values_out, traded = outs
        *refs, normed, whole, downs, out_full, expand_full, contract_full, key_full, value_full, branch, scores_all, send, recv, local = kept
        half = at.half(at.n)
        weight = at.early
        swap = remote(contract_own, contract_full.at[:, half], send.at[21], recv.at[21], at.x())
        swap.start()
        factors = [
            pltpu.make_async_copy(query_all, key_full, local.at[2]),
            pltpu.make_async_copy(out_all, value_full, local.at[3]),
        ]
        for copy in factors:
            copy.start()
        later = [
            pltpu.make_async_copy(contract_own, contract_full.at[:, half], local.at[4]),
            pltpu.make_async_copy(all_down, downs, local.at[7]),
        ]
        for copy in later:
            copy.start()
        later.append(Whole(at, expand_own, expand_got, expand_full, local.at[pl.ds(5, 2)], 0))
        weight.wait()
        scatter = Scatter(at, send, recv, refs)
        scatter.products(lambda rows: dot(mixed[rows], out_full[...]))
        for copy in factors:
            copy.wait()

        def make(b, carry):
            for h in range(HEADS):
                rows = pl.ds(pl.multiple_of(b * BLOCK + h * 64, 64), 64)
                text_keys = texts[b, :, h * HDIM : (h + 1) * HDIM]
                text_values = texts[b, :, COLS + h * HDIM : COLS + (h + 1) * HDIM]
                key_full[rows] = (dot(text_keys, key_full[rows]) * EIGHTH).astype(bf16)
                value_full[rows] = dot(text_values, value_full[rows]).astype(bf16)
            return carry

        lax.fori_loop(0, 8, make, 0)
        made = [
            pltpu.make_async_copy(key_full, keys_out, local.at[8]),
            pltpu.make_async_copy(value_full, values_out, local.at[9]),
        ]
        for copy in made:
            copy.start()
        scatter.middle()
        for copy in later:
            copy.wait()
        scatter.arrive()

        def norm_two(rows, carry):
            total = x[rows].astype(f32) + scatter.total(rows)
            middle[rows] = total
            centred, _ = standard(total)
            normed_two[rows] = (centred * vectors[2:3] + vectors[3:4]).astype(bf16)

        by_rows(BLOCK, 32, norm_two)

        trade = Trade(at, weights, traded, send, recv, local.at[20], 22)

        def score(rows, carry):
            scores_all[rows] = dot_flip(key_full[rows], normed_two[...])

        by_rows(D, QUARTER, score)

        def cross(b, carry):
            rows = pl.ds(pl.multiple_of(b * BLOCK, BLOCK), BLOCK)
            scores = scores_all[rows].reshape(HEADS, 64, BLOCK)
            raised = jnp.exp(scores - jnp.max(scores, axis=1, keepdims=True))
            p = raised / jnp.sum(raised, axis=1, keepdims=True)
            p = p.reshape(BLOCK, BLOCK).T.astype(bf16)
            weights[b] = p
            trade.give(b)
            part = dot(p, value_full[rows])

            @pl.when(b == 0)
            def _():
                branch[...] = part

            @pl.when(b > 0)
            def _():
                branch[...] += part

            return carry

        lax.fori_loop(0, 8, cross, 0)

        def norm_three(rows, carry):
            total = middle[rows] + branch[rows]
            after[rows] = total
            centred, _ = standard(total)
            normed[rows] = (centred * vectors[4:5] + vectors[5:6]).astype(bf16)

        by_rows(BLOCK, 32, norm_three)
        gather = Gather(at, normed, whole, send, recv, local.at[10], 10)
        gather.begin()
        at.flush(0, 1, 2, 3)
        swap.wait_recv()
        keep_contract = pltpu.make_async_copy(contract_full, contract_out, local.at[11])
        keep_contract.start()
        keep = Keep(whole, all_rows, local, 12)

        def ahead(rows, carry):
            grad[rows] = dot_flip(downs[rows], contract_full[...]).astype(bf16)

        by_rows(D, BLOCK, ahead)

        def work(s, rows):
            keep.block(s, rows)
            hidden = dot(whole[rows], expand_full[...])
            bell = 0.5 * (1.0 + lax.erf(hidden * ROOT_HALF))
            activated[rows] = (hidden * bell).astype(bf16)
            slope = bell + hidden * jnp.exp(-0.5 * hidden * hidden) * GAUSS_NORM
            grad[rows] = (grad[rows].astype(f32) * slope).astype(bf16)

        gather.each(work)
        at.flush()
        keep.wait()
        keep_contract.wait()
        trade.end()
        for copy in made:
            copy.wait()
        scatter.end()
        swap.wait_send()

    results, _ = call(
        body,
        number,
        [attended, *out_w, x, vectors, query_all, out_all, texts, all_down, *expand_w, contract],
        [
            shape(BLOCK, D, dtype=f32),
            shape(BLOCK, D, dtype=f32),
            shape(BLOCK, D),
            shape(8, BLOCK, BLOCK),
            shape(D, D),
            shape(D, HALF),
            shape(D, HALF),
            shape(HALF, D),
            shape(D, D),
            shape(D, D),
            shape(8, BLOCK, BLOCK),
        ],
        [
            *Scatter.scratch,
            VMEM((BLOCK, D), bf16),
            VMEM((D, D), bf16),
            VMEM((D, D), bf16),
            VMEM((COLS, D), bf16),
            VMEM((D, HALF), bf16),
            VMEM((HALF, D), bf16),
            VMEM((D, D), bf16),
            VMEM((D, D), bf16),
            VMEM((BLOCK, D), f32),
            VMEM((D, BLOCK), f32),
            *sems(30),
        ],
        (),
        lambda at: Trade.peers(at) + [("x", at.x())],
        early=lambda at, ins, kept: Whole(at, ins[1], ins[2], kept[len(Scatter.scratch) + 3], kept[-1].at[pl.ds(0, 2)], 1),
        spaces=[VMEM, ANY, ANY, VMEM, VMEM, ANY, ANY, VMEM, ANY, ANY, ANY, ANY],
        out_spaces=[VMEM, VMEM, VMEM, VMEM, ANY, VMEM, VMEM, ANY, ANY, ANY, ANY],
    )
    return results


def backward_rest(
    number, grad, expand_w, after, middle, vectors, down, keys, values, weights, out_w, contract_sum, expand_sum, beside
):
    def body(at, ins, outs, kept):
        grad, expand_own, expand_got, after, middle, vectors, down, keys, values, weights, out_own, out_got = ins[:12]
        grad_rows, rounded_two, traded, all_two, all_rows, grad_mixed, grad_vectors = outs[:7]
        *refs, rounded, whole, second, out_full, expand_full, key_full, value_full, grad_scores, grads_all, send, recv, local = kept
        reduces = [
            Reduce(at, ins[12], outs[7], refs[7:11], send, recv, local, 32, 16, False),
            Reduce(at, ins[13], outs[8], refs[11:15], send, recv, local, 42, 18, True, True),
        ]
        refs = refs[:7]
        for reduce in reduces:
            reduce.first()
        weight = at.early
        later = [
            pltpu.make_async_copy(keys, key_full, local.at[2]),
            pltpu.make_async_copy(values, value_full, local.at[3]),
        ]
        for copy in later:
            copy.start()
        later.append(Whole(at, out_own, out_got, out_full, local.at[pl.ds(4, 2)], 1))
        weight.wait()
        scatter = Scatter(at, send, recv, refs)
        scatter.products(lambda rows: dot_flip(grad[rows], expand_full[...]))
        scatter.middle()
        for copy in later:
            copy.wait()
        scatter.arrive()

        def norm_three(rows, carry):
            incoming = scatter.total(rows)
            centred, factor = standard(after[rows])
            total = down[rows].astype(f32) + norm_back(incoming, centred, factor, vectors[4:5])
            grad_rows[rows] = total
            rounded_two[rows] = total.astype(bf16)
            return two_sums(incoming, centred, carry)

        gains, shifts = by_rows(BLOCK, 32, norm_three, no_sums())
        before = Gather(at, rounded_two, all_two, send, recv, local.at[6], 10)
        before.begin()
        for reduce in reduces:
            reduce.second()
        grad_vectors[4:5] = gains
        grad_vectors[5:6] = shifts

        trade = Trade(at, grad_scores, traded, send, recv, local.at[20], 52)

        def score(rows, carry):
            grads_all[rows] = dot_flip(value_full[rows], rounded_two[...])

        by_rows(D, QUARTER, score)

        def cross(b, carry):
            rows = pl.ds(pl.multiple_of(b * BLOCK, BLOCK), BLOCK)
            p = weights[b].astype(f32).T.reshape(HEADS, 64, BLOCK)
            dp = grads_all[rows].reshape(HEADS, 64, BLOCK)
            ds = p * (dp - jnp.sum(p * dp, axis=1, keepdims=True))
            ds = ds.reshape(BLOCK, BLOCK).T.astype(bf16)
            grad_scores[b] = ds
            trade.give(b)
            part = dot(ds, key_full[rows])

            @pl.when(b == 0)
            def _():
                second[...] = part

            @pl.when(b > 0)
            def _():
                second[...] += part

            @pl.when(b == 3)
            def _():
                before.pass_on()

            @pl.when(b == 5)
            def _():
                for reduce in reduces:
                    reduce.third()

            return carry

        lax.fori_loop(0, 8, cross, 0)
        at.flush(1)
        for reduce in reduces:
            reduce.fourth()
        at.start_beside()

        def norm_two(rows, carry):
            incoming = second[rows]
            centred, factor = standard(middle[rows])
            total = grad_rows[rows] + norm_back(incoming, centred, factor, vectors[2:3])
            grad_rows[rows] = total
            rounded[rows] = total.astype(bf16)
            return two_sums(incoming, centred, carry)

        gains, shifts = by_rows(BLOCK, 32, norm_two, no_sums())
        grad_vectors[2:3] = gains
        grad_vectors[3:4] = shifts
        gather = Gather(at, rounded, whole, send, recv, local.at[7], 21)
        before.pass_near()
        gather.begin()
        at.flush(0, 6)
        before.pass_far()
        keep = Keep(whole, all_rows, local, 8)

        def work(s, rows):
            keep.block(s, rows)
            grad_mixed[rows] = dot_flip(whole[rows], out_full[...]).astype(bf16)

        gather.each(work)
        at.flush()
        before.got(4, 7, 8, 9, 10)
        before.end()
        trade.end()
        keep.wait()
        scatter.end()
        for reduce in reduces:
            reduce.end()

    return call(
        body,
        number,
        [grad, *expand_w, after, middle, vectors, down, keys, values, weights, *out_w, contract_sum, expand_sum],
        [
            shape(BLOCK, D, dtype=f32),
            shape(BLOCK, D),
            shape(8, BLOCK, BLOCK),
            shape(D, D),
            shape(D, D),
            shape(D, COLS),
            shape(8, D, dtype=f32),
            shape(4, 2, 96, HALF),
            shape(4, 2, 96, HALF),
        ],
        [
            *Scatter.scratch,
            *Reduce.scratch(96, False),
            *Reduce.scratch(96, True, True),
            VMEM((BLOCK, D), bf16),
            VMEM((D, D), bf16),
            VMEM((BLOCK, D), f32),
            VMEM((COLS, D), bf16),
            VMEM((D, HALF), bf16),
            VMEM((D, D), bf16),
            VMEM((D, D), bf16),
            VMEM((8, BLOCK, BLOCK), bf16),
            VMEM((D, BLOCK), f32),
            *sems(60),
        ],
        beside,
        lambda at: Trade.peers(at) + Reduce.peers(at),
        early=lambda at, ins, kept: Whole(at, ins[1], ins[2], kept[len(Scatter.scratch) + 12], kept[-1].at[pl.ds(0, 2)], 0),
        spaces=[VMEM, ANY, ANY, VMEM, VMEM, VMEM, VMEM, ANY, ANY, VMEM, ANY, ANY, ANY, ANY],
        out_spaces=[VMEM, VMEM, ANY, ANY, ANY, VMEM, VMEM, ANY, ANY],
        late=True,
    )


def causal_backward(number, joined, grad, logs, activated, contract, after, normed_two, part, beside):
    at_once = 512

    def body(at, ins, outs, kept):
        (qkv, go, log_rows, activated, contract, after, block, part), (out, result, all_rows, summed) = ins, outs
        *refs, parts, key_sum, value_sum, send, recv, local = kept
        reduce = Reduce(at, part, summed, refs[7:], send, recv, local, 21, 1, False)
        reduce.first()
        gather = Gather(at, block, all_rows, send, recv, local.at[0], 10)
        gather.begin()
        scatter = Scatter(at, send, recv, refs[:7])
        scatter.products(lambda rows: dot(activated[rows], contract[...]))
        gather.pass_on()
        for i in range(4):
            for h in range(HEADS):
                a = i * COLS + h * HDIM
                piece = qkv[:, a : a + HDIM] if i < 3 else go[:, h * HDIM : (h + 1) * HDIM]
                parts[i, h] = piece * EIGHTH if i == 0 else piece
        square = (at_once, at_once)
        seen = lax.broadcasted_iota(jnp.int32, square, 1) >= lax.broadcasted_iota(jnp.int32, square, 0)
        blocks = D // at_once

        def one(h, carry):
            turned = parts[1, h].T
            query_parts = []
            for i in reversed(range(blocks)):
                before, upto = i * at_once, (i + 1) * at_once
                rows = slice(before, upto)
                q, g = parts[0, h, rows], parts[3, h, rows]
                k, v = parts[1, h, 0:upto], parts[2, h, 0:upto]
                p = jnp.exp(dot_flip(k, q) - log_rows[pl.ds(h, 1), rows])
                last = jnp.where(seen, p[before:], 0.0)
                p = jnp.concatenate((p[:before], last), axis=0) if i else last
                dp = dot_flip(v, g)
                ds = (p * (dp - jnp.sum(p * dp, axis=0, keepdims=True))).astype(bf16)
                value_part, key_part = dot(p.astype(bf16), g), dot(ds, q)
                if i == blocks - 1:
                    key_sum[0:upto, :] = key_part
                    value_sum[0:upto, :] = value_part
                else:
                    key_sum[0:upto, :] += key_part
                    value_sum[0:upto, :] += value_part
                query_parts.append((dot(turned[:, 0:upto], ds) * EIGHTH).T)
                if i == blocks - 1:

                    @pl.when(h == 1)
                    def _():
                        reduce.second()

                    @pl.when(h == 2)
                    def _():
                        reduce.fourth()

            parts[0, h] = jnp.concatenate(query_parts[::-1], axis=0).astype(bf16)
            parts[1, h] = key_sum[...].astype(bf16)
            parts[2, h] = value_sum[...].astype(bf16)

            @pl.when(h == 0)
            def _():
                gather.pass_near()

            @pl.when(h == 1)
            def _():
                scatter.middle()
                gather.pass_far()
                reduce.third()

            return carry

        lax.fori_loop(0, HEADS, one, 0)
        for i in range(3):
            out[:, i * COLS : (i + 1) * COLS] = jnp.concatenate([parts[i, h] for h in range(HEADS)], axis=1)
        scatter.arrive()

        def finish(rows, carry):
            result[rows] = (after[rows] + scatter.total(rows)).astype(bf16)

        at.flush(0)
        by_rows(BLOCK, 32, finish)
        at.flush(1)
        gather.got(4, 7, 8, 9, 10)
        gather.end()
        scatter.end()
        reduce.end()

    return call(
        body,
        number,
        [joined, grad, logs, activated, contract, after, normed_two, part],
        [shape(D, 3 * COLS), shape(BLOCK, D), shape(D, D), shape(4, 2, 72, HALF)],
        [
            *Scatter.scratch,
            *Reduce.scratch(72, False),
            VMEM((4, HEADS, D, HDIM), bf16),
            VMEM((D, HDIM), f32),
            VMEM((D, HDIM), f32),
            *sems(31),
        ],
        beside,
        lambda at: ring_peers(at) + Reduce.peers(at),
        spaces=[VMEM] * 7 + [ANY],
        out_spaces=[VMEM, VMEM, ANY, ANY],
    )


def leave(number, grad, joined, x, vectors, grad_rows, sums, late, text_part, beside):
    relay = Relay(jax.ShapeDtypeStruct((BLOCK, D), bf16), True)
    some = 64 // 8

    def ring(at):
        return [{"wide": lax.rem(at.w + k, 8)} for k in range(1, 8)]

    x_steps = ((0, 1), (1, 0), (1, 1))

    def group(at):
        return [(b, {"wide": lax.rem(at.w + k, 8), "narrow": lax.rem(at.n + b, 2)}) for k in range(8) for b in range(2)][1:]

    def peers(at):
        known = ring_peers(at) + relay.peers(at) + Reduce.peers(at)
        known += [(f"w{k}", peer) for k, peer in enumerate(ring(at), 1)]
        return known + [(f"g{i}", peer) for i, (b, peer) in enumerate(group(at)) if b]

    def body(at, ins, outs, kept):
        grad, weight, x, vectors, before, late, text, one, two = ins
        result, out_one, out_two, vector_sums, text_out = outs
        refs, kept = kept[:7], kept[7:]
        reduces = [
            Reduce(at, one, out_one, kept[0:4], kept[-3], kept[-2], kept[-1], 12, 1, False),
            Reduce(at, two, out_two, kept[4:8], kept[-3], kept[-2], kept[-1], 22, 3, True),
        ]
        rounded, parts, ring_parts, ring_sum, x_parts, x_sum, z_parts, text_parts, text_sum, send, recv, local = kept[8:]
        me = at.spot(at.y, at.c)

        def move(slot, source, target, peer):
            return remote(source, target, send.at[slot], recv.at[slot], peer)

        to_ring, to_group = ring(at), group(at)
        slot = 32
        trades = []
        for peer in to_ring:
            there = at.spot(lax.div(peer["wide"], 2), lax.rem(peer["wide"], 2))
            trades.append(move(slot, text.at[there], text_parts.at[me], peer))
            slot += 1
        text_own = pltpu.make_async_copy(text.at[me], text_parts.at[me], local.at[5])
        texts = []
        for b, peer in to_group:
            n = lax.rem(at.n + b, 2)
            texts.append(move(slot, text_sum.at[:, at.half(n)], text_out.at[at.n, me], peer))
            slot += 1
        text_stay = pltpu.make_async_copy(text_sum.at[:, at.half(at.n)], text_out.at[at.n, me], local.at[6])
        rings = []
        for peer in to_ring:
            rings.append(move(slot, parts, ring_parts.at[at.w], peer))
            slot += 1
        ring_own = pltpu.make_async_copy(parts, ring_parts.at[at.w], local.at[7])
        spreads = []
        for a, b in x_steps:
            half = ring_sum.at[:, at.half(lax.rem(at.n + b, 2))]
            spreads.append(move(slot, half, x_parts.at[at.s, at.n], at.at_x(a, b)))
            slot += 1
        x_own = pltpu.make_async_copy(ring_sum.at[:, at.half(at.n)], x_parts.at[at.s, at.n], local.at[8])
        lasts = []
        for k in (1, 2, 3):
            lasts.append(move(slot, x_sum, z_parts.at[at.z], at.at_z(k)))
            slot += 1

        for reduce in reduces:
            reduce.first()
        text_own.start()
        for copy in trades:
            copy.start()
        scatter = Scatter(at, send, recv, refs)
        scatter.products(lambda rows: dot(grad[rows], weight[...]))
        scatter.middle()
        for reduce in reduces:
            reduce.second()
        text_own.wait()
        for copy in trades:
            copy.wait_recv()
        total = text_parts[0].astype(f32)
        for i in range(1, 8):
            total += text_parts[i].astype(f32)
        text_sum[...] = total.astype(bf16)
        text_stay.start()
        for copy in texts:
            copy.start()
        scatter.arrive()

        def norm(rows, carry):
            incoming = scatter.total(rows)
            centred, factor = standard(x[rows].astype(f32))
            total = before[rows] + norm_back(incoming, centred, factor, vectors[0:1])
            rounded[rows] = total.astype(bf16)
            return two_sums(incoming, centred, carry)

        gains, shifts = by_rows(BLOCK, 32, norm, no_sums())
        moving = functools.partial(relay_run, relay, at, rounded, result, send, recv, local.at[0], 10)
        moving(False)
        parts[0:1] = gains
        parts[1:2] = shifts
        parts[2:6] = late[2:6]
        parts[6:8] = jnp.zeros((2, D), f32)
        ring_own.start()
        for copy in rings:
            copy.start()
        for reduce in reduces:
            reduce.third()
        ring_own.wait()
        for copy in rings:
            copy.wait_recv()
        total = ring_parts[0]
        for i in range(1, 8):
            total += ring_parts[i]
        ring_sum[...] = total
        x_own.start()
        for copy in spreads:
            copy.start()
        for reduce in reduces:
            reduce.fourth()
        at.start_beside()
        x_own.wait()
        for copy in spreads:
            copy.wait_recv()
        total = x_parts[0, 0] + x_parts[0, 1] + x_parts[1, 0] + x_parts[1, 1]
        x_sum[...] = total
        for copy in lasts:
            copy.start()
        z_parts[pl.ds(at.z, 1)] = total.reshape(1, 8, HALF)
        for copy in lasts:
            copy.wait_recv()
        vector_sums[...] = z_parts[0] + z_parts[1] + z_parts[2] + z_parts[3]
        at.flush()
        moving(True)
        text_stay.wait()
        for copy in texts:
            copy.wait()
        for copy in trades + rings + spreads + lasts:
            copy.wait_send()
        scatter.end()
        for reduce in reduces:
            reduce.end()

    return call(
        body,
        number,
        [grad, joined, x, vectors, grad_rows, late, text_part, *sums],
        [
            shape(384, HALF),
            shape(4, 2, 72, HALF),
            shape(4, 2, 48, HALF),
            shape(8, HALF, dtype=f32),
            shape(2, 8, some, HALF),
        ],
        [
            *Scatter.scratch,
            *Reduce.scratch(72, False),
            *Reduce.scratch(48, True),
            VMEM((BLOCK, D), bf16),
            VMEM((8, D), f32),
            VMEM((8, 8, D), f32),
            VMEM((8, D), f32),
            VMEM((2, 2, 8, HALF), f32),
            VMEM((8, HALF), f32),
            VMEM((4, 8, HALF), f32),
            VMEM((8, some, D), bf16),
            VMEM((some, D), bf16),
            *sems(32 + 7 + 15 + 7 + 6),
        ],
        beside,
        peers,
        spaces=[VMEM, VMEM, VMEM, VMEM, VMEM, VMEM, ANY, ANY, ANY],
        out_spaces=[ANY, ANY, ANY, VMEM, ANY],
        late=True,
    )


def on_device(
    layer_input,
    text_states,
    cotangent,
    first_gain,
    first_shift,
    query_weight,
    key_weight,
    value_weight,
    output_weight,
    second_gain,
    second_shift,
    cross_query,
    cross_key,
    cross_value,
    cross_output,
    third_gain,
    third_shift,
    expand_weight,
    contract_weight,
):
    gains = (first_gain, first_shift, second_gain, second_shift, third_gain, third_shift)
    weights = [query_weight.T, key_weight.T, value_weight.T]
    query_t = cross_query.T
    pairs_t = cross_key.T, cross_value.T
    n = lax.axis_index("narrow")

    results, ((down,), (out_got,), (text_got,)) = enter(
        1,
        layer_input,
        gains,
        weights,
        query_t,
        cross_output,
        text_states,
        pairs_t,
        [Relay(cotangent), Give(output_weight), GiveClip(text_states)],
    )
    x, vectors, joined, all_one, qkv, query_all, out_quarter, text_pair = results
    (attended, logs, all_down, out_all), ((texts,), (expand_got,)) = causal_forward(
        2, qkv, down, out_quarter, [ToSpots(text_pair), Give(expand_weight)]
    )
    out_w, expand_w = (output_weight, out_got), (expand_weight, expand_got)
    results = forward_rest(3, attended, out_w, x, vectors, query_all, out_all, texts, all_down, expand_w, contract_weight)
    middle, after, normed_two, cross_p, all_three, activated, grad_expand, contract, all_keys, all_values, traded_p = results

    contract_part = outer(activated, all_down).astype(bf16).reshape(4, 2, 96, D)
    expand_part = outer(all_three, grad_expand).astype(bf16).reshape(2, 4, 2, 96, HALF)
    results, ((query_got,), (cross_got,)) = backward_rest(
        4,
        grad_expand,
        expand_w,
        after,
        middle,
        vectors,
        down,
        all_keys,
        all_values,
        cross_p,
        out_w,
        contract_part,
        expand_part,
        [Give(query_t), Give(cross_output)],
    )
    grad_one, _, grad_scores, all_mid_two, all_mid_one, grad_attended, late, contract_grad, expand_grad = results

    own_first = n == 0

    def whole(own, got):
        return jnp.concatenate((jnp.where(own_first, own, got), jnp.where(own_first, got, own)), axis=1)

    def heads(what, a, b):
        return jnp.einsum(what, a, b, preferred_element_type=f32)

    text = whole(lax.dynamic_index_in_dim(text_states, n, 0, False), text_got)
    text_heads = text_pair.reshape(64, 2, HEADS, HDIM)
    grad_values = outer(traded_p.reshape(D, COLS), all_mid_two).astype(bf16).reshape(HEADS, 64, D)
    heads_out = whole(cross_output, cross_got).reshape(HEADS, HDIM, D)
    grad_text_values = heads("hkf,hdf->khd", grad_values, heads_out).reshape(64, COLS).astype(bf16)
    grad_cross = heads("khd,hkf->hdf", text_heads[:, 1], grad_values).reshape(COLS, D)
    value_part = jnp.concatenate((grad_cross, outer(grad_text_values, text), outer(attended, all_mid_one)), axis=0)
    (grad_qkv, layer_output, all_two, value_grad), pairs_got = causal_backward(
        5,
        qkv,
        grad_attended,
        logs,
        activated,
        contract,
        after,
        normed_two,
        value_part.astype(bf16).reshape(4, 2, 72, D),
        [Give(part) for part in pairs_t],
    )

    joined_part = outer(grad_qkv, all_one).astype(bf16).reshape(4, 2, 72, D)
    grad_keys = outer(grad_scores.reshape(D, COLS), all_two).astype(bf16).reshape(HEADS, 64, D)
    heads_query = whole(query_t, query_got).reshape(HEADS, HDIM, D)
    grad_text_keys = (heads("hkf,hdf->khd", grad_keys, heads_query) * EIGHTH).reshape(64, COLS).astype(bf16)
    grad_query = heads("khd,hkf->hdf", text_heads[:, 0], grad_keys).reshape(COLS, D) * EIGHTH
    key_part = jnp.concatenate((grad_query, outer(grad_text_keys, text)), axis=0).astype(bf16).reshape(4, 2, 48, D)
    text_part = dot(grad_text_keys, whole(pairs_t[0], pairs_got[0][0]))
    text_part += dot(grad_text_values, whole(pairs_t[1], pairs_got[1][0]))
    text_part = text_part.astype(bf16).reshape(8, 8, D)

    (input_grad, joined_grad, key_grad, parts, text_grad), ((layer_output,),) = leave(
        6,
        grad_qkv,
        joined,
        x,
        vectors,
        grad_one,
        (joined_part, key_part),
        late,
        text_part,
        [Relay(layer_output, True)],
    )
    joined_grad, key_grad, value_grad, expand_grad, contract_grad = (
        grad.reshape(-1, HALF).astype(f32) for grad in (joined_grad, key_grad, value_grad, expand_grad, contract_grad)
    )
    return (
        layer_output,
        input_grad.astype(f32),
        text_grad.reshape(2, 64, HALF).astype(f32),
        parts[0],
        parts[1],
        joined_grad[:COLS].T,
        joined_grad[COLS : 2 * COLS].T,
        joined_grad[2 * COLS :].T,
        value_grad[2 * COLS :],
        parts[2],
        parts[3],
        key_grad[:COLS].T,
        key_grad[COLS:].T,
        value_grad[COLS : 2 * COLS].T,
        value_grad[:COLS],
        parts[4],
        parts[5],
        expand_grad,
        contract_grad,
    )


def solution(mesh):
    return jax.shard_map(
        on_device,
        mesh=mesh,
        in_specs=(
            P(("dp", "wide"), "narrow"),
            P("dp", None, "narrow"),
            P(("dp", "wide"), "narrow"),
            P("narrow"),
            P("narrow"),
            P("narrow", "wide"),
            P("narrow", "wide"),
            P("narrow", "wide"),
            P("wide", "narrow"),
            P("narrow"),
            P("narrow"),
            P("narrow", "wide"),
            P("narrow", "wide"),
            P("narrow", "wide"),
            P("wide", "narrow"),
            P("narrow"),
            P("narrow"),
            P("narrow", "wide"),
            P("wide", "narrow"),
        ),
        out_specs=(
            P(("dp", "wide"), "narrow"),
            P(("dp", "wide"), "narrow"),
            P("dp", None, "narrow"),
            P("narrow"),
            P("narrow"),
            P("narrow", "wide"),
            P("narrow", "wide"),
            P("narrow", "wide"),
            P("wide", "narrow"),
            P("narrow"),
            P("narrow"),
            P("narrow", "wide"),
            P("narrow", "wide"),
            P("narrow", "wide"),
            P("wide", "narrow"),
            P("narrow"),
            P("narrow"),
            P("narrow", "wide"),
            P("wide", "narrow"),
        ),
        check_vma=False,
    )
```
